32 devices in a mesh: fsdp: 4 (over z), ctx: 4 (over x, core), tp: 2 (over y).
Axes of the slice: x: 2, y: 2, z: 4, core: 2. Of those that a mesh axis runs over, the one named last changes fastest.
Arguments:
- layer_input: bfloat16 [4, 8, 512, 768], P(None, 'fsdp', 'ctx'), may hold values from -6 to 6
- doc_ids: int32 [4, 8, 512], P(None, 'fsdp', 'ctx'), may hold values from 0 to 3, never falling along the last dimension, each value on 1 to 256 neighbouring positions
- w_qkv: bfloat16 [3, 768, 768], P(None, 'fsdp', 'tp'), may hold values from -0.21875 to 0.21875
- b_qv: float32 [2, 768], P(None, 'tp'), may hold values from -3 to 3
- w_out: bfloat16 [768, 768], P('tp', 'fsdp'), may hold values from -0.625 to 0.625
- b_out: float32 [768], replicated, may hold values from -2 to 2
- ln1_gain: float32 [768], replicated, may hold values from 0.1 to 1.9
- ln1_bias: float32 [768], replicated, may hold values from -2 to 2
- w_up: bfloat16 [768, 3072], P('fsdp', 'tp'), may hold values from -0.21875 to 0.21875
- b_up: float32 [3072], P('tp'), may hold values from -3 to 3
- w_down: bfloat16 [3072, 768], P('tp', 'fsdp'), may hold values from -0.109375 to 0.109375
- b_down: float32 [768], replicated, may hold values from -2 to 2
- ln2_gain: float32 [768], replicated, may hold values from 0.1 to 1.9
- ln2_bias: float32 [768], replicated, may hold values from -2 to 2
- out_grad: bfloat16 [4, 8, 512, 768], P(None, 'fsdp', 'ctx'), may hold values from -6 to 6
Outputs:
- layer_output: bfloat16 [4, 8, 512, 768], P(None, 'fsdp', 'ctx')
- grad_x: bfloat16 [4, 8, 512, 768], P(None, 'fsdp', 'ctx')
- grad_w_qkv: float32 [3, 768, 768], P(None, 'fsdp', 'tp')
- grad_b_qv: float32 [2, 768], P(None, 'tp')
- grad_w_out: float32 [768, 768], P('tp', 'fsdp')
- grad_b_out: float32 [768], replicated
- grad_ln1_gain: float32 [768], replicated
- grad_ln1_bias: float32 [768], replicated
- grad_w_up: float32 [768, 3072], P('fsdp', 'tp')
- grad_b_up: float32 [3072], P('tp')
- grad_w_down: float32 [3072, 768], P('tp', 'fsdp')
- grad_b_down: float32 [768], replicated
- grad_ln2_gain: float32 [768], replicated
- grad_ln2_bias: float32 [768], replicated
The draws below stay inside these ranges and needn't reach their ends.
Inputs may be any that keep to these rules, and one draw needn't show every extreme that they name: `doc_ids`: within each sequence of 512 tokens the ids never fall and each of the 4 ids marks one run of 1 to 256 tokens.
All inputs are finite; a program needn't handle non-finite values.
Results may differ from the reference program's by a relative error of at most 0.02.
Values may be sent and summed in bfloat16 or wider, within the bound.
No kernel may reach another device: no remote copies, remote signals or barrier semaphores. Data moves between devices by JAX's collectives and lax.ppermute only.
A program may use at most 128 MiB of HBM per device.

```python
import math
import jax
import jax.numpy as jnp
import numpy as np
from jax import lax

D = 768
HEADS = 12
HEAD_DIM = 64
FF = 3072
LEN = 512
MICRO = 4
DOCS = 4
DOC_MOST = 256
NSEQ = 8


def block_scale(key, extent, cuts, low, top_value):
    level = 1.0
    for axis_at, parts in cuts:
        steps = jax.random.uniform(jax.random.fold_in(jax.random.fold_in(key, 6), axis_at), (parts,), jnp.float32, low / len(cuts), top_value / len(cuts))
        level = level * jnp.repeat(jnp.exp(steps), extent[axis_at] // parts).reshape((-1,) + (1,) * (len(extent) - 1 - axis_at))
    return level


def split_up(count, total, reach, slope):
    loads = [(1 << 20) // math.isqrt(rank ** slope) + 1 for rank in range(2, count + 1)]
    surplus, counts = total - reach - (count - 1), [1] * (count - 1)
    while surplus > 0:
        candidates = [i for i in range(count - 1) if counts[i] < reach]
        mass, remaining = sum([loads[i] for i in candidates]), surplus
        for i in candidates:
            addition = min(reach - counts[i], max(1, remaining * loads[i] // mass), surplus)
            counts[i] = counts[i] + addition
            surplus = surplus - addition
    return np.array([reach] + counts)


def ragged_sizes(key, count, total, limit, lean):
    if count == 2:
        one = jax.random.randint(key, (), max(1, total - limit), min(limit, total - 1) + 1)
        return jnp.stack([one, total - one])
    sizes = jnp.asarray(split_up(count, total, limit, lean), jnp.int32)
    pairs = (count - 1) // 2
    donor, sink = sizes[1:1 + 2 * pairs:2], sizes[2:2 + 2 * pairs:2]
    room = jnp.minimum(donor - 1, limit - sink)
    passed = jax.random.randint(jax.random.fold_in(key, 1), (pairs,), 0, 1 << 20) % (room + 1)
    sizes = sizes.at[1:1 + 2 * pairs:2].set(donor - passed).at[2:2 + 2 * pairs:2].set(sink + passed)
    return sizes[jax.random.permutation(jax.random.fold_in(key, 2), count)]


def scatter_about(own_key, shape, scale, bound, cuts=(), dtype=jnp.bfloat16):
    values = jax.random.normal(own_key, shape, jnp.float32) * scale
    if len(cuts) > 0:
        values = block_scale(own_key, shape, cuts, -0.22, 0.18) * values
    return jnp.clip(values, min=-bound, max=bound).astype(dtype)


def setup_inputs(seed: int = 0) -> dict:
    keys = jax.random.split(jax.random.key(seed), 16)
    layer_input = scatter_about(keys[0], (MICRO, NSEQ, LEN, D), 1.0, 6.0, ((1, 4), (2, 4)))
    doc_ids = jax.vmap(lambda own: jnp.searchsorted(jnp.cumsum(ragged_sizes(own, DOCS, LEN, DOC_MOST, 1)), jnp.arange(LEN), side="right"))(jax.random.split(keys[1], MICRO * NSEQ)).reshape((MICRO, NSEQ, LEN)).astype(jnp.int32)
    w_qkv = scatter_about(keys[2], (3, D, D), D ** -0.5, 0.21875, ((1, 4), (2, 2)))
    b_qv = scatter_about(keys[3], (2, D), 0.5, 3.0, ((1, 2),), jnp.float32)
    w_out = scatter_about(keys[4], (D, D), (D // 8) ** -0.5, 0.625, ((0, 2), (1, 4)))
    b_out = scatter_about(keys[5], (D,), 0.3, 2.0, (), jnp.float32)
    ln1_gain = jnp.clip(1.0 + 0.18 * jax.random.normal(keys[6], (D,), jnp.float32), 0.1, 1.9)
    ln1_bias = scatter_about(keys[7], (D,), 0.3, 2.0, (), jnp.float32)
    w_up = scatter_about(keys[8], (D, FF), D ** -0.5, 0.21875, ((0, 4), (1, 2)))
    b_up = scatter_about(keys[9], (FF,), 0.5, 3.0, ((0, 2),), jnp.float32)
    w_down = scatter_about(keys[10], (FF, D), FF ** -0.5, 0.109375, ((0, 2), (1, 4)))
    b_down = scatter_about(keys[11], (D,), 0.3, 2.0, (), jnp.float32)
    ln2_gain = jnp.clip(1.0 + 0.18 * jax.random.normal(keys[12], (D,), jnp.float32), 0.1, 1.9)
    ln2_bias = scatter_about(keys[13], (D,), 0.3, 2.0, (), jnp.float32)
    out_grad = scatter_about(keys[14], (MICRO, NSEQ, LEN, D), 1.0, 6.0, ((1, 4), (2, 4)))
    return {"layer_input": layer_input, "doc_ids": doc_ids, "w_qkv": w_qkv, "b_qv": b_qv, "w_out": w_out, "b_out": b_out, "ln1_gain": ln1_gain, "ln1_bias": ln1_bias, "w_up": w_up, "b_up": b_up, "w_down": w_down, "b_down": b_down, "ln2_gain": ln2_gain, "ln2_bias": ln2_bias, "out_grad": out_grad}


@jax.custom_vjp
def low(v):
    return lax.optimization_barrier(v.astype(jnp.bfloat16)).astype(jnp.float32)

@jax.custom_vjp
def low_back(v):
    return v

def low_keep(v):
    return (low(v), None)

def low_pass(kept, grad):
    return (grad,)

def back_keep(v):
    return (v, None)

def back_low(kept, grad):
    return (low(grad),)
low.defvjp(low_keep, low_pass)
low_back.defvjp(back_keep, back_low)

def normalize(values_in, gain, shift):
    mean = lax.optimization_barrier(jnp.mean(values_in, axis=-1, keepdims=True))
    centred = values_in - mean
    var = lax.optimization_barrier(jnp.mean(centred * centred, axis=-1, keepdims=True))
    return centred * lax.rsqrt(var + 1e-12) * gain + shift

def layer(params, rows, ids):
    w_qkv, b_qv, w_out, b_out, ln1_gain, ln1_bias, w_up, b_up, w_down, b_down, ln2_gain, ln2_bias = params
    highest = lax.Precision.HIGHEST
    bias_three = jnp.stack([b_qv[0], jnp.zeros_like(b_qv[0]), b_qv[1]])
    proj = jnp.einsum('td,cde->cte', rows, w_qkv, precision=highest) + bias_three[:, None, :]
    proj = low(low_back(proj))
    length = rows.shape[0]
    split = proj.reshape(3, length, HEADS, HEAD_DIM)
    query, keys_all, values_all = (split[0], split[1], split[2])
    scores = low_back(0.125 * jnp.einsum('qhd,khd->hqk', query, keys_all, precision=highest))
    allowed = ids[:, None] == ids[None, :]
    masked = jnp.where(allowed[None], scores, -1e+30)
    probs = low(jax.nn.softmax(masked, axis=-1))
    mixed = jnp.einsum('hqk,khd->qhd', probs, values_all, precision=highest).reshape(length, D)
    mixed = low(low_back(mixed))
    branch = low_back(jnp.dot(mixed, w_out, precision=highest))
    first = normalize(rows + branch + b_out, ln1_gain, ln1_bias)
    hidden = low_back(jnp.dot(low(first), w_up, precision=highest) + b_up)
    activation = low(jax.nn.gelu(hidden, approximate=False))
    second = low_back(jnp.dot(activation, w_down, precision=highest))
    return normalize(first + second + b_down, ln2_gain, ln2_bias)

def reference(layer_input, doc_ids, w_qkv, b_qv, w_out, b_out, ln1_gain, ln1_bias, w_up, b_up, w_down, b_down, ln2_gain, ln2_bias, out_grad):
    params = tuple((weight.astype(jnp.float32) for weight in (w_qkv, b_qv, w_out, b_out, ln1_gain, ln1_bias, w_up, b_up, w_down, b_down, ln2_gain, ln2_bias)))
    number = layer_input.shape[0] * layer_input.shape[1]
    rows_all = layer_input.astype(jnp.float32).reshape(number, LEN, D)
    ids_all = doc_ids.reshape(number, LEN)
    cot_all = out_grad.astype(jnp.float32).reshape(number, LEN, D)

    def advance(running, element):
        rows, ids, cotangent = element
        result, pullback = jax.vjp(lambda params_now, rows_now: layer(params_now, rows_now, ids), params, rows)
        grad_params, grad_rows = pullback(cotangent)
        running = jax.tree.map(lambda left, right: left + right, running, grad_params)
        return (running, (result.astype(jnp.bfloat16), grad_rows.astype(jnp.bfloat16)))
    zero_tree = jax.tree.map(jnp.zeros_like, params)
    running, (outputs, grad_rows) = lax.scan(advance, zero_tree, (rows_all, ids_all, cot_all))
    return (outputs.reshape(layer_input.shape), grad_rows.reshape(layer_input.shape), running[0], running[1], running[2], running[3], running[4], running[5], running[6], running[7], running[8], running[9], running[10], running[11])
```

```python
import functools
import jax
import jax.numpy as jnp
from jax import lax
from jax.experimental import pallas as pl
from jax.experimental.pallas import tpu as pltpu
from jax.sharding import PartitionSpec as P

HEAD_DIM = 64
AXES = ("fsdp", "ctx", "tp")
F32 = jnp.float32
BF16 = jnp.bfloat16
NEG = -1e30


def normalize_rows(values_in):
    mean = jnp.mean(values_in, axis=-1, keepdims=True)
    centred = values_in - mean
    var = jnp.mean(centred * centred, axis=-1, keepdims=True)
    scale = lax.rsqrt(var + 1e-12)
    return (centred * scale, scale)


def normalize_back(grad_hat, normed, scale):
    first_mean = jnp.mean(grad_hat, axis=-1, keepdims=True)
    second_mean = jnp.mean(grad_hat * normed, axis=-1, keepdims=True)
    return scale * (grad_hat - first_mean - normed * second_mean)


def partner(dim, z, c, t):
    if dim == "core":
        return z, c ^ 1, t
    if dim == "x":
        return z, c ^ 2, t
    if dim == "y":
        return z, c, t ^ 1
    return z ^ int(dim[1:]), c, t


def exchange(value, dims, sizes):
    nz, nc, nt = sizes
    pairs = []
    for z in range(nz):
        for c in range(nc):
            for t in range(nt):
                tz, tc, tt = partner(dims[c & 1], z, c, t)
                pairs.append(((z * nc + c) * nt + t, (tz * nc + tc) * nt + tt))
    return lax.ppermute(value, AXES, pairs)


GATHER_ORDER = (("z1", "z2", "y", "x"), ("z1", "z2", "x", "y"))
SCATTER_ORDER = (("x", "y", "z1", "z2"), ("y", "z1", "z2", "x"))
PACK_ORDER = tuple(order[::-1] for order in SCATTER_ORDER)


def piece_place(order, core, here, index):
    z, x, t = here
    for bit, dim in enumerate(order):
        flip = (index >> bit) & 1
        if dim == "x":
            x = x ^ flip
        elif dim == "y":
            t = t ^ flip
        else:
            z = z ^ (flip * int(dim[1:]))
    return z * 4 + x * 2 + core, t


def position():
    c = lax.axis_index("ctx")
    return lax.axis_index("fsdp"), lax.div(c, 2), lax.rem(c, 2), lax.axis_index("tp")


def places(orders):
    z, x, k, t = position()
    rows = []
    for mine in (0, 1):
        core = k if mine == 0 else 1 - k
        for i in range(16):
            r0, t0 = piece_place(orders[0], core, (z, x, t), i)
            r1, t1 = piece_place(orders[1], core, (z, x, t), i)
            rows.append(jnp.where(core == 0, r0, r1))
            rows.append(jnp.where(core == 0, t0, t1))
    return jnp.stack(rows).astype(jnp.int32)


def unpack_kernel(place_ref, own_ref, sib_ref, out_ref, sem):
    rows, cols = own_ref.shape[1:]
    copies = []
    for half, ref in ((0, own_ref), (1, sib_ref)):
        for i in range(16):
            at = (half * 16 + i) * 2
            row = pl.multiple_of(place_ref[at] * rows, rows)
            col = pl.multiple_of(place_ref[at + 1] * cols, cols)
            copy = pltpu.make_async_copy(
                ref.at[i], out_ref.at[pl.ds(row, rows), pl.ds(col, cols)], sem.at[half * 16 + i]
            )
            copy.start()
            copies.append(copy)
    for copy in copies:
        copy.wait()


def unpack(place, own, sib):
    _, rows, cols = own.shape
    return pl.pallas_call(
        unpack_kernel,
        out_shape=jax.ShapeDtypeStruct((16 * rows, 2 * cols), own.dtype),
        in_specs=[
            pl.BlockSpec(memory_space=pltpu.SMEM),
            pl.BlockSpec(memory_space=pl.ANY),
            pl.BlockSpec(memory_space=pl.ANY),
        ],
        out_specs=pl.BlockSpec(memory_space=pltpu.VMEM),
        scratch_shapes=[pltpu.SemaphoreType.DMA((32,))],
        cost_estimate=pl.CostEstimate(flops=0, transcendentals=0, bytes_accessed=4 * own.size * 2 * 2),
    )(place, own, sib)


def gather_weight(shard, place, sizes):
    rows, cols = shard.shape
    part = rows // 4
    mine = lax.dynamic_slice_in_dim(shard, lax.axis_index("ctx") * part, part, 0)[None]
    for step in range(4):
        got = exchange(mine, (GATHER_ORDER[0][step], GATHER_ORDER[1][step]), sizes)
        mine = jnp.concatenate([mine, got], axis=0)
    return unpack(place, mine, exchange(mine, ("core", "core"), sizes))


def dw_kernel(place_ref, a_ref, b_ref, own_ref, sib_ref, full, sem):
    rows, cols = own_ref.shape[1:]
    a_t = a_ref[...].T
    for half in range(2):
        full[:, half * cols : (half + 1) * cols] = jnp.dot(
            a_t, b_ref[:, half * cols : (half + 1) * cols], preferred_element_type=F32
        ).astype(BF16)
    copies = []
    for half, ref in ((1, sib_ref), (0, own_ref)):
        for i in range(16):
            at = (half * 16 + i) * 2
            row = pl.multiple_of(place_ref[at] * rows, rows)
            col = pl.multiple_of(place_ref[at + 1] * cols, cols)
            copy = pltpu.make_async_copy(
                full.at[pl.ds(row, rows), pl.ds(col, cols)], ref.at[i], sem.at[half * 16 + i]
            )
            copy.start()
            copies.append(copy)
    for copy in copies:
        copy.wait()


def weight_pieces(place, a, b):
    tokens, width = a.shape
    wide = b.shape[1]
    shape = jax.ShapeDtypeStruct((16, width // 16, wide // 2), BF16)
    return pl.pallas_call(
        dw_kernel,
        out_shape=(shape, shape),
        in_specs=[
            pl.BlockSpec(memory_space=pltpu.SMEM),
            pl.BlockSpec(memory_space=pltpu.VMEM),
            pl.BlockSpec(memory_space=pltpu.VMEM),
        ],
        out_specs=(pl.BlockSpec(memory_space=pl.ANY), pl.BlockSpec(memory_space=pl.ANY)),
        scratch_shapes=[pltpu.VMEM((width, wide), BF16), pltpu.SemaphoreType.DMA((32,))],
        cost_estimate=pl.CostEstimate(
            flops=2 * tokens * width * wide,
            transcendentals=0,
            bytes_accessed=2 * (tokens * (width + wide) + width * wide),
        ),
    )(place, a, b)


def add_up(left, right):
    return (left.astype(F32) + right.astype(F32)).astype(BF16)


def reduce_grad(place, a, b, sizes):
    own, sib = weight_pieces(place, a, b)
    acc = add_up(own, exchange(sib, ("core", "core"), sizes))
    for step in range(4):
        half = acc.shape[0] // 2
        got = exchange(acc[half:], (SCATTER_ORDER[0][step], SCATTER_ORDER[1][step]), sizes)
        acc = add_up(acc[:half], got)
    return lax.all_gather(acc[0], "ctx", axis=0, tiled=True).astype(F32)


def attend_kernel(q_ref, k_ref, v_ref, idc_ref, idr_ref, o_ref, p_ref):
    length = q_ref.shape[0]
    lane = lax.broadcasted_iota(jnp.int32, (1, 128), 1)
    keys, values = k_ref[...], v_ref[...]
    block = 128
    for at in range(0, length, block):
        rows = pl.ds(at, block)
        query = q_ref[rows, :]
        allowed = idc_ref[rows, :] == idr_ref[...]
        outs = []
        for head in range(2):
            here = (lane >= 64 * head) & (lane < 64 * head + 64)
            one = jnp.where(here, query, jnp.zeros_like(query))
            scores = lax.dot_general(one, keys, (((1,), (1,)), ((), ())), preferred_element_type=F32)
            masked = jnp.where(allowed, scores * 0.125, NEG)
            top = jnp.max(masked, axis=-1, keepdims=True)
            raised = jnp.exp(masked - top)
            probs = (raised * (1.0 / jnp.sum(raised, axis=-1, keepdims=True))).astype(BF16)
            p_ref[head, rows, :] = probs
            outs.append(jnp.dot(probs, values, preferred_element_type=F32))
        o_ref[rows, :] = jnp.where(lane < 64, outs[0], outs[1]).astype(BF16)


def attend(proj, ids, heads):
    length = proj.shape[0]
    pairs = heads // 2
    half = pairs // 2
    spot = lambda which: pl.BlockSpec(
        (length, 128), lambda g: (0, (g // half) * 3 * half + which * half + g % half)
    )
    return pl.pallas_call(
        attend_kernel,
        grid=(pairs,),
        out_shape=(
            jax.ShapeDtypeStruct((length, heads * HEAD_DIM), BF16),
            jax.ShapeDtypeStruct((heads, length, length), BF16),
        ),
        in_specs=[
            spot(0),
            spot(1),
            spot(2),
            pl.BlockSpec((length, 1), lambda g: (0, 0)),
            pl.BlockSpec((1, length), lambda g: (0, 0)),
        ],
        out_specs=(
            pl.BlockSpec((length, 128), lambda g: (0, g)),
            pl.BlockSpec((2, length, length), lambda g: (g, 0, 0)),
        ),
        cost_estimate=pl.CostEstimate(
            flops=8 * heads * length * length * HEAD_DIM * 2,
            transcendentals=heads * length * length,
            bytes_accessed=2 * heads * length * length + 8 * length * heads * HEAD_DIM,
        ),
    )(proj, proj, proj, ids[:, None], ids[None, :])


def attend_back_kernel(q_ref, k_ref, v_ref, p_ref, g_ref, dq_ref, dk_ref, dv_ref):
    length = q_ref.shape[0]
    lane = lax.broadcasted_iota(jnp.int32, (1, 128), 1)
    query, keys, values, grad = q_ref[...], k_ref[...], v_ref[...], g_ref[...]
    block = 128
    dks, dvs = [], []
    dqs = [[], []]
    for head in range(2):
        here = (lane >= 64 * head) & (lane < 64 * head + 64)
        only = jnp.where(here, grad, jnp.zeros_like(grad))
        parts = []
        for at in range(0, length, block):
            probs = p_ref[head, at : at + block, :]
            wide = probs.astype(F32)
            gp = lax.dot_general(
                only[at : at + block], values, (((1,), (1,)), ((), ())), preferred_element_type=F32
            )
            weighted = jnp.sum(wide * gp, axis=-1, keepdims=True)
            gs = (wide * (gp - weighted)).astype(BF16)
            dqs[head].append(jnp.dot(gs, keys, preferred_element_type=F32))
            parts.append(gs)
        gs = jnp.concatenate(parts, axis=0)
        dks.append(lax.dot_general(gs, query, (((0,), (0,)), ((), ())), preferred_element_type=F32))
        dvs.append(
            lax.dot_general(p_ref[head], grad, (((0,), (0,)), ((), ())), preferred_element_type=F32)
        )
    low = lane < 64
    dq = jnp.where(low, jnp.concatenate(dqs[0], axis=0), jnp.concatenate(dqs[1], axis=0))
    dq_ref[...] = (dq * 0.125).astype(BF16)
    dk_ref[...] = (jnp.where(low, dks[0], dks[1]) * 0.125).astype(BF16)
    dv_ref[...] = jnp.where(low, dvs[0], dvs[1]).astype(BF16)


def attend_back(proj, probs, grad_mixed, heads):
    length = proj.shape[0]
    pairs = heads // 2
    half = pairs // 2
    spot = lambda which: pl.BlockSpec(
        (length, 128), lambda g: (0, (g // half) * 3 * half + which * half + g % half)
    )
    plain = pl.BlockSpec((length, 128), lambda g: (0, g))
    shape = jax.ShapeDtypeStruct((length, heads * HEAD_DIM), BF16)
    return pl.pallas_call(
        attend_back_kernel,
        grid=(pairs,),
        out_shape=(shape, shape, shape),
        in_specs=[
            spot(0),
            spot(1),
            spot(2),
            pl.BlockSpec((2, length, length), lambda g: (g, 0, 0)),
            plain,
        ],
        out_specs=(plain, plain, plain),
        cost_estimate=pl.CostEstimate(
            flops=16 * heads * length * length * HEAD_DIM * 2,
            transcendentals=0,
            bytes_accessed=2 * heads * length * length + 14 * length * heads * HEAD_DIM,
        ),
    )(proj, proj, proj, probs, grad_mixed)


def split_halves(value, parts):
    half = value[0].shape[1] // 2
    return jnp.concatenate(
        [part[:, y * half : (y + 1) * half] for y in range(2) for part in value], axis=1
    )


def body(
    layer_input,
    doc_ids,
    w_qkv,
    b_qv,
    w_out,
    b_out,
    ln1_gain,
    ln1_bias,
    w_up,
    b_up,
    w_down,
    b_down,
    ln2_gain,
    ln2_bias,
    out_grad,
):
    sizes = (lax.axis_size("fsdp"), lax.axis_size("ctx"), lax.axis_size("tp"))
    micro, seqs, local_len, width = layer_input.shape
    length = local_len * sizes[1]
    shard_rows, local_width = w_qkv.shape[1:]
    local_units = w_up.shape[1]
    heads = width // HEAD_DIM
    fast = sizes == (4, 4, 2)
    t = lax.axis_index("tp")
    c = lax.axis_index("ctx")

    def gather(shard):
        if fast:
            return gather_weight(shard, places(GATHER_ORDER), sizes)
        rows = lax.all_gather(shard, "fsdp", axis=0, tiled=True)
        return lax.all_gather(rows, "tp", axis=1, tiled=True)

    def reduce(a, b):
        if fast:
            return reduce_grad(places(PACK_ORDER), a, b, sizes)
        full = lax.dot_general(a, b, (((0,), (0,)), ((), ())), preferred_element_type=F32)
        part = lax.psum_scatter(full.astype(BF16), "tp", scatter_dimension=1, tiled=True)
        part = lax.psum_scatter(part, "fsdp", scatter_dimension=0, tiled=True)
        return lax.psum(part, "ctx").astype(F32)

    def whole_sequence(value):
        mine = lax.dynamic_index_in_dim(value, t, 1, keepdims=False)
        return lax.all_to_all(mine, "ctx", 0, 0, tiled=True).reshape(length, width)

    def spread_sequence(value):
        chunks = jnp.broadcast_to(
            value.reshape(sizes[1], 1, local_len, width), (sizes[1], sizes[2], local_len, width)
        ).reshape(sizes[1] * sizes[2], local_len, width)
        out = lax.all_to_all(chunks, ("ctx", "tp"), 0, 0, tiled=True)
        return out.reshape(micro, seqs, local_len, width)

    wq_shard = jnp.swapaxes(w_qkv, 0, 1).reshape(shard_rows, 3 * local_width)
    rows_b = whole_sequence(layer_input)
    wq = gather(wq_shard)
    all_ids = lax.all_gather(doc_ids, "ctx", axis=2, tiled=True)
    ids = lax.dynamic_index_in_dim(
        lax.dynamic_index_in_dim(all_ids, c, 0, keepdims=False), t, 0, keepdims=False
    )
    small = jnp.concatenate([b_qv.reshape(-1), b_up])
    small = lax.all_gather(small, "tp", axis=0, tiled=False)
    bias_qv = small[:, : 2 * local_width].reshape(2, 2, local_width)
    bias_three = jnp.stack(
        [bias_qv[:, 0], jnp.zeros_like(bias_qv[:, 0]), bias_qv[:, 1]], axis=1
    ).reshape(-1)
    bias_up = small[:, 2 * local_width :].reshape(-1)

    cot = whole_sequence(out_grad)
    wo_t = gather(w_out.T)
    wu = gather(w_up)
    wd_t = gather(w_down.T)

    rows_f = rows_b.astype(F32)
    proj = (jnp.dot(rows_b, wq, preferred_element_type=F32) + bias_three).astype(BF16)
    mixed, probs = attend(proj, ids, heads)
    nt = (((1,), (1,)), ((), ()))
    branch = lax.dot_general(mixed, wo_t, nt, preferred_element_type=F32)
    normed1, scale1 = normalize_rows(rows_f + branch + b_out)
    first = normed1 * ln1_gain + ln1_bias
    first_b = first.astype(BF16)
    hidden = jnp.dot(first_b, wu, preferred_element_type=F32) + bias_up
    activation, gelu_pull = jax.vjp(lambda value: jax.nn.gelu(value, approximate=False), hidden)
    act_b = activation.astype(BF16)
    second = lax.dot_general(act_b, wd_t, nt, preferred_element_type=F32)
    normed2, scale2 = normalize_rows(first + second + b_down)
    result = (normed2 * ln2_gain + ln2_bias).astype(BF16)
    layer_output = spread_sequence(result)

    incoming = cot.astype(F32)
    grad_gain2 = jnp.sum(incoming * normed2, axis=0)
    grad_shift2 = jnp.sum(incoming, axis=0)
    grad_z2 = normalize_back(incoming * ln2_gain, normed2, scale2)
    grad_bdown = jnp.sum(grad_z2, axis=0)
    grad_second = grad_z2.astype(BF16)
    grad_wdown = reduce(grad_second, act_b)
    grad_act = jnp.dot(grad_second, wd_t, preferred_element_type=F32)
    (grad_hidden,) = gelu_pull(grad_act)
    grad_hidden = grad_hidden.astype(BF16)
    grad_bup = jnp.sum(grad_hidden.astype(F32), axis=0)
    grad_wup = reduce(first_b, grad_hidden)
    grad_first = grad_z2 + lax.dot_general(grad_hidden, wu, nt, preferred_element_type=F32)
    grad_gain1 = jnp.sum(grad_first * normed1, axis=0)
    grad_shift1 = jnp.sum(grad_first, axis=0)
    grad_z1 = normalize_back(grad_first * ln1_gain, normed1, scale1)
    grad_bout = jnp.sum(grad_z1, axis=0)
    grad_branch = grad_z1.astype(BF16)
    grad_wout = reduce(grad_branch, mixed)
    grad_mixed = jnp.dot(grad_branch, wo_t, preferred_element_type=F32).astype(BF16)
    dq, dk, dv = attend_back(proj, probs, grad_mixed, heads)
    grad_bqv = jnp.stack([jnp.sum(dq.astype(F32), axis=0), jnp.sum(dv.astype(F32), axis=0)])
    grad_proj = split_halves((dq, dk, dv), 3)
    grad_wq = reduce(rows_b, grad_proj)
    back = lax.dot_general(grad_proj, wq, nt, preferred_element_type=F32)
    grad_x = spread_sequence((grad_z1 + back).astype(BF16))

    vectors = (
        grad_bqv.reshape(-1),
        grad_bout,
        grad_gain1,
        grad_shift1,
        grad_bup,
        grad_bdown,
        grad_gain2,
        grad_shift2,
    )
    flat = lax.psum(jnp.concatenate(vectors), AXES)
    cuts = []
    at = 0
    for vector in vectors:
        cuts.append(flat[at : at + vector.shape[0]])
        at += vector.shape[0]
    out_bqv = lax.dynamic_slice_in_dim(cuts[0].reshape(2, width), t * local_width, local_width, 1)
    out_bup = lax.dynamic_slice_in_dim(cuts[4], t * local_units, local_units, 0)
    return (
        layer_output,
        grad_x,
        jnp.swapaxes(grad_wq.reshape(shard_rows, 3, local_width), 0, 1),
        out_bqv,
        grad_wout.T,
        cuts[1],
        cuts[2],
        cuts[3],
        grad_wup,
        out_bup,
        grad_wdown.T,
        cuts[5],
        cuts[6],
        cuts[7],
    )


def solution(mesh):
    return jax.shard_map(
        body,
        mesh=mesh,
        in_specs=(
            P(None, "fsdp", "ctx", None),
            P(None, "fsdp", "ctx"),
            P(None, "fsdp", "tp"),
            P(None, "tp"),
            P("tp", "fsdp"),
            P(),
            P(),
            P(),
            P("fsdp", "tp"),
            P("tp"),
            P("tp", "fsdp"),
            P(),
            P(),
            P(),
            P(None, "fsdp", "ctx", None),
        ),
        out_specs=(
            P(None, "fsdp", "ctx", None),
            P(None, "fsdp", "ctx", None),
            P(None, "fsdp", "tp"),
            P(None, "tp"),
            P("tp", "fsdp"),
            P(),
            P(),
            P(),
            P("fsdp", "tp"),
            P("tp"),
            P("tp", "fsdp"),
            P(),
            P(),
            P(),
        ),
        check_vma=False,
    )
```

```python
import jax
import jax.numpy as jnp
from jax import lax
from jax.experimental import pallas as pl
from jax.experimental.pallas import tpu as pltpu
from jax.sharding import PartitionSpec as P

HEAD_DIM = 64
AXES = ("fsdp", "ctx", "tp")
F32 = jnp.float32
BF16 = jnp.bfloat16
NEG = -1e30
NT = (((1,), (1,)), ((), ()))
VMEM = pl.BlockSpec(memory_space=pltpu.VMEM)
SMEM = pl.BlockSpec(memory_space=pltpu.SMEM)
ANY = pl.BlockSpec(memory_space=pl.ANY)


def partner(dim, z, c, t):
    if dim == "core":
        return z, c ^ 1, t
    if dim == "x":
        return z, c ^ 2, t
    if dim == "y":
        return z, c, t ^ 1
    return z ^ int(dim[1:]), c, t


def exchange(value, dims, sizes):
    nz, nc, nt = sizes
    pairs = []
    for z in range(nz):
        for c in range(nc):
            for t in range(nt):
                tz, tc, tt = partner(dims[c & 1], z, c, t)
                pairs.append(((z * nc + c) * nt + t, (tz * nc + tc) * nt + tt))
    return lax.ppermute(value, AXES, pairs)


GATHER_ORDER = (("z2", "z1", "y", "x"), ("z2", "z1", "x", "y"))
SCATTER_ORDER = (("x", "y", "z1", "z2"), ("y", "z1", "z2", "x"))
PACK_ORDER = tuple(order[::-1] for order in SCATTER_ORDER)
CORE = (("core", "core"),)
GATHER_STEPS = tuple(zip(*GATHER_ORDER)) + CORE
SCATTER_STEPS = CORE + tuple(zip(*SCATTER_ORDER))


def piece_place(order, core, here, index):
    z, x, t = here
    for bit, dim in enumerate(order):
        flip = (index >> bit) & 1
        if dim == "x":
            x = x ^ flip
        elif dim == "y":
            t = t ^ flip
        else:
            z = z ^ (flip * int(dim[1:]))
    return z * 4 + x * 2 + core, t


def places(orders):
    c = lax.axis_index("ctx")
    here = (lax.axis_index("fsdp"), lax.div(c, 2), lax.axis_index("tp"))
    k = lax.rem(c, 2)
    rows = []
    for core in (k, 1 - k):
        for i in range(16):
            r0, t0 = piece_place(orders[0], core, here, i)
            r1, t1 = piece_place(orders[1], core, here, i)
            rows.append(jnp.where(core == 0, r0, r1))
            rows.append(jnp.where(core == 0, t0, t1))
    return jnp.stack(rows + [here[2]]).astype(jnp.int32)


def plain_places():
    rows = [place for half in range(2) for i in range(16) for place in (i, half)]
    return jnp.stack([jnp.asarray(row) for row in rows] + [lax.axis_index("tp")]).astype(jnp.int32)


def after(value, *first):
    return lax.optimization_barrier((value, first))[0]


def piece_copies(info_ref, own_ref, sib_ref, sem, whole, low, cols, collect, base=0):
    rows = own_ref.shape[1]
    stride = whole.shape[1] // 2
    copies = []
    for half, ref in ((0, own_ref), (1, sib_ref)):
        for i in range(16):
            at = (half * 16 + i) * 2
            row = pl.multiple_of(info_ref[at] * rows, rows)
            col = pl.multiple_of(info_ref[at + 1] * stride, 128)
            one = ref.at[i, :, pl.ds(low, cols)]
            two = whole.at[pl.ds(row, rows), pl.ds(col, cols)]
            src, dst = (one, two) if collect else (two, one)
            copy = pltpu.make_async_copy(src, dst, sem.at[base + half * 16 + i])
            copy.start()
            copies.append(copy)
    return copies


def finish(copies):
    for copy in copies:
        copy.wait()


def tiles(count, step):
    def run(one):
        lax.fori_loop(0, count // step, lambda i, carry: (one(pl.multiple_of(i * step, step)), carry)[1], 0)

    return run


def row_mean(value):
    return jnp.mean(value, axis=-1, keepdims=True)


def struct(shape, dtype):
    return jax.ShapeDtypeStruct(shape, dtype)


def call(kernel, name, outs, specs, out_specs, scratch, time, room, args):
    return pl.pallas_call(
        kernel,
        name=name,
        out_shape=outs,
        in_specs=specs,
        out_specs=out_specs,
        scratch_shapes=scratch,
        compiler_params=pltpu.CompilerParams(vmem_limit_bytes=room << 20),
        cost_estimate=pl.CostEstimate(flops=time * 10**9, transcendentals=0, bytes_accessed=10**6),
    )(*args)


B_OUT, GAIN1, SHIFT1, B_DOWN, GAIN2, SHIFT2 = range(6)


def unpack_kernel(info_ref, own_ref, sib_ref, *refs):
    outs, sem = refs[:-1], refs[-1]
    copies = []
    low = 0
    for i, out in enumerate(outs):
        cols = out.shape[1] // 2
        copies += piece_copies(info_ref, own_ref, sib_ref, sem, out, low, cols, True, 32 * i)
        low += cols
    finish(copies)


def unpack(info, own, sib, widths):
    rows = own.shape[0] * own.shape[1]
    return call(
        unpack_kernel,
        "unpack",
        tuple(struct((rows, width), BF16) for width in widths),
        [SMEM, ANY, ANY],
        (VMEM,) * len(widths),
        [pltpu.SemaphoreType.DMA((32 * len(widths),))],
        5,
        16,
        (info, own, sib),
    )


def project_kernel(info_ref, weight_ref, given_ref, small_ref, proj_ref, x_ref, mask_ref):
    count, more = given_ref.shape[:2]
    block = more - 8
    for i in range(count):
        x_ref[i * block : (i + 1) * block, :] = given_ref[i, 0:block, :]
    ids = [given_ref[i, block : block + 8, 0:block].astype(F32)[0:1] for i in range(count)]
    for kb in range(count):
        column = jnp.broadcast_to(ids[kb], (block, block)).T
        for qb in range(count):
            mask_ref[kb * block : (kb + 1) * block, qb * block : (qb + 1) * block] = jnp.where(
                column == jnp.broadcast_to(ids[qb], (block, block)), 0.0, NEG
            )
    width = proj_ref.shape[1] // 6
    for y in range(2):
        row = pl.ds(info_ref[64] ^ y, 1)
        for which in range(3):
            at = (y * 3 + which) * width
            value = jnp.dot(x_ref[...], weight_ref[:, at : at + width], preferred_element_type=F32)
            if which != 1:
                low = 0 if which == 0 else width
                value = value + small_ref[row, low : low + width]
            proj_ref[:, at : at + width] = value.astype(BF16)


def project(info, weight, given, small):
    width, wide = weight.shape
    length = given.shape[0] * (given.shape[1] - 8)
    return call(
        project_kernel,
        "project",
        (struct((length, wide), BF16), struct((length, width), BF16), struct((length, length), F32)),
        [SMEM, VMEM, VMEM, VMEM],
        (VMEM,) * 3,
        [],
        5,
        16,
        (info, weight, given, small),
    )


def attend_kernel(proj_ref, mask_ref, o_ref, p_ref, *, y):
    length = proj_ref.shape[0]
    pairs = o_ref.shape[1] // 128
    lane = lax.broadcasted_iota(jnp.int32, (1, 128), 1)

    def pair(g, carry):
        take = lambda which: proj_ref[:, pl.ds(pl.multiple_of(((y * 3 + which) * pairs + g) * 128, 128), 128)]
        query = take(0) * jnp.asarray(0.125, BF16)
        keys = take(1)
        values_t = take(2).T
        outs = []
        for head in range(2):
            here = (lane >= 64 * head) & (lane < 64 * head + 64)
            only = jnp.where(here, keys, jnp.zeros_like(keys))
            row = []
            for at in range(0, length, 256):
                scores = lax.dot_general(only, query[at : at + 256], NT, preferred_element_type=F32)
                scores = scores + mask_ref[:, at : at + 256]
                top = jnp.max(scores, axis=0, keepdims=True)
                raised = jnp.exp(scores - top)
                total = jnp.sum(raised, axis=0, keepdims=True)
                probs = (raised * (1.0 / total)).astype(BF16)
                p_ref[2 * g + head, :, at : at + 256] = probs
                row.append(
                    jnp.dot(values_t[64 * head : 64 * head + 64], probs, preferred_element_type=F32)
                )
            outs.append(jnp.concatenate(row, axis=1))
        both = jnp.concatenate(outs, axis=0).astype(BF16)
        o_ref[:, pl.ds(pl.multiple_of(g * 128, 128), 128)] = both.T
        return carry

    lax.fori_loop(0, pairs, pair, 0)


def attend(proj, mask, y):
    length, wide = proj.shape
    half = wide // 6
    return call(
        lambda *refs: attend_kernel(*refs, y=y),
        "attend",
        (struct((length, half), BF16), struct((half // HEAD_DIM, length, length), BF16)),
        [VMEM, VMEM],
        (VMEM, VMEM),
        [],
        12,
        16,
        (proj, mask),
    )


def middle_kernel(
    info_ref, w_out, w_up, mixed0_ref, mixed1_ref, x_ref, table_ref, small_ref,
    normed_ref, scale_ref, first_ref, act_ref, slope_ref,
):
    length, units = act_ref.shape
    narrow, half = w_out.shape[1] // 2, units // 2
    normed_ref[...] = lax.dot_general(
        mixed0_ref[...], w_out[:, :narrow], NT, preferred_element_type=F32
    ) + lax.dot_general(mixed1_ref[...], w_out[:, narrow:], NT, preferred_element_type=F32)

    @tiles(length, 64)
    def _(at):
        here = pl.ds(at, 64)
        value = x_ref[here, :].astype(F32) + normed_ref[here, :] + table_ref[B_OUT : B_OUT + 1, :]
        centred = value - row_mean(value)
        scale = lax.rsqrt(row_mean(centred * centred) + 1e-12)
        unit = centred * scale
        normed_ref[here, :] = unit
        scale_ref[here, :] = scale
        first_ref[here, :] = (
            unit * table_ref[GAIN1 : GAIN1 + 1, :] + table_ref[SHIFT1 : SHIFT1 + 1, :]
        ).astype(BF16)

    for y in range(2):
        row = pl.ds(info_ref[64] ^ y, 1)

        @tiles(half, 256)
        def _(at):
            here = pl.ds(pl.multiple_of(y * half + at, 256), 256)
            bias = small_ref[row, pl.ds(pl.multiple_of(2 * narrow + at, 256), 256)]
            hidden = jnp.dot(first_ref[...], w_up[:, here], preferred_element_type=F32) + bias
            phi = 0.5 + 0.5 * lax.erf(hidden * 0.7071067811865476)
            act_ref[:, here] = (hidden * phi).astype(BF16)
            bell = jnp.exp(-0.5 * hidden * hidden) * 0.3989422804014327
            slope_ref[:, here] = (phi + hidden * bell).astype(BF16)


def middle(info, w_out, w_up, mixed0, mixed1, x, table, small):
    length, width = x.shape
    units = w_up.shape[1]
    return call(
        middle_kernel,
        "middle",
        (
            struct((length, width), F32),
            struct((length, 1), F32),
            struct((length, width), BF16),
            struct((length, units), BF16),
            struct((length, units), BF16),
        ),
        [SMEM] + [VMEM] * 7,
        (VMEM,) * 5,
        [],
        12,
        20,
        (info, w_out, w_up, mixed0, mixed1, x, table, small),
    )


def turn_kernel(
    pack_ref, weight_ref, act_ref, normed_ref, cot_ref, table_ref,
    chunks_ref, gz_ref, gzb_ref, sums_ref, down_own, down_sib, full, sem,
):
    length = act_ref.shape[0]
    block = chunks_ref.shape[1]
    gz_ref[...] = lax.dot_general(act_ref[...], weight_ref[...], NT, preferred_element_type=F32)
    sums_ref[...] = jnp.zeros_like(sums_ref)
    row = lambda which: table_ref[which : which + 1, :]

    @tiles(length, 64)
    def _(at):
        here = pl.ds(at, 64)
        value = normed_ref[here, :] * row(GAIN1) + row(SHIFT1) + gz_ref[here, :] + row(B_DOWN)
        centred = value - row_mean(value)
        scale = lax.rsqrt(row_mean(centred * centred) + 1e-12)
        unit = centred * scale
        result = (unit * row(GAIN2) + row(SHIFT2)).astype(BF16)
        chunk = lax.div(at, block)
        low = pl.multiple_of(lax.rem(at, block), 64)
        for copy in range(2):
            chunks_ref[2 * chunk + copy, pl.ds(low, 64), :] = result
        coming = cot_ref[here, :].astype(F32)
        raised = coming * row(GAIN2)
        back = scale * (raised - row_mean(raised) - unit * row_mean(raised * unit))
        gz_ref[here, :] = back
        gzb_ref[here, :] = back.astype(BF16)
        sums_ref[0:1, :] += jnp.sum(coming * unit, axis=0, keepdims=True)
        sums_ref[1:2, :] += jnp.sum(coming, axis=0, keepdims=True)
        sums_ref[2:3, :] += jnp.sum(back, axis=0, keepdims=True)

    back_t = gzb_ref[...].T

    @tiles(full.shape[1], 1024)
    def _(at):
        here = pl.ds(at, 1024)
        full[:, here] = jnp.dot(back_t, act_ref[:, here], preferred_element_type=F32).astype(BF16)

    finish(piece_copies(pack_ref, down_own, down_sib, sem, full, 0, down_own.shape[2], False))


def turn(pack, weight, act, normed, cot, table, chunk):
    length, units = act.shape
    width = normed.shape[1]
    piece = struct((16, width // 16, units // 2), BF16)
    return call(
        turn_kernel,
        "turn",
        (
            struct((2 * length // chunk, chunk, width), BF16),
            struct((length, width), F32),
            struct((length, width), BF16),
            struct((8, width), F32),
            piece,
            piece,
        ),
        [SMEM] + [VMEM] * 5,
        (VMEM, VMEM, VMEM, VMEM, ANY, ANY),
        [pltpu.VMEM((width, units), BF16), pltpu.SemaphoreType.DMA((32,))],
        14,
        24,
        (pack, weight, act, normed, cot, table),
    )


def hidden_back_kernel(weight_ref, gzb_ref, slope_ref, gh_ref, sum_ref):
    @tiles(gh_ref.shape[1], 512)
    def _(at):
        here = pl.ds(at, 512)
        back = jnp.dot(gzb_ref[...], weight_ref[:, here], preferred_element_type=F32)
        back = (back * slope_ref[:, here].astype(F32)).astype(BF16)
        gh_ref[:, here] = back
        sum_ref[:, here] = jnp.sum(back.astype(F32), axis=0, keepdims=True)


def hidden_back(weight, gzb, slope):
    length, units = slope.shape
    return call(
        hidden_back_kernel,
        "hidden_back",
        (struct((length, units), BF16), struct((1, units), F32)),
        [VMEM] * 3,
        (VMEM, VMEM),
        [],
        12,
        20,
        (weight, gzb, slope),
    )


def first_back_kernel(
    pack_ref, w_out, w_up, gh_ref, gz_ref, normed_ref, scale_ref, table_ref, first_ref, mixed0_ref, mixed1_ref,
    gz1_ref, gm_ref, sums_ref, pieces_own, pieces_sib, branch, d_out, d_up, sem,
):
    narrow = w_out.shape[1] // 2
    half = w_up.shape[1] // 2
    length = gh_ref.shape[0]
    first_t = first_ref[...].T

    @tiles(d_up.shape[1], 1024)
    def _(at):
        here = pl.ds(at, 1024)
        d_up[:, here] = jnp.dot(first_t, gh_ref[:, here], preferred_element_type=F32).astype(BF16)

    sent = piece_copies(pack_ref, pieces_own, pieces_sib, sem, d_up, narrow, half, False)
    gz1_ref[...] = lax.dot_general(gh_ref[...], w_up[...], NT, preferred_element_type=F32)
    sums_ref[...] = jnp.zeros_like(sums_ref)

    @tiles(length, 64)
    def _(at):
        here = pl.ds(at, 64)
        coming = gz_ref[here, :] + gz1_ref[here, :]
        unit = normed_ref[here, :]
        raised = coming * table_ref[GAIN1 : GAIN1 + 1, :]
        back = scale_ref[here, :] * (raised - row_mean(raised) - unit * row_mean(raised * unit))
        gz1_ref[here, :] = back
        branch[here, :] = back.astype(BF16)
        sums_ref[0:1, :] += jnp.sum(coming * unit, axis=0, keepdims=True)
        sums_ref[1:2, :] += jnp.sum(coming, axis=0, keepdims=True)
        sums_ref[2:3, :] += jnp.sum(back, axis=0, keepdims=True)

    branch_t = branch[...].T
    d_out[:, :narrow] = jnp.dot(branch_t, mixed0_ref[...], preferred_element_type=F32).astype(BF16)
    d_out[:, narrow:] = jnp.dot(branch_t, mixed1_ref[...], preferred_element_type=F32).astype(BF16)
    sent += piece_copies(pack_ref, pieces_own, pieces_sib, sem, d_out, 0, narrow, False, 32)
    gm_ref[...] = jnp.dot(branch[...], w_out[...], preferred_element_type=F32).astype(BF16)
    finish(sent)


def first_back(pack, w_out, w_up, gh, gz, normed, scale, table, first_b, mixed0, mixed1):
    length, units = gh.shape
    width = gz.shape[1]
    piece = struct((16, width // 16, (units + width) // 2), BF16)
    return call(
        first_back_kernel,
        "first_back",
        (
            struct((length, width), F32),
            struct((length, width), BF16),
            struct((8, width), F32),
            piece,
            piece,
        ),
        [SMEM] + [VMEM] * 10,
        (VMEM, VMEM, VMEM, ANY, ANY),
        [
            pltpu.VMEM((length, width), BF16),
            pltpu.VMEM((width, width), BF16),
            pltpu.VMEM((width, units), BF16),
            pltpu.SemaphoreType.DMA((64,)),
        ],
        20,
        30,
        (pack, w_out, w_up, gh, gz, normed, scale, table, first_b, mixed0, mixed1),
    )


def attend_back_kernel(proj_ref, p_ref, gm_ref, dq_ref, dk_ref, dv_ref, dst, dqt, *, y):
    length = proj_ref.shape[0]
    pairs = dq_ref.shape[1] // 128
    lane = lax.broadcasted_iota(jnp.int32, (1, 128), 1)
    low = lane < 64

    def pair(g, carry):
        take = lambda which: proj_ref[:, pl.ds(pl.multiple_of(((y * 3 + which) * pairs + g) * 128, 128), 128)]
        query, keys, values = take(0), take(1), take(2)
        grad = gm_ref[:, pl.ds(pl.multiple_of((y * pairs + g) * 128, 128), 128)]
        keys_t = keys.T
        dks, dvs = [], []
        for head in range(2):
            here = low if head == 0 else jnp.logical_not(low)
            only = jnp.where(here, values, jnp.zeros_like(values))
            for at in range(0, length, 256):
                cols = slice(at, at + 256)
                gp = lax.dot_general(only, grad[cols], NT, preferred_element_type=F32)
                probs = p_ref[2 * g + head, :, cols].astype(F32)
                weighted = jnp.sum(probs * gp, axis=0, keepdims=True)
                dst[:, cols] = (probs * (gp - weighted)).astype(BF16)
            dqt[64 * head : 64 * head + 64, :] = (
                jnp.dot(keys_t[64 * head : 64 * head + 64], dst[...], preferred_element_type=F32) * 0.125
            ).astype(BF16)
            dks.append(jnp.dot(dst[...], query, preferred_element_type=F32))
            dvs.append(jnp.dot(p_ref[2 * g + head], grad, preferred_element_type=F32))
        cols = pl.ds(pl.multiple_of(g * 128, 128), 128)
        dq_ref[:, cols] = dqt[...].T
        dk_ref[:, cols] = (jnp.where(low, dks[0], dks[1]) * 0.125).astype(BF16)
        dv_ref[:, cols] = jnp.where(low, dvs[0], dvs[1]).astype(BF16)
        return carry

    lax.fori_loop(0, pairs, pair, 0)


def attend_back(proj, probs, grad_mixed, y):
    length, wide = proj.shape
    shape = struct((length, wide // 6), BF16)
    return call(
        lambda *refs: attend_back_kernel(*refs, y=y),
        "attend_back",
        (shape, shape, shape),
        [VMEM] * 3,
        (VMEM,) * 3,
        [pltpu.VMEM((length, length), BF16), pltpu.VMEM((128, length), BF16)],
        14,
        16,
        (proj, probs, grad_mixed),
    )


def last_kernel(pack_ref, x_ref, *refs):
    parts, (sums_ref, pieces_own, pieces_sib, whole, sem) = refs[:6], refs[6:]
    half = parts[0].shape[1]
    sums_ref[...] = jnp.zeros_like(sums_ref)
    x_t = x_ref[...].T
    for y in range(2):
        for which in range(3):
            at = (y * 3 + which) * half
            value = parts[y * 3 + which][...]
            whole[:, at : at + half] = jnp.dot(x_t, value, preferred_element_type=F32).astype(BF16)
            if which != 1:
                r = which // 2
                sums_ref[r : r + 1, y * half : y * half + half] = jnp.sum(
                    value.astype(F32), axis=0, keepdims=True
                )
    finish(piece_copies(pack_ref, pieces_own, pieces_sib, sem, whole, 0, 3 * half, False))


def last(pack, x, parts):
    length, width = x.shape
    piece = struct((16, width // 16, 3 * width // 2), BF16)
    return call(
        last_kernel,
        "last",
        (struct((8, width), F32), piece, piece),
        [SMEM] + [VMEM] * 7,
        (VMEM, ANY, ANY),
        [pltpu.VMEM((width, 3 * width), BF16), pltpu.SemaphoreType.DMA((32,))],
        10,
        16,
        (pack, x) + tuple(parts),
    )


def input_back_kernel(weight_ref, gz1_ref, *refs):
    parts, chunks_ref = refs[:6], refs[6]
    half = parts[0].shape[1]
    total = gz1_ref[...]
    for i, part in enumerate(parts):
        total = total + lax.dot_general(
            part[...], weight_ref[:, i * half : (i + 1) * half], NT, preferred_element_type=F32
        )
    total = total.astype(BF16)
    count, block = chunks_ref.shape[:2]
    for i in range(count):
        at = i // 2 * block
        chunks_ref[i] = total[at : at + block]


def input_back(weight, gz1, parts, chunk):
    length, width = gz1.shape
    return call(
        input_back_kernel,
        "input_back",
        struct((2 * length // chunk, chunk, width), BF16),
        [VMEM] * 8,
        VMEM,
        [],
        8,
        20,
        (weight, gz1) + tuple(parts),
    )


def settle_kernel(owner_ref, pair_ref, got_ref, *refs, cuts):
    outs, four = refs[: len(cuts)], refs[len(cuts)]
    rows = pair_ref.shape[1]
    for i in range(4):
        ref = (pair_ref, got_ref)[i // 2]
        four[pl.ds(pl.multiple_of(owner_ref[i] * rows, 16), rows), :] = ref[i % 2].astype(F32)
    for out, (low, high, form) in zip(outs, cuts):
        if form == "plain":
            out[...] = four[:, low:high]
        else:
            step = (high - low) // 3
            for j in range(3):
                out[j] = four[:, low + j * step : low + (j + 1) * step]


def settle(owners, pair, got, cuts):
    _, rows, cols = pair.shape
    shapes = {"plain": lambda n: (4 * rows, n), "three": lambda n: (3, 4 * rows, n // 3)}
    return call(
        lambda *refs: settle_kernel(*refs, cuts=cuts),
        "settle",
        tuple(struct(shapes[form](high - low), F32) for low, high, form in cuts),
        [SMEM, VMEM, VMEM],
        (VMEM,) * len(cuts),
        [pltpu.VMEM((4 * rows, cols), F32)],
        3,
        10,
        (owners, pair, got),
    )


def add_up(terms, low, high):
    total = terms[0][low:high].astype(F32)
    for term in terms[1:]:
        total = total + term[low:high].astype(F32)
    return total.astype(BF16)


def cut(full):
    rows, cols = full.shape
    both = full.reshape(16, rows // 16, 2, cols // 2)
    return both[:, :, 0], both[:, :, 1]


def gather_plain(shard):
    rows = lax.all_gather(shard, "fsdp", axis=0, tiled=True)
    return lax.all_gather(rows, "tp", axis=1, tiled=True)


def reduce_plain(own, sib):
    rows = own.shape[0] * own.shape[1]
    full = jnp.concatenate([own.reshape(rows, -1), sib.reshape(rows, -1)], axis=1)
    part = lax.psum_scatter(full, "tp", scatter_dimension=1, tiled=True)
    part = lax.psum_scatter(part, "fsdp", scatter_dimension=0, tiled=True)
    return lax.psum(part, "ctx").astype(F32)


def body(
    layer_input,
    doc_ids,
    w_qkv,
    b_qv,
    w_out,
    b_out,
    ln1_gain,
    ln1_bias,
    w_up,
    b_up,
    w_down,
    b_down,
    ln2_gain,
    ln2_bias,
    out_grad,
):
    sizes = (lax.axis_size("fsdp"), lax.axis_size("ctx"), lax.axis_size("tp"))
    devices = sizes[0] * sizes[1] * sizes[2]
    micro, seqs, local_len, width = layer_input.shape
    length = local_len * sizes[1]
    shard_rows, local_width = w_qkv.shape[1:]
    local_units = w_up.shape[1]
    heads = width // HEAD_DIM
    fast = sizes == (4, 4, 2)
    t = lax.axis_index("tp")
    c = lax.axis_index("ctx")

    def mine(value):
        return lax.dynamic_index_in_dim(value, t, 1, keepdims=False)

    def to_owners(chunks):
        return lax.all_to_all(chunks, "ctx", 0, 0, tiled=True)

    def spread(chunks):
        out = lax.all_to_all(chunks, ("ctx", "tp"), 0, 0, tiled=True)
        return out.reshape(micro, seqs, local_len, width)

    shards = (
        jnp.swapaxes(w_qkv, 0, 1).reshape(shard_rows, 3 * local_width),
        jnp.concatenate([w_out.T, w_up], axis=1),
        w_down.T,
    )
    ids = mine(doc_ids).astype(BF16)[:, None, :]
    ids = jnp.pad(ids, ((0, 0), (0, 7), (0, width - local_len)))
    given = to_owners(jnp.concatenate([mine(layer_input), ids], axis=1))
    small = jnp.concatenate([b_qv.reshape(-1), b_up])[None]
    small = jnp.concatenate([small, exchange(small, ("y", "y"), sizes)], axis=0)
    table = jnp.stack([b_out, ln1_gain, ln1_bias, b_down, ln2_gain, ln2_bias, b_out, b_out])

    def swap(value, step):
        return exchange(value, GATHER_STEPS[step], sizes)

    def shed(value, step):
        return exchange(value, SCATTER_STEPS[step], sizes)

    def joined(*parts):
        return jnp.concatenate(parts, axis=0)

    if fast:
        place, pack = places(GATHER_ORDER), places(PACK_ORDER)
        part = shard_rows // 4
        h1, h2, h3 = [lax.dynamic_slice_in_dim(s, c * part, part, 0)[None] for s in shards]
        h1 = joined(h1, swap(h1, 0))
        h1 = joined(h1, swap(h1, 1))
        h1, given, small, table = lax.optimization_barrier((h1, given, small, table))
        h2 = after(h2, h1)
        g1, g2 = swap(h1, 2), swap(h2, 0)
        h1, h2 = joined(h1, g1), joined(h2, g2)
        h1, h2 = after(h1, h2), after(h2, h1)
        g1, g2 = swap(h1, 3), swap(h2, 1)
        h1, h2 = joined(h1, g1), joined(h2, g2)
        h1, h2, h3 = after(h1, h2), after(h2, h1), after(h3, h1)
        g1, g2, g3 = swap(h1, 4), swap(h2, 2), swap(h3, 0)
        (wq,) = unpack(place, after(h1, h2, h3), g1, (3 * width,))
        proj, rows_b, mask = project(place, wq, given, small)
        g2, g3, cot_from = after(g2, proj), after(g3, proj), after(out_grad, proj)
        h2, h3 = joined(h2, g2), joined(h3, g3)
        g2, g3 = swap(h2, 3), swap(h3, 1)
        mixed0, probs0 = attend(after(proj, h2, h3), mask, 0)
        g3 = after(g3, mixed0)
        h3 = joined(h3, g3)
        mixed1, probs1 = attend(after(proj, h3, mixed0), mask, 1)
        g2 = after(g2, mixed1)
        h2 = joined(h2, g2)
        h3 = after(h3, h2)
        g2, g3 = swap(h2, 4), swap(h3, 2)
        wo, wu = unpack(place, h2, g2, (width, 2 * local_units))
        h3 = joined(h3, after(g3, g2))
        g3 = swap(h3, 3)
        cot = to_owners(mine(after(cot_from, g2))).reshape(length, width)
    else:
        place = pack = plain_places()
        parts = (shards[0], w_out.T, w_up, w_down.T)
        pieces = [cut(gather_plain(s)) for s in parts]
        (wq,) = unpack(place, *pieces[0], (3 * width,))
        (wo,) = unpack(place, *pieces[1], (width,))
        (wu,) = unpack(place, *pieces[2], (2 * local_units,))
        (wd,) = unpack(place, *pieces[3], (2 * local_units,))
        cot = to_owners(mine(out_grad)).reshape(length, width)
        proj, rows_b, mask = project(place, wq, given, small)
        mixed0, probs0 = attend(proj, mask, 0)
        mixed1, probs1 = attend(proj, mask, 1)
        h3 = mixed0

    normed1, scale1, first_b, act, slope = middle(
        place, wo, wu, after(mixed0, h3), mixed1, rows_b, table, small
    )
    if fast:
        h3 = joined(h3, after(g3, act))
        (wd,) = unpack(place, h3, swap(h3, 4), (2 * local_units,))
    chunks, gz, gzb, sums2, down_own, down_sib = turn(pack, wd, act, normed1, cot, table, local_len)

    layer_output = spread(chunks)
    if fast:
        got = shed(down_sib, 0)
        gzb = after(gzb, down_sib, chunks)
    gh, sum_up = hidden_back(wd, gzb, slope)
    if fast:
        down = [down_own, after(got, gh)]
        send = add_up(down, 8, 16)
        got = shed(send, 1)
        gh = after(gh, send)
    gz1, grad_mixed, sums1, up_own, up_sib = first_back(
        pack, wo, wu, gh, gz, normed1, scale1, table, first_b, mixed0, mixed1
    )
    if fast:
        down = [v[:8] for v in down] + [after(got, grad_mixed)]
        send = add_up(down, 4, 8)
        got, got2 = shed(send, 2), shed(up_sib, 0)
        grad_mixed = after(grad_mixed, send, up_sib, layer_output)
    parts0 = attend_back(proj, probs0, grad_mixed, 0)
    if fast:
        down = [v[:4] for v in down] + [after(got, parts0[0])]
        up = [up_own, after(got2, parts0[0])]
        send, send2 = add_up(down, 2, 4), add_up(up, 8, 16)
        got, got2 = shed(send, 3), shed(send2, 1)
        grad_mixed = after(grad_mixed, send, send2)
    parts1 = attend_back(proj, probs1, grad_mixed, 1)
    if fast:
        down = [v[:2] for v in down] + [after(got, parts1[0])]
        send = add_up(down, 1, 2)
        got = shed(send, 4)
        parts1 = [after(parts1[0], send)] + list(parts1[1:])
    parts = list(parts0) + list(parts1)
    sums3, qkv_own, qkv_sib = last(pack, rows_b, parts)

    flat = jnp.concatenate(
        [sums3[:2].reshape(-1), sums1[:3].reshape(-1), sums2[:3].reshape(-1), sum_up.reshape(-1)]
    ).reshape(devices, 1, -1)
    if fast:
        down = [v[:1] for v in down] + [after(got, qkv_sib)]
        pair1 = add_up(down, 0, 1)
        got3 = shed(qkv_sib, 0)
        got = exchange(pair1, ("x", "x"), sizes)
        parts[0] = after(parts[0], qkv_sib, pair1, flat)
    chunks = grad_rows = input_back(wq, gz1, parts, local_len)
    part = lax.all_to_all(flat, AXES, 0, 0, tiled=True)
    part = jnp.sum(part, axis=0, keepdims=True)
    flat = lax.all_to_all(jnp.broadcast_to(part, (devices,) + part.shape[1:]), AXES, 0, 0, tiled=True)
    flat = flat.reshape(-1)
    if fast:
        owners = jnp.stack([c, c ^ 2, c ^ 1, c ^ 3]).astype(jnp.int32)
        got2, got3, got = after(got2, grad_rows), after(got3, grad_rows), after(got, grad_rows)
        up = [v[:8] for v in up] + [got2]
        qkv = [qkv_own, got3]
        send2, send3 = add_up(up, 4, 8), add_up(qkv, 8, 16)
        got3, got2 = shed(send3, 1), shed(send2, 2)
        pair1 = joined(pair1, got)
        got1 = exchange(pair1, ("core", "core"), sizes)
        grad_x = spread(after(chunks, send2, send3))
        up = [v[:4] for v in up] + [got2]
        send2 = add_up(up, 2, 4)
        got2 = shed(send2, 3)
        qkv = [v[:8] for v in qkv] + [got3]
        send3 = after(add_up(qkv, 4, 8), send2)
        got3 = shed(send3, 2)
        up = [v[:2] for v in up] + [got2]
        send2 = add_up(up, 1, 2)
        got2 = shed(send2, 4)
        qkv = [v[:4] for v in qkv] + [got3]
        send3 = add_up(qkv, 2, 4)
        got3 = shed(send3, 3)
        (grad_down,) = settle(owners, pair1, got1, ((0, local_units, "plain"),))
        up = [v[:1] for v in up] + [got2]
        pair2 = add_up(up, 0, 1)
        pair2 = joined(pair2, exchange(pair2, ("x", "x"), sizes))
        qkv = [v[:2] for v in qkv] + [got3]
        send3 = add_up(qkv, 1, 2)
        got3 = shed(send3, 4)
        got2 = exchange(pair2, ("core", "core"), sizes)
        grad_wout, grad_up = settle(
            owners, pair2, got2, ((0, local_width, "plain"), (local_width, local_width + local_units, "plain"))
        )
        qkv = [v[:1] for v in qkv] + [got3]
        pair3 = add_up(qkv, 0, 1)
        pair3 = joined(pair3, exchange(pair3, ("x", "x"), sizes))
        got3 = exchange(pair3, ("core", "core"), sizes)
        (grad_qkv,) = settle(owners, pair3, got3, ((0, 3 * local_width, "three"),))
    else:
        grad_x = spread(chunks)
        grad_down = reduce_plain(down_own, down_sib)
        both = reduce_plain(up_own, up_sib)
        grad_wout, grad_up = both[:, :local_width], both[:, local_width:]
        grad_qkv = reduce_plain(qkv_own, qkv_sib)
        grad_qkv = jnp.swapaxes(grad_qkv.reshape(shard_rows, 3, local_width), 0, 1)

    vector = lambda i: flat[i * width : (i + 1) * width]
    out_bqv = lax.dynamic_slice_in_dim(flat[: 2 * width].reshape(2, width), t * local_width, local_width, 1)
    out_bup = lax.dynamic_slice_in_dim(flat[8 * width :], t * local_units, local_units, 0)
    return (
        layer_output,
        grad_x,
        grad_qkv,
        out_bqv,
        grad_wout.T,
        vector(4),
        vector(2),
        vector(3),
        grad_up,
        out_bup,
        grad_down.T,
        vector(7),
        vector(5),
        vector(6),
    )


def solution(mesh):
    return jax.shard_map(
        body,
        mesh=mesh,
        in_specs=(
            P(None, "fsdp", "ctx", None),
            P(None, "fsdp", "ctx"),
            P(None, "fsdp", "tp"),
            P(None, "tp"),
            P("tp", "fsdp"),
            P(),
            P(),
            P(),
            P("fsdp", "tp"),
            P("tp"),
            P("tp", "fsdp"),
            P(),
            P(),
            P(),
            P(None, "fsdp", "ctx", None),
        ),
        out_specs=(
            P(None, "fsdp", "ctx", None),
            P(None, "fsdp", "ctx", None),
            P(None, "fsdp", "tp"),
            P(None, "tp"),
            P("tp", "fsdp"),
            P(),
            P(),
            P(),
            P("fsdp", "tp"),
            P("tp"),
            P("tp", "fsdp"),
            P(),
            P(),
            P(),
        ),
        check_vma=False,
    )
```

```python
import jax
import jax.numpy as jnp
from jax import lax
from jax.experimental import pallas as pl
from jax.experimental.pallas import tpu as pltpu
from jax.sharding import PartitionSpec as P

HEAD_DIM = 64
AXES = ("fsdp", "ctx", "tp")
F32 = jnp.float32
BF16 = jnp.bfloat16
NEG = -1e30
NT = (((1,), (1,)), ((), ()))
VMEM = pl.BlockSpec(memory_space=pltpu.VMEM)
SMEM = pl.BlockSpec(memory_space=pltpu.SMEM)
ANY = pl.BlockSpec(memory_space=pl.ANY)


def partner(dim, z, c, t):
    if dim == "core":
        return z, c ^ 1, t
    if dim == "x":
        return z, c ^ 2, t
    if dim == "y":
        return z, c, t ^ 1
    return z ^ int(dim[1:]), c, t


def exchange(value, dims, sizes):
    nz, nc, nt = sizes
    pairs = []
    for z in range(nz):
        for c in range(nc):
            for t in range(nt):
                tz, tc, tt = partner(dims[c & 1], z, c, t)
                pairs.append(((z * nc + c) * nt + t, (tz * nc + tc) * nt + tt))
    return lax.ppermute(value, AXES, pairs)


GATHER = (
    (("z2", "z1", "y", "x"), ("z2", "z1", "x", "y")),
    (("z2", "z1", "y", "x"), ("z2", "z1", "x", "y")),
    (("z2", "z1", "x", "y"), ("y", "x", "z2", "z1")),
)
SCATTER = (
    (("x", "y", "z1", "z2"), ("y", "z1", "z2", "x")),
    (("x", "y", "z1", "z2"), ("z1", "z2", "y", "x")),
    (("y", "x", "z1", "z2"), ("z1", "z2", "x", "y")),
)
CORE = ("core", "core")
X = ("x", "x")
Y = ("y", "y")


def piece_place(order, core, here, index):
    z, x, t = here
    for bit, dim in enumerate(order):
        flip = (index >> bit) & 1
        if dim == "x":
            x = x ^ flip
        elif dim == "y":
            t = t ^ flip
        else:
            z = z ^ (flip * int(dim[1:]))
    return z * 4 + x * 2 + core, t


def places(orders):
    if orders is None:
        return [(i, half) for half in range(2) for i in range(16)]
    c = lax.axis_index("ctx")
    here = (lax.axis_index("fsdp"), c >> 1, lax.axis_index("tp"))
    spots = []
    for core in (c & 1, 1 - (c & 1)):
        for i in range(16):
            r0, t0 = piece_place(orders[0], core, here, i)
            r1, t1 = piece_place(orders[1], core, here, i)
            spots.append((jnp.where(core == 0, r0, r1), jnp.where(core == 0, t0, t1)))
    return spots


def packing(orders):
    return tuple(order[::-1] for order in orders)


def after(value, *first):
    return lax.optimization_barrier((value, first))[0]


def phase(*values):
    return lax.optimization_barrier(values)


def piece_copies(spots, own_ref, sib_ref, sem, whole, low, cols, collect, base=0):
    rows = whole.shape[0] // 16
    stride = whole.shape[1] // 2
    copies = []
    for half, ref in ((0, own_ref), (1, sib_ref)):
        for i in range(16):
            row, col = spots[half * 16 + i]
            row, col = row * rows, col * stride
            if not isinstance(row, int):
                row, col = pl.multiple_of(row, rows), pl.multiple_of(col, 128)
            one = ref.at[pl.ds(i * rows, rows), pl.ds(low, cols)]
            two = whole.at[pl.ds(row, rows), pl.ds(col, cols)]
            src, dst = (one, two) if collect else (two, one)
            copy = pltpu.make_async_copy(src, dst, sem.at[base + half * 16 + i])
            copy.start()
            copies.append(copy)
    return copies


def finish(copies):
    for copy in copies:
        copy.wait()


def tiles(count, step):
    def run(one):
        lax.fori_loop(0, count // step, lambda i, carry: (one(pl.multiple_of(i * step, step)), carry)[1], 0)

    return run


def row_mean(value):
    return jnp.mean(value, axis=-1, keepdims=True)


def struct(shape, dtype):
    return jax.ShapeDtypeStruct(shape, dtype)


def call(kernel, name, outs, specs, out_specs, scratch, time, room, args):
    return pl.pallas_call(
        kernel,
        name=name,
        out_shape=outs,
        in_specs=specs,
        out_specs=out_specs,
        scratch_shapes=scratch,
        compiler_params=pltpu.CompilerParams(vmem_limit_bytes=room << 20),
        cost_estimate=pl.CostEstimate(flops=time * 10**9, transcendentals=0, bytes_accessed=10**6),
    )(*args)


B_OUT, GAIN1, SHIFT1, B_DOWN, GAIN2, SHIFT2 = range(6)


def unpack_kernel(own_ref, sib_ref, *refs, orders):
    outs, sem = refs[:-1], refs[-1]
    copies = []
    spots = places(orders)
    low = 0
    for i, out in enumerate(outs):
        cols = out.shape[1] // 2
        copies += piece_copies(spots, own_ref, sib_ref, sem, out, low, cols, True, 32 * i)
        low += cols
    finish(copies)


def unpack(orders, own, sib, widths):
    rows = own.shape[0]
    return call(
        lambda *refs: unpack_kernel(*refs, orders=orders),
        "unpack",
        tuple(struct((rows, width), BF16) for width in widths),
        [ANY, ANY],
        (VMEM,) * len(widths),
        [pltpu.SemaphoreType.DMA((32 * len(widths),))],
        5,
        1,
        (own, sib),
    )


def sources(refs, fast):
    c = lax.axis_index("ctx") if fast else 0
    own, core, x = refs
    return [(c ^ 0, own, 0), (c ^ 1, core, 0), (c ^ 2, x, 0), (c ^ 3, x, 1)]


def project_kernel(weight_ref, own_ref, core_ref, far_ref, small_ref, proj_ref, x_ref, mask_ref, ids, *, fast):
    block = own_ref.shape[1] - 8
    count = 4
    for spot, ref, i in sources((own_ref, core_ref, far_ref), fast):
        x_ref[pl.ds(pl.multiple_of(spot * block, block), block), :] = ref[i, 0:block, :]
        ids[pl.ds(spot, 1), :] = ref[i, block:, 0:block].astype(F32)[0:1]
    for kb in range(count):
        column = jnp.broadcast_to(ids[kb : kb + 1], (block, block)).T
        for qb in range(count):
            mask_ref[kb * block : (kb + 1) * block, qb * block : (qb + 1) * block] = jnp.where(
                column == jnp.broadcast_to(ids[qb : qb + 1], (block, block)), 0.0, NEG
            )
    width = proj_ref.shape[1] // 6
    for y in range(2):
        row = pl.ds(lax.axis_index("tp") ^ y, 1)
        for which in range(3):
            at = (y * 3 + which) * width
            value = jnp.dot(x_ref[...], weight_ref[:, at : at + width], preferred_element_type=F32)
            if which != 1:
                low = 0 if which == 0 else width
                value = value + small_ref[row, low : low + width]
            proj_ref[:, at : at + width] = value.astype(BF16)


def project(weight, given, small, fast):
    width, wide = weight.shape
    block = given[0].shape[1] - 8
    length = 4 * block
    return call(
        lambda *refs: project_kernel(*refs, fast=fast),
        "project",
        (
            struct((length, wide), BF16),
            struct((length, width), BF16),
            struct((length, length), F32),
        ),
        [VMEM] * 5,
        (VMEM,) * 3,
        [pltpu.VMEM((8, block), F32)],
        5,
        6,
        (weight,) + tuple(given) + (small,),
    )


def attend_kernel(proj_ref, mask_ref, o_ref, p_ref, *, y):
    length = proj_ref.shape[0]
    pairs = o_ref.shape[1] // 128
    lane = lax.broadcasted_iota(jnp.int32, (1, 128), 1)

    def pair(g, carry):
        take = lambda which: proj_ref[:, pl.ds(pl.multiple_of(((y * 3 + which) * pairs + g) * 128, 128), 128)]
        query = take(0) * jnp.asarray(0.125, BF16)
        keys = take(1)
        values_t = take(2).T
        outs = []
        for head in range(2):
            here = (lane >= 64 * head) & (lane < 64 * head + 64)
            only = jnp.where(here, keys, jnp.zeros_like(keys))
            row = []
            for at in range(0, length, 256):
                scores = lax.dot_general(only, query[at : at + 256], NT, preferred_element_type=F32)
                scores = scores + mask_ref[:, at : at + 256]
                top = jnp.max(scores, axis=0, keepdims=True)
                raised = jnp.exp(scores - top)
                total = jnp.sum(raised, axis=0, keepdims=True)
                probs = (raised * (1.0 / total)).astype(BF16)
                p_ref[2 * g + head, :, at : at + 256] = probs
                row.append(
                    jnp.dot(values_t[64 * head : 64 * head + 64], probs, preferred_element_type=F32)
                )
            outs.append(jnp.concatenate(row, axis=1))
        both = jnp.concatenate(outs, axis=0).astype(BF16)
        o_ref[:, pl.ds(pl.multiple_of(g * 128, 128), 128)] = both.T
        return carry

    lax.fori_loop(0, pairs, pair, 0)


def attend(proj, mask, y):
    length, wide = proj.shape
    half = wide // 6
    return call(
        lambda *refs: attend_kernel(*refs, y=y),
        "attend",
        (struct((length, half), BF16), struct((half // HEAD_DIM, length, length), BF16)),
        [VMEM, VMEM],
        (VMEM, VMEM),
        [],
        12,
        6,
        (proj, mask),
    )


def middle_kernel(
    w_out, w_up, mixed0_ref, mixed1_ref, x_ref, table_ref, small_ref,
    normed_ref, scale_ref, first_ref, act_ref, slope_ref,
):
    length, units = act_ref.shape
    narrow, half = w_out.shape[1] // 2, units // 2
    normed_ref[...] = lax.dot_general(
        mixed0_ref[...], w_out[:, :narrow], NT, preferred_element_type=F32
    ) + lax.dot_general(mixed1_ref[...], w_out[:, narrow:], NT, preferred_element_type=F32)

    @tiles(length, 64)
    def _(at):
        here = pl.ds(at, 64)
        value = x_ref[here, :].astype(F32) + normed_ref[here, :] + table_ref[B_OUT : B_OUT + 1, :]
        centred = value - row_mean(value)
        scale = lax.rsqrt(row_mean(centred * centred) + 1e-12)
        unit = centred * scale
        normed_ref[here, :] = unit
        scale_ref[here, :] = scale
        first_ref[here, :] = (
            unit * table_ref[GAIN1 : GAIN1 + 1, :] + table_ref[SHIFT1 : SHIFT1 + 1, :]
        ).astype(BF16)

    for y in range(2):
        row = pl.ds(lax.axis_index("tp") ^ y, 1)

        @tiles(half, 256)
        def _(at):
            here = pl.ds(pl.multiple_of(y * half + at, 256), 256)
            bias = small_ref[row, pl.ds(pl.multiple_of(2 * narrow + at, 256), 256)]
            hidden = jnp.dot(first_ref[...], w_up[:, here], preferred_element_type=F32) + bias
            phi = 0.5 + 0.5 * lax.erf(hidden * 0.7071067811865476)
            act_ref[:, here] = (hidden * phi).astype(BF16)
            bell = jnp.exp(-0.5 * hidden * hidden) * 0.3989422804014327
            slope_ref[:, here] = (phi + hidden * bell).astype(BF16)


def middle(w_out, w_up, mixed0, mixed1, x, table, small):
    length, width = x.shape
    units = w_up.shape[1]
    return call(
        middle_kernel,
        "middle",
        (
            struct((length, width), F32),
            struct((length, 1), F32),
            struct((length, width), BF16),
            struct((length, units), BF16),
            struct((length, units), BF16),
        ),
        [VMEM] * 7,
        (VMEM,) * 5,
        [],
        12,
        6,
        (w_out, w_up, mixed0, mixed1, x, table, small),
    )


def turn_kernel(
    weight_ref, act_ref, normed_ref, own_ref, core_ref, far_ref, table_ref,
    chunks_ref, gz_ref, gzb_ref, sums_ref, down_own, down_sib, full, cot_ref, sem, *, orders,
):
    length = act_ref.shape[0]
    block = chunks_ref.shape[1]
    for spot, ref, i in sources((own_ref, core_ref, far_ref), orders is not None):
        cot_ref[pl.ds(pl.multiple_of(spot * block, block), block), :] = ref[i]
    gz_ref[...] = lax.dot_general(act_ref[...], weight_ref[...], NT, preferred_element_type=F32)
    sums_ref[...] = jnp.zeros_like(sums_ref)
    row = lambda which: table_ref[which : which + 1, :]

    @tiles(length, 64)
    def _(at):
        here = pl.ds(at, 64)
        value = normed_ref[here, :] * row(GAIN1) + row(SHIFT1) + gz_ref[here, :] + row(B_DOWN)
        centred = value - row_mean(value)
        scale = lax.rsqrt(row_mean(centred * centred) + 1e-12)
        unit = centred * scale
        result = (unit * row(GAIN2) + row(SHIFT2)).astype(BF16)
        chunk = lax.div(at, block)
        if orders is not None:
            c = lax.axis_index("ctx") ^ chunk
            chunk = (c & 1) * 2 + (c >> 1)
        chunks_ref[chunk, pl.ds(pl.multiple_of(lax.rem(at, block), 64), 64), :] = result
        coming = cot_ref[here, :].astype(F32)
        raised = coming * row(GAIN2)
        back = scale * (raised - row_mean(raised) - unit * row_mean(raised * unit))
        gz_ref[here, :] = back
        gzb_ref[here, :] = back.astype(BF16)
        sums_ref[0:1, :] += jnp.sum(coming * unit, axis=0, keepdims=True)
        sums_ref[1:2, :] += jnp.sum(coming, axis=0, keepdims=True)
        sums_ref[2:3, :] += jnp.sum(back, axis=0, keepdims=True)

    back_t = gzb_ref[...].T

    @tiles(full.shape[1], 1024)
    def _(at):
        here = pl.ds(at, 1024)
        full[:, here] = jnp.dot(back_t, act_ref[:, here], preferred_element_type=F32).astype(BF16)

    finish(piece_copies(places(orders), down_own, down_sib, sem, full, 0, down_own.shape[1], False))


def turn(orders, weight, act, normed, cot, table, chunk):
    length, units = act.shape
    width = normed.shape[1]
    piece = struct((width, units // 2), BF16)
    return call(
        lambda *refs: turn_kernel(*refs, orders=orders),
        "turn",
        (
            struct((length // chunk, chunk, width), BF16),
            struct((length, width), F32),
            struct((length, width), BF16),
            struct((8, width), F32),
            piece,
            piece,
        ),
        [VMEM] * 7,
        (VMEM, VMEM, VMEM, VMEM, ANY, ANY),
        [pltpu.VMEM((width, units), BF16), pltpu.VMEM((length, width), BF16), pltpu.SemaphoreType.DMA((32,))],
        14,
        10,
        (weight, act, normed) + tuple(cot) + (table,),
    )


def hidden_back_kernel(weight_ref, gzb_ref, slope_ref, gh_ref, sum_ref):
    @tiles(gh_ref.shape[1], 512)
    def _(at):
        here = pl.ds(at, 512)
        back = jnp.dot(gzb_ref[...], weight_ref[:, here], preferred_element_type=F32)
        back = (back * slope_ref[:, here].astype(F32)).astype(BF16)
        gh_ref[:, here] = back
        sum_ref[:, here] = jnp.sum(back.astype(F32), axis=0, keepdims=True)


def hidden_back(weight, gzb, slope):
    length, units = slope.shape
    return call(
        hidden_back_kernel,
        "hidden_back",
        (struct((length, units), BF16), struct((1, units), F32)),
        [VMEM] * 3,
        (VMEM, VMEM),
        [],
        12,
        6,
        (weight, gzb, slope),
    )


def first_back_kernel(
    w_out, w_up, gh_ref, gz_ref, normed_ref, scale_ref, table_ref, first_ref, mixed0_ref, mixed1_ref,
    gz1_ref, gm_ref, sums_ref, pieces_own, pieces_sib, branch, d_out, d_up, sem, *, orders,
):
    narrow = w_out.shape[1] // 2
    half = w_up.shape[1] // 2
    length = gh_ref.shape[0]
    first_t = first_ref[...].T
    spots = places(orders)

    @tiles(d_up.shape[1], 1024)
    def _(at):
        here = pl.ds(at, 1024)
        d_up[:, here] = jnp.dot(first_t, gh_ref[:, here], preferred_element_type=F32).astype(BF16)

    sent = piece_copies(spots, pieces_own, pieces_sib, sem, d_up, narrow, half, False)
    gz1_ref[...] = lax.dot_general(gh_ref[...], w_up[...], NT, preferred_element_type=F32)
    sums_ref[...] = jnp.zeros_like(sums_ref)

    @tiles(length, 64)
    def _(at):
        here = pl.ds(at, 64)
        coming = gz_ref[here, :] + gz1_ref[here, :]
        unit = normed_ref[here, :]
        raised = coming * table_ref[GAIN1 : GAIN1 + 1, :]
        back = scale_ref[here, :] * (raised - row_mean(raised) - unit * row_mean(raised * unit))
        gz1_ref[here, :] = back
        branch[here, :] = back.astype(BF16)
        sums_ref[0:1, :] += jnp.sum(coming * unit, axis=0, keepdims=True)
        sums_ref[1:2, :] += jnp.sum(coming, axis=0, keepdims=True)
        sums_ref[2:3, :] += jnp.sum(back, axis=0, keepdims=True)

    branch_t = branch[...].T
    d_out[:, :narrow] = jnp.dot(branch_t, mixed0_ref[...], preferred_element_type=F32).astype(BF16)
    d_out[:, narrow:] = jnp.dot(branch_t, mixed1_ref[...], preferred_element_type=F32).astype(BF16)
    sent += piece_copies(spots, pieces_own, pieces_sib, sem, d_out, 0, narrow, False, 32)
    gm_ref[...] = jnp.dot(branch[...], w_out[...], preferred_element_type=F32).astype(BF16)
    finish(sent)


def first_back(orders, w_out, w_up, gh, gz, normed, scale, table, first_b, mixed0, mixed1):
    length, units = gh.shape
    width = gz.shape[1]
    piece = struct((width, (units + width) // 2), BF16)
    return call(
        lambda *refs: first_back_kernel(*refs, orders=orders),
        "first_back",
        (
            struct((length, width), F32),
            struct((length, width), BF16),
            struct((8, width), F32),
            piece,
            piece,
        ),
        [VMEM] * 10,
        (VMEM, VMEM, VMEM, ANY, ANY),
        [
            pltpu.VMEM((length, width), BF16),
            pltpu.VMEM((width, width), BF16),
            pltpu.VMEM((width, units), BF16),
            pltpu.SemaphoreType.DMA((64,)),
        ],
        20,
        14,
        (w_out, w_up, gh, gz, normed, scale, table, first_b, mixed0, mixed1),
    )


def attend_back_kernel(proj_ref, p_ref, gm_ref, dq_ref, dk_ref, dv_ref, dst, dqt, *, y):
    length = proj_ref.shape[0]
    pairs = dq_ref.shape[1] // 128
    lane = lax.broadcasted_iota(jnp.int32, (1, 128), 1)
    low = lane < 64

    def pair(g, carry):
        take = lambda which: proj_ref[:, pl.ds(pl.multiple_of(((y * 3 + which) * pairs + g) * 128, 128), 128)]
        query, keys, values = take(0), take(1), take(2)
        grad = gm_ref[:, pl.ds(pl.multiple_of((y * pairs + g) * 128, 128), 128)]
        keys_t = keys.T
        dks, dvs = [], []
        for head in range(2):
            here = low if head == 0 else jnp.logical_not(low)
            only = jnp.where(here, values, jnp.zeros_like(values))
            for at in range(0, length, 256):
                cols = slice(at, at + 256)
                gp = lax.dot_general(only, grad[cols], NT, preferred_element_type=F32)
                probs = p_ref[2 * g + head, :, cols].astype(F32)
                weighted = jnp.sum(probs * gp, axis=0, keepdims=True)
                dst[:, cols] = (probs * (gp - weighted)).astype(BF16)
            dqt[64 * head : 64 * head + 64, :] = (
                jnp.dot(keys_t[64 * head : 64 * head + 64], dst[...], preferred_element_type=F32) * 0.125
            ).astype(BF16)
            dks.append(jnp.dot(dst[...], query, preferred_element_type=F32))
            dvs.append(jnp.dot(p_ref[2 * g + head], grad, preferred_element_type=F32))
        cols = pl.ds(pl.multiple_of(g * 128, 128), 128)
        dq_ref[:, cols] = dqt[...].T
        dk_ref[:, cols] = (jnp.where(low, dks[0], dks[1]) * 0.125).astype(BF16)
        dv_ref[:, cols] = jnp.where(low, dvs[0], dvs[1]).astype(BF16)
        return carry

    lax.fori_loop(0, pairs, pair, 0)


def attend_back(proj, probs, grad_mixed, y):
    length, wide = proj.shape
    shape = struct((length, wide // 6), BF16)
    return call(
        lambda *refs: attend_back_kernel(*refs, y=y),
        "attend_back",
        (shape, shape, shape),
        [VMEM] * 3,
        (VMEM,) * 3,
        [pltpu.VMEM((length, length), BF16), pltpu.VMEM((128, length), BF16)],
        2,
        6,
        (proj, probs, grad_mixed),
    )


def last_kernel(x_ref, sums1_ref, sums2_ref, sum_up_ref, *refs, orders):
    parts, (pieces_own, pieces_sib, whole, vec, sem) = refs[:6], refs[6:]
    half = parts[0].shape[1]
    rows = whole.shape[0]
    x_t = x_ref[...].T
    sums = [[], []]
    for y in range(2):
        for which in range(3):
            at = (y * 3 + which) * half
            value = parts[y * 3 + which][...]
            whole[:, at : at + half] = jnp.dot(x_t, value, preferred_element_type=F32).astype(BF16)
            if which != 1:
                sums[which // 2].append(jnp.sum(value.astype(F32), axis=0, keepdims=True))
    sent = piece_copies(places(orders), pieces_own, pieces_sib, sem, whole, 0, 3 * half, False)
    vectors = sums[0] + sums[1] + [ref[i : i + 1, :] for ref in (sums1_ref, sums2_ref) for i in range(3)]
    at = 0
    across = vec.shape[1] // 128
    wide = []
    for vector in vectors + [sum_up_ref[...]]:
        for low in range(0, vector.shape[1], 128):
            wide.append(vector[:, low : low + 128])
    for row in range(8):
        vec[row : row + 1, :] = jnp.concatenate(wide[row * across : (row + 1) * across], axis=1)
    pieces_own[rows:, :] = vec[...].astype(BF16)
    pieces_sib[rows:, :] = vec[...].astype(BF16)
    finish(sent)


def last(orders, x, sums1, sums2, sum_up, parts):
    length, width = x.shape
    piece = struct((width + 8, 3 * width // 2), BF16)
    return call(
        lambda *refs: last_kernel(*refs, orders=orders),
        "last",
        (piece, piece),
        [VMEM] * 10,
        (VMEM, VMEM),
        [
            pltpu.VMEM((width, 3 * width), BF16),
            pltpu.VMEM((8, 3 * width // 2), F32),
            pltpu.SemaphoreType.DMA((32,)),
        ],
        1,
        8,
        (x, sums1, sums2, sum_up) + tuple(parts),
    )


def vectors_kernel(one_ref, two_ref, qv_ref, up_ref, *refs):
    t = lax.axis_index("tp")
    rows, cols = one_ref.shape
    across = cols // 128
    value = one_ref[rows - 8 :, :].astype(F32)
    if two_ref is not None:
        value = value + two_ref[rows - 8 :, :].astype(F32)

    def block(at):
        row, low = at // across, at % across * 128
        return value[row : row + 1, low : low + 128]

    def take(out, row, first, other, count):
        for i in range(count):
            one = block(first + i)
            if other != first:
                one = jnp.where(t == 0, one, block(other + i))
            if row is None:
                out[i * 128 : (i + 1) * 128] = one[0]
            else:
                out[row : row + 1, i * 128 : (i + 1) * 128] = one

    narrow, wide = qv_ref.shape[1] // 128, up_ref.shape[0] // 128
    for which in range(2):
        take(qv_ref, which, 2 * which * narrow, (2 * which + 1) * narrow, narrow)
    for i, ref in enumerate(refs):
        take(ref, None, (4 + 2 * i) * narrow, (4 + 2 * i) * narrow, 2 * narrow)
    base = (4 + 2 * len(refs)) * narrow
    take(up_ref, None, base, base + wide, wide)


def vectors(one, two, local_width, local_units):
    shapes = [(2, local_width), (local_units,)] + [(2 * local_width,)] * 6
    given = (one,) if two is None else (one, two)

    def kernel(*refs):
        if two is None:
            refs = (refs[0], None) + refs[1:]
        vectors_kernel(*refs)

    return call(
        kernel,
        "vectors",
        tuple(struct(shape, F32) for shape in shapes),
        [VMEM] * len(given),
        (VMEM,) * 8,
        [],
        1,
        4,
        given,
    )


def add_kernel(*refs, low, high, vec, count):
    terms, out = refs[:-1], refs[-1]
    total = terms[0][low:high, :].astype(F32)
    for term in terms[1:count]:
        total = total + term[low:high, :].astype(F32)
    out[: high - low, :] = total.astype(BF16)
    if vec:
        total = 0.0
        for i in vec:
            total = total + terms[i][terms[i].shape[0] - 8 :, :].astype(F32)
        out[high - low :, :] = total.astype(BF16)


def add_up(terms, low, high, vec=(), lone=()):
    count, terms = len(terms), list(terms) + list(lone)
    cols = terms[0].shape[1]
    return call(
        lambda *refs: add_kernel(*refs, low=low, high=high, vec=vec, count=count),
        "add",
        struct((high - low + (8 if vec else 0), cols), BF16),
        [VMEM] * len(terms),
        VMEM,
        [],
        1,
        4,
        tuple(terms),
    )


def deliver_kernel(own_ref, core_ref, x_ref, y_ref, out_ref):
    c, t = lax.axis_index("ctx"), lax.axis_index("tp")
    sources = [(own_ref, 0), (core_ref, 0), (x_ref, 0), (x_ref, 1)] + [(y_ref, i) for i in range(4)]
    for i, (ref, at) in enumerate(sources):
        ctx = c ^ ((i & 1) + (i & 2))
        out_ref[ctx * 2 + (t ^ (i >> 2))] = ref[at]


def deliver(own, core, x, y):
    return call(
        deliver_kernel,
        "deliver",
        struct((2 * own.shape[0],) + own.shape[1:], BF16),
        [VMEM] * 4,
        VMEM,
        [],
        3,
        6,
        (own, core, x, y),
    )


def input_back_kernel(weight_ref, gz1_ref, *refs, fast):
    parts, chunks_ref = refs[:6], refs[6]
    half = parts[0].shape[1]
    total = gz1_ref[...]
    for i, part in enumerate(parts):
        total = total + lax.dot_general(
            part[...], weight_ref[:, i * half : (i + 1) * half], NT, preferred_element_type=F32
        )
    total = total.astype(BF16)
    count, block = chunks_ref.shape[:2]
    for i in range(count):
        spot = i
        if fast:
            c = lax.axis_index("ctx") ^ i
            spot = (c & 1) * 2 + (c >> 1)
        chunks_ref[spot] = total[i * block : (i + 1) * block]


def input_back(weight, gz1, parts, chunk, fast):
    length, width = gz1.shape
    return call(
        lambda *refs: input_back_kernel(*refs, fast=fast),
        "input_back",
        struct((length // chunk, chunk, width), BF16),
        [VMEM] * 8,
        VMEM,
        [],
        1,
        6,
        (weight, gz1) + tuple(parts),
    )


def settle_kernel(pair_ref, got_ref, *refs, cuts):
    outs, four = refs[: len(cuts)], refs[len(cuts)]
    rows = pair_ref.shape[0] // 2
    for i in range(4):
        ref = (pair_ref, got_ref)[i // 2]
        owner = lax.axis_index("ctx") ^ ((i & 1) * 2 + (i >> 1))
        low = i % 2 * rows
        four[pl.ds(pl.multiple_of(owner * rows, 16), rows), :] = ref[low : low + rows, :].astype(F32)
    for out, (low, high, form) in zip(outs, cuts):
        if form == "plain":
            out[...] = four[:, low:high]
        else:
            step = (high - low) // 3
            for j in range(3):
                out[j] = four[:, low + j * step : low + (j + 1) * step]


def settle(pair, got, cuts):
    rows, cols = pair.shape[0] // 2, pair.shape[1]
    shapes = {"plain": lambda n: (4 * rows, n), "three": lambda n: (3, 4 * rows, n // 3)}
    return call(
        lambda *refs: settle_kernel(*refs, cuts=cuts),
        "settle",
        tuple(struct(shapes[form](high - low), F32) for low, high, form in cuts),
        [VMEM, VMEM],
        (VMEM,) * len(cuts),
        [pltpu.VMEM((4 * rows, cols), F32)],
        3,
        6,
        (pair, got),
    )


def cut(full):
    rows, cols = full.shape
    return full[:, : cols // 2], full[:, cols // 2 :]


def gather_plain(shard):
    rows = lax.all_gather(shard, "fsdp", axis=0, tiled=True)
    return lax.all_gather(rows, "tp", axis=1, tiled=True)


def reduce_plain(own, sib):
    full = jnp.concatenate([own, sib], axis=1)
    part = lax.psum_scatter(full, "tp", scatter_dimension=1, tiled=True)
    part = lax.psum_scatter(part, "fsdp", scatter_dimension=0, tiled=True)
    return lax.psum(part, "ctx").astype(F32)


def body(
    layer_input,
    doc_ids,
    w_qkv,
    b_qv,
    w_out,
    b_out,
    ln1_gain,
    ln1_bias,
    w_up,
    b_up,
    w_down,
    b_down,
    ln2_gain,
    ln2_bias,
    out_grad,
):
    sizes = (lax.axis_size("fsdp"), lax.axis_size("ctx"), lax.axis_size("tp"))
    micro, seqs, local_len, width = layer_input.shape
    length = local_len * sizes[1]
    shard_rows, local_width = w_qkv.shape[1:]
    local_units = w_up.shape[1]
    heads = width // HEAD_DIM
    fast = sizes == (4, 4, 2)
    t = lax.axis_index("tp")
    c = lax.axis_index("ctx")

    def mine(value):
        return lax.dynamic_index_in_dim(value, t, 1, keepdims=False)

    def to_owners(chunks):
        return lax.all_to_all(chunks, "ctx", 0, 0, tiled=True)

    def spread(chunks):
        out = lax.all_to_all(chunks, ("ctx", "tp"), 0, 0, tiled=True)
        return out.reshape(micro, seqs, local_len, width)

    shards = (
        jnp.swapaxes(w_qkv, 0, 1).reshape(shard_rows, 3 * local_width),
        jnp.concatenate([w_out.T, w_up], axis=1),
        w_down.T,
    )
    ids = mine(doc_ids).astype(BF16)[:, None, :]
    ids = jnp.pad(ids, ((0, 0), (0, 7), (0, width - local_len)))
    rows_in = jnp.concatenate([mine(layer_input), ids], axis=1)
    cot_in = mine(out_grad)
    small = jnp.concatenate([b_qv.reshape(-1), b_up])[None]
    table = jnp.stack([b_out, ln1_gain, ln1_bias, b_down, ln2_gain, ln2_bias, b_out, b_out])
    gathers = GATHER if fast else (None,) * 3
    packs = tuple(packing(order) for order in SCATTER) if fast else (None,) * 3

    def swap(value, group, step):
        order = tuple(zip(*GATHER[group])) + (CORE,)
        return exchange(value, order[step], sizes)

    def shed(value, group, step):
        order = (CORE,) + tuple(zip(*SCATTER[group]))
        return exchange(value, order[step], sizes)

    def joined(*parts):
        return jnp.concatenate(parts, axis=0)

    if fast:
        def seen(value):
            return [lax.dynamic_index_in_dim(value, c ^ i, 0, keepdims=True) for i in range(4)]

        part = shard_rows // 4
        h1, h2, h3 = [lax.dynamic_slice_in_dim(s, c * part, part, 0) for s in shards]
        x0, x1, x2, x3 = seen(rows_in)
        g1, xk = phase(swap(h1, 0, 0), exchange(joined(x1, x3), CORE, sizes))
        h1 = joined(h1, g1)
        g1, xx, table = phase(swap(h1, 0, 1), exchange(joined(x2, xk[1:]), X, sizes), table)
        given = (x0, xk, xx)
        h1 = joined(h1, g1)
        h1, h2, small, cot_in = phase(h1, h2, small, cot_in)
        c0, c1, c2, c3 = seen(cot_in)
        g1, g2, got, ck = phase(
            swap(h1, 0, 2), swap(h2, 1, 0), exchange(small, Y, sizes), exchange(joined(c1, c3), CORE, sizes)
        )
        small = joined(small, got)
        h1, h2 = phase(joined(h1, g1), joined(h2, g2))
        g1, g2 = phase(swap(h1, 0, 3), swap(h2, 1, 1))
        h1, h2, h3 = phase(joined(h1, g1), joined(h2, g2), h3)
        g1, g2, g3 = swap(h1, 0, 4), swap(h2, 1, 2), swap(h3, 2, 0)
        (wq,) = unpack(gathers[0], h1, g1, (3 * width,))
        proj, rows_b, mask = project(wq, given, small, fast)
        proj, g2, g3, c2, ck = phase(proj, g2, g3, c2, ck)
        h2, h3 = joined(h2, g2), joined(h3, g3)
        g2, g3 = swap(h2, 1, 3), swap(h3, 2, 1)
        mixed0, probs0 = attend(after(proj, h2, h3), mask, 0)
        mixed0, g3 = phase(mixed0, g3)
        h3 = joined(h3, g3)
        g3 = swap(h3, 2, 2)
        mixed1, probs1 = attend(after(proj, h3, mixed0), mask, 1)
        mixed1, g2, g3 = phase(mixed1, g2, g3)
        h2, h3, c_send = phase(joined(h2, g2), joined(h3, g3), joined(c2, ck[1:]))
        g2, g3, cx = swap(h2, 1, 4), swap(h3, 2, 3), exchange(c_send, X, sizes)
        cot = (c0, ck, cx)
        wo, wu = unpack(gathers[1], h2, g2, (width, 2 * local_units))
    else:
        parts = (shards[0], w_out.T, w_up, w_down.T)
        pieces = [cut(gather_plain(s)) for s in parts]
        (wq,) = unpack(None, *pieces[0], (3 * width,))
        (wo,) = unpack(None, *pieces[1], (width,))
        (wu,) = unpack(None, *pieces[2], (2 * local_units,))
        (wd,) = unpack(None, *pieces[3], (2 * local_units,))
        order = lambda value: (value[:1], value[1:3], value[2:])
        given, cot = order(to_owners(rows_in)), order(to_owners(cot_in))
        small = joined(small, exchange(small, Y, sizes))
        proj, rows_b, mask = project(wq, given, small, fast)
        mixed0, probs0 = attend(proj, mask, 0)
        mixed1, probs1 = attend(proj, mask, 1)

    normed1, scale1, first_b, act, slope = middle(wo, wu, mixed0, mixed1, rows_b, table, small)
    if fast:
        act, g3, cx = phase(act, g3, cx)
        cot = (c0, ck, cx)
        h3 = joined(h3, g3)
        (wd,) = unpack(gathers[2], h3, swap(h3, 2, 4), (2 * local_units,))
    chunks, gz, gzb, sums2, down_own, down_sib = turn(packs[2], wd, act, normed1, cot, table, local_len)

    rows = shard_rows // 4
    if fast:
        down_sib, chunks, gzb = phase(down_sib, chunks, gzb)
        got, core_out = shed(down_sib, 2, 0), exchange(chunks[2:], CORE, sizes)
    gh, sum_up = hidden_back(wd, gzb, slope)
    if fast:
        gh, got, core_out = phase(gh, got, core_out)
        down = [down_own, got]
        send, x_send, gh = phase(
            add_up(down, 8 * rows, 16 * rows), joined(chunks[1:2], core_out[1:2]), gh
        )
        got, x_out = shed(send, 2, 1), exchange(x_send, X, sizes)
    gz1, grad_mixed, sums1, up_own, up_sib = first_back(
        packs[1], wo, wu, gh, gz, normed1, scale1, table, first_b, mixed0, mixed1
    )
    if fast:
        grad_mixed, up_sib, got, x_out = phase(grad_mixed, up_sib, got, x_out)
        down = down + [got]
        send, y_send, grad_mixed = phase(
            add_up(down, 4 * rows, 8 * rows), joined(chunks[:1], core_out[:1], x_out), grad_mixed
        )
        got, got2 = shed(send, 2, 2), shed(up_sib, 1, 0)
    parts0 = attend_back(proj, probs0, grad_mixed, 0)
    if fast:
        head, got2, grad_mixed = phase(parts0[0], got2, grad_mixed)
        parts0 = (head,) + tuple(parts0[1:])
        up = [up_own, got2]
        send2, grad_mixed, y_send = phase(add_up(up, 8 * rows, 16 * rows), grad_mixed, y_send)
        got2, y_out = shed(send2, 1, 1), exchange(y_send, Y, sizes)
    parts1 = attend_back(proj, probs1, grad_mixed, 1)
    parts = list(parts0) + list(parts1)
    chunks2 = input_back(wq, gz1, parts, local_len, fast)
    parts[0] = after(parts[0], chunks2)
    qkv_own, qkv_sib = last(packs[0], rows_b, sums1, sums2, sum_up, parts)
    if fast:
        chunks2, qkv_sib, got, got2, y_out = phase(chunks2, qkv_sib, got, got2, y_out)
        down, up = down + [got], up + [got2]
        send = add_up(down, 2 * rows, 4 * rows)
        send2 = add_up(up, 4 * rows, 8 * rows)
        qkv_sib, send, send2, chunks2 = phase(qkv_sib, send, send2, chunks2)
        got3, got, got2, core_x = (
            shed(qkv_sib, 0, 0), shed(send, 2, 3), shed(send2, 1, 2), exchange(chunks2[2:], CORE, sizes)
        )
        got3, core_x = phase(got3, core_x)
        qkv = [qkv_own, got3]
        sent3 = add_up(qkv, 8 * rows, 16 * rows, (0, 1))
        x_send = joined(chunks2[1:2], core_x[1:2])
        got3 = shed(sent3, 0, 1)
        sent3, x_send, got = phase(sent3, x_send, got)
        down = down + [got]
        got = shed(add_up(down, rows, 2 * rows), 2, 4)
        got3, got2 = phase(got3, got2)
        up, qkv = up + [got2], qkv + [got3]
        send3 = add_up(qkv, 4 * rows, 8 * rows, (3, 2), [sent3])
        send2 = add_up(up, 2 * rows, 4 * rows)
        send3, send2, x_send, got = phase(send3, send2, x_send, got)
        got3, got2, x_x = shed(send3, 0, 2), shed(send2, 1, 3), exchange(x_send, X, sizes)
        pair1 = add_up(down + [got], 0, rows)
        pair1, send3 = phase(pair1, send3)
        got = exchange(pair1, X, sizes)
        got3, got2, got, x_x = phase(got3, got2, got, x_x)
        up, qkv = up + [got2], qkv + [got3]
        sent3 = add_up(qkv, 2 * rows, 4 * rows, (4, 3), [send3])
        send2 = add_up(up, rows, 2 * rows)
        pair1, y_send = joined(pair1, got), joined(chunks2[:1], core_x[:1], x_x)
        sent3, send2, pair1, y_send = phase(sent3, send2, pair1, y_send)
        got3, got2, got1 = shed(sent3, 0, 3), shed(send2, 1, 4), exchange(pair1, CORE, sizes)
        y_x = exchange(y_send, Y, sizes)
        layer_output = deliver(chunks, core_out, x_out, y_out)
        got3, got2, got1, layer_output = phase(got3, got2, got1, layer_output)
        up, qkv = up + [got2], qkv + [got3]
        send3 = add_up(qkv, rows, 2 * rows, (5, 4), [sent3])
        pair2 = add_up(up, 0, rows)
        send3, pair2, got1 = phase(send3, pair2, got1)
        got3, got2 = shed(send3, 0, 4), exchange(pair2, X, sizes)
        (grad_down,) = settle(pair1, got1, ((0, local_units, "plain"),))
        got3, got2, grad_down, y_x = phase(got3, got2, grad_down, y_x)
        qkv = qkv + [got3]
        pair3, pair2 = phase(add_up(qkv, 0, rows), joined(pair2, got2))
        got, got2 = exchange(pair3, X, sizes), exchange(pair2, CORE, sizes)
        vec = vectors(after(send3, pair3), got3, local_width, local_units)
        grad_wout, grad_up = settle(
            pair2, got2, ((0, local_width, "plain"), (local_width, local_width + local_units, "plain"))
        )
        got, grad_up, bup = phase(got, grad_up, vec[1])
        vec = (vec[0], bup) + tuple(vec[2:])
        pair3 = joined(pair3, got)
        got3 = exchange(pair3, CORE, sizes)
        grad_x = deliver(chunks2, core_x, x_x, y_x)
        (grad_qkv,) = settle(pair3, after(got3, grad_x), ((0, 3 * local_width, "three"),))
        layer_output = layer_output.reshape(micro, seqs, local_len, width)
        grad_x = grad_x.reshape(micro, seqs, local_len, width)
    else:
        layer_output = spread(jnp.repeat(chunks, 2, axis=0))
        grad_x = spread(jnp.repeat(chunks2, 2, axis=0))
        vec = lax.psum(qkv_own[width:].astype(F32), AXES)
        vec = vectors(vec, None, local_width, local_units)
        grad_down = reduce_plain(down_own, down_sib)
        both = reduce_plain(up_own, up_sib)
        grad_wout, grad_up = both[:, :local_width], both[:, local_width:]
        grad_qkv = reduce_plain(qkv_own[:width], qkv_sib[:width])
        grad_qkv = jnp.swapaxes(grad_qkv.reshape(shard_rows, 3, local_width), 0, 1)

    out_bqv, out_bup, g1, s1, bout, g2, s2, bdown = vec
    return (
        layer_output,
        grad_x,
        grad_qkv,
        out_bqv,
        grad_wout.T,
        bout,
        g1,
        s1,
        grad_up,
        out_bup,
        grad_down.T,
        bdown,
        g2,
        s2,
    )


def solution(mesh):
    return jax.shard_map(
        body,
        mesh=mesh,
        in_specs=(
            P(None, "fsdp", "ctx", None),
            P(None, "fsdp", "ctx"),
            P(None, "fsdp", "tp"),
            P(None, "tp"),
            P("tp", "fsdp"),
            P(),
            P(),
            P(),
            P("fsdp", "tp"),
            P("tp"),
            P("tp", "fsdp"),
            P(),
            P(),
            P(),
            P(None, "fsdp", "ctx", None),
        ),
        out_specs=(
            P(None, "fsdp", "ctx", None),
            P(None, "fsdp", "ctx", None),
            P(None, "fsdp", "tp"),
            P(None, "tp"),
            P("tp", "fsdp"),
            P(),
            P(),
            P(),
            P("fsdp", "tp"),
            P("tp"),
            P("tp", "fsdp"),
            P(),
            P(),
            P(),
        ),
        check_vma=False,
    )
```

```python
import jax
import jax.numpy as jnp
from jax import lax
from jax.experimental import pallas as pl
from jax.experimental.pallas import tpu as pltpu
from jax.sharding import PartitionSpec as P

HEAD_DIM = 64
AXES = ("fsdp", "ctx", "tp")
F32 = jnp.float32
BF16 = jnp.bfloat16
NEG = -1e30
NT = (((1,), (1,)), ((), ()))
VMEM = pl.BlockSpec(memory_space=pltpu.VMEM)
SMEM = pl.BlockSpec(memory_space=pltpu.SMEM)
ANY = pl.BlockSpec(memory_space=pl.ANY)


def partner(dim, z, c, t):
    if dim == "core":
        return z, c ^ 1, t
    if dim == "x":
        return z, c ^ 2, t
    if dim == "x+core":
        return z, c ^ 3, t
    if dim == "y":
        return z, c, t ^ 1
    return z ^ int(dim[1:]), c, t


def exchange(value, dims, sizes):
    nz, nc, nt = sizes
    pairs = []
    for z in range(nz):
        for c in range(nc):
            for t in range(nt):
                tz, tc, tt = partner(dims[c & 1], z, c, t)
                pairs.append(((z * nc + c) * nt + t, (tz * nc + tc) * nt + tt))
    return lax.ppermute(value, AXES, pairs)


GATHER = (
    (("z2", "z1", "y", "x"), ("z1", "z2", "x", "y")),
    (("z2", "z1", "y", "x"), ("z1", "z2", "x", "y")),
    (("z2", "z1", "x", "y"), ("y", "x", "z2", "z1")),
)
SCATTER = (
    (("x", "y", "z1", "z2"), ("y", "z1", "z2", "x")),
    (("x", "y", "z1", "z2"), ("z1", "z2", "y", "x")),
    (("y", "x", "z1", "z2"), ("z1", "z2", "x", "y")),
)
CORE = ("core", "core")
X = ("x", "x")
FAR = ("x+core", "x+core")
Y = ("y", "y")


def piece_place(order, core, here, index):
    z, x, t = here
    for bit, dim in enumerate(order):
        flip = (index >> bit) & 1
        if dim == "x":
            x = x ^ flip
        elif dim == "y":
            t = t ^ flip
        else:
            z = z ^ (flip * int(dim[1:]))
    return z * 4 + x * 2 + core, t


def places(orders):
    if orders is None:
        return [(i, half) for half in range(2) for i in range(16)]
    c = lax.axis_index("ctx")
    here = (lax.axis_index("fsdp"), c >> 1, lax.axis_index("tp"))
    spots = []
    for core in (c & 1, 1 - (c & 1)):
        for i in range(16):
            r0, t0 = piece_place(orders[0], core, here, i)
            r1, t1 = piece_place(orders[1], core, here, i)
            spots.append((jnp.where(core == 0, r0, r1), jnp.where(core == 0, t0, t1)))
    return spots


def packing(orders):
    return tuple(order[::-1] for order in orders)


def after(value, *first):
    return lax.optimization_barrier((value, first))[0]


def phase(*values):
    return lax.optimization_barrier(values)


def at_rows(place, count, unit=0):
    start = place * count
    return pl.ds(start if isinstance(start, int) else pl.multiple_of(start, unit or count), count)


def piece_copies(spots, own_ref, sib_ref, sem, whole, low, cols, base=0):
    rows = whole.shape[0] // 16
    copies = []
    for half, ref in ((0, own_ref), (1, sib_ref)):
        for i in range(16):
            row, col = spots[half * 16 + i]
            copy = pltpu.make_async_copy(
                ref.at[pl.ds(i * rows, rows), pl.ds(low, cols)],
                whole.at[at_rows(row, rows), at_rows(col, cols, 128)],
                sem.at[base + half * 16 + i],
            )
            copy.start()
            copies.append(copy)
    return copies


def pack(spots, own_ref, sib_ref, whole, low, cols):
    rows = whole.shape[0] // 16
    for half, ref in ((0, own_ref), (1, sib_ref)):
        for i in range(16):
            row, col = spots[half * 16 + i]
            ref[i * rows : (i + 1) * rows, low : low + cols] = whole[at_rows(row, rows), at_rows(col, cols, 128)]


def finish(copies):
    for copy in copies:
        copy.wait()


def tiles(count, step):
    def run(one):
        lax.fori_loop(0, count // step, lambda i, carry: (one(pl.multiple_of(i * step, step)), carry)[1], 0)

    return run


def row_mean(value):
    return jnp.mean(value, axis=-1, keepdims=True)


def struct(shape, dtype):
    return jax.ShapeDtypeStruct(shape, dtype)


def call(kernel, name, outs, specs, out_specs, scratch, time, room, args):
    return pl.pallas_call(
        kernel,
        name=name,
        out_shape=outs,
        in_specs=specs,
        out_specs=out_specs,
        scratch_shapes=scratch,
        compiler_params=pltpu.CompilerParams(vmem_limit_bytes=room << 20),
        cost_estimate=pl.CostEstimate(flops=time * 10**9, transcendentals=0, bytes_accessed=10**6),
    )(*args)


B_OUT, GAIN1, SHIFT1, B_DOWN, GAIN2, SHIFT2 = range(6)


def unpack_kernel(own_ref, sib_ref, *refs, orders):
    outs, sem = refs[:-1], refs[-1]
    copies = []
    spots = places(orders)
    low = 0
    for i, out in enumerate(outs):
        cols = out.shape[1] // 2
        copies += piece_copies(spots, own_ref, sib_ref, sem, out, low, cols, 32 * i)
        low += cols
    finish(copies)


def unpack(orders, own, sib, widths):
    rows = own.shape[0]
    return call(
        lambda *refs: unpack_kernel(*refs, orders=orders),
        "unpack",
        tuple(struct((rows, width), BF16) for width in widths),
        [ANY, ANY],
        (VMEM,) * len(widths),
        [pltpu.SemaphoreType.DMA((32 * len(widths),))],
        5,
        2,
        (own, sib),
    )


def sources(refs, fast):
    c = lax.axis_index("ctx") if fast else 0
    own, core, x = refs
    return [(c ^ 0, own, 0), (c ^ 1, core, 0), (c ^ 2, x, 0), (c ^ 3, x, 1)]


def tables_kernel(qv_ref, up_ref, *refs):
    rows, (table_ref, small_ref) = refs[:-2], refs[-2:]
    table_ref[...] = jnp.zeros_like(table_ref)
    for i, ref in enumerate(rows):
        table_ref[i : i + 1, :] = ref[...][None]
    width = qv_ref.shape[1]
    small_ref[:, :width] = qv_ref[0:1, :]
    small_ref[:, width : 2 * width] = qv_ref[1:2, :]
    small_ref[:, 2 * width :] = up_ref[...][None]


def tables(b_qv, b_up, rows):
    return call(
        tables_kernel,
        "tables",
        (struct((8, rows[0].shape[0]), F32), struct((1, b_qv.size + b_up.size), F32)),
        [VMEM] * (2 + len(rows)),
        (VMEM, VMEM),
        [],
        1,
        3,
        (b_qv, b_up) + tuple(rows),
    )


def project_kernel(weight_ref, own_ref, core_ref, far_ref, small_ref, proj_ref, x_ref, mask_ref, ids, *, fast):
    block = own_ref.shape[1] - 8
    count = 4
    for spot, ref, i in sources((own_ref, core_ref, far_ref), fast):
        x_ref[pl.ds(pl.multiple_of(spot * block, block), block), :] = ref[i, 0:block, :]
        ids[pl.ds(spot, 1), :] = ref[i, block:, 0:block].astype(F32)[0:1]
    for kb in range(count):
        column = jnp.broadcast_to(ids[kb : kb + 1], (block, block)).T
        for qb in range(count):
            mask_ref[kb * block : (kb + 1) * block, qb * block : (qb + 1) * block] = jnp.where(
                column == jnp.broadcast_to(ids[qb : qb + 1], (block, block)), 0.0, NEG
            )
    width = proj_ref.shape[1] // 6
    for y in range(2):
        row = pl.ds(lax.axis_index("tp") ^ y, 1)
        for which in range(3):
            at = (y * 3 + which) * width
            value = jnp.dot(x_ref[...], weight_ref[:, at : at + width], preferred_element_type=F32)
            if which != 1:
                low = 0 if which == 0 else width
                value = value + small_ref[row, low : low + width]
            proj_ref[:, at : at + width] = value.astype(BF16)


def project(weight, given, small, fast):
    width, wide = weight.shape
    block = given[0].shape[1] - 8
    length = 4 * block
    return call(
        lambda *refs: project_kernel(*refs, fast=fast),
        "project",
        (
            struct((length, wide), BF16),
            struct((length, width), BF16),
            struct((length, length), F32),
        ),
        [VMEM] * 5,
        (VMEM,) * 3,
        [pltpu.VMEM((8, block), F32)],
        5,
        3,
        (weight,) + tuple(given) + (small,),
    )


def attend_kernel(proj_ref, mask_ref, o_ref, p_ref, *, y):
    length = proj_ref.shape[0]
    pairs = o_ref.shape[1] // 128
    lane = lax.broadcasted_iota(jnp.int32, (1, 128), 1)

    def pair(g, carry):
        take = lambda which: proj_ref[:, pl.ds(pl.multiple_of(((y * 3 + which) * pairs + g) * 128, 128), 128)]
        query = take(0) * jnp.asarray(0.125, BF16)
        keys = take(1)
        values_t = take(2).T
        outs = []
        for head in range(2):
            here = (lane >= 64 * head) & (lane < 64 * head + 64)
            only = jnp.where(here, keys, jnp.zeros_like(keys))
            row = []
            for at in range(0, length, 256):
                scores = lax.dot_general(only, query[at : at + 256], NT, preferred_element_type=F32)
                scores = scores + mask_ref[:, at : at + 256]
                top = jnp.max(scores, axis=0, keepdims=True)
                raised = jnp.exp(scores - top)
                total = jnp.sum(raised, axis=0, keepdims=True)
                probs = (raised * (1.0 / total)).astype(BF16)
                p_ref[2 * g + head, :, at : at + 256] = probs
                row.append(
                    jnp.dot(values_t[64 * head : 64 * head + 64], probs, preferred_element_type=F32)
                )
            outs.append(jnp.concatenate(row, axis=1))
        both = jnp.concatenate(outs, axis=0).astype(BF16)
        o_ref[:, pl.ds(pl.multiple_of(g * 128, 128), 128)] = both.T
        return carry

    lax.fori_loop(0, pairs, pair, 0)


def attend(proj, mask, y):
    length, wide = proj.shape
    half = wide // 6
    return call(
        lambda *refs: attend_kernel(*refs, y=y),
        "attend",
        (struct((length, half), BF16), struct((half // HEAD_DIM, length, length), BF16)),
        [VMEM, VMEM],
        (VMEM, VMEM),
        [],
        12,
        3,
        (proj, mask),
    )


def middle_kernel(
    w_out, w_up, mixed0_ref, mixed1_ref, x_ref, table_ref, small_ref,
    normed_ref, scale_ref, first_ref, act_ref, slope_ref,
):
    length, units = act_ref.shape
    narrow, half = w_out.shape[1] // 2, units // 2
    normed_ref[...] = lax.dot_general(
        mixed0_ref[...], w_out[:, :narrow], NT, preferred_element_type=F32
    ) + lax.dot_general(mixed1_ref[...], w_out[:, narrow:], NT, preferred_element_type=F32)

    @tiles(length, 64)
    def _(at):
        here = pl.ds(at, 64)
        value = x_ref[here, :].astype(F32) + normed_ref[here, :] + table_ref[B_OUT : B_OUT + 1, :]
        centred = value - row_mean(value)
        scale = lax.rsqrt(row_mean(centred * centred) + 1e-12)
        unit = centred * scale
        normed_ref[here, :] = unit
        scale_ref[here, :] = scale
        first_ref[here, :] = (
            unit * table_ref[GAIN1 : GAIN1 + 1, :] + table_ref[SHIFT1 : SHIFT1 + 1, :]
        ).astype(BF16)

    for y in range(2):
        row = pl.ds(lax.axis_index("tp") ^ y, 1)

        @tiles(half, 256)
        def _(at):
            here = pl.ds(pl.multiple_of(y * half + at, 256), 256)
            bias = small_ref[row, pl.ds(pl.multiple_of(2 * narrow + at, 256), 256)]
            hidden = jnp.dot(first_ref[...], w_up[:, here], preferred_element_type=F32) + bias
            phi = 0.5 + 0.5 * lax.erf(hidden * 0.7071067811865476)
            act_ref[:, here] = (hidden * phi).astype(BF16)
            bell = jnp.exp(-0.5 * hidden * hidden) * 0.3989422804014327
            slope_ref[:, here] = (phi + hidden * bell).astype(BF16)


def middle(w_out, w_up, mixed0, mixed1, x, table, small):
    length, width = x.shape
    units = w_up.shape[1]
    return call(
        middle_kernel,
        "middle",
        (
            struct((length, width), F32),
            struct((length, 1), F32),
            struct((length, width), BF16),
            struct((length, units), BF16),
            struct((length, units), BF16),
        ),
        [VMEM] * 7,
        (VMEM,) * 5,
        [],
        12,
        3,
        (w_out, w_up, mixed0, mixed1, x, table, small),
    )


def turn_kernel(
    weight_ref, act_ref, normed_ref, own_ref, core_ref, far_ref, table_ref,
    chunks_ref, gz_ref, gzb_ref, sums_ref, down_own, down_sib, full, cot_ref, *, orders,
):
    length = act_ref.shape[0]
    block = chunks_ref.shape[1]
    for spot, ref, i in sources((own_ref, core_ref, far_ref), orders is not None):
        cot_ref[pl.ds(pl.multiple_of(spot * block, block), block), :] = ref[i]
    gz_ref[...] = lax.dot_general(act_ref[...], weight_ref[...], NT, preferred_element_type=F32)
    sums_ref[...] = jnp.zeros_like(sums_ref)
    row = lambda which: table_ref[which : which + 1, :]

    @tiles(length, 64)
    def _(at):
        here = pl.ds(at, 64)
        value = normed_ref[here, :] * row(GAIN1) + row(SHIFT1) + gz_ref[here, :] + row(B_DOWN)
        centred = value - row_mean(value)
        scale = lax.rsqrt(row_mean(centred * centred) + 1e-12)
        unit = centred * scale
        result = (unit * row(GAIN2) + row(SHIFT2)).astype(BF16)
        chunk = lax.div(at, block)
        if orders is not None:
            c = lax.axis_index("ctx") ^ chunk
            chunk = (c & 1) * 2 + (c >> 1)
        chunks_ref[chunk, pl.ds(pl.multiple_of(lax.rem(at, block), 64), 64), :] = result
        coming = cot_ref[here, :].astype(F32)
        raised = coming * row(GAIN2)
        back = scale * (raised - row_mean(raised) - unit * row_mean(raised * unit))
        gz_ref[here, :] = back
        gzb_ref[here, :] = back.astype(BF16)
        sums_ref[0:1, :] += jnp.sum(coming * unit, axis=0, keepdims=True)
        sums_ref[1:2, :] += jnp.sum(coming, axis=0, keepdims=True)
        sums_ref[2:3, :] += jnp.sum(back, axis=0, keepdims=True)

    back_t = gzb_ref[...].T

    @tiles(full.shape[1], 1024)
    def _(at):
        here = pl.ds(at, 1024)
        full[:, here] = jnp.dot(back_t, act_ref[:, here], preferred_element_type=F32).astype(BF16)

    pack(places(orders), down_own, down_sib, full, 0, down_own.shape[1])


def turn(orders, weight, act, normed, cot, table, chunk):
    length, units = act.shape
    width = normed.shape[1]
    piece = struct((width, units // 2), BF16)
    return call(
        lambda *refs: turn_kernel(*refs, orders=orders),
        "turn",
        (
            struct((length // chunk, chunk, width), BF16),
            struct((length, width), F32),
            struct((length, width), BF16),
            struct((8, width), F32),
            piece,
            piece,
        ),
        [VMEM] * 7,
        (VMEM,) * 6,
        [pltpu.VMEM((width, units), BF16), pltpu.VMEM((length, width), BF16)],
        14,
        10,
        (weight, act, normed) + tuple(cot) + (table,),
    )


def hidden_back_kernel(weight_ref, gzb_ref, slope_ref, gh_ref, sum_ref):
    @tiles(gh_ref.shape[1], 512)
    def _(at):
        here = pl.ds(at, 512)
        back = jnp.dot(gzb_ref[...], weight_ref[:, here], preferred_element_type=F32)
        back = (back * slope_ref[:, here].astype(F32)).astype(BF16)
        gh_ref[:, here] = back
        sum_ref[:, here] = jnp.sum(back.astype(F32), axis=0, keepdims=True)


def hidden_back(weight, gzb, slope):
    length, units = slope.shape
    return call(
        hidden_back_kernel,
        "hidden_back",
        (struct((length, units), BF16), struct((1, units), F32)),
        [VMEM] * 3,
        (VMEM, VMEM),
        [],
        12,
        3,
        (weight, gzb, slope),
    )


def first_back_kernel(
    w_out, w_up, gh_ref, gz_ref, normed_ref, scale_ref, table_ref, first_ref, mixed0_ref, mixed1_ref,
    gz1_ref, gm_ref, sums_ref, pieces_own, pieces_sib, branch, d_out, d_up, *, orders,
):
    narrow = w_out.shape[1] // 2
    half = w_up.shape[1] // 2
    length = gh_ref.shape[0]
    first_t = first_ref[...].T
    spots = places(orders)

    @tiles(d_up.shape[1], 1024)
    def _(at):
        here = pl.ds(at, 1024)
        d_up[:, here] = jnp.dot(first_t, gh_ref[:, here], preferred_element_type=F32).astype(BF16)

    pack(spots, pieces_own, pieces_sib, d_up, narrow, half)
    gz1_ref[...] = lax.dot_general(gh_ref[...], w_up[...], NT, preferred_element_type=F32)
    sums_ref[...] = jnp.zeros_like(sums_ref)

    @tiles(length, 64)
    def _(at):
        here = pl.ds(at, 64)
        coming = gz_ref[here, :] + gz1_ref[here, :]
        unit = normed_ref[here, :]
        raised = coming * table_ref[GAIN1 : GAIN1 + 1, :]
        back = scale_ref[here, :] * (raised - row_mean(raised) - unit * row_mean(raised * unit))
        gz1_ref[here, :] = back
        branch[here, :] = back.astype(BF16)
        sums_ref[0:1, :] += jnp.sum(coming * unit, axis=0, keepdims=True)
        sums_ref[1:2, :] += jnp.sum(coming, axis=0, keepdims=True)
        sums_ref[2:3, :] += jnp.sum(back, axis=0, keepdims=True)

    branch_t = branch[...].T
    d_out[:, :narrow] = jnp.dot(branch_t, mixed0_ref[...], preferred_element_type=F32).astype(BF16)
    d_out[:, narrow:] = jnp.dot(branch_t, mixed1_ref[...], preferred_element_type=F32).astype(BF16)
    pack(spots, pieces_own, pieces_sib, d_out, 0, narrow)
    gm_ref[...] = jnp.dot(branch[...], w_out[...], preferred_element_type=F32).astype(BF16)


def first_back(orders, w_out, w_up, gh, gz, normed, scale, table, first_b, mixed0, mixed1):
    length, units = gh.shape
    width = gz.shape[1]
    piece = struct((width, (units + width) // 2), BF16)
    return call(
        lambda *refs: first_back_kernel(*refs, orders=orders),
        "first_back",
        (
            struct((length, width), F32),
            struct((length, width), BF16),
            struct((8, width), F32),
            piece,
            piece,
        ),
        [VMEM] * 10,
        (VMEM,) * 5,
        [
            pltpu.VMEM((length, width), BF16),
            pltpu.VMEM((width, width), BF16),
            pltpu.VMEM((width, units), BF16),
        ],
        20,
        12,
        (w_out, w_up, gh, gz, normed, scale, table, first_b, mixed0, mixed1),
    )


def attend_back_kernel(proj_ref, p_ref, gm_ref, dq_ref, dk_ref, dv_ref, dst, dqt, *, y):
    length = proj_ref.shape[0]
    pairs = dq_ref.shape[1] // 128
    lane = lax.broadcasted_iota(jnp.int32, (1, 128), 1)
    low = lane < 64

    def pair(g, carry):
        take = lambda which: proj_ref[:, pl.ds(pl.multiple_of(((y * 3 + which) * pairs + g) * 128, 128), 128)]
        query, keys, values = take(0), take(1), take(2)
        grad = gm_ref[:, pl.ds(pl.multiple_of((y * pairs + g) * 128, 128), 128)]
        keys_t = keys.T
        dks, dvs = [], []
        for head in range(2):
            here = low if head == 0 else jnp.logical_not(low)
            only = jnp.where(here, values, jnp.zeros_like(values))
            for at in range(0, length, 256):
                cols = slice(at, at + 256)
                gp = lax.dot_general(only, grad[cols], NT, preferred_element_type=F32)
                probs = p_ref[2 * g + head, :, cols].astype(F32)
                weighted = jnp.sum(probs * gp, axis=0, keepdims=True)
                dst[:, cols] = (probs * (gp - weighted)).astype(BF16)
            dqt[64 * head : 64 * head + 64, :] = (
                jnp.dot(keys_t[64 * head : 64 * head + 64], dst[...], preferred_element_type=F32) * 0.125
            ).astype(BF16)
            dks.append(jnp.dot(dst[...], query, preferred_element_type=F32))
            dvs.append(jnp.dot(p_ref[2 * g + head], grad, preferred_element_type=F32))
        cols = pl.ds(pl.multiple_of(g * 128, 128), 128)
        dq_ref[:, cols] = dqt[...].T
        dk_ref[:, cols] = (jnp.where(low, dks[0], dks[1]) * 0.125).astype(BF16)
        dv_ref[:, cols] = jnp.where(low, dvs[0], dvs[1]).astype(BF16)
        return carry

    lax.fori_loop(0, pairs, pair, 0)


def attend_back(proj, probs, grad_mixed, y):
    length, wide = proj.shape
    shape = struct((length, wide // 6), BF16)
    return call(
        lambda *refs: attend_back_kernel(*refs, y=y),
        "attend_back",
        (shape, shape, shape),
        [VMEM] * 3,
        (VMEM,) * 3,
        [pltpu.VMEM((length, length), BF16), pltpu.VMEM((128, length), BF16)],
        2,
        4,
        (proj, probs, grad_mixed),
    )


def last_kernel(x_ref, sums1_ref, sums2_ref, sum_up_ref, *refs, orders):
    parts, (pieces_own, pieces_sib, whole, vec) = refs[:6], refs[6:]
    half = parts[0].shape[1]
    rows = whole.shape[0]
    x_t = x_ref[...].T
    sums = [[], []]
    for y in range(2):
        for which in range(3):
            at = (y * 3 + which) * half
            value = parts[y * 3 + which][...]
            whole[:, at : at + half] = jnp.dot(x_t, value, preferred_element_type=F32).astype(BF16)
            if which != 1:
                sums[which // 2].append(jnp.sum(value.astype(F32), axis=0, keepdims=True))
    pack(places(orders), pieces_own, pieces_sib, whole, 0, 3 * half)
    vectors = sums[0] + sums[1] + [ref[i : i + 1, :] for ref in (sums1_ref, sums2_ref) for i in range(3)]
    at = 0
    across = vec.shape[1] // 128
    wide = []
    for vector in vectors + [sum_up_ref[...]]:
        for low in range(0, vector.shape[1], 128):
            wide.append(vector[:, low : low + 128])
    for row in range(8):
        vec[row : row + 1, :] = jnp.concatenate(wide[row * across : (row + 1) * across], axis=1)
    pieces_own[rows:, :] = vec[...].astype(BF16)
    pieces_sib[rows:, :] = vec[...].astype(BF16)


def last(orders, x, sums1, sums2, sum_up, parts):
    length, width = x.shape
    piece = struct((width + 8, 3 * width // 2), BF16)
    return call(
        lambda *refs: last_kernel(*refs, orders=orders),
        "last",
        (piece, piece),
        [VMEM] * 10,
        (VMEM, VMEM),
        [
            pltpu.VMEM((width, 3 * width), BF16),
            pltpu.VMEM((8, 3 * width // 2), F32),
        ],
        1,
        7,
        (x, sums1, sums2, sum_up) + tuple(parts),
    )


def vectors_kernel(one_ref, two_ref, qv_ref, up_ref, *refs):
    t = lax.axis_index("tp")
    rows, cols = one_ref.shape
    across = cols // 128
    value = one_ref[rows - 8 :, :].astype(F32)
    if two_ref is not None:
        value = value + two_ref[rows - 8 :, :].astype(F32)

    def block(at):
        row, low = at // across, at % across * 128
        return value[row : row + 1, low : low + 128]

    def take(out, row, first, other, count):
        for i in range(count):
            one = block(first + i)
            if other != first:
                one = jnp.where(t == 0, one, block(other + i))
            if row is None:
                out[i * 128 : (i + 1) * 128] = one[0]
            else:
                out[row : row + 1, i * 128 : (i + 1) * 128] = one

    narrow, wide = qv_ref.shape[1] // 128, up_ref.shape[0] // 128
    for which in range(2):
        take(qv_ref, which, 2 * which * narrow, (2 * which + 1) * narrow, narrow)
    for i, ref in enumerate(refs):
        take(ref, None, (4 + 2 * i) * narrow, (4 + 2 * i) * narrow, 2 * narrow)
    base = (4 + 2 * len(refs)) * narrow
    take(up_ref, None, base, base + wide, wide)


def vectors(one, two, local_width, local_units):
    shapes = [(2, local_width), (local_units,)] + [(2 * local_width,)] * 6
    given = (one,) if two is None else (one, two)

    def kernel(*refs):
        if two is None:
            refs = (refs[0], None) + refs[1:]
        vectors_kernel(*refs)

    return call(
        kernel,
        "vectors",
        tuple(struct(shape, F32) for shape in shapes),
        [VMEM] * len(given),
        (VMEM,) * 8,
        [],
        1,
        4,
        given,
    )


def add_kernel(*refs, low, high, vec, count):
    terms, out = refs[:-1], refs[-1]
    total = terms[0][low:high, :].astype(F32)
    for term in terms[1:count]:
        total = total + term[low:high, :].astype(F32)
    out[: high - low, :] = total.astype(BF16)
    if vec:
        total = 0.0
        for i in vec:
            total = total + terms[i][terms[i].shape[0] - 8 :, :].astype(F32)
        out[high - low :, :] = total.astype(BF16)


def add_up(terms, low, high, vec=(), lone=()):
    count, terms = len(terms), list(terms) + list(lone)
    cols = terms[0].shape[1]
    return call(
        lambda *refs: add_kernel(*refs, low=low, high=high, vec=vec, count=count),
        "add",
        struct((high - low + (8 if vec else 0), cols), BF16),
        [VMEM] * len(terms),
        VMEM,
        [],
        1,
        4,
        tuple(terms),
    )


def deliver_kernel(own_ref, core_ref, x_ref, y_ref, out_ref):
    c, t = lax.axis_index("ctx"), lax.axis_index("tp")
    sources = [(own_ref, 0), (core_ref, 0), (x_ref, 0), (x_ref, 1)] + [(y_ref, i) for i in range(4)]
    for i, (ref, at) in enumerate(sources):
        ctx = c ^ ((i & 1) + (i & 2))
        out_ref[ctx * 2 + (t ^ (i >> 2))] = ref[at]


def deliver(own, core, x, y):
    return call(
        deliver_kernel,
        "deliver",
        struct((2 * own.shape[0],) + own.shape[1:], BF16),
        [VMEM] * 4,
        VMEM,
        [],
        3,
        7,
        (own, core, x, y),
    )


def input_back_kernel(weight_ref, gz1_ref, *refs, fast):
    parts, chunks_ref = refs[:6], refs[6]
    half = parts[0].shape[1]
    total = gz1_ref[...]
    for i, part in enumerate(parts):
        total = total + lax.dot_general(
            part[...], weight_ref[:, i * half : (i + 1) * half], NT, preferred_element_type=F32
        )
    total = total.astype(BF16)
    count, block = chunks_ref.shape[:2]
    for i in range(count):
        spot = i
        if fast:
            c = lax.axis_index("ctx") ^ i
            spot = (c & 1) * 2 + (c >> 1)
        chunks_ref[spot] = total[i * block : (i + 1) * block]


def input_back(weight, gz1, parts, chunk, fast):
    length, width = gz1.shape
    return call(
        lambda *refs: input_back_kernel(*refs, fast=fast),
        "input_back",
        struct((length // chunk, chunk, width), BF16),
        [VMEM] * 8,
        VMEM,
        [],
        1,
        3,
        (weight, gz1) + tuple(parts),
    )


def settle_kernel(pair_ref, got_ref, *refs, cuts):
    outs, four = refs[: len(cuts)], refs[len(cuts)]
    rows = pair_ref.shape[0] // 2
    for i in range(4):
        ref = (pair_ref, got_ref)[i // 2]
        owner = lax.axis_index("ctx") ^ ((i & 1) * 2 + (i >> 1))
        low = i % 2 * rows
        four[pl.ds(pl.multiple_of(owner * rows, 16), rows), :] = ref[low : low + rows, :].astype(F32)
    for out, (low, high, form) in zip(outs, cuts):
        if form == "plain":
            out[...] = four[:, low:high]
        else:
            step = (high - low) // 3
            for j in range(3):
                out[j] = four[:, low + j * step : low + (j + 1) * step]


def settle(pair, got, cuts):
    rows, cols = pair.shape[0] // 2, pair.shape[1]
    shapes = {"plain": lambda n: (4 * rows, n), "three": lambda n: (3, 4 * rows, n // 3)}
    return call(
        lambda *refs: settle_kernel(*refs, cuts=cuts),
        "settle",
        tuple(struct(shapes[form](high - low), F32) for low, high, form in cuts),
        [VMEM, VMEM],
        (VMEM,) * len(cuts),
        [pltpu.VMEM((4 * rows, cols), F32)],
        3,
        7,
        (pair, got),
    )


def cut(full):
    rows, cols = full.shape
    return full[:, : cols // 2], full[:, cols // 2 :]


def gather_plain(shard):
    rows = lax.all_gather(shard, "fsdp", axis=0, tiled=True)
    return lax.all_gather(rows, "tp", axis=1, tiled=True)


def reduce_plain(own, sib):
    full = jnp.concatenate([own, sib], axis=1)
    part = lax.psum_scatter(full, "tp", scatter_dimension=1, tiled=True)
    part = lax.psum_scatter(part, "fsdp", scatter_dimension=0, tiled=True)
    return lax.psum(part, "ctx").astype(F32)


def body(
    layer_input,
    doc_ids,
    w_qkv,
    b_qv,
    w_out,
    b_out,
    ln1_gain,
    ln1_bias,
    w_up,
    b_up,
    w_down,
    b_down,
    ln2_gain,
    ln2_bias,
    out_grad,
):
    sizes = (lax.axis_size("fsdp"), lax.axis_size("ctx"), lax.axis_size("tp"))
    micro, seqs, local_len, width = layer_input.shape
    length = local_len * sizes[1]
    shard_rows, local_width = w_qkv.shape[1:]
    local_units = w_up.shape[1]
    heads = width // HEAD_DIM
    fast = sizes == (4, 4, 2)
    t = lax.axis_index("tp")
    c = lax.axis_index("ctx")

    def mine(value):
        return lax.dynamic_index_in_dim(value, t, 1, keepdims=False)

    def to_owners(chunks):
        return lax.all_to_all(chunks, "ctx", 0, 0, tiled=True)

    def spread(chunks):
        out = lax.all_to_all(chunks, ("ctx", "tp"), 0, 0, tiled=True)
        return out.reshape(micro, seqs, local_len, width)

    shards = (
        jnp.swapaxes(w_qkv, 0, 1).reshape(shard_rows, 3 * local_width),
        jnp.concatenate([w_out.T, w_up], axis=1),
        w_down.T,
    )
    ids = mine(doc_ids).astype(BF16)[:, None, :]
    ids = jnp.pad(ids, ((0, 0), (0, 7), (0, width - local_len)))
    rows_in = jnp.concatenate([mine(layer_input), ids], axis=1)
    cot_in = mine(out_grad)
    gathers = GATHER if fast else (None,) * 3
    packs = tuple(packing(order) for order in SCATTER) if fast else (None,) * 3

    def swap(value, group, step):
        order = tuple(zip(*GATHER[group])) + (CORE,)
        return exchange(value, order[step], sizes)

    def shed(value, group, step):
        order = (CORE,) + tuple(zip(*SCATTER[group]))
        return exchange(value, order[step], sizes)

    def joined(*parts):
        return jnp.concatenate(parts, axis=0)

    if fast:
        def seen(value):
            return [lax.dynamic_index_in_dim(value, c ^ i, 0, keepdims=True) for i in range(4)]

        part = shard_rows // 4
        h1 = lax.dynamic_slice_in_dim(w_qkv, c * part, part, 1)
        h1 = jnp.swapaxes(h1, 0, 1).reshape(part, 3 * local_width)
        h2, h3 = [lax.dynamic_slice_in_dim(s, c * part, part, 0) for s in shards[1:]]
        g1 = swap(h1, 0, 0)
        x0, x1, x2, x3 = seen(after(rows_in, h1))
        g1, x1, x2, x3, h2, h3, cot_in, b_up = phase(g1, x1, x2, x3, h2, h3, cot_in, b_up)
        h1 = joined(h1, g1)
        g1, g3, xk, xx, xd = phase(
            swap(h1, 0, 1), swap(h3, 2, 0), exchange(x1, CORE, sizes), exchange(x2, X, sizes), exchange(x3, FAR, sizes)
        )
        given = (x0, xk, joined(xx, xd))
        h1, h2, h3, cot_in, b_up = phase(joined(h1, g1), h2, joined(h3, g3), cot_in, b_up)
        g1, g2, g3 = swap(h1, 0, 2), swap(h2, 1, 0), swap(h3, 2, 1)
        c0, c1, c2, c3 = seen(cot_in)
        c_send = joined(c1, c3)
        table, small = tables(b_qv, b_up, (b_out, ln1_gain, ln1_bias, b_down, ln2_gain, ln2_bias))
        g1, g2, g3, c_send, small = phase(g1, g2, g3, c_send, small)
        h1, h2, h3 = phase(joined(h1, g1), joined(h2, g2), joined(h3, g3))
        g1, g2, ck, got = phase(
            swap(h1, 0, 3), swap(h2, 1, 1), exchange(c_send, CORE, sizes), exchange(small, Y, sizes)
        )
        small = joined(small, got)
        h1, h2, h3 = phase(joined(h1, g1), joined(h2, g2), h3)
        g1, g2, g3 = swap(h1, 0, 4), swap(h2, 1, 2), swap(h3, 2, 2)
        (wq,) = unpack(gathers[0], h1, g1, (3 * width,))
        proj, rows_b, mask = project(wq, given, small, fast)
        proj, g2, c2, ck = phase(proj, g2, c2, ck)
        h2 = joined(h2, g2)
        g2 = swap(h2, 1, 3)
        mixed0, probs0 = attend(after(proj, h2), mask, 0)
        mixed0, g3 = phase(mixed0, g3)
        h3 = joined(h3, g3)
        g3 = swap(h3, 2, 3)
        mixed1, probs1 = attend(after(proj, h3, mixed0), mask, 1)
        mixed1, g2 = phase(mixed1, g2)
        h2, c_send = phase(joined(h2, g2), joined(c2, ck[1:]))
        g2, cx = swap(h2, 1, 4), exchange(c_send, X, sizes)
        wo, wu = unpack(gathers[1], h2, g2, (width, 2 * local_units))
    else:
        parts = (shards[0], w_out.T, w_up, w_down.T)
        pieces = [cut(gather_plain(s)) for s in parts]
        (wq,) = unpack(None, *pieces[0], (3 * width,))
        (wo,) = unpack(None, *pieces[1], (width,))
        (wu,) = unpack(None, *pieces[2], (2 * local_units,))
        (wd,) = unpack(None, *pieces[3], (2 * local_units,))
        order = lambda value: (value[:1], value[1:3], value[2:])
        given, cot = order(to_owners(rows_in)), order(to_owners(cot_in))
        table, small = tables(b_qv, b_up, (b_out, ln1_gain, ln1_bias, b_down, ln2_gain, ln2_bias))
        small = joined(small, exchange(small, Y, sizes))
        proj, rows_b, mask = project(wq, given, small, fast)
        mixed0, probs0 = attend(proj, mask, 0)
        mixed1, probs1 = attend(proj, mask, 1)

    normed1, scale1, first_b, act, slope = middle(wo, wu, mixed0, mixed1, rows_b, table, small)
    if fast:
        act, g3, cx = phase(act, g3, cx)
        cot = (c0, ck, cx)
        h3 = joined(h3, g3)
        (wd,) = unpack(gathers[2], h3, swap(h3, 2, 4), (2 * local_units,))
    chunks, gz, gzb, sums2, down_own, down_sib = turn(packs[2], wd, act, normed1, cot, table, local_len)

    rows = shard_rows // 4
    if fast:
        down_sib, chunks, gzb = phase(down_sib, chunks, gzb)
        got, core_out = shed(down_sib, 2, 0), exchange(chunks[2:], CORE, sizes)
    gh, sum_up = hidden_back(wd, gzb, slope)
    if fast:
        gh, got, core_out = phase(gh, got, core_out)
        down = [down_own, got]
        send, x_send, gh = phase(
            add_up(down, 8 * rows, 16 * rows), joined(chunks[1:2], core_out[1:2]), gh
        )
        got, x_out = shed(send, 2, 1), exchange(x_send, X, sizes)
    gz1, grad_mixed, sums1, up_own, up_sib = first_back(
        packs[1], wo, wu, gh, gz, normed1, scale1, table, first_b, mixed0, mixed1
    )
    if fast:
        grad_mixed, up_sib, got, x_out = phase(grad_mixed, up_sib, got, x_out)
        down = down + [got]
        send, y_send, grad_mixed = phase(
            add_up(down, 4 * rows, 8 * rows), joined(chunks[:1], core_out[:1], x_out), grad_mixed
        )
        got, got2 = shed(send, 2, 2), shed(up_sib, 1, 0)
    parts0 = attend_back(proj, probs0, grad_mixed, 0)
    if fast:
        head, got2, grad_mixed = phase(parts0[0], got2, grad_mixed)
        parts0 = (head,) + tuple(parts0[1:])
        up = [up_own, got2]
        send2, grad_mixed, y_send = phase(add_up(up, 8 * rows, 16 * rows), grad_mixed, y_send)
        got2, y_out = shed(send2, 1, 1), exchange(y_send, Y, sizes)
    parts1 = attend_back(proj, probs1, grad_mixed, 1)
    parts = list(parts0) + list(parts1)
    chunks2 = input_back(wq, gz1, parts, local_len, fast)
    parts[0] = after(parts[0], chunks2)
    qkv_own, qkv_sib = last(packs[0], rows_b, sums1, sums2, sum_up, parts)
    if fast:
        chunks2, qkv_sib, got, got2, y_out = phase(chunks2, qkv_sib, got, got2, y_out)
        down, up = down + [got], up + [got2]
        send = add_up(down, 2 * rows, 4 * rows)
        send2 = add_up(up, 4 * rows, 8 * rows)
        qkv_sib, send, send2, chunks2 = phase(qkv_sib, send, send2, chunks2)
        got3, got, got2, core_x = (
            shed(qkv_sib, 0, 0), shed(send, 2, 3), shed(send2, 1, 2), exchange(chunks2[2:], CORE, sizes)
        )
        got3, core_x = phase(got3, core_x)
        qkv = [qkv_own, got3]
        sent3 = add_up(qkv, 8 * rows, 16 * rows, (0, 1))
        x_send = joined(chunks2[1:2], core_x[1:2])
        got3 = shed(sent3, 0, 1)
        got3, x_send = phase(got3, x_send)
        qkv = qkv + [got3]
        send3 = add_up(qkv, 4 * rows, 8 * rows, (3, 2), [sent3])
        got3 = shed(send3, 0, 2)
        send3, got, x_send = phase(send3, got, x_send)
        down = down + [got]
        send = add_up(down, rows, 2 * rows)
        got, x_x = shed(send, 2, 4), exchange(x_send, X, sizes)
        send, got2 = phase(send, got2)
        up = up + [got2]
        send2 = add_up(up, 2 * rows, 4 * rows)
        got2 = shed(send2, 1, 3)
        got3, send2 = phase(got3, send2)
        qkv = qkv + [got3]
        sent3 = add_up(qkv, 2 * rows, 4 * rows, (4, 3), [send3])
        got3 = shed(sent3, 0, 3)
        sent3, got, x_x = phase(sent3, got, x_x)
        pair1 = add_up(down + [got], 0, rows)
        y_send = joined(chunks2[:1], core_x[:1], x_x)
        got, y_x = exchange(pair1, X, sizes), exchange(y_send, Y, sizes)
        pair1, got2 = phase(pair1, got2)
        up = up + [got2]
        send2 = add_up(up, rows, 2 * rows)
        got2 = shed(send2, 1, 4)
        layer_output = deliver(chunks, core_out, x_out, after(y_out, send2))
        got3, layer_output = phase(got3, layer_output)
        qkv = qkv + [got3]
        send3 = add_up(qkv, rows, 2 * rows, (5, 4), [sent3])
        got3 = shed(send3, 0, 4)
        send3, got, got2 = phase(send3, got, got2)
        pair1 = joined(pair1, got)
        up = up + [got2]
        pair2 = add_up(up, 0, rows)
        got1, got2 = exchange(pair1, CORE, sizes), exchange(pair2, X, sizes)
        got3, pair1, pair2 = phase(got3, pair1, pair2)
        qkv = qkv + [got3]
        pair3 = add_up(qkv, 0, rows)
        got = exchange(pair3, X, sizes)
        vec = vectors(after(send3, pair3), got3, local_width, local_units)
        pair3, got1, bup = phase(pair3, got1, vec[1])
        vec = (vec[0], bup) + tuple(vec[2:])
        (grad_down,) = settle(pair1, got1, ((0, local_units, "plain"),))
        grad_down, got2 = phase(grad_down, got2)
        pair2 = joined(pair2, got2)
        got2 = exchange(pair2, CORE, sizes)
        got, pair2 = phase(got, pair2)
        pair3 = joined(pair3, got)
        got3 = exchange(pair3, CORE, sizes)
        pair3, got2 = phase(pair3, got2)
        grad_wout, grad_up = settle(
            pair2, got2, ((0, local_width, "plain"), (local_width, local_width + local_units, "plain"))
        )
        grad_x = deliver(chunks2, core_x, x_x, after(y_x, grad_up))
        (grad_qkv,) = settle(pair3, after(got3, grad_x), ((0, 3 * local_width, "three"),))
        layer_output = layer_output.reshape(micro, seqs, local_len, width)
        grad_x = grad_x.reshape(micro, seqs, local_len, width)
    else:
        layer_output = spread(jnp.repeat(chunks, 2, axis=0))
        grad_x = spread(jnp.repeat(chunks2, 2, axis=0))
        vec = lax.psum(qkv_own[width:].astype(F32), AXES)
        vec = vectors(vec, None, local_width, local_units)
        grad_down = reduce_plain(down_own, down_sib)
        both = reduce_plain(up_own, up_sib)
        grad_wout, grad_up = both[:, :local_width], both[:, local_width:]
        grad_qkv = reduce_plain(qkv_own[:width], qkv_sib[:width])
        grad_qkv = jnp.swapaxes(grad_qkv.reshape(shard_rows, 3, local_width), 0, 1)

    out_bqv, out_bup, g1, s1, bout, g2, s2, bdown = vec
    return (
        layer_output,
        grad_x,
        grad_qkv,
        out_bqv,
        grad_wout.T,
        bout,
        g1,
        s1,
        grad_up,
        out_bup,
        grad_down.T,
        bdown,
        g2,
        s2,
    )


def solution(mesh):
    return jax.shard_map(
        body,
        mesh=mesh,
        in_specs=(
            P(None, "fsdp", "ctx", None),
            P(None, "fsdp", "ctx"),
            P(None, "fsdp", "tp"),
            P(None, "tp"),
            P("tp", "fsdp"),
            P(),
            P(),
            P(),
            P("fsdp", "tp"),
            P("tp"),
            P("tp", "fsdp"),
            P(),
            P(),
            P(),
            P(None, "fsdp", "ctx", None),
        ),
        out_specs=(
            P(None, "fsdp", "ctx", None),
            P(None, "fsdp", "ctx", None),
            P(None, "fsdp", "tp"),
            P(None, "tp"),
            P("tp", "fsdp"),
            P(),
            P(),
            P(),
            P("fsdp", "tp"),
            P("tp"),
            P("tp", "fsdp"),
            P(),
            P(),
            P(),
        ),
        check_vma=False,
    )
```

```python
import jax
import jax.numpy as jnp
from jax import lax
from jax.experimental import pallas as pl
from jax.experimental.pallas import tpu as pltpu
from jax.sharding import PartitionSpec as P

HEAD_DIM = 64
AXES = ("fsdp", "ctx", "tp")
F32 = jnp.float32
BF16 = jnp.bfloat16
NEG = -1e30
NT = (((1,), (1,)), ((), ()))
VMEM = pl.BlockSpec(memory_space=pltpu.VMEM)
SMEM = pl.BlockSpec(memory_space=pltpu.SMEM)
ANY = pl.BlockSpec(memory_space=pl.ANY)


def partner(dim, z, c, t):
    if dim == "core":
        return z, c ^ 1, t
    if dim == "x":
        return z, c ^ 2, t
    if dim == "x+core":
        return z, c ^ 3, t
    if dim == "y":
        return z, c, t ^ 1
    return z ^ int(dim[1:]), c, t


def exchange(value, dims, sizes):
    nz, nc, nt = sizes
    pairs = []
    for z in range(nz):
        for c in range(nc):
            for t in range(nt):
                tz, tc, tt = partner(dims[c & 1], z, c, t)
                pairs.append(((z * nc + c) * nt + t, (tz * nc + tc) * nt + tt))
    return lax.ppermute(value, AXES, pairs)


GATHER = (
    (("z2", "z1", "y", "x"), ("z1", "z2", "x", "y")),
    (("z2", "z1", "y", "x"), ("z1", "z2", "x", "y")),
    (("z2", "z1", "x", "y"), ("y", "x", "z2", "z1")),
)
SCATTER = (
    (("x", "y", "z1", "z2"), ("y", "x", "z2", "z1")),
    (("x", "y", "z1", "z2"), ("z1", "z2", "y", "x")),
    (("y", "x", "z1", "z2"), ("z1", "z2", "x", "y")),
)
CORE = ("core", "core")
X = ("x", "x")
FAR = ("x+core", "x+core")
Y = ("y", "y")


def piece_place(order, core, here, index):
    z, x, t = here
    for bit, dim in enumerate(order):
        flip = (index >> bit) & 1
        if dim == "x":
            x = x ^ flip
        elif dim == "y":
            t = t ^ flip
        else:
            z = z ^ (flip * int(dim[1:]))
    return z * 4 + x * 2 + core, t


def places(orders):
    if orders is None:
        return [(i, half) for half in range(2) for i in range(16)]
    c = lax.axis_index("ctx")
    here = (lax.axis_index("fsdp"), c >> 1, lax.axis_index("tp"))
    spots = []
    for core in (c & 1, 1 - (c & 1)):
        for i in range(16):
            r0, t0 = piece_place(orders[0], core, here, i)
            r1, t1 = piece_place(orders[1], core, here, i)
            spots.append((jnp.where(core == 0, r0, r1), jnp.where(core == 0, t0, t1)))
    return spots


def packing(orders):
    return tuple(order[::-1] for order in orders)


def after(value, *first):
    return lax.optimization_barrier((value, first))[0]


def phase(*values):
    return lax.optimization_barrier(values)


def at_rows(place, count, unit=0):
    start = place * count
    return pl.ds(start if isinstance(start, int) else pl.multiple_of(start, unit or count), count)


def piece_copies(spots, own_ref, sib_ref, sem, whole, low, cols, base=0):
    rows = whole.shape[0] // 16
    copies = []
    for half, ref in ((0, own_ref), (1, sib_ref)):
        for i in range(16):
            row, col = spots[half * 16 + i]
            copy = pltpu.make_async_copy(
                ref.at[pl.ds(i * rows, rows), pl.ds(low, cols)],
                whole.at[at_rows(row, rows), at_rows(col, cols, 128)],
                sem.at[base + half * 16 + i],
            )
            copy.start()
            copies.append(copy)
    return copies


def pack(spots, own_ref, sib_ref, whole, low, cols):
    rows = whole.shape[0] // 16
    for half, ref in ((0, own_ref), (1, sib_ref)):
        for i in range(16):
            row, col = spots[half * 16 + i]
            ref[i * rows : (i + 1) * rows, low : low + cols] = whole[at_rows(row, rows), at_rows(col, cols, 128)]


def finish(copies):
    for copy in copies:
        copy.wait()


def tiles(count, step):
    def run(one):
        lax.fori_loop(0, count // step, lambda i, carry: (one(pl.multiple_of(i * step, step)), carry)[1], 0)

    return run


def row_mean(value):
    return jnp.mean(value, axis=-1, keepdims=True)


def struct(shape, dtype):
    return jax.ShapeDtypeStruct(shape, dtype)


def call(kernel, name, outs, specs, out_specs, scratch, time, room, args):
    return pl.pallas_call(
        kernel,
        name=name,
        out_shape=outs,
        in_specs=specs,
        out_specs=out_specs,
        scratch_shapes=scratch,
        compiler_params=pltpu.CompilerParams(vmem_limit_bytes=room << 20),
        cost_estimate=pl.CostEstimate(flops=time * 10**9, transcendentals=0, bytes_accessed=10**6),
    )(*args)


B_OUT, GAIN1, SHIFT1, B_DOWN, GAIN2, SHIFT2 = range(6)


def unpack_kernel(own_ref, sib_ref, *refs, orders):
    outs, sem = refs[:-1], refs[-1]
    copies = []
    spots = places(orders)
    low = 0
    for i, out in enumerate(outs):
        cols = out.shape[1] // 2
        copies += piece_copies(spots, own_ref, sib_ref, sem, out, low, cols, 32 * i)
        low += cols
    finish(copies)


def unpack(orders, own, sib, widths):
    rows = own.shape[0]
    return call(
        lambda *refs: unpack_kernel(*refs, orders=orders),
        "unpack",
        tuple(struct((rows, width), BF16) for width in widths),
        [ANY, ANY],
        (VMEM,) * len(widths),
        [pltpu.SemaphoreType.DMA((32 * len(widths),))],
        5,
        2,
        (own, sib),
    )


def sources(refs, fast):
    c = lax.axis_index("ctx") if fast else 0
    own, core, x = refs
    return [(c ^ 0, own, 0), (c ^ 1, core, 0), (c ^ 2, x, 0), (c ^ 3, x, 1)]


def tables_kernel(qv_ref, up_ref, *refs):
    rows, (table_ref, small_ref) = refs[:-2], refs[-2:]
    table_ref[...] = jnp.zeros_like(table_ref)
    for i, ref in enumerate(rows):
        table_ref[i : i + 1, :] = ref[...][None]
    width = qv_ref.shape[1]
    small_ref[:, :width] = qv_ref[0:1, :]
    small_ref[:, width : 2 * width] = qv_ref[1:2, :]
    small_ref[:, 2 * width :] = up_ref[...][None]


def tables(b_qv, b_up, rows):
    return call(
        tables_kernel,
        "tables",
        (struct((8, rows[0].shape[0]), F32), struct((1, b_qv.size + b_up.size), F32)),
        [VMEM] * (2 + len(rows)),
        (VMEM, VMEM),
        [],
        1,
        3,
        (b_qv, b_up) + tuple(rows),
    )


def project_kernel(weight_ref, own_ref, core_ref, far_ref, small_ref, proj_ref, x_ref, mask_ref, ids, *, fast):
    block = own_ref.shape[1] - 8
    count = 4
    for spot, ref, i in sources((own_ref, core_ref, far_ref), fast):
        x_ref[pl.ds(pl.multiple_of(spot * block, block), block), :] = ref[i, 0:block, :]
        ids[pl.ds(spot, 1), :] = ref[i, block:, 0:block].astype(F32)[0:1]
    for kb in range(count):
        column = jnp.broadcast_to(ids[kb : kb + 1], (block, block)).T
        for qb in range(count):
            mask_ref[kb * block : (kb + 1) * block, qb * block : (qb + 1) * block] = jnp.where(
                column == jnp.broadcast_to(ids[qb : qb + 1], (block, block)), 0.0, NEG
            )
    width = proj_ref.shape[1] // 6
    for y in range(2):
        row = pl.ds(lax.axis_index("tp") ^ y, 1)
        for which in range(3):
            at = (y * 3 + which) * width
            value = jnp.dot(x_ref[...], weight_ref[:, at : at + width], preferred_element_type=F32)
            if which != 1:
                low = 0 if which == 0 else width
                value = value + small_ref[row, low : low + width]
            proj_ref[:, at : at + width] = value.astype(BF16)


def project(weight, given, small, fast):
    width, wide = weight.shape
    block = given[0].shape[1] - 8
    length = 4 * block
    return call(
        lambda *refs: project_kernel(*refs, fast=fast),
        "project",
        (
            struct((length, wide), BF16),
            struct((length, width), BF16),
            struct((length, length), F32),
        ),
        [VMEM] * 5,
        (VMEM,) * 3,
        [pltpu.VMEM((8, block), F32)],
        5,
        3,
        (weight,) + tuple(given) + (small,),
    )


def attend_kernel(proj_ref, mask_ref, o_ref, p_ref, *, y):
    length = proj_ref.shape[0]
    pairs = o_ref.shape[1] // 128
    lane = lax.broadcasted_iota(jnp.int32, (1, 128), 1)

    def pair(g, carry):
        take = lambda which: proj_ref[:, pl.ds(pl.multiple_of(((y * 3 + which) * pairs + g) * 128, 128), 128)]
        query = take(0) * jnp.asarray(0.125, BF16)
        keys = take(1)
        values_t = take(2).T
        outs = []
        for head in range(2):
            here = (lane >= 64 * head) & (lane < 64 * head + 64)
            only = jnp.where(here, keys, jnp.zeros_like(keys))
            row = []
            for at in range(0, length, 256):
                scores = lax.dot_general(only, query[at : at + 256], NT, preferred_element_type=F32)
                scores = scores + mask_ref[:, at : at + 256]
                top = jnp.max(scores, axis=0, keepdims=True)
                raised = jnp.exp(scores - top)
                total = jnp.sum(raised, axis=0, keepdims=True)
                probs = (raised * (1.0 / total)).astype(BF16)
                p_ref[2 * g + head, :, at : at + 256] = probs
                row.append(
                    jnp.dot(values_t[64 * head : 64 * head + 64], probs, preferred_element_type=F32)
                )
            outs.append(jnp.concatenate(row, axis=1))
        both = jnp.concatenate(outs, axis=0).astype(BF16)
        o_ref[:, pl.ds(pl.multiple_of(g * 128, 128), 128)] = both.T
        return carry

    lax.fori_loop(0, pairs, pair, 0)


def attend(proj, mask, y):
    length, wide = proj.shape
    half = wide // 6
    return call(
        lambda *refs: attend_kernel(*refs, y=y),
        "attend",
        (struct((length, half), BF16), struct((half // HEAD_DIM, length, length), BF16)),
        [VMEM, VMEM],
        (VMEM, VMEM),
        [],
        12,
        3,
        (proj, mask),
    )


def middle_kernel(
    w_out, w_up, mixed0_ref, mixed1_ref, x_ref, table_ref, small_ref,
    normed_ref, scale_ref, first_ref, act_ref, slope_ref,
):
    length, units = act_ref.shape
    narrow, half = w_out.shape[1] // 2, units // 2
    normed_ref[...] = lax.dot_general(
        mixed0_ref[...], w_out[:, :narrow], NT, preferred_element_type=F32
    ) + lax.dot_general(mixed1_ref[...], w_out[:, narrow:], NT, preferred_element_type=F32)

    @tiles(length, 64)
    def _(at):
        here = pl.ds(at, 64)
        value = x_ref[here, :].astype(F32) + normed_ref[here, :] + table_ref[B_OUT : B_OUT + 1, :]
        centred = value - row_mean(value)
        scale = lax.rsqrt(row_mean(centred * centred) + 1e-12)
        unit = centred * scale
        normed_ref[here, :] = unit
        scale_ref[here, :] = scale
        first_ref[here, :] = (
            unit * table_ref[GAIN1 : GAIN1 + 1, :] + table_ref[SHIFT1 : SHIFT1 + 1, :]
        ).astype(BF16)

    for y in range(2):
        row = pl.ds(lax.axis_index("tp") ^ y, 1)

        @tiles(half, 256)
        def _(at):
            here = pl.ds(pl.multiple_of(y * half + at, 256), 256)
            bias = small_ref[row, pl.ds(pl.multiple_of(2 * narrow + at, 256), 256)]
            hidden = jnp.dot(first_ref[...], w_up[:, here], preferred_element_type=F32) + bias
            phi = 0.5 + 0.5 * lax.erf(hidden * 0.7071067811865476)
            act_ref[:, here] = (hidden * phi).astype(BF16)
            bell = jnp.exp(-0.5 * hidden * hidden) * 0.3989422804014327
            slope_ref[:, here] = (phi + hidden * bell).astype(BF16)


def middle(w_out, w_up, mixed0, mixed1, x, table, small):
    length, width = x.shape
    units = w_up.shape[1]
    return call(
        middle_kernel,
        "middle",
        (
            struct((length, width), F32),
            struct((length, 1), F32),
            struct((length, width), BF16),
            struct((length, units), BF16),
            struct((length, units), BF16),
        ),
        [VMEM] * 7,
        (VMEM,) * 5,
        [],
        12,
        3,
        (w_out, w_up, mixed0, mixed1, x, table, small),
    )


def turn_kernel(
    weight_ref, act_ref, normed_ref, own_ref, core_ref, far_ref, table_ref,
    chunks_ref, gz_ref, gzb_ref, sums_ref, down_own, down_sib, full, cot_ref, *, orders,
):
    length = act_ref.shape[0]
    block = chunks_ref.shape[1]
    for spot, ref, i in sources((own_ref, core_ref, far_ref), orders is not None):
        cot_ref[pl.ds(pl.multiple_of(spot * block, block), block), :] = ref[i]
    gz_ref[...] = lax.dot_general(act_ref[...], weight_ref[...], NT, preferred_element_type=F32)
    sums_ref[...] = jnp.zeros_like(sums_ref)
    row = lambda which: table_ref[which : which + 1, :]

    @tiles(length, 64)
    def _(at):
        here = pl.ds(at, 64)
        value = normed_ref[here, :] * row(GAIN1) + row(SHIFT1) + gz_ref[here, :] + row(B_DOWN)
        centred = value - row_mean(value)
        scale = lax.rsqrt(row_mean(centred * centred) + 1e-12)
        unit = centred * scale
        result = (unit * row(GAIN2) + row(SHIFT2)).astype(BF16)
        chunk = lax.div(at, block)
        if orders is not None:
            c = lax.axis_index("ctx") ^ chunk
            chunk = (c & 1) * 2 + (c >> 1)
        chunks_ref[chunk, pl.ds(pl.multiple_of(lax.rem(at, block), 64), 64), :] = result
        coming = cot_ref[here, :].astype(F32)
        raised = coming * row(GAIN2)
        back = scale * (raised - row_mean(raised) - unit * row_mean(raised * unit))
        gz_ref[here, :] = back
        gzb_ref[here, :] = back.astype(BF16)
        sums_ref[0:1, :] += jnp.sum(coming * unit, axis=0, keepdims=True)
        sums_ref[1:2, :] += jnp.sum(coming, axis=0, keepdims=True)
        sums_ref[2:3, :] += jnp.sum(back, axis=0, keepdims=True)

    back_t = gzb_ref[...].T

    @tiles(full.shape[1], 1024)
    def _(at):
        here = pl.ds(at, 1024)
        full[:, here] = jnp.dot(back_t, act_ref[:, here], preferred_element_type=F32).astype(BF16)

    pack(places(orders), down_own, down_sib, full, 0, down_own.shape[1])


def turn(orders, weight, act, normed, cot, table, chunk):
    length, units = act.shape
    width = normed.shape[1]
    piece = struct((width, units // 2), BF16)
    return call(
        lambda *refs: turn_kernel(*refs, orders=orders),
        "turn",
        (
            struct((length // chunk, chunk, width), BF16),
            struct((length, width), F32),
            struct((length, width), BF16),
            struct((8, width), F32),
            piece,
            piece,
        ),
        [VMEM] * 7,
        (VMEM,) * 6,
        [pltpu.VMEM((width, units), BF16), pltpu.VMEM((length, width), BF16)],
        14,
        10,
        (weight, act, normed) + tuple(cot) + (table,),
    )


def hidden_back_kernel(weight_ref, gzb_ref, slope_ref, gh_ref, sum_ref):
    @tiles(gh_ref.shape[1], 512)
    def _(at):
        here = pl.ds(at, 512)
        back = jnp.dot(gzb_ref[...], weight_ref[:, here], preferred_element_type=F32)
        back = (back * slope_ref[:, here].astype(F32)).astype(BF16)
        gh_ref[:, here] = back
        sum_ref[:, here] = jnp.sum(back.astype(F32), axis=0, keepdims=True)


def hidden_back(weight, gzb, slope):
    length, units = slope.shape
    return call(
        hidden_back_kernel,
        "hidden_back",
        (struct((length, units), BF16), struct((1, units), F32)),
        [VMEM] * 3,
        (VMEM, VMEM),
        [],
        12,
        3,
        (weight, gzb, slope),
    )


def first_back_kernel(
    w_out, w_up, gh_ref, gz_ref, normed_ref, scale_ref, table_ref, first_ref, mixed0_ref, mixed1_ref,
    gz1_ref, gm_ref, sums_ref, pieces_own, pieces_sib, branch, d_out, d_up, *, orders,
):
    narrow = w_out.shape[1] // 2
    half = w_up.shape[1] // 2
    length = gh_ref.shape[0]
    first_t = first_ref[...].T
    spots = places(orders)

    @tiles(d_up.shape[1], 1024)
    def _(at):
        here = pl.ds(at, 1024)
        d_up[:, here] = jnp.dot(first_t, gh_ref[:, here], preferred_element_type=F32).astype(BF16)

    pack(spots, pieces_own, pieces_sib, d_up, narrow, half)
    gz1_ref[...] = lax.dot_general(gh_ref[...], w_up[...], NT, preferred_element_type=F32)
    sums_ref[...] = jnp.zeros_like(sums_ref)

    @tiles(length, 64)
    def _(at):
        here = pl.ds(at, 64)
        coming = gz_ref[here, :] + gz1_ref[here, :]
        unit = normed_ref[here, :]
        raised = coming * table_ref[GAIN1 : GAIN1 + 1, :]
        back = scale_ref[here, :] * (raised - row_mean(raised) - unit * row_mean(raised * unit))
        gz1_ref[here, :] = back
        branch[here, :] = back.astype(BF16)
        sums_ref[0:1, :] += jnp.sum(coming * unit, axis=0, keepdims=True)
        sums_ref[1:2, :] += jnp.sum(coming, axis=0, keepdims=True)
        sums_ref[2:3, :] += jnp.sum(back, axis=0, keepdims=True)

    branch_t = branch[...].T
    d_out[:, :narrow] = jnp.dot(branch_t, mixed0_ref[...], preferred_element_type=F32).astype(BF16)
    d_out[:, narrow:] = jnp.dot(branch_t, mixed1_ref[...], preferred_element_type=F32).astype(BF16)
    pack(spots, pieces_own, pieces_sib, d_out, 0, narrow)
    gm_ref[...] = jnp.dot(branch[...], w_out[...], preferred_element_type=F32).astype(BF16)


def first_back(orders, w_out, w_up, gh, gz, normed, scale, table, first_b, mixed0, mixed1):
    length, units = gh.shape
    width = gz.shape[1]
    piece = struct((width, (units + width) // 2), BF16)
    return call(
        lambda *refs: first_back_kernel(*refs, orders=orders),
        "first_back",
        (
            struct((length, width), F32),
            struct((length, width), BF16),
            struct((8, width), F32),
            piece,
            piece,
        ),
        [VMEM] * 10,
        (VMEM,) * 5,
        [
            pltpu.VMEM((length, width), BF16),
            pltpu.VMEM((width, width), BF16),
            pltpu.VMEM((width, units), BF16),
        ],
        20,
        12,
        (w_out, w_up, gh, gz, normed, scale, table, first_b, mixed0, mixed1),
    )


def attend_back_kernel(proj_ref, p_ref, gm_ref, dq_ref, dk_ref, dv_ref, dst, dqt, *, y):
    length = proj_ref.shape[0]
    pairs = dq_ref.shape[1] // 128
    lane = lax.broadcasted_iota(jnp.int32, (1, 128), 1)
    low = lane < 64

    def pair(g, carry):
        take = lambda which: proj_ref[:, pl.ds(pl.multiple_of(((y * 3 + which) * pairs + g) * 128, 128), 128)]
        query, keys, values = take(0), take(1), take(2)
        grad = gm_ref[:, pl.ds(pl.multiple_of((y * pairs + g) * 128, 128), 128)]
        keys_t = keys.T
        dks, dvs = [], []
        for head in range(2):
            here = low if head == 0 else jnp.logical_not(low)
            only = jnp.where(here, values, jnp.zeros_like(values))
            for at in range(0, length, 256):
                cols = slice(at, at + 256)
                gp = lax.dot_general(only, grad[cols], NT, preferred_element_type=F32)
                probs = p_ref[2 * g + head, :, cols].astype(F32)
                weighted = jnp.sum(probs * gp, axis=0, keepdims=True)
                dst[:, cols] = (probs * (gp - weighted)).astype(BF16)
            dqt[64 * head : 64 * head + 64, :] = (
                jnp.dot(keys_t[64 * head : 64 * head + 64], dst[...], preferred_element_type=F32) * 0.125
            ).astype(BF16)
            dks.append(jnp.dot(dst[...], query, preferred_element_type=F32))
            dvs.append(jnp.dot(p_ref[2 * g + head], grad, preferred_element_type=F32))
        cols = pl.ds(pl.multiple_of(g * 128, 128), 128)
        dq_ref[:, cols] = dqt[...].T
        dk_ref[:, cols] = (jnp.where(low, dks[0], dks[1]) * 0.125).astype(BF16)
        dv_ref[:, cols] = jnp.where(low, dvs[0], dvs[1]).astype(BF16)
        return carry

    lax.fori_loop(0, pairs, pair, 0)


def attend_back(proj, probs, grad_mixed, y):
    length, wide = proj.shape
    shape = struct((length, wide // 6), BF16)
    return call(
        lambda *refs: attend_back_kernel(*refs, y=y),
        "attend_back",
        (shape, shape, shape),
        [VMEM] * 3,
        (VMEM,) * 3,
        [pltpu.VMEM((length, length), BF16), pltpu.VMEM((128, length), BF16)],
        2,
        4,
        (proj, probs, grad_mixed),
    )


def last_kernel(x_ref, sums1_ref, sums2_ref, sum_up_ref, *refs, orders):
    parts, (pieces_own, pieces_sib, whole, vec) = refs[:6], refs[6:]
    half = parts[0].shape[1]
    rows = whole.shape[0]
    x_t = x_ref[...].T
    sums = [[], []]
    for y in range(2):
        for which in range(3):
            at = (y * 3 + which) * half
            value = parts[y * 3 + which][...]
            whole[:, at : at + half] = jnp.dot(x_t, value, preferred_element_type=F32).astype(BF16)
            if which != 1:
                sums[which // 2].append(jnp.sum(value.astype(F32), axis=0, keepdims=True))
    pack(places(orders), pieces_own, pieces_sib, whole, 0, 3 * half)
    vectors = sums[0] + sums[1] + [ref[i : i + 1, :] for ref in (sums1_ref, sums2_ref) for i in range(3)]
    at = 0
    across = vec.shape[1] // 128
    wide = []
    for vector in vectors + [sum_up_ref[...]]:
        for low in range(0, vector.shape[1], 128):
            wide.append(vector[:, low : low + 128])
    for row in range(8):
        vec[row : row + 1, :] = jnp.concatenate(wide[row * across : (row + 1) * across], axis=1)
    pieces_own[rows:, :] = vec[...].astype(BF16)
    pieces_sib[rows:, :] = vec[...].astype(BF16)


def last(orders, x, sums1, sums2, sum_up, parts):
    length, width = x.shape
    piece = struct((width + 8, 3 * width // 2), BF16)
    return call(
        lambda *refs: last_kernel(*refs, orders=orders),
        "last",
        (piece, piece),
        [VMEM] * 10,
        (VMEM, VMEM),
        [
            pltpu.VMEM((width, 3 * width), BF16),
            pltpu.VMEM((8, 3 * width // 2), F32),
        ],
        1,
        7,
        (x, sums1, sums2, sum_up) + tuple(parts),
    )


def vectors_kernel(one_ref, two_ref, qv_ref, up_ref, *refs):
    t = lax.axis_index("tp")
    rows, cols = one_ref.shape
    across = cols // 128
    value = one_ref[rows - 8 :, :].astype(F32)
    if two_ref is not None:
        value = value + two_ref[rows - 8 :, :].astype(F32)

    def block(at):
        row, low = at // across, at % across * 128
        return value[row : row + 1, low : low + 128]

    def take(out, row, first, other, count):
        for i in range(count):
            one = block(first + i)
            if other != first:
                one = jnp.where(t == 0, one, block(other + i))
            if row is None:
                out[i * 128 : (i + 1) * 128] = one[0]
            else:
                out[row : row + 1, i * 128 : (i + 1) * 128] = one

    narrow, wide = qv_ref.shape[1] // 128, up_ref.shape[0] // 128
    for which in range(2):
        take(qv_ref, which, 2 * which * narrow, (2 * which + 1) * narrow, narrow)
    for i, ref in enumerate(refs):
        take(ref, None, (4 + 2 * i) * narrow, (4 + 2 * i) * narrow, 2 * narrow)
    base = (4 + 2 * len(refs)) * narrow
    take(up_ref, None, base, base + wide, wide)


def vectors(one, two, local_width, local_units):
    shapes = [(2, local_width), (local_units,)] + [(2 * local_width,)] * 6
    given = (one,) if two is None else (one, two)

    def kernel(*refs):
        if two is None:
            refs = (refs[0], None) + refs[1:]
        vectors_kernel(*refs)

    return call(
        kernel,
        "vectors",
        tuple(struct(shape, F32) for shape in shapes),
        [VMEM] * len(given),
        (VMEM,) * 8,
        [],
        1,
        4,
        given,
    )


def add_kernel(*refs, low, high, vec, count):
    terms, out = refs[:-1], refs[-1]
    total = terms[0][low:high, :].astype(F32)
    for term in terms[1:count]:
        total = total + term[low:high, :].astype(F32)
    out[: high - low, :] = total.astype(BF16)
    if vec:
        total = 0.0
        for i in vec:
            total = total + terms[i][terms[i].shape[0] - 8 :, :].astype(F32)
        out[high - low :, :] = total.astype(BF16)


def add_up(terms, low, high, vec=(), lone=(), time=1):
    count, terms = len(terms), list(terms) + list(lone)
    cols = terms[0].shape[1]
    return call(
        lambda *refs: add_kernel(*refs, low=low, high=high, vec=vec, count=count),
        "add",
        struct((high - low + (8 if vec else 0), cols), BF16),
        [VMEM] * len(terms),
        VMEM,
        [],
        time,
        4,
        tuple(terms),
    )


def deliver_kernel(own_ref, core_ref, x_ref, y_ref, out_ref):
    c, t = lax.axis_index("ctx"), lax.axis_index("tp")
    sources = [(own_ref, 0), (core_ref, 0), (x_ref, 0), (x_ref, 1)] + [(y_ref, i) for i in range(4)]
    for i, (ref, at) in enumerate(sources):
        ctx = c ^ ((i & 1) + (i & 2))
        out_ref[ctx * 2 + (t ^ (i >> 2))] = ref[at]


def deliver(own, core, x, y):
    return call(
        deliver_kernel,
        "deliver",
        struct((2 * own.shape[0],) + own.shape[1:], BF16),
        [VMEM] * 4,
        VMEM,
        [],
        3,
        7,
        (own, core, x, y),
    )


def input_back_kernel(weight_ref, gz1_ref, *refs, fast):
    parts, chunks_ref = refs[:6], refs[6]
    half = parts[0].shape[1]
    total = gz1_ref[...]
    for i, part in enumerate(parts):
        total = total + lax.dot_general(
            part[...], weight_ref[:, i * half : (i + 1) * half], NT, preferred_element_type=F32
        )
    total = total.astype(BF16)
    count, block = chunks_ref.shape[:2]
    for i in range(count):
        spot = i
        if fast:
            c = lax.axis_index("ctx") ^ i
            spot = (c & 1) * 2 + (c >> 1)
        chunks_ref[spot] = total[i * block : (i + 1) * block]


def input_back(weight, gz1, parts, chunk, fast):
    length, width = gz1.shape
    return call(
        lambda *refs: input_back_kernel(*refs, fast=fast),
        "input_back",
        struct((length // chunk, chunk, width), BF16),
        [VMEM] * 8,
        VMEM,
        [],
        1,
        3,
        (weight, gz1) + tuple(parts),
    )


def settle_kernel(*refs, cuts, count):
    given, outs, four = refs[:count], refs[count:-1], refs[-1]
    rows = four.shape[0] // 4
    for i in range(4):
        ref = given[i * count // 4]
        owner = lax.axis_index("ctx") ^ ((i & 1) * 2 + (i >> 1))
        low = i % (4 // count) * rows
        four[pl.ds(pl.multiple_of(owner * rows, 16), rows), :] = ref[low : low + rows, :].astype(F32)
    for out, (low, high, form) in zip(outs, cuts):
        if form == "plain":
            out[...] = four[:, low:high]
        else:
            step = (high - low) // 3
            for j in range(3):
                out[j] = four[:, low + j * step : low + (j + 1) * step]


def settle(given, cuts):
    rows, cols = given[0].shape[0] * len(given) // 4, given[0].shape[1]
    shapes = {"plain": lambda n: (4 * rows, n), "three": lambda n: (3, 4 * rows, n // 3)}
    return call(
        lambda *refs: settle_kernel(*refs, cuts=cuts, count=len(given)),
        "settle",
        tuple(struct(shapes[form](high - low), F32) for low, high, form in cuts),
        [VMEM] * len(given),
        (VMEM,) * len(cuts),
        [pltpu.VMEM((4 * rows, cols), F32)],
        3,
        7,
        tuple(given),
    )


def cut(full):
    rows, cols = full.shape
    return full[:, : cols // 2], full[:, cols // 2 :]


def gather_plain(shard):
    rows = lax.all_gather(shard, "fsdp", axis=0, tiled=True)
    return lax.all_gather(rows, "tp", axis=1, tiled=True)


def reduce_plain(own, sib):
    full = jnp.concatenate([own, sib], axis=1)
    part = lax.psum_scatter(full, "tp", scatter_dimension=1, tiled=True)
    part = lax.psum_scatter(part, "fsdp", scatter_dimension=0, tiled=True)
    return lax.psum(part, "ctx").astype(F32)


def body(
    layer_input,
    doc_ids,
    w_qkv,
    b_qv,
    w_out,
    b_out,
    ln1_gain,
    ln1_bias,
    w_up,
    b_up,
    w_down,
    b_down,
    ln2_gain,
    ln2_bias,
    out_grad,
):
    sizes = (lax.axis_size("fsdp"), lax.axis_size("ctx"), lax.axis_size("tp"))
    micro, seqs, local_len, width = layer_input.shape
    length = local_len * sizes[1]
    shard_rows, local_width = w_qkv.shape[1:]
    local_units = w_up.shape[1]
    heads = width // HEAD_DIM
    fast = sizes == (4, 4, 2)
    t = lax.axis_index("tp")
    c = lax.axis_index("ctx")

    def mine(value):
        return lax.dynamic_index_in_dim(value, t, 1, keepdims=False)

    def to_owners(chunks):
        return lax.all_to_all(chunks, "ctx", 0, 0, tiled=True)

    def spread(chunks):
        out = lax.all_to_all(chunks, ("ctx", "tp"), 0, 0, tiled=True)
        return out.reshape(micro, seqs, local_len, width)

    shards = (
        jnp.swapaxes(w_qkv, 0, 1).reshape(shard_rows, 3 * local_width),
        jnp.concatenate([w_out.T, w_up], axis=1),
        w_down.T,
    )
    ids = mine(doc_ids).astype(BF16)[:, None, :]
    ids = jnp.pad(ids, ((0, 0), (0, 7), (0, width - local_len)))
    rows_in = jnp.concatenate([mine(layer_input), ids], axis=1)
    cot_in = mine(out_grad)
    gathers = GATHER if fast else (None,) * 3
    packs = tuple(packing(order) for order in SCATTER) if fast else (None,) * 3

    def swap(value, group, step):
        order = tuple(zip(*GATHER[group])) + (CORE,)
        return exchange(value, order[step], sizes)

    def shed(value, group, step):
        order = (CORE,) + tuple(zip(*SCATTER[group]))
        return exchange(value, order[step], sizes)

    def joined(*parts):
        return jnp.concatenate(parts, axis=0)

    if fast:
        def seen(value):
            return [lax.dynamic_index_in_dim(value, c ^ i, 0, keepdims=True) for i in range(4)]

        part = shard_rows // 4
        h1 = lax.dynamic_slice_in_dim(w_qkv, c * part, part, 1)
        h1 = jnp.swapaxes(h1, 0, 1).reshape(part, 3 * local_width)
        h2, h3 = [lax.dynamic_slice_in_dim(s, c * part, part, 0) for s in shards[1:]]
        g1 = swap(h1, 0, 0)
        x0, x1, x2, x3 = seen(after(rows_in, h1))
        g1, x1, x2, x3, h2, h3, cot_in, b_up = phase(g1, x1, x2, x3, h2, h3, cot_in, b_up)
        h1 = joined(h1, g1)
        g1, g3, xk, xx, xd = phase(
            swap(h1, 0, 1), swap(h3, 2, 0), exchange(x1, CORE, sizes), exchange(x2, X, sizes), exchange(x3, FAR, sizes)
        )
        given = (x0, xk, joined(xx, xd))
        h1, h2, h3, cot_in, b_up = phase(joined(h1, g1), h2, joined(h3, g3), cot_in, b_up)
        g1, g2, g3 = swap(h1, 0, 2), swap(h2, 1, 0), swap(h3, 2, 1)
        c0, c1, c2, c3 = seen(cot_in)
        c_send = joined(c1, c3)
        table, small = tables(b_qv, b_up, (b_out, ln1_gain, ln1_bias, b_down, ln2_gain, ln2_bias))
        g1, g2, g3, c_send, small = phase(g1, g2, g3, c_send, small)
        h1, h2, h3 = phase(joined(h1, g1), joined(h2, g2), joined(h3, g3))
        g1, g2, ck, got = phase(
            swap(h1, 0, 3), swap(h2, 1, 1), exchange(c_send, CORE, sizes), exchange(small, Y, sizes)
        )
        small = joined(small, got)
        h1, h2, h3 = phase(joined(h1, g1), joined(h2, g2), h3)
        g1, g2, g3 = swap(h1, 0, 4), swap(h2, 1, 2), swap(h3, 2, 2)
        (wq,) = unpack(gathers[0], h1, g1, (3 * width,))
        proj, rows_b, mask = project(wq, given, small, fast)
        proj, g2, c2, ck = phase(proj, g2, c2, ck)
        h2 = joined(h2, g2)
        g2 = swap(h2, 1, 3)
        mixed0, probs0 = attend(after(proj, h2), mask, 0)
        mixed0, g3 = phase(mixed0, g3)
        h3 = joined(h3, g3)
        g3 = swap(h3, 2, 3)
        mixed1, probs1 = attend(after(proj, h3, mixed0), mask, 1)
        mixed1, g2 = phase(mixed1, g2)
        h2, c_send = phase(joined(h2, g2), joined(c2, ck[1:]))
        g2, cx = swap(h2, 1, 4), exchange(c_send, X, sizes)
        wo, wu = unpack(gathers[1], h2, g2, (width, 2 * local_units))
    else:
        parts = (shards[0], w_out.T, w_up, w_down.T)
        pieces = [cut(gather_plain(s)) for s in parts]
        (wq,) = unpack(None, *pieces[0], (3 * width,))
        (wo,) = unpack(None, *pieces[1], (width,))
        (wu,) = unpack(None, *pieces[2], (2 * local_units,))
        (wd,) = unpack(None, *pieces[3], (2 * local_units,))
        order = lambda value: (value[:1], value[1:3], value[2:])
        given, cot = order(to_owners(rows_in)), order(to_owners(cot_in))
        table, small = tables(b_qv, b_up, (b_out, ln1_gain, ln1_bias, b_down, ln2_gain, ln2_bias))
        small = joined(small, exchange(small, Y, sizes))
        proj, rows_b, mask = project(wq, given, small, fast)
        mixed0, probs0 = attend(proj, mask, 0)
        mixed1, probs1 = attend(proj, mask, 1)

    normed1, scale1, first_b, act, slope = middle(wo, wu, mixed0, mixed1, rows_b, table, small)
    if fast:
        act, g3, cx = phase(act, g3, cx)
        cot = (c0, ck, cx)
        h3 = joined(h3, g3)
        (wd,) = unpack(gathers[2], h3, swap(h3, 2, 4), (2 * local_units,))
    chunks, gz, gzb, sums2, down_own, down_sib = turn(packs[2], wd, act, normed1, cot, table, local_len)

    rows = shard_rows // 4
    if fast:
        down_sib, chunks, gzb = phase(down_sib, chunks, gzb)
        got, core_out = shed(down_sib, 2, 0), exchange(chunks[2:], CORE, sizes)
    gh, sum_up = hidden_back(wd, gzb, slope)
    if fast:
        gh, got, core_out = phase(gh, got, core_out)
        down = [down_own, got]
        send, x_send, gh = phase(
            add_up(down, 8 * rows, 16 * rows), joined(chunks[1:2], core_out[1:2]), gh
        )
        got, x_out = shed(send, 2, 1), exchange(x_send, X, sizes)
    gz1, grad_mixed, sums1, up_own, up_sib = first_back(
        packs[1], wo, wu, gh, gz, normed1, scale1, table, first_b, mixed0, mixed1
    )
    if fast:
        grad_mixed, up_sib, got, x_out = phase(grad_mixed, up_sib, got, x_out)
        down = down + [got]
        send, y_send, grad_mixed = phase(
            add_up(down, 4 * rows, 8 * rows), joined(chunks[:1], core_out[:1], x_out), grad_mixed
        )
        got, got2 = shed(send, 2, 2), shed(up_sib, 1, 0)
    parts0 = attend_back(proj, probs0, grad_mixed, 0)
    if fast:
        head, got2, grad_mixed = phase(parts0[0], got2, grad_mixed)
        parts0 = (head,) + tuple(parts0[1:])
        up = [up_own, got2]
        send2, grad_mixed, y_send = phase(add_up(up, 8 * rows, 16 * rows), grad_mixed, y_send)
        got2, y_out = shed(send2, 1, 1), exchange(y_send, Y, sizes)
    parts1 = attend_back(proj, probs1, grad_mixed, 1)
    parts = list(parts0) + list(parts1)
    chunks2 = input_back(wq, gz1, parts, local_len, fast)
    parts[0] = after(parts[0], chunks2)
    qkv_own, qkv_sib = last(packs[0], rows_b, sums1, sums2, sum_up, parts)
    if fast:
        got3, core_x = shed(qkv_sib, 0, 0), exchange(chunks2[2:], CORE, sizes)
        chunks2, qkv_own, got2, y_out, got = phase(chunks2, qkv_own, got2, y_out, got)
        down, up = down + [got], up + [got2]
        send = add_up(down, 2 * rows, 4 * rows)
        send2 = add_up(up, 4 * rows, 8 * rows, time=30)
        send, send2, got3 = phase(send, send2, got3)
        got, got2 = shed(send, 2, 3), shed(send2, 1, 2)
        got3, core_x = phase(got3, core_x)
        qkv = [qkv_own, got3]
        sent3 = add_up(qkv, 8 * rows, 16 * rows, (0, 1))
        x_send = joined(chunks2[1:2], core_x[1:2])
        got3 = shed(sent3, 0, 1)
        got3, x_send = phase(got3, x_send)
        qkv = qkv + [got3]
        send3 = add_up(qkv, 4 * rows, 8 * rows, (3, 2), [sent3])
        got3 = shed(send3, 0, 2)
        send3, got, x_send = phase(send3, got, x_send)
        down = down + [got]
        send = add_up(down, rows, 2 * rows)
        got, x_x = shed(send, 2, 4), exchange(x_send, X, sizes)
        send, got2 = phase(send, got2)
        up = up + [got2]
        send2 = add_up(up, 2 * rows, 4 * rows)
        got2 = shed(send2, 1, 3)
        got3, send2 = phase(got3, send2)
        qkv = qkv + [got3]
        sent3 = add_up(qkv, 2 * rows, 4 * rows, (4, 3), [send3])
        got3 = shed(sent3, 0, 3)
        sent3, got, x_x = phase(sent3, got, x_x)
        pair1 = add_up(down + [got], 0, rows)
        y_send = joined(chunks2[:1], core_x[:1], x_x)
        got, y_x = exchange(pair1, X, sizes), exchange(y_send, Y, sizes)
        pair1, got2 = phase(pair1, got2)
        up = up + [got2]
        send2 = add_up(up, rows, 2 * rows)
        got2 = shed(send2, 1, 4)
        layer_output = deliver(chunks, core_out, x_out, after(y_out, send2))
        got3, layer_output = phase(got3, layer_output)
        qkv = qkv + [got3]
        send3 = add_up(qkv, rows, 2 * rows, (5, 4), [sent3])
        got3 = shed(send3, 0, 4)
        send3, got, got2 = phase(send3, got, got2)
        pair1 = joined(pair1, got)
        up = up + [got2]
        pair2 = add_up(up, 0, rows)
        got1, got2 = exchange(pair1, CORE, sizes), exchange(pair2, X, sizes)
        got3, pair1, pair2 = phase(got3, pair1, pair2)
        qkv = qkv + [got3]
        sent_last = got3
        piece = add_up(qkv, 0, rows)
        got3 = [exchange(piece, dims, sizes) for dims in (X, CORE, FAR)]
        vec = vectors(after(send3, piece), sent_last, local_width, local_units)
        piece, got1, bup = phase(piece, got1, vec[1])
        vec = (vec[0], bup) + tuple(vec[2:])
        (grad_down,) = settle((pair1, got1), ((0, local_units, "plain"),))
        grad_down, got2 = phase(grad_down, got2)
        pair2 = joined(pair2, got2)
        got2 = exchange(pair2, CORE, sizes)
        pair2, y_x = phase(pair2, y_x)
        grad_x = deliver(chunks2, core_x, x_x, y_x)
        grad_x, *got3 = phase(grad_x, *got3)
        (grad_qkv,) = settle([piece] + got3, ((0, 3 * local_width, "three"),))
        grad_wout, grad_up = settle(
            (pair2, after(got2, grad_qkv)),
            ((0, local_width, "plain"), (local_width, local_width + local_units, "plain")),
        )
        layer_output = layer_output.reshape(micro, seqs, local_len, width)
        grad_x = grad_x.reshape(micro, seqs, local_len, width)
    else:
        layer_output = spread(jnp.repeat(chunks, 2, axis=0))
        grad_x = spread(jnp.repeat(chunks2, 2, axis=0))
        vec = lax.psum(qkv_own[width:].astype(F32), AXES)
        vec = vectors(vec, None, local_width, local_units)
        grad_down = reduce_plain(down_own, down_sib)
        both = reduce_plain(up_own, up_sib)
        grad_wout, grad_up = both[:, :local_width], both[:, local_width:]
        grad_qkv = reduce_plain(qkv_own[:width], qkv_sib[:width])
        grad_qkv = jnp.swapaxes(grad_qkv.reshape(shard_rows, 3, local_width), 0, 1)

    out_bqv, out_bup, g1, s1, bout, g2, s2, bdown = vec
    return (
        layer_output,
        grad_x,
        grad_qkv,
        out_bqv,
        grad_wout.T,
        bout,
        g1,
        s1,
        grad_up,
        out_bup,
        grad_down.T,
        bdown,
        g2,
        s2,
    )


def solution(mesh):
    return jax.shard_map(
        body,
        mesh=mesh,
        in_specs=(
            P(None, "fsdp", "ctx", None),
            P(None, "fsdp", "ctx"),
            P(None, "fsdp", "tp"),
            P(None, "tp"),
            P("tp", "fsdp"),
            P(),
            P(),
            P(),
            P("fsdp", "tp"),
            P("tp"),
            P("tp", "fsdp"),
            P(),
            P(),
            P(),
            P(None, "fsdp", "ctx", None),
        ),
        out_specs=(
            P(None, "fsdp", "ctx", None),
            P(None, "fsdp", "ctx", None),
            P(None, "fsdp", "tp"),
            P(None, "tp"),
            P("tp", "fsdp"),
            P(),
            P(),
            P(),
            P("fsdp", "tp"),
            P("tp"),
            P("tp", "fsdp"),
            P(),
            P(),
            P(),
        ),
        check_vma=False,
    )
```

```python
import jax
import jax.numpy as jnp
from jax import lax
from jax.experimental import pallas as pl
from jax.experimental.pallas import tpu as pltpu
from jax.sharding import PartitionSpec as P

HEAD_DIM = 64
AXES = ("fsdp", "ctx", "tp")
F32 = jnp.float32
BF16 = jnp.bfloat16
NEG = -1e30
NT = (((1,), (1,)), ((), ()))
VMEM = pl.BlockSpec(memory_space=pltpu.VMEM)
SMEM = pl.BlockSpec(memory_space=pltpu.SMEM)
ANY = pl.BlockSpec(memory_space=pl.ANY)


def partner(dim, z, c, t):
    if dim == "core":
        return z, c ^ 1, t
    if dim == "x":
        return z, c ^ 2, t
    if dim == "x+core":
        return z, c ^ 3, t
    if dim == "y":
        return z, c, t ^ 1
    return z ^ int(dim[1:]), c, t


def exchange(value, dims, sizes):
    nz, nc, nt = sizes
    pairs = []
    for z in range(nz):
        for c in range(nc):
            for t in range(nt):
                tz, tc, tt = partner(dims[c & 1], z, c, t)
                pairs.append(((z * nc + c) * nt + t, (tz * nc + tc) * nt + tt))
    return lax.ppermute(value, AXES, pairs)


GATHER = (
    (("z2", "z1", "y", "x"), ("z1", "z2", "x", "y")),
    (("z2", "z1", "y", "x"), ("z1", "z2", "x", "y")),
    (("z2", "z1", "x", "y"), ("y", "x", "z2", "z1")),
)
SCATTER = (
    (("x", "y", "z1", "z2"), ("y", "x", "z2", "z1")),
    (("x", "y", "z1", "z2"), ("z1", "z2", "y", "x")),
    (("y", "x", "z1", "z2"), ("z1", "z2", "x", "y")),
)
CORE = ("core", "core")
X = ("x", "x")
FAR = ("x+core", "x+core")
Y = ("y", "y")


def piece_place(order, core, here, index):
    z, x, t = here
    for bit, dim in enumerate(order):
        flip = (index >> bit) & 1
        if dim == "x":
            x = x ^ flip
        elif dim == "y":
            t = t ^ flip
        else:
            z = z ^ (flip * int(dim[1:]))
    return z * 4 + x * 2 + core, t


def places(orders):
    if orders is None:
        return [(i, half) for half in range(2) for i in range(16)]
    c = lax.axis_index("ctx")
    here = (lax.axis_index("fsdp"), c >> 1, lax.axis_index("tp"))
    spots = []
    for core in (c & 1, 1 - (c & 1)):
        for i in range(16):
            r0, t0 = piece_place(orders[0], core, here, i)
            r1, t1 = piece_place(orders[1], core, here, i)
            spots.append((jnp.where(core == 0, r0, r1), jnp.where(core == 0, t0, t1)))
    return spots


def packing(orders):
    return tuple(order[::-1] for order in orders)


def after(value, *first):
    return lax.optimization_barrier((value, first))[0]


def phase(*values):
    return lax.optimization_barrier(values)


def at_rows(place, count, unit=0):
    start = place * count
    return pl.ds(start if isinstance(start, int) else pl.multiple_of(start, unit or count), count)


def piece_copies(spots, near, far, sem, whole, low, cols, base=0):
    rows = whole.shape[0] // 16
    copies = []
    each = 16 // len(near)
    for half, refs in ((0, near), (1, far)):
        for i in range(16):
            row, col = spots[half * 16 + i]
            copy = pltpu.make_async_copy(
                refs[i // each].at[pl.ds(i % each * rows, rows), pl.ds(low, cols)],
                whole.at[at_rows(row, rows), at_rows(col, cols, 128)],
                sem.at[base + half * 16 + i],
            )
            copy.start()
            copies.append(copy)
    return copies


def pack(spots, own_ref, sib_ref, whole, low, cols):
    rows = whole.shape[0] // 16
    for half, ref in ((0, own_ref), (1, sib_ref)):
        for i in range(16):
            row, col = spots[half * 16 + i]
            ref[i * rows : (i + 1) * rows, low : low + cols] = whole[at_rows(row, rows), at_rows(col, cols, 128)]


def finish(copies):
    for copy in copies:
        copy.wait()


def tiles(count, step):
    def run(one):
        lax.fori_loop(0, count // step, lambda i, carry: (one(pl.multiple_of(i * step, step)), carry)[1], 0)

    return run


def row_mean(value):
    return jnp.mean(value, axis=-1, keepdims=True)


def struct(shape, dtype):
    return jax.ShapeDtypeStruct(shape, dtype)


def call(kernel, name, outs, specs, out_specs, scratch, time, room, args):
    return pl.pallas_call(
        kernel,
        name=name,
        out_shape=outs,
        in_specs=specs,
        out_specs=out_specs,
        scratch_shapes=scratch,
        compiler_params=pltpu.CompilerParams(vmem_limit_bytes=room << 20),
        cost_estimate=pl.CostEstimate(flops=time * 10**9, transcendentals=0, bytes_accessed=10**6),
    )(*args)


B_OUT, GAIN1, SHIFT1, B_DOWN, GAIN2, SHIFT2 = range(6)


def unpack_kernel(*refs, orders, count):
    near, far, outs, sem = refs[:count], refs[count : 2 * count], refs[2 * count : -1], refs[-1]
    copies = []
    spots = places(orders)
    low = 0
    for i, out in enumerate(outs):
        cols = out.shape[1] // 2
        copies += piece_copies(spots, near, far, sem, out, low, cols, 32 * i)
        low += cols
    finish(copies)


def unpack(orders, near, far, widths):
    count = len(near)
    rows = near[0].shape[0] * count
    return call(
        lambda *refs: unpack_kernel(*refs, orders=orders, count=count),
        "unpack",
        tuple(struct((rows, width), BF16) for width in widths),
        [ANY] * (2 * count),
        (VMEM,) * len(widths),
        [pltpu.SemaphoreType.DMA((32 * len(widths),))],
        5,
        2,
        tuple(near) + tuple(far),
    )


def sources(refs, fast):
    c = lax.axis_index("ctx") if fast else 0
    own, core, x = refs
    return [(c ^ 0, own, 0), (c ^ 1, core, 0), (c ^ 2, x, 0), (c ^ 3, x, 1)]


def tables_kernel(qv_ref, up_ref, *refs):
    rows, (table_ref, small_ref) = refs[:-2], refs[-2:]
    table_ref[...] = jnp.zeros_like(table_ref)
    for i, ref in enumerate(rows):
        table_ref[i : i + 1, :] = ref[...][None]
    width = qv_ref.shape[1]
    small_ref[:, :width] = qv_ref[0:1, :]
    small_ref[:, width : 2 * width] = qv_ref[1:2, :]
    small_ref[:, 2 * width :] = up_ref[...][None]


def tables(b_qv, b_up, rows):
    return call(
        tables_kernel,
        "tables",
        (struct((8, rows[0].shape[0]), F32), struct((1, b_qv.size + b_up.size), F32)),
        [VMEM] * (2 + len(rows)),
        (VMEM, VMEM),
        [],
        1,
        3,
        (b_qv, b_up) + tuple(rows),
    )


def project_kernel(weight_ref, own_ref, core_ref, far_ref, small_ref, proj_ref, x_ref, mask_ref, ids, *, fast):
    block = own_ref.shape[1] - 8
    count = 4
    for spot, ref, i in sources((own_ref, core_ref, far_ref), fast):
        x_ref[pl.ds(pl.multiple_of(spot * block, block), block), :] = ref[i, 0:block, :]
        ids[pl.ds(spot, 1), :] = ref[i, block:, 0:block].astype(F32)[0:1]
    for kb in range(count):
        column = jnp.broadcast_to(ids[kb : kb + 1], (block, block)).T
        for qb in range(count):
            mask_ref[kb * block : (kb + 1) * block, qb * block : (qb + 1) * block] = jnp.where(
                column == jnp.broadcast_to(ids[qb : qb + 1], (block, block)), 0.0, NEG
            )
    width = proj_ref.shape[1] // 6
    for y in range(2):
        row = pl.ds(lax.axis_index("tp") ^ y, 1)
        for which in range(3):
            at = (y * 3 + which) * width
            value = jnp.dot(x_ref[...], weight_ref[:, at : at + width], preferred_element_type=F32)
            if which != 1:
                low = 0 if which == 0 else width
                value = value + small_ref[row, low : low + width]
            proj_ref[:, at : at + width] = value.astype(BF16)


def project(weight, given, small, fast):
    width, wide = weight.shape
    block = given[0].shape[1] - 8
    length = 4 * block
    return call(
        lambda *refs: project_kernel(*refs, fast=fast),
        "project",
        (
            struct((length, wide), BF16),
            struct((length, width), BF16),
            struct((length, length), F32),
        ),
        [VMEM] * 5,
        (VMEM,) * 3,
        [pltpu.VMEM((8, block), F32)],
        5,
        3,
        (weight,) + tuple(given) + (small,),
    )


def attend_kernel(proj_ref, mask_ref, o_ref, p_ref, *, y):
    length = proj_ref.shape[0]
    pairs = o_ref.shape[1] // 128
    lane = lax.broadcasted_iota(jnp.int32, (1, 128), 1)

    def pair(g, carry):
        take = lambda which: proj_ref[:, pl.ds(pl.multiple_of(((y * 3 + which) * pairs + g) * 128, 128), 128)]
        query = take(0) * jnp.asarray(0.125, BF16)
        keys = take(1)
        values_t = take(2).T
        outs = []
        for head in range(2):
            here = (lane >= 64 * head) & (lane < 64 * head + 64)
            only = jnp.where(here, keys, jnp.zeros_like(keys))
            row = []
            for at in range(0, length, 256):
                scores = lax.dot_general(only, query[at : at + 256], NT, preferred_element_type=F32)
                scores = scores + mask_ref[:, at : at + 256]
                top = jnp.max(scores, axis=0, keepdims=True)
                raised = jnp.exp(scores - top)
                total = jnp.sum(raised, axis=0, keepdims=True)
                probs = (raised * (1.0 / total)).astype(BF16)
                p_ref[2 * g + head, :, at : at + 256] = probs
                row.append(
                    jnp.dot(values_t[64 * head : 64 * head + 64], probs, preferred_element_type=F32)
                )
            outs.append(jnp.concatenate(row, axis=1))
        both = jnp.concatenate(outs, axis=0).astype(BF16)
        o_ref[:, pl.ds(pl.multiple_of(g * 128, 128), 128)] = both.T
        return carry

    lax.fori_loop(0, pairs, pair, 0)


def attend(proj, mask, y):
    length, wide = proj.shape
    half = wide // 6
    return call(
        lambda *refs: attend_kernel(*refs, y=y),
        "attend",
        (struct((length, half), BF16), struct((half // HEAD_DIM, length, length), BF16)),
        [VMEM, VMEM],
        (VMEM, VMEM),
        [],
        12,
        3,
        (proj, mask),
    )


def middle_kernel(
    w_out, w_up, mixed0_ref, mixed1_ref, x_ref, table_ref, small_ref,
    normed_ref, scale_ref, first_ref, act_ref, slope_ref,
):
    length, units = act_ref.shape
    narrow, half = w_out.shape[1] // 2, units // 2
    normed_ref[...] = lax.dot_general(
        mixed0_ref[...], w_out[:, :narrow], NT, preferred_element_type=F32
    ) + lax.dot_general(mixed1_ref[...], w_out[:, narrow:], NT, preferred_element_type=F32)

    @tiles(length, 64)
    def _(at):
        here = pl.ds(at, 64)
        value = x_ref[here, :].astype(F32) + normed_ref[here, :] + table_ref[B_OUT : B_OUT + 1, :]
        centred = value - row_mean(value)
        scale = lax.rsqrt(row_mean(centred * centred) + 1e-12)
        unit = centred * scale
        normed_ref[here, :] = unit
        scale_ref[here, :] = scale
        first_ref[here, :] = (
            unit * table_ref[GAIN1 : GAIN1 + 1, :] + table_ref[SHIFT1 : SHIFT1 + 1, :]
        ).astype(BF16)

    for y in range(2):
        row = pl.ds(lax.axis_index("tp") ^ y, 1)

        @tiles(half, 256)
        def _(at):
            here = pl.ds(pl.multiple_of(y * half + at, 256), 256)
            bias = small_ref[row, pl.ds(pl.multiple_of(2 * narrow + at, 256), 256)]
            hidden = jnp.dot(first_ref[...], w_up[:, here], preferred_element_type=F32) + bias
            phi = 0.5 + 0.5 * lax.erf(hidden * 0.7071067811865476)
            act_ref[:, here] = (hidden * phi).astype(BF16)
            bell = jnp.exp(-0.5 * hidden * hidden) * 0.3989422804014327
            slope_ref[:, here] = (phi + hidden * bell).astype(BF16)


def middle(w_out, w_up, mixed0, mixed1, x, table, small):
    length, width = x.shape
    units = w_up.shape[1]
    return call(
        middle_kernel,
        "middle",
        (
            struct((length, width), F32),
            struct((length, 1), F32),
            struct((length, width), BF16),
            struct((length, units), BF16),
            struct((length, units), BF16),
        ),
        [VMEM] * 7,
        (VMEM,) * 5,
        [],
        12,
        3,
        (w_out, w_up, mixed0, mixed1, x, table, small),
    )


def turn_kernel(
    weight_ref, act_ref, normed_ref, own_ref, core_ref, far_ref, table_ref,
    chunks_ref, gz_ref, gzb_ref, sums_ref, down_own, down_sib, full, cot_ref, *, orders,
):
    length = act_ref.shape[0]
    block = chunks_ref.shape[1]
    for spot, ref, i in sources((own_ref, core_ref, far_ref), orders is not None):
        cot_ref[pl.ds(pl.multiple_of(spot * block, block), block), :] = ref[i]
    gz_ref[...] = lax.dot_general(act_ref[...], weight_ref[...], NT, preferred_element_type=F32)
    sums_ref[...] = jnp.zeros_like(sums_ref)
    row = lambda which: table_ref[which : which + 1, :]

    @tiles(length, 64)
    def _(at):
        here = pl.ds(at, 64)
        value = normed_ref[here, :] * row(GAIN1) + row(SHIFT1) + gz_ref[here, :] + row(B_DOWN)
        centred = value - row_mean(value)
        scale = lax.rsqrt(row_mean(centred * centred) + 1e-12)
        unit = centred * scale
        result = (unit * row(GAIN2) + row(SHIFT2)).astype(BF16)
        chunk = lax.div(at, block)
        if orders is not None:
            c = lax.axis_index("ctx") ^ chunk
            chunk = (c & 1) * 2 + (c >> 1)
        chunks_ref[chunk, pl.ds(pl.multiple_of(lax.rem(at, block), 64), 64), :] = result
        coming = cot_ref[here, :].astype(F32)
        raised = coming * row(GAIN2)
        back = scale * (raised - row_mean(raised) - unit * row_mean(raised * unit))
        gz_ref[here, :] = back
        gzb_ref[here, :] = back.astype(BF16)
        sums_ref[0:1, :] += jnp.sum(coming * unit, axis=0, keepdims=True)
        sums_ref[1:2, :] += jnp.sum(coming, axis=0, keepdims=True)
        sums_ref[2:3, :] += jnp.sum(back, axis=0, keepdims=True)

    back_t = gzb_ref[...].T

    @tiles(full.shape[1], 1024)
    def _(at):
        here = pl.ds(at, 1024)
        full[:, here] = jnp.dot(back_t, act_ref[:, here], preferred_element_type=F32).astype(BF16)

    pack(places(orders), down_own, down_sib, full, 0, down_own.shape[1])


def turn(orders, weight, act, normed, cot, table, chunk):
    length, units = act.shape
    width = normed.shape[1]
    piece = struct((width, units // 2), BF16)
    return call(
        lambda *refs: turn_kernel(*refs, orders=orders),
        "turn",
        (
            struct((length // chunk, chunk, width), BF16),
            struct((length, width), F32),
            struct((length, width), BF16),
            struct((8, width), F32),
            piece,
            piece,
        ),
        [VMEM] * 7,
        (VMEM,) * 6,
        [pltpu.VMEM((width, units), BF16), pltpu.VMEM((length, width), BF16)],
        14,
        10,
        (weight, act, normed) + tuple(cot) + (table,),
    )


def hidden_back_kernel(weight_ref, gzb_ref, slope_ref, gh_ref, sum_ref):
    @tiles(gh_ref.shape[1], 512)
    def _(at):
        here = pl.ds(at, 512)
        back = jnp.dot(gzb_ref[...], weight_ref[:, here], preferred_element_type=F32)
        back = (back * slope_ref[:, here].astype(F32)).astype(BF16)
        gh_ref[:, here] = back
        sum_ref[:, here] = jnp.sum(back.astype(F32), axis=0, keepdims=True)


def hidden_back(weight, gzb, slope):
    length, units = slope.shape
    return call(
        hidden_back_kernel,
        "hidden_back",
        (struct((length, units), BF16), struct((1, units), F32)),
        [VMEM] * 3,
        (VMEM, VMEM),
        [],
        12,
        3,
        (weight, gzb, slope),
    )


def first_back_kernel(
    w_out, w_up, gh_ref, gz_ref, normed_ref, scale_ref, table_ref, first_ref, mixed0_ref, mixed1_ref,
    gz1_ref, gm_ref, sums_ref, pieces_own, pieces_sib, branch, d_out, d_up, *, orders,
):
    narrow = w_out.shape[1] // 2
    half = w_up.shape[1] // 2
    length = gh_ref.shape[0]
    first_t = first_ref[...].T
    spots = places(orders)

    @tiles(d_up.shape[1], 1024)
    def _(at):
        here = pl.ds(at, 1024)
        d_up[:, here] = jnp.dot(first_t, gh_ref[:, here], preferred_element_type=F32).astype(BF16)

    pack(spots, pieces_own, pieces_sib, d_up, narrow, half)
    gz1_ref[...] = lax.dot_general(gh_ref[...], w_up[...], NT, preferred_element_type=F32)
    sums_ref[...] = jnp.zeros_like(sums_ref)

    @tiles(length, 64)
    def _(at):
        here = pl.ds(at, 64)
        coming = gz_ref[here, :] + gz1_ref[here, :]
        unit = normed_ref[here, :]
        raised = coming * table_ref[GAIN1 : GAIN1 + 1, :]
        back = scale_ref[here, :] * (raised - row_mean(raised) - unit * row_mean(raised * unit))
        gz1_ref[here, :] = back
        branch[here, :] = back.astype(BF16)
        sums_ref[0:1, :] += jnp.sum(coming * unit, axis=0, keepdims=True)
        sums_ref[1:2, :] += jnp.sum(coming, axis=0, keepdims=True)
        sums_ref[2:3, :] += jnp.sum(back, axis=0, keepdims=True)

    branch_t = branch[...].T
    d_out[:, :narrow] = jnp.dot(branch_t, mixed0_ref[...], preferred_element_type=F32).astype(BF16)
    d_out[:, narrow:] = jnp.dot(branch_t, mixed1_ref[...], preferred_element_type=F32).astype(BF16)
    pack(spots, pieces_own, pieces_sib, d_out, 0, narrow)
    gm_ref[...] = jnp.dot(branch[...], w_out[...], preferred_element_type=F32).astype(BF16)


def first_back(orders, w_out, w_up, gh, gz, normed, scale, table, first_b, mixed0, mixed1):
    length, units = gh.shape
    width = gz.shape[1]
    piece = struct((width, (units + width) // 2), BF16)
    return call(
        lambda *refs: first_back_kernel(*refs, orders=orders),
        "first_back",
        (
            struct((length, width), F32),
            struct((length, width), BF16),
            struct((8, width), F32),
            piece,
            piece,
        ),
        [VMEM] * 10,
        (VMEM,) * 5,
        [
            pltpu.VMEM((length, width), BF16),
            pltpu.VMEM((width, width), BF16),
            pltpu.VMEM((width, units), BF16),
        ],
        20,
        12,
        (w_out, w_up, gh, gz, normed, scale, table, first_b, mixed0, mixed1),
    )


def attend_back_kernel(proj_ref, p_ref, gm_ref, dq_ref, dk_ref, dv_ref, dst, dqt, *, y):
    length = proj_ref.shape[0]
    pairs = dq_ref.shape[1] // 128
    lane = lax.broadcasted_iota(jnp.int32, (1, 128), 1)
    low = lane < 64

    def pair(g, carry):
        take = lambda which: proj_ref[:, pl.ds(pl.multiple_of(((y * 3 + which) * pairs + g) * 128, 128), 128)]
        query, keys, values = take(0), take(1), take(2)
        grad = gm_ref[:, pl.ds(pl.multiple_of((y * pairs + g) * 128, 128), 128)]
        keys_t = keys.T
        dks, dvs = [], []
        for head in range(2):
            here = low if head == 0 else jnp.logical_not(low)
            only = jnp.where(here, values, jnp.zeros_like(values))
            for at in range(0, length, 256):
                cols = slice(at, at + 256)
                gp = lax.dot_general(only, grad[cols], NT, preferred_element_type=F32)
                probs = p_ref[2 * g + head, :, cols].astype(F32)
                weighted = jnp.sum(probs * gp, axis=0, keepdims=True)
                dst[:, cols] = (probs * (gp - weighted)).astype(BF16)
            dqt[64 * head : 64 * head + 64, :] = (
                jnp.dot(keys_t[64 * head : 64 * head + 64], dst[...], preferred_element_type=F32) * 0.125
            ).astype(BF16)
            dks.append(jnp.dot(dst[...], query, preferred_element_type=F32))
            dvs.append(jnp.dot(p_ref[2 * g + head], grad, preferred_element_type=F32))
        cols = pl.ds(pl.multiple_of(g * 128, 128), 128)
        dq_ref[:, cols] = dqt[...].T
        dk_ref[:, cols] = (jnp.where(low, dks[0], dks[1]) * 0.125).astype(BF16)
        dv_ref[:, cols] = jnp.where(low, dvs[0], dvs[1]).astype(BF16)
        return carry

    lax.fori_loop(0, pairs, pair, 0)


def attend_back(proj, probs, grad_mixed, y):
    length, wide = proj.shape
    shape = struct((length, wide // 6), BF16)
    return call(
        lambda *refs: attend_back_kernel(*refs, y=y),
        "attend_back",
        (shape, shape, shape),
        [VMEM] * 3,
        (VMEM,) * 3,
        [pltpu.VMEM((length, length), BF16), pltpu.VMEM((128, length), BF16)],
        1,
        4,
        (proj, probs, grad_mixed),
    )


def last_kernel(x_ref, sums1_ref, sums2_ref, sum_up_ref, *refs, orders):
    parts, (pieces_own, pieces_sib, whole, vec) = refs[:6], refs[6:]
    half = parts[0].shape[1]
    rows = whole.shape[0]
    x_t = x_ref[...].T
    sums = [[], []]
    for y in range(2):
        for which in range(3):
            at = (y * 3 + which) * half
            value = parts[y * 3 + which][...]
            whole[:, at : at + half] = jnp.dot(x_t, value, preferred_element_type=F32).astype(BF16)
            if which != 1:
                sums[which // 2].append(jnp.sum(value.astype(F32), axis=0, keepdims=True))
    pack(places(orders), pieces_own, pieces_sib, whole, 0, 3 * half)
    vectors = sums[0] + sums[1] + [ref[i : i + 1, :] for ref in (sums1_ref, sums2_ref) for i in range(3)]
    at = 0
    across = vec.shape[1] // 128
    wide = []
    for vector in vectors + [sum_up_ref[...]]:
        for low in range(0, vector.shape[1], 128):
            wide.append(vector[:, low : low + 128])
    for row in range(8):
        vec[row : row + 1, :] = jnp.concatenate(wide[row * across : (row + 1) * across], axis=1)
    pieces_own[rows:, :] = vec[...].astype(BF16)
    pieces_sib[rows:, :] = vec[...].astype(BF16)


def last(orders, x, sums1, sums2, sum_up, parts):
    length, width = x.shape
    piece = struct((width + 8, 3 * width // 2), BF16)
    return call(
        lambda *refs: last_kernel(*refs, orders=orders),
        "last",
        (piece, piece),
        [VMEM] * 10,
        (VMEM, VMEM),
        [
            pltpu.VMEM((width, 3 * width), BF16),
            pltpu.VMEM((8, 3 * width // 2), F32),
        ],
        10,
        7,
        (x, sums1, sums2, sum_up) + tuple(parts),
    )


def vectors_kernel(one_ref, two_ref, qv_ref, up_ref, *refs):
    t = lax.axis_index("tp")
    rows, cols = one_ref.shape
    across = cols // 128
    value = one_ref[rows - 8 :, :].astype(F32)
    if two_ref is not None:
        value = value + two_ref[rows - 8 :, :].astype(F32)

    def block(at):
        row, low = at // across, at % across * 128
        return value[row : row + 1, low : low + 128]

    def take(out, row, first, other, count):
        for i in range(count):
            one = block(first + i)
            if other != first:
                one = jnp.where(t == 0, one, block(other + i))
            if row is None:
                out[i * 128 : (i + 1) * 128] = one[0]
            else:
                out[row : row + 1, i * 128 : (i + 1) * 128] = one

    narrow, wide = qv_ref.shape[1] // 128, up_ref.shape[0] // 128
    for which in range(2):
        take(qv_ref, which, 2 * which * narrow, (2 * which + 1) * narrow, narrow)
    for i, ref in enumerate(refs):
        take(ref, None, (4 + 2 * i) * narrow, (4 + 2 * i) * narrow, 2 * narrow)
    base = (4 + 2 * len(refs)) * narrow
    take(up_ref, None, base, base + wide, wide)


def vectors(one, two, local_width, local_units):
    shapes = [(2, local_width), (local_units,)] + [(2 * local_width,)] * 6
    given = (one,) if two is None else (one, two)

    def kernel(*refs):
        if two is None:
            refs = (refs[0], None) + refs[1:]
        vectors_kernel(*refs)

    return call(
        kernel,
        "vectors",
        tuple(struct(shape, F32) for shape in shapes),
        [VMEM] * len(given),
        (VMEM,) * 8,
        [],
        1,
        4,
        given,
    )


def add_kernel(*refs, low, high, vec, count):
    terms, out = refs[:-1], refs[-1]
    total = terms[0][low:high, :].astype(F32)
    for term in terms[1:count]:
        total = total + term[low:high, :].astype(F32)
    out[: high - low, :] = total.astype(BF16)
    if vec:
        total = 0.0
        for i in vec:
            total = total + terms[i][terms[i].shape[0] - 8 :, :].astype(F32)
        out[high - low :, :] = total.astype(BF16)


def add_up(terms, low, high, vec=(), lone=(), time=1):
    count, terms = len(terms), list(terms) + list(lone)
    cols = terms[0].shape[1]
    return call(
        lambda *refs: add_kernel(*refs, low=low, high=high, vec=vec, count=count),
        "add",
        struct((high - low + (8 if vec else 0), cols), BF16),
        [VMEM] * len(terms),
        VMEM,
        [],
        time,
        4,
        tuple(terms),
    )


def deliver_kernel(own_ref, core_ref, x_ref, y_ref, out_ref):
    c, t = lax.axis_index("ctx"), lax.axis_index("tp")
    sources = [(own_ref, 0), (core_ref, 0), (x_ref, 0), (x_ref, 1)] + [(y_ref, i) for i in range(4)]
    for i, (ref, at) in enumerate(sources):
        ctx = c ^ ((i & 1) + (i & 2))
        out_ref[ctx * 2 + (t ^ (i >> 2))] = ref[at]


def deliver(own, core, x, y):
    return call(
        deliver_kernel,
        "deliver",
        struct((2 * own.shape[0],) + own.shape[1:], BF16),
        [VMEM] * 4,
        VMEM,
        [],
        3,
        7,
        (own, core, x, y),
    )


def input_back_kernel(weight_ref, gz1_ref, *refs, fast):
    parts, chunks_ref = refs[:6], refs[6]
    half = parts[0].shape[1]
    total = gz1_ref[...]
    for i, part in enumerate(parts):
        total = total + lax.dot_general(
            part[...], weight_ref[:, i * half : (i + 1) * half], NT, preferred_element_type=F32
        )
    total = total.astype(BF16)
    count, block = chunks_ref.shape[:2]
    for i in range(count):
        spot = i
        if fast:
            c = lax.axis_index("ctx") ^ i
            spot = (c & 1) * 2 + (c >> 1)
        chunks_ref[spot] = total[i * block : (i + 1) * block]


def input_back(weight, gz1, parts, chunk, fast):
    length, width = gz1.shape
    return call(
        lambda *refs: input_back_kernel(*refs, fast=fast),
        "input_back",
        struct((length // chunk, chunk, width), BF16),
        [VMEM] * 8,
        VMEM,
        [],
        2,
        3,
        (weight, gz1) + tuple(parts),
    )


def settle_kernel(*refs, cuts, count):
    given, outs, four = refs[:count], refs[count:-1], refs[-1]
    rows = four.shape[0] // 4
    for i in range(4):
        ref = given[i * count // 4]
        owner = lax.axis_index("ctx") ^ ((i & 1) * 2 + (i >> 1))
        low = i % (4 // count) * rows
        four[pl.ds(pl.multiple_of(owner * rows, 16), rows), :] = ref[low : low + rows, :].astype(F32)
    for out, (low, high, form) in zip(outs, cuts):
        if form == "plain":
            out[...] = four[:, low:high]
        else:
            step = (high - low) // 3
            for j in range(3):
                out[j] = four[:, low + j * step : low + (j + 1) * step]


def settle(given, cuts):
    rows, cols = given[0].shape[0] * len(given) // 4, given[0].shape[1]
    shapes = {"plain": lambda n: (4 * rows, n), "three": lambda n: (3, 4 * rows, n // 3)}
    return call(
        lambda *refs: settle_kernel(*refs, cuts=cuts, count=len(given)),
        "settle",
        tuple(struct(shapes[form](high - low), F32) for low, high, form in cuts),
        [VMEM] * len(given),
        (VMEM,) * len(cuts),
        [pltpu.VMEM((4 * rows, cols), F32)],
        3,
        7,
        tuple(given),
    )


def cut(full):
    rows, cols = full.shape
    return full[:, : cols // 2], full[:, cols // 2 :]


def gather_plain(shard):
    rows = lax.all_gather(shard, "fsdp", axis=0, tiled=True)
    return lax.all_gather(rows, "tp", axis=1, tiled=True)


def reduce_plain(own, sib):
    full = jnp.concatenate([own, sib], axis=1)
    part = lax.psum_scatter(full, "tp", scatter_dimension=1, tiled=True)
    part = lax.psum_scatter(part, "fsdp", scatter_dimension=0, tiled=True)
    return lax.psum(part, "ctx").astype(F32)


def body(
    layer_input,
    doc_ids,
    w_qkv,
    b_qv,
    w_out,
    b_out,
    ln1_gain,
    ln1_bias,
    w_up,
    b_up,
    w_down,
    b_down,
    ln2_gain,
    ln2_bias,
    out_grad,
):
    sizes = (lax.axis_size("fsdp"), lax.axis_size("ctx"), lax.axis_size("tp"))
    micro, seqs, local_len, width = layer_input.shape
    length = local_len * sizes[1]
    shard_rows, local_width = w_qkv.shape[1:]
    local_units = w_up.shape[1]
    heads = width // HEAD_DIM
    fast = sizes == (4, 4, 2)
    t = lax.axis_index("tp")
    c = lax.axis_index("ctx")

    def mine(value):
        return lax.dynamic_index_in_dim(value, t, 1, keepdims=False)

    def to_owners(chunks):
        return lax.all_to_all(chunks, "ctx", 0, 0, tiled=True)

    def spread(chunks):
        out = lax.all_to_all(chunks, ("ctx", "tp"), 0, 0, tiled=True)
        return out.reshape(micro, seqs, local_len, width)

    shards = (
        jnp.swapaxes(w_qkv, 0, 1).reshape(shard_rows, 3 * local_width),
        jnp.concatenate([w_out.T, w_up], axis=1),
        w_down.T,
    )
    ids = mine(doc_ids).astype(BF16)[:, None, :]
    ids = jnp.pad(ids, ((0, 0), (0, 7), (0, width - local_len)))
    rows_in = jnp.concatenate([mine(layer_input), ids], axis=1)
    cot_in = mine(out_grad)
    gathers = GATHER if fast else (None,) * 3
    packs = tuple(packing(order) for order in SCATTER) if fast else (None,) * 3

    def swap(value, group, step):
        order = tuple(zip(*GATHER[group])) + (CORE,)
        return exchange(value, order[step], sizes)

    def shed(value, group, step):
        order = (CORE,) + tuple(zip(*SCATTER[group]))
        return exchange(value, order[step], sizes)

    def joined(*parts):
        return jnp.concatenate(parts, axis=0)

    if fast:
        def seen(value):
            return [lax.dynamic_index_in_dim(value, c ^ i, 0, keepdims=True) for i in range(4)]

        part = shard_rows // 4
        h1 = lax.dynamic_slice_in_dim(w_qkv, c * part, part, 1)
        h1 = jnp.swapaxes(h1, 0, 1).reshape(part, 3 * local_width)
        h2, h3 = [lax.dynamic_slice_in_dim(s, c * part, part, 0) for s in shards[1:]]
        g1 = swap(h1, 0, 0)
        x0, x1, x2, x3 = seen(after(rows_in, h1))
        g1, x1, x2, x3, h2, h3, cot_in, b_up = phase(g1, x1, x2, x3, h2, h3, cot_in, b_up)
        h1 = joined(h1, g1)
        g1, g3, xk, xx, xd = phase(
            swap(h1, 0, 1), swap(h3, 2, 0), exchange(x1, CORE, sizes), exchange(x2, X, sizes), exchange(x3, FAR, sizes)
        )
        given = (x0, xk, joined(xx, xd))
        h1, h2, h3, cot_in, b_up = phase(joined(h1, g1), h2, joined(h3, g3), cot_in, b_up)
        g1, g2, g3 = swap(h1, 0, 2), swap(h2, 1, 0), swap(h3, 2, 1)
        c0, c1, c2, c3 = seen(cot_in)
        c_send = joined(c1, c3)
        table, small = tables(b_qv, b_up, (b_out, ln1_gain, ln1_bias, b_down, ln2_gain, ln2_bias))
        g1, g2, g3, c_send, small = phase(g1, g2, g3, c_send, small)
        h1, h2, h3 = phase(joined(h1, g1), joined(h2, g2), joined(h3, g3))
        g1, g2, ck, got, f1 = phase(
            swap(h1, 0, 3),
            swap(h2, 1, 1),
            exchange(c_send, CORE, sizes),
            exchange(small, Y, sizes),
            exchange(h1, CORE, sizes),
        )
        small = joined(small, got)
        g1, h2, h3 = phase(g1, joined(h2, g2), h3)
        k1, g2, g3 = exchange(g1, CORE, sizes), swap(h2, 1, 2), swap(h3, 2, 2)
        (wq,) = unpack(gathers[0], (h1, g1), (f1, k1), (3 * width,))
        proj, rows_b, mask = project(wq, given, small, fast)
        proj, g2, c2, ck = phase(proj, g2, c2, ck)
        h2 = joined(h2, g2)
        g2 = swap(h2, 1, 3)
        mixed0, probs0 = attend(after(proj, h2), mask, 0)
        mixed0, g3, h2 = phase(mixed0, g3, h2)
        h3 = joined(h3, g3)
        f2, g3, f3 = exchange(h2, CORE, sizes), swap(h3, 2, 3), exchange(h3, CORE, sizes)
        mixed1, probs1 = attend(after(proj, h3, mixed0), mask, 1)
        mixed1, g2, f2 = phase(mixed1, g2, f2)
        g2, c_send = phase(g2, joined(c2, ck[1:]))
        k2, cx = exchange(g2, CORE, sizes), exchange(c_send, X, sizes)
        wo, wu = unpack(gathers[1], (h2, g2), (f2, k2), (width, 2 * local_units))
    else:
        parts = (shards[0], w_out.T, w_up, w_down.T)
        pieces = [cut(gather_plain(s)) for s in parts]
        split = lambda pair: ((pair[0],), (pair[1],))
        (wq,) = unpack(None, *split(pieces[0]), (3 * width,))
        (wo,) = unpack(None, *split(pieces[1]), (width,))
        (wu,) = unpack(None, *split(pieces[2]), (2 * local_units,))
        (wd,) = unpack(None, *split(pieces[3]), (2 * local_units,))
        order = lambda value: (value[:1], value[1:3], value[2:])
        given, cot = order(to_owners(rows_in)), order(to_owners(cot_in))
        table, small = tables(b_qv, b_up, (b_out, ln1_gain, ln1_bias, b_down, ln2_gain, ln2_bias))
        small = joined(small, exchange(small, Y, sizes))
        proj, rows_b, mask = project(wq, given, small, fast)
        mixed0, probs0 = attend(proj, mask, 0)
        mixed1, probs1 = attend(proj, mask, 1)

    normed1, scale1, first_b, act, slope = middle(wo, wu, mixed0, mixed1, rows_b, table, small)
    if fast:
        act, g3, f3, cx = phase(act, g3, f3, cx)
        cot = (c0, ck, cx)
        (wd,) = unpack(gathers[2], (h3, g3), (f3, exchange(g3, CORE, sizes)), (2 * local_units,))
    chunks, gz, gzb, sums2, down_own, down_sib = turn(packs[2], wd, act, normed1, cot, table, local_len)

    rows = shard_rows // 4
    if fast:
        down_sib, chunks, gzb = phase(down_sib, chunks, gzb)
        got, core_out = shed(down_sib, 2, 0), exchange(chunks[2:], CORE, sizes)
    gh, sum_up = hidden_back(wd, gzb, slope)
    if fast:
        gh, got, core_out = phase(gh, got, core_out)
        down = [down_own, got]
        send, x_send, gh = phase(
            add_up(down, 8 * rows, 16 * rows), joined(chunks[1:2], core_out[1:2]), gh
        )
        got, x_out = shed(send, 2, 1), exchange(x_send, X, sizes)
    gz1, grad_mixed, sums1, up_own, up_sib = first_back(
        packs[1], wo, wu, gh, gz, normed1, scale1, table, first_b, mixed0, mixed1
    )
    if fast:
        grad_mixed, up_sib, got, x_out = phase(grad_mixed, up_sib, got, x_out)
        down = down + [got]
        send, y_send, grad_mixed = phase(
            add_up(down, 4 * rows, 8 * rows), joined(chunks[:1], core_out[:1], x_out), grad_mixed
        )
        got, got2, y_out = shed(send, 2, 2), shed(up_sib, 1, 0), exchange(y_send, Y, sizes)
    parts0 = attend_back(proj, probs0, grad_mixed, 0)
    if fast:
        head, got2, grad_mixed = phase(parts0[0], got2, grad_mixed)
        parts0 = (head,) + tuple(parts0[1:])
        up = [up_own, got2]
        send2, grad_mixed = phase(add_up(up, 8 * rows, 16 * rows), grad_mixed)
        got2 = shed(send2, 1, 1)
    parts1 = attend_back(proj, probs1, grad_mixed, 1)
    parts = list(parts0) + list(parts1)
    if fast:
        parts[3], got = phase(parts[3], got)
        down = down + [got]
        send = add_up(down, 2 * rows, 4 * rows)
        got = shed(send, 2, 3)
        parts[3], send = phase(parts[3], send)
    chunks2 = input_back(wq, gz1, parts, local_len, fast)
    if fast:
        chunks2, y_out = phase(chunks2, y_out)
    parts[0] = after(parts[0], chunks2)
    qkv_own, qkv_sib = last(packs[0], rows_b, sums1, sums2, sum_up, parts)
    if fast:
        got3, core_x = shed(qkv_sib, 0, 0), exchange(chunks2[2:], CORE, sizes)
        chunks2, qkv_own, got2 = phase(chunks2, qkv_own, got2)
        up = up + [got2]
        send2 = add_up(up, 4 * rows, 8 * rows, time=30)
        send2, got3 = phase(send2, got3)
        got2 = shed(send2, 1, 2)
        got3, core_x = phase(got3, core_x)
        qkv = [qkv_own, got3]
        sent3 = add_up(qkv, 8 * rows, 16 * rows, (0, 1))
        x_send = joined(chunks2[1:2], core_x[1:2])
        got3 = shed(sent3, 0, 1)
        got3, x_send = phase(got3, x_send)
        qkv = qkv + [got3]
        send3 = add_up(qkv, 4 * rows, 8 * rows, (3, 2), [sent3])
        got3 = shed(send3, 0, 2)
        send3, got, x_send = phase(send3, got, x_send)
        down = down + [got]
        send = add_up(down, rows, 2 * rows)
        got, x_x = shed(send, 2, 4), exchange(x_send, X, sizes)
        send, got2 = phase(send, got2)
        up = up + [got2]
        send2 = add_up(up, 2 * rows, 4 * rows)
        got2 = shed(send2, 1, 3)
        got3, send2 = phase(got3, send2)
        qkv = qkv + [got3]
        sent3 = add_up(qkv, 2 * rows, 4 * rows, (4, 3), [send3])
        got3 = shed(sent3, 0, 3)
        sent3, got, x_x = phase(sent3, got, x_x)
        pair1 = add_up(down + [got], 0, rows)
        y_send = joined(chunks2[:1], core_x[:1], x_x)
        got, y_x = exchange(pair1, X, sizes), exchange(y_send, Y, sizes)
        pair1, got2 = phase(pair1, got2)
        up = up + [got2]
        send2 = add_up(up, rows, 2 * rows)
        got2 = shed(send2, 1, 4)
        layer_output = deliver(chunks, core_out, x_out, after(y_out, send2))
        got3, layer_output = phase(got3, layer_output)
        qkv = qkv + [got3]
        send3 = add_up(qkv, rows, 2 * rows, (5, 4), [sent3])
        got3 = shed(send3, 0, 4)
        send3, got, got2 = phase(send3, got, got2)
        pair1 = joined(pair1, got)
        up = up + [got2]
        pair2 = add_up(up, 0, rows)
        got1, got2 = exchange(pair1, CORE, sizes), exchange(pair2, X, sizes)
        got3, pair1, pair2 = phase(got3, pair1, pair2)
        qkv = qkv + [got3]
        sent_last = got3
        piece = add_up(qkv, 0, rows)
        got3 = [exchange(piece, dims, sizes) for dims in (X, CORE, FAR)]
        vec = vectors(after(send3, piece), sent_last, local_width, local_units)
        piece, got1, bup = phase(piece, got1, vec[1])
        vec = (vec[0], bup) + tuple(vec[2:])
        (grad_down,) = settle((pair1, got1), ((0, local_units, "plain"),))
        grad_down, got2 = phase(grad_down, got2)
        pair2 = joined(pair2, got2)
        got2 = exchange(pair2, CORE, sizes)
        pair2, y_x = phase(pair2, y_x)
        grad_x = deliver(chunks2, core_x, x_x, y_x)
        grad_x, *got3 = phase(grad_x, *got3)
        (grad_qkv,) = settle([piece] + got3, ((0, 3 * local_width, "three"),))
        grad_wout, grad_up = settle(
            (pair2, after(got2, grad_qkv)),
            ((0, local_width, "plain"), (local_width, local_width + local_units, "plain")),
        )
        layer_output = layer_output.reshape(micro, seqs, local_len, width)
        grad_x = grad_x.reshape(micro, seqs, local_len, width)
    else:
        layer_output = spread(jnp.repeat(chunks, 2, axis=0))
        grad_x = spread(jnp.repeat(chunks2, 2, axis=0))
        vec = lax.psum(qkv_own[width:].astype(F32), AXES)
        vec = vectors(vec, None, local_width, local_units)
        grad_down = reduce_plain(down_own, down_sib)
        both = reduce_plain(up_own, up_sib)
        grad_wout, grad_up = both[:, :local_width], both[:, local_width:]
        grad_qkv = reduce_plain(qkv_own[:width], qkv_sib[:width])
        grad_qkv = jnp.swapaxes(grad_qkv.reshape(shard_rows, 3, local_width), 0, 1)

    out_bqv, out_bup, g1, s1, bout, g2, s2, bdown = vec
    return (
        layer_output,
        grad_x,
        grad_qkv,
        out_bqv,
        grad_wout.T,
        bout,
        g1,
        s1,
        grad_up,
        out_bup,
        grad_down.T,
        bdown,
        g2,
        s2,
    )


def solution(mesh):
    return jax.shard_map(
        body,
        mesh=mesh,
        in_specs=(
            P(None, "fsdp", "ctx", None),
            P(None, "fsdp", "ctx"),
            P(None, "fsdp", "tp"),
            P(None, "tp"),
            P("tp", "fsdp"),
            P(),
            P(),
            P(),
            P("fsdp", "tp"),
            P("tp"),
            P("tp", "fsdp"),
            P(),
            P(),
            P(),
            P(None, "fsdp", "ctx", None),
        ),
        out_specs=(
            P(None, "fsdp", "ctx", None),
            P(None, "fsdp", "ctx", None),
            P(None, "fsdp", "tp"),
            P(None, "tp"),
            P("tp", "fsdp"),
            P(),
            P(),
            P(),
            P("fsdp", "tp"),
            P("tp"),
            P("tp", "fsdp"),
            P(),
            P(),
            P(),
        ),
        check_vma=False,
    )
```

```python
import jax
import jax.numpy as jnp
from jax import lax
from jax.experimental import pallas as pl
from jax.experimental.pallas import tpu as pltpu
from jax.sharding import PartitionSpec as P

HEAD_DIM = 64
AXES = ("fsdp", "ctx", "tp")
F32 = jnp.float32
BF16 = jnp.bfloat16
NEG = -1e30
NT = (((1,), (1,)), ((), ()))
VMEM = pl.BlockSpec(memory_space=pltpu.VMEM)
SMEM = pl.BlockSpec(memory_space=pltpu.SMEM)
ANY = pl.BlockSpec(memory_space=pl.ANY)


def partner(dim, z, c, t):
    if dim == "core":
        return z, c ^ 1, t
    if dim == "x":
        return z, c ^ 2, t
    if dim == "x+core":
        return z, c ^ 3, t
    if dim == "y":
        return z, c, t ^ 1
    return z ^ int(dim[1:]), c, t


def exchange(value, dims, sizes):
    nz, nc, nt = sizes
    pairs = []
    for z in range(nz):
        for c in range(nc):
            for t in range(nt):
                tz, tc, tt = partner(dims[c & 1], z, c, t)
                pairs.append(((z * nc + c) * nt + t, (tz * nc + tc) * nt + tt))
    return lax.ppermute(value, AXES, pairs)


GATHER = (
    (("z2", "z1", "y", "x"), ("z1", "z2", "x", "y")),
    (("z2", "z1", "y", "x"), ("z1", "z2", "x", "y")),
    (("x", "z2", "z1", "y"), ("y", "x", "z2", "z1")),
)
SCATTER = (
    (("x", "y", "z1", "z2"), ("y", "x", "z2", "z1")),
    (("x", "y", "z1", "z2"), ("z1", "z2", "y", "x")),
    (("y", "x", "z1", "z2"), ("z1", "z2", "x", "y")),
)
CORE = ("core", "core")
X = ("x", "x")
FAR = ("x+core", "x+core")
Y = ("y", "y")


def piece_place(order, core, here, index):
    z, x, t = here
    for bit, dim in enumerate(order):
        flip = (index >> bit) & 1
        if dim == "x":
            x = x ^ flip
        elif dim == "y":
            t = t ^ flip
        else:
            z = z ^ (flip * int(dim[1:]))
    return z * 4 + x * 2 + core, t


def places(orders):
    if orders is None:
        return [(i, half) for half in range(2) for i in range(16)]
    c = lax.axis_index("ctx")
    here = (lax.axis_index("fsdp"), c >> 1, lax.axis_index("tp"))
    spots = []
    for core in (c & 1, 1 - (c & 1)):
        for i in range(16):
            r0, t0 = piece_place(orders[0], core, here, i)
            r1, t1 = piece_place(orders[1], core, here, i)
            spots.append((jnp.where(core == 0, r0, r1), jnp.where(core == 0, t0, t1)))
    return spots


def packing(orders):
    return tuple(order[::-1] for order in orders)


def after(value, *first):
    return lax.optimization_barrier((value, first))[0]


def phase(*values):
    return lax.optimization_barrier(values)


def at_rows(place, count, unit=0):
    start = place * count
    return pl.ds(start if isinstance(start, int) else pl.multiple_of(start, unit or count), count)


def piece_copies(spots, near, far, sem, whole, low, cols, base=0):
    rows = whole.shape[0] // 16
    copies = []
    each = 16 // len(near)
    for half, refs in ((0, near), (1, far)):
        for i in range(16):
            row, col = spots[half * 16 + i]
            copy = pltpu.make_async_copy(
                refs[i // each].at[pl.ds(i % each * rows, rows), pl.ds(low, cols)],
                whole.at[at_rows(row, rows), at_rows(col, cols, 128)],
                sem.at[base + half * 16 + i],
            )
            copy.start()
            copies.append(copy)
    return copies


def pack(spots, own_ref, sib_ref, whole, low, cols):
    rows = whole.shape[0] // 16
    for half, ref in ((0, own_ref), (1, sib_ref)):
        for i in range(16):
            row, col = spots[half * 16 + i]
            ref[i * rows : (i + 1) * rows, low : low + cols] = whole[at_rows(row, rows), at_rows(col, cols, 128)]


def finish(copies):
    for copy in copies:
        copy.wait()


def tiles(count, step):
    def run(one):
        lax.fori_loop(0, count // step, lambda i, carry: (one(pl.multiple_of(i * step, step)), carry)[1], 0)

    return run


def row_mean(value):
    return jnp.mean(value, axis=-1, keepdims=True)


def struct(shape, dtype):
    return jax.ShapeDtypeStruct(shape, dtype)


def call(kernel, name, outs, specs, out_specs, scratch, time, room, args):
    return pl.pallas_call(
        kernel,
        name=name,
        out_shape=outs,
        in_specs=specs,
        out_specs=out_specs,
        scratch_shapes=scratch,
        compiler_params=pltpu.CompilerParams(vmem_limit_bytes=room << 20),
        cost_estimate=pl.CostEstimate(flops=time * 10**9, transcendentals=0, bytes_accessed=10**6),
    )(*args)


B_OUT, GAIN1, SHIFT1, B_DOWN, GAIN2, SHIFT2 = range(6)


def unpack_kernel(*refs, orders, count):
    near, far, outs, sem = refs[:count], refs[count : 2 * count], refs[2 * count : -1], refs[-1]
    copies = []
    spots = places(orders)
    low = 0
    for i, out in enumerate(outs):
        cols = out.shape[1] // 2
        copies += piece_copies(spots, near, far, sem, out, low, cols, 32 * i)
        low += cols
    finish(copies)


def unpack(orders, near, far, widths):
    count = len(near)
    rows = near[0].shape[0] * count
    return call(
        lambda *refs: unpack_kernel(*refs, orders=orders, count=count),
        "unpack",
        tuple(struct((rows, width), BF16) for width in widths),
        [ANY] * (2 * count),
        (VMEM,) * len(widths),
        [pltpu.SemaphoreType.DMA((32 * len(widths),))],
        5,
        2,
        tuple(near) + tuple(far),
    )


def sources(refs, fast):
    c = lax.axis_index("ctx") if fast else 0
    own, core, x = refs
    return [(c ^ 0, own, 0), (c ^ 1, core, 0), (c ^ 2, x, 0), (c ^ 3, x, 1)]


def tables_kernel(qv_ref, up_ref, *refs):
    rows, (table_ref, small_ref) = refs[:-2], refs[-2:]
    table_ref[...] = jnp.zeros_like(table_ref)
    for i, ref in enumerate(rows):
        table_ref[i : i + 1, :] = ref[...][None]
    width = qv_ref.shape[1]
    small_ref[:, :width] = qv_ref[0:1, :]
    small_ref[:, width : 2 * width] = qv_ref[1:2, :]
    small_ref[:, 2 * width :] = up_ref[...][None]


def tables(b_qv, b_up, rows):
    return call(
        tables_kernel,
        "tables",
        (struct((8, rows[0].shape[0]), F32), struct((1, b_qv.size + b_up.size), F32)),
        [VMEM] * (2 + len(rows)),
        (VMEM, VMEM),
        [],
        1,
        3,
        (b_qv, b_up) + tuple(rows),
    )


def project_kernel(weight_ref, own_ref, core_ref, far_ref, small_ref, proj_ref, x_ref, mask_ref, ids, *, fast):
    block = own_ref.shape[1] - 8
    count = 4
    for spot, ref, i in sources((own_ref, core_ref, far_ref), fast):
        x_ref[pl.ds(pl.multiple_of(spot * block, block), block), :] = ref[i, 0:block, :]
        ids[pl.ds(spot, 1), :] = ref[i, block:, 0:block].astype(F32)[0:1]
    for kb in range(count):
        column = jnp.broadcast_to(ids[kb : kb + 1], (block, block)).T
        for qb in range(count):
            mask_ref[kb * block : (kb + 1) * block, qb * block : (qb + 1) * block] = jnp.where(
                column == jnp.broadcast_to(ids[qb : qb + 1], (block, block)), 0.0, NEG
            )
    width = proj_ref.shape[1] // 6
    for y in range(2):
        row = pl.ds(lax.axis_index("tp") ^ y, 1)
        for which in range(3):
            at = (y * 3 + which) * width
            value = jnp.dot(x_ref[...], weight_ref[:, at : at + width], preferred_element_type=F32)
            if which != 1:
                low = 0 if which == 0 else width
                value = value + small_ref[row, low : low + width]
            proj_ref[:, at : at + width] = value.astype(BF16)


def project(weight, given, small, fast):
    width, wide = weight.shape
    block = given[0].shape[1] - 8
    length = 4 * block
    return call(
        lambda *refs: project_kernel(*refs, fast=fast),
        "project",
        (
            struct((length, wide), BF16),
            struct((length, width), BF16),
            struct((length, length), F32),
        ),
        [VMEM] * 5,
        (VMEM,) * 3,
        [pltpu.VMEM((8, block), F32)],
        5,
        3,
        (weight,) + tuple(given) + (small,),
    )


def attend_kernel(proj_ref, mask_ref, o_ref, p_ref, *, y):
    length = proj_ref.shape[0]
    pairs = o_ref.shape[1] // 128
    lane = lax.broadcasted_iota(jnp.int32, (1, 128), 1)

    def pair(g, carry):
        take = lambda which: proj_ref[:, pl.ds(pl.multiple_of(((y * 3 + which) * pairs + g) * 128, 128), 128)]
        query = take(0) * jnp.asarray(0.125, BF16)
        keys = take(1)
        values_t = take(2).T
        outs = []
        for head in range(2):
            here = (lane >= 64 * head) & (lane < 64 * head + 64)
            only = jnp.where(here, keys, jnp.zeros_like(keys))
            row = []
            for at in range(0, length, 256):
                scores = lax.dot_general(only, query[at : at + 256], NT, preferred_element_type=F32)
                scores = scores + mask_ref[:, at : at + 256]
                top = jnp.max(scores, axis=0, keepdims=True)
                raised = jnp.exp(scores - top)
                total = jnp.sum(raised, axis=0, keepdims=True)
                probs = (raised * (1.0 / total)).astype(BF16)
                p_ref[2 * g + head, :, at : at + 256] = probs
                row.append(
                    jnp.dot(values_t[64 * head : 64 * head + 64], probs, preferred_element_type=F32)
                )
            outs.append(jnp.concatenate(row, axis=1))
        both = jnp.concatenate(outs, axis=0).astype(BF16)
        o_ref[:, pl.ds(pl.multiple_of(g * 128, 128), 128)] = both.T
        return carry

    lax.fori_loop(0, pairs, pair, 0)


def attend(proj, mask, y):
    length, wide = proj.shape
    half = wide // 6
    return call(
        lambda *refs: attend_kernel(*refs, y=y),
        "attend",
        (struct((length, half), BF16), struct((half // HEAD_DIM, length, length), BF16)),
        [VMEM, VMEM],
        (VMEM, VMEM),
        [],
        12,
        3,
        (proj, mask),
    )


def middle_kernel(
    w_out, w_up, mixed0_ref, mixed1_ref, x_ref, table_ref, small_ref,
    normed_ref, scale_ref, first_ref, act_ref, slope_ref,
):
    length, units = act_ref.shape
    narrow, half = w_out.shape[1] // 2, units // 2
    normed_ref[...] = lax.dot_general(
        mixed0_ref[...], w_out[:, :narrow], NT, preferred_element_type=F32
    ) + lax.dot_general(mixed1_ref[...], w_out[:, narrow:], NT, preferred_element_type=F32)

    @tiles(length, 64)
    def _(at):
        here = pl.ds(at, 64)
        value = x_ref[here, :].astype(F32) + normed_ref[here, :] + table_ref[B_OUT : B_OUT + 1, :]
        centred = value - row_mean(value)
        scale = lax.rsqrt(row_mean(centred * centred) + 1e-12)
        unit = centred * scale
        normed_ref[here, :] = unit
        scale_ref[here, :] = scale
        first_ref[here, :] = (
            unit * table_ref[GAIN1 : GAIN1 + 1, :] + table_ref[SHIFT1 : SHIFT1 + 1, :]
        ).astype(BF16)

    for y in range(2):
        row = pl.ds(lax.axis_index("tp") ^ y, 1)

        @tiles(half, 256)
        def _(at):
            here = pl.ds(pl.multiple_of(y * half + at, 256), 256)
            bias = small_ref[row, pl.ds(pl.multiple_of(2 * narrow + at, 256), 256)]
            hidden = jnp.dot(first_ref[...], w_up[:, here], preferred_element_type=F32) + bias
            phi = 0.5 + 0.5 * lax.erf(hidden * 0.7071067811865476)
            act_ref[:, here] = (hidden * phi).astype(BF16)
            bell = jnp.exp(-0.5 * hidden * hidden) * 0.3989422804014327
            slope_ref[:, here] = (phi + hidden * bell).astype(BF16)


def middle(w_out, w_up, mixed0, mixed1, x, table, small):
    length, width = x.shape
    units = w_up.shape[1]
    return call(
        middle_kernel,
        "middle",
        (
            struct((length, width), F32),
            struct((length, 1), F32),
            struct((length, width), BF16),
            struct((length, units), BF16),
            struct((length, units), BF16),
        ),
        [VMEM] * 7,
        (VMEM,) * 5,
        [],
        12,
        3,
        (w_out, w_up, mixed0, mixed1, x, table, small),
    )


def turn_kernel(
    weight_ref, act_ref, normed_ref, own_ref, core_ref, far_ref, table_ref,
    chunks_ref, gz_ref, gzb_ref, sums_ref, down_own, down_sib, full, cot_ref, *, orders,
):
    length = act_ref.shape[0]
    block = chunks_ref.shape[1]
    for spot, ref, i in sources((own_ref, core_ref, far_ref), orders is not None):
        cot_ref[pl.ds(pl.multiple_of(spot * block, block), block), :] = ref[i]
    gz_ref[...] = lax.dot_general(act_ref[...], weight_ref[...], NT, preferred_element_type=F32)
    sums_ref[...] = jnp.zeros_like(sums_ref)
    row = lambda which: table_ref[which : which + 1, :]

    @tiles(length, 64)
    def _(at):
        here = pl.ds(at, 64)
        value = normed_ref[here, :] * row(GAIN1) + row(SHIFT1) + gz_ref[here, :] + row(B_DOWN)
        centred = value - row_mean(value)
        scale = lax.rsqrt(row_mean(centred * centred) + 1e-12)
        unit = centred * scale
        result = (unit * row(GAIN2) + row(SHIFT2)).astype(BF16)
        chunk = lax.div(at, block)
        if orders is not None:
            c = lax.axis_index("ctx") ^ chunk
            chunk = (c & 1) * 2 + (c >> 1)
        chunks_ref[chunk, pl.ds(pl.multiple_of(lax.rem(at, block), 64), 64), :] = result
        coming = cot_ref[here, :].astype(F32)
        raised = coming * row(GAIN2)
        back = scale * (raised - row_mean(raised) - unit * row_mean(raised * unit))
        gz_ref[here, :] = back
        gzb_ref[here, :] = back.astype(BF16)
        sums_ref[0:1, :] += jnp.sum(coming * unit, axis=0, keepdims=True)
        sums_ref[1:2, :] += jnp.sum(coming, axis=0, keepdims=True)
        sums_ref[2:3, :] += jnp.sum(back, axis=0, keepdims=True)

    back_t = gzb_ref[...].T

    @tiles(full.shape[1], 1024)
    def _(at):
        here = pl.ds(at, 1024)
        full[:, here] = jnp.dot(back_t, act_ref[:, here], preferred_element_type=F32).astype(BF16)

    pack(places(orders), down_own, down_sib, full, 0, down_own.shape[1])


def turn(orders, weight, act, normed, cot, table, chunk):
    length, units = act.shape
    width = normed.shape[1]
    piece = struct((width, units // 2), BF16)
    return call(
        lambda *refs: turn_kernel(*refs, orders=orders),
        "turn",
        (
            struct((length // chunk, chunk, width), BF16),
            struct((length, width), F32),
            struct((length, width), BF16),
            struct((8, width), F32),
            piece,
            piece,
        ),
        [VMEM] * 7,
        (VMEM,) * 6,
        [pltpu.VMEM((width, units), BF16), pltpu.VMEM((length, width), BF16)],
        14,
        10,
        (weight, act, normed) + tuple(cot) + (table,),
    )


def hidden_back_kernel(weight_ref, gzb_ref, slope_ref, gh_ref, sum_ref):
    @tiles(gh_ref.shape[1], 512)
    def _(at):
        here = pl.ds(at, 512)
        back = jnp.dot(gzb_ref[...], weight_ref[:, here], preferred_element_type=F32)
        back = (back * slope_ref[:, here].astype(F32)).astype(BF16)
        gh_ref[:, here] = back
        sum_ref[:, here] = jnp.sum(back.astype(F32), axis=0, keepdims=True)


def hidden_back(weight, gzb, slope):
    length, units = slope.shape
    return call(
        hidden_back_kernel,
        "hidden_back",
        (struct((length, units), BF16), struct((1, units), F32)),
        [VMEM] * 3,
        (VMEM, VMEM),
        [],
        12,
        3,
        (weight, gzb, slope),
    )


def first_back_kernel(
    w_out, w_up, gh_ref, gz_ref, normed_ref, scale_ref, table_ref, first_ref, mixed0_ref, mixed1_ref,
    gz1_ref, gm_ref, sums_ref, pieces_own, pieces_sib, branch, d_out, d_up, *, orders,
):
    narrow = w_out.shape[1] // 2
    half = w_up.shape[1] // 2
    length = gh_ref.shape[0]
    first_t = first_ref[...].T
    spots = places(orders)

    @tiles(d_up.shape[1], 1024)
    def _(at):
        here = pl.ds(at, 1024)
        d_up[:, here] = jnp.dot(first_t, gh_ref[:, here], preferred_element_type=F32).astype(BF16)

    pack(spots, pieces_own, pieces_sib, d_up, narrow, half)
    gz1_ref[...] = lax.dot_general(gh_ref[...], w_up[...], NT, preferred_element_type=F32)
    sums_ref[...] = jnp.zeros_like(sums_ref)

    @tiles(length, 64)
    def _(at):
        here = pl.ds(at, 64)
        coming = gz_ref[here, :] + gz1_ref[here, :]
        unit = normed_ref[here, :]
        raised = coming * table_ref[GAIN1 : GAIN1 + 1, :]
        back = scale_ref[here, :] * (raised - row_mean(raised) - unit * row_mean(raised * unit))
        gz1_ref[here, :] = back
        branch[here, :] = back.astype(BF16)
        sums_ref[0:1, :] += jnp.sum(coming * unit, axis=0, keepdims=True)
        sums_ref[1:2, :] += jnp.sum(coming, axis=0, keepdims=True)
        sums_ref[2:3, :] += jnp.sum(back, axis=0, keepdims=True)

    branch_t = branch[...].T
    d_out[:, :narrow] = jnp.dot(branch_t, mixed0_ref[...], preferred_element_type=F32).astype(BF16)
    d_out[:, narrow:] = jnp.dot(branch_t, mixed1_ref[...], preferred_element_type=F32).astype(BF16)
    pack(spots, pieces_own, pieces_sib, d_out, 0, narrow)
    gm_ref[...] = jnp.dot(branch[...], w_out[...], preferred_element_type=F32).astype(BF16)


def first_back(orders, w_out, w_up, gh, gz, normed, scale, table, first_b, mixed0, mixed1):
    length, units = gh.shape
    width = gz.shape[1]
    piece = struct((width, (units + width) // 2), BF16)
    return call(
        lambda *refs: first_back_kernel(*refs, orders=orders),
        "first_back",
        (
            struct((length, width), F32),
            struct((length, width), BF16),
            struct((8, width), F32),
            piece,
            piece,
        ),
        [VMEM] * 10,
        (VMEM,) * 5,
        [
            pltpu.VMEM((length, width), BF16),
            pltpu.VMEM((width, width), BF16),
            pltpu.VMEM((width, units), BF16),
        ],
        20,
        12,
        (w_out, w_up, gh, gz, normed, scale, table, first_b, mixed0, mixed1),
    )


def attend_back_kernel(proj_ref, p_ref, gm_ref, dq_ref, dk_ref, dv_ref, dst, dqt, *, y):
    length = proj_ref.shape[0]
    pairs = dq_ref.shape[1] // 128
    lane = lax.broadcasted_iota(jnp.int32, (1, 128), 1)
    low = lane < 64

    def pair(g, carry):
        take = lambda which: proj_ref[:, pl.ds(pl.multiple_of(((y * 3 + which) * pairs + g) * 128, 128), 128)]
        query, keys, values = take(0), take(1), take(2)
        grad = gm_ref[:, pl.ds(pl.multiple_of((y * pairs + g) * 128, 128), 128)]
        keys_t = keys.T
        dks, dvs = [], []
        for head in range(2):
            here = low if head == 0 else jnp.logical_not(low)
            only = jnp.where(here, values, jnp.zeros_like(values))
            for at in range(0, length, 256):
                cols = slice(at, at + 256)
                gp = lax.dot_general(only, grad[cols], NT, preferred_element_type=F32)
                probs = p_ref[2 * g + head, :, cols].astype(F32)
                weighted = jnp.sum(probs * gp, axis=0, keepdims=True)
                dst[:, cols] = (probs * (gp - weighted)).astype(BF16)
            dqt[64 * head : 64 * head + 64, :] = (
                jnp.dot(keys_t[64 * head : 64 * head + 64], dst[...], preferred_element_type=F32) * 0.125
            ).astype(BF16)
            dks.append(jnp.dot(dst[...], query, preferred_element_type=F32))
            dvs.append(jnp.dot(p_ref[2 * g + head], grad, preferred_element_type=F32))
        cols = pl.ds(pl.multiple_of(g * 128, 128), 128)
        dq_ref[:, cols] = dqt[...].T
        dk_ref[:, cols] = (jnp.where(low, dks[0], dks[1]) * 0.125).astype(BF16)
        dv_ref[:, cols] = jnp.where(low, dvs[0], dvs[1]).astype(BF16)
        return carry

    lax.fori_loop(0, pairs, pair, 0)


def attend_back(proj, probs, grad_mixed, y):
    length, wide = proj.shape
    shape = struct((length, wide // 6), BF16)
    return call(
        lambda *refs: attend_back_kernel(*refs, y=y),
        "attend_back",
        (shape, shape, shape),
        [VMEM] * 3,
        (VMEM,) * 3,
        [pltpu.VMEM((length, length), BF16), pltpu.VMEM((128, length), BF16)],
        1,
        4,
        (proj, probs, grad_mixed),
    )


def last_kernel(x_ref, sums1_ref, sums2_ref, sum_up_ref, *refs, orders):
    parts, (pieces_own, pieces_sib, whole, vec) = refs[:6], refs[6:]
    half = parts[0].shape[1]
    rows = whole.shape[0]
    x_t = x_ref[...].T
    sums = [[], []]
    for y in range(2):
        for which in range(3):
            at = (y * 3 + which) * half
            value = parts[y * 3 + which][...]
            whole[:, at : at + half] = jnp.dot(x_t, value, preferred_element_type=F32).astype(BF16)
            if which != 1:
                sums[which // 2].append(jnp.sum(value.astype(F32), axis=0, keepdims=True))
    pack(places(orders), pieces_own, pieces_sib, whole, 0, 3 * half)
    vectors = sums[0] + sums[1] + [ref[i : i + 1, :] for ref in (sums1_ref, sums2_ref) for i in range(3)]
    at = 0
    across = vec.shape[1] // 128
    wide = []
    for vector in vectors + [sum_up_ref[...]]:
        for low in range(0, vector.shape[1], 128):
            wide.append(vector[:, low : low + 128])
    for row in range(8):
        vec[row : row + 1, :] = jnp.concatenate(wide[row * across : (row + 1) * across], axis=1)
    pieces_own[rows:, :] = vec[...].astype(BF16)
    pieces_sib[rows:, :] = vec[...].astype(BF16)


def last(orders, x, sums1, sums2, sum_up, parts):
    length, width = x.shape
    piece = struct((width + 8, 3 * width // 2), BF16)
    return call(
        lambda *refs: last_kernel(*refs, orders=orders),
        "last",
        (piece, piece),
        [VMEM] * 10,
        (VMEM, VMEM),
        [
            pltpu.VMEM((width, 3 * width), BF16),
            pltpu.VMEM((8, 3 * width // 2), F32),
        ],
        10,
        7,
        (x, sums1, sums2, sum_up) + tuple(parts),
    )


def vectors_kernel(one_ref, two_ref, qv_ref, up_ref, *refs):
    t = lax.axis_index("tp")
    rows, cols = one_ref.shape
    across = cols // 128
    value = one_ref[rows - 8 :, :].astype(F32)
    if two_ref is not None:
        value = value + two_ref[rows - 8 :, :].astype(F32)

    def block(at):
        row, low = at // across, at % across * 128
        return value[row : row + 1, low : low + 128]

    def take(out, row, first, other, count):
        for i in range(count):
            one = block(first + i)
            if other != first:
                one = jnp.where(t == 0, one, block(other + i))
            if row is None:
                out[i * 128 : (i + 1) * 128] = one[0]
            else:
                out[row : row + 1, i * 128 : (i + 1) * 128] = one

    narrow, wide = qv_ref.shape[1] // 128, up_ref.shape[0] // 128
    for which in range(2):
        take(qv_ref, which, 2 * which * narrow, (2 * which + 1) * narrow, narrow)
    for i, ref in enumerate(refs):
        take(ref, None, (4 + 2 * i) * narrow, (4 + 2 * i) * narrow, 2 * narrow)
    base = (4 + 2 * len(refs)) * narrow
    take(up_ref, None, base, base + wide, wide)


def vectors(one, two, local_width, local_units):
    shapes = [(2, local_width), (local_units,)] + [(2 * local_width,)] * 6
    given = (one,) if two is None else (one, two)

    def kernel(*refs):
        if two is None:
            refs = (refs[0], None) + refs[1:]
        vectors_kernel(*refs)

    return call(
        kernel,
        "vectors",
        tuple(struct(shape, F32) for shape in shapes),
        [VMEM] * len(given),
        (VMEM,) * 8,
        [],
        1,
        4,
        given,
    )


def add_kernel(*refs, low, high, vec, count):
    terms, out = refs[:-1], refs[-1]
    total = terms[0][low:high, :].astype(F32)
    for term in terms[1:count]:
        total = total + term[low:high, :].astype(F32)
    out[: high - low, :] = total.astype(BF16)
    if vec:
        total = 0.0
        for i in vec:
            total = total + terms[i][terms[i].shape[0] - 8 :, :].astype(F32)
        out[high - low :, :] = total.astype(BF16)


def add_up(terms, low, high, vec=(), lone=(), time=1):
    count, terms = len(terms), list(terms) + list(lone)
    cols = terms[0].shape[1]
    return call(
        lambda *refs: add_kernel(*refs, low=low, high=high, vec=vec, count=count),
        "add",
        struct((high - low + (8 if vec else 0), cols), BF16),
        [VMEM] * len(terms),
        VMEM,
        [],
        time,
        4,
        tuple(terms),
    )


def deliver_kernel(own_ref, core_ref, x_ref, y_ref, out_ref):
    c, t = lax.axis_index("ctx"), lax.axis_index("tp")
    sources = [(own_ref, 0), (core_ref, 0), (x_ref, 0), (x_ref, 1)] + [(y_ref, i) for i in range(4)]
    for i, (ref, at) in enumerate(sources):
        ctx = c ^ ((i & 1) + (i & 2))
        out_ref[ctx * 2 + (t ^ (i >> 2))] = ref[at]


def deliver(own, core, x, y):
    return call(
        deliver_kernel,
        "deliver",
        struct((2 * own.shape[0],) + own.shape[1:], BF16),
        [VMEM] * 4,
        VMEM,
        [],
        3,
        7,
        (own, core, x, y),
    )


def input_back_kernel(weight_ref, gz1_ref, *refs, fast):
    parts, chunks_ref = refs[:6], refs[6]
    half = parts[0].shape[1]
    total = gz1_ref[...]
    for i, part in enumerate(parts):
        total = total + lax.dot_general(
            part[...], weight_ref[:, i * half : (i + 1) * half], NT, preferred_element_type=F32
        )
    total = total.astype(BF16)
    count, block = chunks_ref.shape[:2]
    for i in range(count):
        spot = i
        if fast:
            c = lax.axis_index("ctx") ^ i
            spot = (c & 1) * 2 + (c >> 1)
        chunks_ref[spot] = total[i * block : (i + 1) * block]


def input_back(weight, gz1, parts, chunk, fast):
    length, width = gz1.shape
    return call(
        lambda *refs: input_back_kernel(*refs, fast=fast),
        "input_back",
        struct((length // chunk, chunk, width), BF16),
        [VMEM] * 8,
        VMEM,
        [],
        2,
        3,
        (weight, gz1) + tuple(parts),
    )


def settle_kernel(*refs, cuts, count):
    given, outs, four = refs[:count], refs[count:-1], refs[-1]
    rows = four.shape[0] // 4
    for i in range(4):
        ref = given[i * count // 4]
        owner = lax.axis_index("ctx") ^ ((i & 1) * 2 + (i >> 1))
        low = i % (4 // count) * rows
        four[pl.ds(pl.multiple_of(owner * rows, 16), rows), :] = ref[low : low + rows, :].astype(F32)
    for out, (low, high, form) in zip(outs, cuts):
        if form == "plain":
            out[...] = four[:, low:high]
        else:
            step = (high - low) // 3
            for j in range(3):
                out[j] = four[:, low + j * step : low + (j + 1) * step]


def settle(given, cuts):
    rows, cols = given[0].shape[0] * len(given) // 4, given[0].shape[1]
    shapes = {"plain": lambda n: (4 * rows, n), "three": lambda n: (3, 4 * rows, n // 3)}
    return call(
        lambda *refs: settle_kernel(*refs, cuts=cuts, count=len(given)),
        "settle",
        tuple(struct(shapes[form](high - low), F32) for low, high, form in cuts),
        [VMEM] * len(given),
        (VMEM,) * len(cuts),
        [pltpu.VMEM((4 * rows, cols), F32)],
        3,
        7,
        tuple(given),
    )


def cut(full):
    rows, cols = full.shape
    return full[:, : cols // 2], full[:, cols // 2 :]


def gather_plain(shard):
    rows = lax.all_gather(shard, "fsdp", axis=0, tiled=True)
    return lax.all_gather(rows, "tp", axis=1, tiled=True)


def reduce_plain(own, sib):
    full = jnp.concatenate([own, sib], axis=1)
    part = lax.psum_scatter(full, "tp", scatter_dimension=1, tiled=True)
    part = lax.psum_scatter(part, "fsdp", scatter_dimension=0, tiled=True)
    return lax.psum(part, "ctx").astype(F32)


def body(
    layer_input,
    doc_ids,
    w_qkv,
    b_qv,
    w_out,
    b_out,
    ln1_gain,
    ln1_bias,
    w_up,
    b_up,
    w_down,
    b_down,
    ln2_gain,
    ln2_bias,
    out_grad,
):
    sizes = (lax.axis_size("fsdp"), lax.axis_size("ctx"), lax.axis_size("tp"))
    micro, seqs, local_len, width = layer_input.shape
    length = local_len * sizes[1]
    shard_rows, local_width = w_qkv.shape[1:]
    local_units = w_up.shape[1]
    heads = width // HEAD_DIM
    fast = sizes == (4, 4, 2)
    t = lax.axis_index("tp")
    c = lax.axis_index("ctx")

    def mine(value):
        return lax.dynamic_index_in_dim(value, t, 1, keepdims=False)

    def to_owners(chunks):
        return lax.all_to_all(chunks, "ctx", 0, 0, tiled=True)

    def spread(chunks):
        out = lax.all_to_all(chunks, ("ctx", "tp"), 0, 0, tiled=True)
        return out.reshape(micro, seqs, local_len, width)

    shards = (
        jnp.swapaxes(w_qkv, 0, 1).reshape(shard_rows, 3 * local_width),
        jnp.concatenate([w_out.T, w_up], axis=1),
        w_down.T,
    )
    ids = mine(doc_ids).astype(BF16)[:, None, :]
    ids = jnp.pad(ids, ((0, 0), (0, 7), (0, width - local_len)))
    rows_in = jnp.concatenate([mine(layer_input), ids], axis=1)
    cot_in = mine(out_grad)
    gathers = GATHER if fast else (None,) * 3
    packs = tuple(packing(order) for order in SCATTER) if fast else (None,) * 3

    def swap(value, group, step):
        order = tuple(zip(*GATHER[group])) + (CORE,)
        return exchange(value, order[step], sizes)

    def shed(value, group, step):
        order = (CORE,) + tuple(zip(*SCATTER[group]))
        return exchange(value, order[step], sizes)

    def joined(*parts):
        return jnp.concatenate(parts, axis=0)

    if fast:
        def seen(value):
            return [lax.dynamic_index_in_dim(value, c ^ i, 0, keepdims=True) for i in range(4)]

        part = shard_rows // 4
        h1 = lax.dynamic_slice_in_dim(w_qkv, c * part, part, 1)
        h1 = jnp.swapaxes(h1, 0, 1).reshape(part, 3 * local_width)
        h2, h3 = [lax.dynamic_slice_in_dim(s, c * part, part, 0) for s in shards[1:]]
        g1 = swap(h1, 0, 0)
        h3 = after(h3, h1)
        x0, x1, x2, x3 = seen(after(rows_in, h1))
        g1, g3, x1, x2, x3, h2, cot_in, b_up = phase(g1, swap(h3, 2, 0), x1, x2, x3, h2, cot_in, b_up)
        h1, h3 = joined(h1, g1), joined(h3, g3)
        g1, g3, xk, xx, xd = phase(
            swap(h1, 0, 1), swap(h3, 2, 1), exchange(x1, CORE, sizes), exchange(x2, X, sizes), exchange(x3, FAR, sizes)
        )
        given = (x0, xk, joined(xx, xd))
        h1, h2, h3, cot_in, b_up = phase(joined(h1, g1), h2, joined(h3, g3), cot_in, b_up)
        g1, g2 = swap(h1, 0, 2), swap(h2, 1, 0)
        c0, c1, c2, c3 = seen(cot_in)
        c_send = joined(c1, c3)
        table, small = tables(b_qv, b_up, (b_out, ln1_gain, ln1_bias, b_down, ln2_gain, ln2_bias))
        g1, g2, c_send, small = phase(g1, g2, c_send, small)
        h1, h2, h3 = phase(joined(h1, g1), joined(h2, g2), h3)
        g1, g2, ck, got, f1 = phase(
            swap(h1, 0, 3),
            swap(h2, 1, 1),
            exchange(c_send, CORE, sizes),
            exchange(small, Y, sizes),
            exchange(h1, CORE, sizes),
        )
        small = joined(small, got)
        g1, h2, h3 = phase(g1, joined(h2, g2), h3)
        k1, g2, g3 = exchange(g1, CORE, sizes), swap(h2, 1, 2), swap(h3, 2, 2)
        (wq,) = unpack(gathers[0], (h1, g1), (f1, k1), (3 * width,))
        proj, rows_b, mask = project(wq, given, small, fast)
        proj, g2, c2, ck = phase(proj, g2, c2, ck)
        h2 = joined(h2, g2)
        g2 = swap(h2, 1, 3)
        mixed0, probs0 = attend(after(proj, h2), mask, 0)
        mixed0, g3, h2 = phase(mixed0, g3, h2)
        h3 = joined(h3, g3)
        f2, g3, f3 = exchange(h2, CORE, sizes), swap(h3, 2, 3), exchange(h3, CORE, sizes)
        mixed1, probs1 = attend(after(proj, h3, mixed0), mask, 1)
        mixed1, g2, f2 = phase(mixed1, g2, f2)
        g2, c_send = phase(g2, joined(c2, ck[1:]))
        k2, cx = exchange(g2, CORE, sizes), exchange(c_send, X, sizes)
        wo, wu = unpack(gathers[1], (h2, g2), (f2, k2), (width, 2 * local_units))
    else:
        parts = (shards[0], w_out.T, w_up, w_down.T)
        pieces = [cut(gather_plain(s)) for s in parts]
        split = lambda pair: ((pair[0],), (pair[1],))
        (wq,) = unpack(None, *split(pieces[0]), (3 * width,))
        (wo,) = unpack(None, *split(pieces[1]), (width,))
        (wu,) = unpack(None, *split(pieces[2]), (2 * local_units,))
        (wd,) = unpack(None, *split(pieces[3]), (2 * local_units,))
        order = lambda value: (value[:1], value[1:3], value[2:])
        given, cot = order(to_owners(rows_in)), order(to_owners(cot_in))
        table, small = tables(b_qv, b_up, (b_out, ln1_gain, ln1_bias, b_down, ln2_gain, ln2_bias))
        small = joined(small, exchange(small, Y, sizes))
        proj, rows_b, mask = project(wq, given, small, fast)
        mixed0, probs0 = attend(proj, mask, 0)
        mixed1, probs1 = attend(proj, mask, 1)

    normed1, scale1, first_b, act, slope = middle(wo, wu, mixed0, mixed1, rows_b, table, small)
    if fast:
        act, g3, f3, cx = phase(act, g3, f3, cx)
        cot = (c0, ck, cx)
        (wd,) = unpack(gathers[2], (h3, g3), (f3, exchange(g3, CORE, sizes)), (2 * local_units,))
    chunks, gz, gzb, sums2, down_own, down_sib = turn(packs[2], wd, act, normed1, cot, table, local_len)

    rows = shard_rows // 4
    if fast:
        down_sib, chunks, gzb = phase(down_sib, chunks, gzb)
        got, core_out = shed(down_sib, 2, 0), exchange(chunks[2:], CORE, sizes)
    gh, sum_up = hidden_back(wd, gzb, slope)
    if fast:
        gh, got, core_out = phase(gh, got, core_out)
        down = [down_own, got]
        send, x_send, gh = phase(
            add_up(down, 8 * rows, 16 * rows), joined(chunks[1:2], core_out[1:2]), gh
        )
        got, x_out = shed(send, 2, 1), exchange(x_send, X, sizes)
    gz1, grad_mixed, sums1, up_own, up_sib = first_back(
        packs[1], wo, wu, gh, gz, normed1, scale1, table, first_b, mixed0, mixed1
    )
    if fast:
        grad_mixed, up_sib, got, x_out = phase(grad_mixed, up_sib, got, x_out)
        down = down + [got]
        send, y_send, grad_mixed = phase(
            add_up(down, 4 * rows, 8 * rows), joined(chunks[:1], core_out[:1], x_out), grad_mixed
        )
        got, got2, y_out = shed(send, 2, 2), shed(up_sib, 1, 0), exchange(y_send, Y, sizes)
    parts0 = attend_back(proj, probs0, grad_mixed, 0)
    if fast:
        head, got2, grad_mixed = phase(parts0[0], got2, grad_mixed)
        parts0 = (head,) + tuple(parts0[1:])
        up = [up_own, got2]
        send2, grad_mixed = phase(add_up(up, 8 * rows, 16 * rows), grad_mixed)
        got2 = shed(send2, 1, 1)
    parts1 = attend_back(proj, probs1, grad_mixed, 1)
    parts = list(parts0) + list(parts1)
    if fast:
        parts[3], got = phase(parts[3], got)
        down = down + [got]
        send = add_up(down, 2 * rows, 4 * rows)
        got = shed(send, 2, 3)
        parts[3], send = phase(parts[3], send)
    chunks2 = input_back(wq, gz1, parts, local_len, fast)
    if fast:
        chunks2, y_out = phase(chunks2, y_out)
    parts[0] = after(parts[0], chunks2)
    qkv_own, qkv_sib = last(packs[0], rows_b, sums1, sums2, sum_up, parts)
    if fast:
        got3, core_x = shed(qkv_sib, 0, 0), exchange(chunks2[2:], CORE, sizes)
        chunks2, qkv_own, got2 = phase(chunks2, qkv_own, got2)
        up = up + [got2]
        send2 = add_up(up, 4 * rows, 8 * rows, time=30)
        send2, got3 = phase(send2, got3)
        got2 = shed(send2, 1, 2)
        got3, core_x = phase(got3, core_x)
        qkv = [qkv_own, got3]
        sent3 = add_up(qkv, 8 * rows, 16 * rows, (0, 1))
        x_send = joined(chunks2[1:2], core_x[1:2])
        got3 = shed(sent3, 0, 1)
        got3, x_send = phase(got3, x_send)
        qkv = qkv + [got3]
        send3 = add_up(qkv, 4 * rows, 8 * rows, (3, 2), [sent3])
        got3 = shed(send3, 0, 2)
        send3, got, x_send = phase(send3, got, x_send)
        down = down + [got]
        send = add_up(down, rows, 2 * rows)
        got, x_x = shed(send, 2, 4), exchange(x_send, X, sizes)
        send, got2 = phase(send, got2)
        up = up + [got2]
        send2 = add_up(up, 2 * rows, 4 * rows)
        got2 = shed(send2, 1, 3)
        got3, send2 = phase(got3, send2)
        qkv = qkv + [got3]
        sent3 = add_up(qkv, 2 * rows, 4 * rows, (4, 3), [send3])
        got3 = shed(sent3, 0, 3)
        sent3, got, x_x = phase(sent3, got, x_x)
        pair1 = add_up(down + [got], 0, rows)
        y_send = joined(chunks2[:1], core_x[:1], x_x)
        got, y_x = exchange(pair1, X, sizes), exchange(y_send, Y, sizes)
        pair1, got2 = phase(pair1, got2)
        up = up + [got2]
        send2 = add_up(up, rows, 2 * rows)
        got2 = shed(send2, 1, 4)
        layer_output = deliver(chunks, core_out, x_out, after(y_out, send2))
        got3, layer_output = phase(got3, layer_output)
        qkv = qkv + [got3]
        send3 = add_up(qkv, rows, 2 * rows, (5, 4), [sent3])
        got3 = shed(send3, 0, 4)
        send3, got, got2 = phase(send3, got, got2)
        pair1 = joined(pair1, got)
        up = up + [got2]
        pair2 = add_up(up, 0, rows)
        got1, got2 = exchange(pair1, CORE, sizes), exchange(pair2, X, sizes)
        got3, pair1, pair2 = phase(got3, pair1, pair2)
        qkv = qkv + [got3]
        sent_last = got3
        piece = add_up(qkv, 0, rows)
        got3 = [exchange(piece, dims, sizes) for dims in (X, CORE, FAR)]
        vec = vectors(after(send3, piece), sent_last, local_width, local_units)
        piece, got1, bup = phase(piece, got1, vec[1])
        vec = (vec[0], bup) + tuple(vec[2:])
        (grad_down,) = settle((pair1, got1), ((0, local_units, "plain"),))
        grad_down, got2 = phase(grad_down, got2)
        pair2 = joined(pair2, got2)
        got2 = exchange(pair2, CORE, sizes)
        pair2, y_x = phase(pair2, y_x)
        grad_x = deliver(chunks2, core_x, x_x, y_x)
        grad_x, *got3 = phase(grad_x, *got3)
        (grad_qkv,) = settle([piece] + got3, ((0, 3 * local_width, "three"),))
        grad_wout, grad_up = settle(
            (pair2, after(got2, grad_qkv)),
            ((0, local_width, "plain"), (local_width, local_width + local_units, "plain")),
        )
        layer_output = layer_output.reshape(micro, seqs, local_len, width)
        grad_x = grad_x.reshape(micro, seqs, local_len, width)
    else:
        layer_output = spread(jnp.repeat(chunks, 2, axis=0))
        grad_x = spread(jnp.repeat(chunks2, 2, axis=0))
        vec = lax.psum(qkv_own[width:].astype(F32), AXES)
        vec = vectors(vec, None, local_width, local_units)
        grad_down = reduce_plain(down_own, down_sib)
        both = reduce_plain(up_own, up_sib)
        grad_wout, grad_up = both[:, :local_width], both[:, local_width:]
        grad_qkv = reduce_plain(qkv_own[:width], qkv_sib[:width])
        grad_qkv = jnp.swapaxes(grad_qkv.reshape(shard_rows, 3, local_width), 0, 1)

    out_bqv, out_bup, g1, s1, bout, g2, s2, bdown = vec
    return (
        layer_output,
        grad_x,
        grad_qkv,
        out_bqv,
        grad_wout.T,
        bout,
        g1,
        s1,
        grad_up,
        out_bup,
        grad_down.T,
        bdown,
        g2,
        s2,
    )


def solution(mesh):
    return jax.shard_map(
        body,
        mesh=mesh,
        in_specs=(
            P(None, "fsdp", "ctx", None),
            P(None, "fsdp", "ctx"),
            P(None, "fsdp", "tp"),
            P(None, "tp"),
            P("tp", "fsdp"),
            P(),
            P(),
            P(),
            P("fsdp", "tp"),
            P("tp"),
            P("tp", "fsdp"),
            P(),
            P(),
            P(),
            P(None, "fsdp", "ctx", None),
        ),
        out_specs=(
            P(None, "fsdp", "ctx", None),
            P(None, "fsdp", "ctx", None),
            P(None, "fsdp", "tp"),
            P(None, "tp"),
            P("tp", "fsdp"),
            P(),
            P(),
            P(),
            P("fsdp", "tp"),
            P("tp"),
            P("tp", "fsdp"),
            P(),
            P(),
            P(),
        ),
        check_vma=False,
    )
```

```python
import jax
import jax.numpy as jnp
from jax import lax
from jax.experimental import pallas as pl
from jax.experimental.pallas import tpu as pltpu
from jax.sharding import PartitionSpec as P

HEAD_DIM = 64
AXES = ("fsdp", "ctx", "tp")
F32 = jnp.float32
BF16 = jnp.bfloat16
NEG = -1e30
NT = (((1,), (1,)), ((), ()))
VMEM = pl.BlockSpec(memory_space=pltpu.VMEM)
SMEM = pl.BlockSpec(memory_space=pltpu.SMEM)
ANY = pl.BlockSpec(memory_space=pl.ANY)


def partner(dim, z, c, t):
    if dim == "core":
        return z, c ^ 1, t
    if dim == "x":
        return z, c ^ 2, t
    if dim == "x+core":
        return z, c ^ 3, t
    if dim == "y":
        return z, c, t ^ 1
    return z ^ int(dim[1:]), c, t


def exchange(value, dims, sizes):
    nz, nc, nt = sizes
    pairs = []
    for z in range(nz):
        for c in range(nc):
            for t in range(nt):
                tz, tc, tt = partner(dims[c & 1], z, c, t)
                pairs.append(((z * nc + c) * nt + t, (tz * nc + tc) * nt + tt))
    return lax.ppermute(value, AXES, pairs)


GATHER = (
    (("z2", "z1", "y", "x"), ("z1", "z2", "x", "y")),
    (("z2", "z1", "y", "x"), ("z1", "z2", "x", "y")),
    (("x", "z2", "z1", "y"), ("y", "x", "z2", "z1")),
)
SCATTER = (
    (("x", "y", "z1", "z2"), ("y", "x", "z2", "z1")),
    (("x", "y", "z1", "z2"), ("z1", "z2", "y", "x")),
    (("y", "x", "z1", "z2"), ("z1", "z2", "x", "y")),
)
CORE = ("core", "core")
X = ("x", "x")
FAR = ("x+core", "x+core")
Y = ("y", "y")


def piece_place(order, core, here, index):
    z, x, t = here
    for bit, dim in enumerate(order):
        flip = (index >> bit) & 1
        if dim == "x":
            x = x ^ flip
        elif dim == "y":
            t = t ^ flip
        else:
            z = z ^ (flip * int(dim[1:]))
    return z * 4 + x * 2 + core, t


def places(orders):
    if orders is None:
        return [(i, half) for half in range(2) for i in range(16)]
    c = lax.axis_index("ctx")
    here = (lax.axis_index("fsdp"), c >> 1, lax.axis_index("tp"))
    spots = []
    for core in (c & 1, 1 - (c & 1)):
        for i in range(16):
            r0, t0 = piece_place(orders[0], core, here, i)
            r1, t1 = piece_place(orders[1], core, here, i)
            spots.append((jnp.where(core == 0, r0, r1), jnp.where(core == 0, t0, t1)))
    return spots


def packing(orders):
    return tuple(order[::-1] for order in orders)


def after(value, *first):
    return lax.optimization_barrier((value, first))[0]


def phase(*values):
    return lax.optimization_barrier(values)


def at_rows(place, count, unit=0):
    start = place * count
    return pl.ds(start if isinstance(start, int) else pl.multiple_of(start, unit or count), count)


def piece_copies(spots, near, far, sem, whole, low, cols, base=0):
    rows = whole.shape[0] // 16
    copies = []
    each = 16 // len(near)
    for half, refs in ((0, near), (1, far)):
        for i in range(16):
            row, col = spots[half * 16 + i]
            copy = pltpu.make_async_copy(
                refs[i // each].at[pl.ds(i % each * rows, rows), pl.ds(low, cols)],
                whole.at[at_rows(row, rows), at_rows(col, cols, 128)],
                sem.at[base + half * 16 + i],
            )
            copy.start()
            copies.append(copy)
    return copies


def pack(spots, own_ref, sib_ref, whole, low, cols):
    rows = whole.shape[0] // 16
    for half, ref in ((0, own_ref), (1, sib_ref)):
        for i in range(16):
            row, col = spots[half * 16 + i]
            ref[i * rows : (i + 1) * rows, low : low + cols] = whole[at_rows(row, rows), at_rows(col, cols, 128)]


def finish(copies):
    for copy in copies:
        copy.wait()


def tiles(count, step):
    def run(one):
        lax.fori_loop(0, count // step, lambda i, carry: (one(pl.multiple_of(i * step, step)), carry)[1], 0)

    return run


def row_mean(value):
    return jnp.mean(value, axis=-1, keepdims=True)


def struct(shape, dtype):
    return jax.ShapeDtypeStruct(shape, dtype)


def call(kernel, name, outs, specs, out_specs, scratch, time, room, args):
    return pl.pallas_call(
        kernel,
        name=name,
        out_shape=outs,
        in_specs=specs,
        out_specs=out_specs,
        scratch_shapes=scratch,
        compiler_params=pltpu.CompilerParams(vmem_limit_bytes=room << 20),
        cost_estimate=pl.CostEstimate(flops=time * 10**9, transcendentals=0, bytes_accessed=10**6),
    )(*args)


B_OUT, GAIN1, SHIFT1, B_DOWN, GAIN2, SHIFT2 = range(6)


def unpack_kernel(*refs, orders, count):
    near, far, outs, sem = refs[:count], refs[count : 2 * count], refs[2 * count : -1], refs[-1]
    copies = []
    spots = places(orders)
    low = 0
    for i, out in enumerate(outs):
        cols = out.shape[1] // 2
        copies += piece_copies(spots, near, far, sem, out, low, cols, 32 * i)
        low += cols
    finish(copies)


def unpack(orders, near, far, widths):
    count = len(near)
    rows = near[0].shape[0] * count
    return call(
        lambda *refs: unpack_kernel(*refs, orders=orders, count=count),
        "unpack",
        tuple(struct((rows, width), BF16) for width in widths),
        [ANY] * (2 * count),
        (VMEM,) * len(widths),
        [pltpu.SemaphoreType.DMA((32 * len(widths),))],
        5,
        2,
        tuple(near) + tuple(far),
    )


def sources(refs, fast):
    c = lax.axis_index("ctx") if fast else 0
    own, core, x = refs
    return [(c ^ 0, own, 0), (c ^ 1, core, 0), (c ^ 2, x, 0), (c ^ 3, x, 1)]


def tables_kernel(qv_ref, up_ref, *refs):
    rows, (table_ref, small_ref) = refs[:-2], refs[-2:]
    table_ref[...] = jnp.zeros_like(table_ref)
    for i, ref in enumerate(rows):
        table_ref[i : i + 1, :] = ref[...][None]
    width = qv_ref.shape[1]
    small_ref[:, :width] = qv_ref[0:1, :]
    small_ref[:, width : 2 * width] = qv_ref[1:2, :]
    small_ref[:, 2 * width :] = up_ref[...][None]


def tables(b_qv, b_up, rows):
    return call(
        tables_kernel,
        "tables",
        (struct((8, rows[0].shape[0]), F32), struct((1, b_qv.size + b_up.size), F32)),
        [VMEM] * (2 + len(rows)),
        (VMEM, VMEM),
        [],
        1,
        3,
        (b_qv, b_up) + tuple(rows),
    )


def project_kernel(weight_ref, own_ref, core_ref, far_ref, small_ref, proj_ref, x_ref, mask_ref, ids, *, fast):
    block = own_ref.shape[1] - 8
    count = 4
    for spot, ref, i in sources((own_ref, core_ref, far_ref), fast):
        x_ref[pl.ds(pl.multiple_of(spot * block, block), block), :] = ref[i, 0:block, :]
        ids[pl.ds(spot, 1), :] = ref[i, block:, 0:block].astype(F32)[0:1]
    for kb in range(count):
        column = jnp.broadcast_to(ids[kb : kb + 1], (block, block)).T
        for qb in range(count):
            mask_ref[kb * block : (kb + 1) * block, qb * block : (qb + 1) * block] = jnp.where(
                column == jnp.broadcast_to(ids[qb : qb + 1], (block, block)), 0.0, NEG
            )
    width = proj_ref.shape[1] // 6
    for y in range(2):
        row = pl.ds(lax.axis_index("tp") ^ y, 1)
        for which in range(3):
            at = (y * 3 + which) * width
            value = jnp.dot(x_ref[...], weight_ref[:, at : at + width], preferred_element_type=F32)
            if which != 1:
                low = 0 if which == 0 else width
                value = value + small_ref[row, low : low + width]
            proj_ref[:, at : at + width] = value.astype(BF16)


def project(weight, given, small, fast):
    width, wide = weight.shape
    block = given[0].shape[1] - 8
    length = 4 * block
    return call(
        lambda *refs: project_kernel(*refs, fast=fast),
        "project",
        (
            struct((length, wide), BF16),
            struct((length, width), BF16),
            struct((length, length), F32),
        ),
        [VMEM] * 5,
        (VMEM,) * 3,
        [pltpu.VMEM((8, block), F32)],
        5,
        3,
        (weight,) + tuple(given) + (small,),
    )


def attend_kernel(proj_ref, mask_ref, o_ref, p_ref, *, y):
    length = proj_ref.shape[0]
    pairs = o_ref.shape[1] // 128
    lane = lax.broadcasted_iota(jnp.int32, (1, 128), 1)

    def pair(g, carry):
        take = lambda which: proj_ref[:, pl.ds(pl.multiple_of(((y * 3 + which) * pairs + g) * 128, 128), 128)]
        query = take(0) * jnp.asarray(0.125, BF16)
        keys = take(1)
        values_t = take(2).T
        outs = []
        for head in range(2):
            here = (lane >= 64 * head) & (lane < 64 * head + 64)
            only = jnp.where(here, keys, jnp.zeros_like(keys))
            row = []
            for at in range(0, length, 256):
                scores = lax.dot_general(only, query[at : at + 256], NT, preferred_element_type=F32)
                scores = scores + mask_ref[:, at : at + 256]
                top = jnp.max(scores, axis=0, keepdims=True)
                raised = jnp.exp(scores - top)
                total = jnp.sum(raised, axis=0, keepdims=True)
                probs = (raised * (1.0 / total)).astype(BF16)
                p_ref[2 * g + head, :, at : at + 256] = probs
                row.append(
                    jnp.dot(values_t[64 * head : 64 * head + 64], probs, preferred_element_type=F32)
                )
            outs.append(jnp.concatenate(row, axis=1))
        both = jnp.concatenate(outs, axis=0).astype(BF16)
        o_ref[:, pl.ds(pl.multiple_of(g * 128, 128), 128)] = both.T
        return carry

    lax.fori_loop(0, pairs, pair, 0)


def attend(proj, mask, y):
    length, wide = proj.shape
    half = wide // 6
    return call(
        lambda *refs: attend_kernel(*refs, y=y),
        "attend",
        (struct((length, half), BF16), struct((half // HEAD_DIM, length, length), BF16)),
        [VMEM, VMEM],
        (VMEM, VMEM),
        [],
        12,
        3,
        (proj, mask),
    )


def middle_kernel(
    w_out, w_up, mixed0_ref, mixed1_ref, x_ref, table_ref, small_ref,
    normed_ref, scale_ref, first_ref, act_ref, slope_ref,
):
    length, units = act_ref.shape
    narrow, half = w_out.shape[1] // 2, units // 2
    normed_ref[...] = lax.dot_general(
        mixed0_ref[...], w_out[:, :narrow], NT, preferred_element_type=F32
    ) + lax.dot_general(mixed1_ref[...], w_out[:, narrow:], NT, preferred_element_type=F32)

    @tiles(length, 128)
    def _(at):
        here = pl.ds(at, 128)
        value = x_ref[here, :].astype(F32) + normed_ref[here, :] + table_ref[B_OUT : B_OUT + 1, :]
        centred = value - row_mean(value)
        scale = lax.rsqrt(row_mean(centred * centred) + 1e-12)
        unit = centred * scale
        normed_ref[here, :] = unit
        scale_ref[here, :] = scale
        first_ref[here, :] = (
            unit * table_ref[GAIN1 : GAIN1 + 1, :] + table_ref[SHIFT1 : SHIFT1 + 1, :]
        ).astype(BF16)

    for y in range(2):
        row = pl.ds(lax.axis_index("tp") ^ y, 1)

        @tiles(half, 256)
        def _(at):
            here = pl.ds(pl.multiple_of(y * half + at, 256), 256)
            bias = small_ref[row, pl.ds(pl.multiple_of(2 * narrow + at, 256), 256)]
            hidden = jnp.dot(first_ref[...], w_up[:, here], preferred_element_type=F32) + bias
            phi = 0.5 + 0.5 * lax.erf(hidden * 0.7071067811865476)
            act_ref[:, here] = (hidden * phi).astype(BF16)
            bell = jnp.exp(-0.5 * hidden * hidden) * 0.3989422804014327
            slope_ref[:, here] = (phi + hidden * bell).astype(BF16)


def middle(w_out, w_up, mixed0, mixed1, x, table, small):
    length, width = x.shape
    units = w_up.shape[1]
    return call(
        middle_kernel,
        "middle",
        (
            struct((length, width), F32),
            struct((length, 1), F32),
            struct((length, width), BF16),
            struct((length, units), BF16),
            struct((length, units), BF16),
        ),
        [VMEM] * 7,
        (VMEM,) * 5,
        [],
        12,
        3,
        (w_out, w_up, mixed0, mixed1, x, table, small),
    )


def turn_kernel(
    weight_ref, act_ref, normed_ref, own_ref, core_ref, far_ref, table_ref,
    chunks_ref, gz_ref, gzb_ref, sums_ref, down_own, down_sib, full, cot_ref, *, orders,
):
    length = act_ref.shape[0]
    block = chunks_ref.shape[1]
    for spot, ref, i in sources((own_ref, core_ref, far_ref), orders is not None):
        cot_ref[pl.ds(pl.multiple_of(spot * block, block), block), :] = ref[i]
    gz_ref[...] = lax.dot_general(act_ref[...], weight_ref[...], NT, preferred_element_type=F32)
    sums_ref[...] = jnp.zeros_like(sums_ref)
    row = lambda which: table_ref[which : which + 1, :]

    @tiles(length, 128)
    def _(at):
        here = pl.ds(at, 128)
        value = normed_ref[here, :] * row(GAIN1) + row(SHIFT1) + gz_ref[here, :] + row(B_DOWN)
        centred = value - row_mean(value)
        scale = lax.rsqrt(row_mean(centred * centred) + 1e-12)
        unit = centred * scale
        result = (unit * row(GAIN2) + row(SHIFT2)).astype(BF16)
        chunk = lax.div(at, block)
        if orders is not None:
            c = lax.axis_index("ctx") ^ chunk
            chunk = (c & 1) * 2 + (c >> 1)
        chunks_ref[chunk, pl.ds(pl.multiple_of(lax.rem(at, block), 128), 128), :] = result
        coming = cot_ref[here, :].astype(F32)
        raised = coming * row(GAIN2)
        back = scale * (raised - row_mean(raised) - unit * row_mean(raised * unit))
        gz_ref[here, :] = back
        gzb_ref[here, :] = back.astype(BF16)
        sums_ref[0:1, :] += jnp.sum(coming * unit, axis=0, keepdims=True)
        sums_ref[1:2, :] += jnp.sum(coming, axis=0, keepdims=True)
        sums_ref[2:3, :] += jnp.sum(back, axis=0, keepdims=True)

    back_t = gzb_ref[...].T

    @tiles(full.shape[1], 1024)
    def _(at):
        here = pl.ds(at, 1024)
        full[:, here] = jnp.dot(back_t, act_ref[:, here], preferred_element_type=F32).astype(BF16)

    pack(places(orders), down_own, down_sib, full, 0, down_own.shape[1])


def turn(orders, weight, act, normed, cot, table, chunk):
    length, units = act.shape
    width = normed.shape[1]
    piece = struct((width, units // 2), BF16)
    return call(
        lambda *refs: turn_kernel(*refs, orders=orders),
        "turn",
        (
            struct((length // chunk, chunk, width), BF16),
            struct((length, width), F32),
            struct((length, width), BF16),
            struct((8, width), F32),
            piece,
            piece,
        ),
        [VMEM] * 7,
        (VMEM,) * 6,
        [pltpu.VMEM((width, units), BF16), pltpu.VMEM((length, width), BF16)],
        14,
        10,
        (weight, act, normed) + tuple(cot) + (table,),
    )


def hidden_back_kernel(weight_ref, gzb_ref, slope_ref, gh_ref, sum_ref):
    @tiles(gh_ref.shape[1], 512)
    def _(at):
        here = pl.ds(at, 512)
        back = jnp.dot(gzb_ref[...], weight_ref[:, here], preferred_element_type=F32)
        back = (back * slope_ref[:, here].astype(F32)).astype(BF16)
        gh_ref[:, here] = back
        sum_ref[:, here] = jnp.sum(back.astype(F32), axis=0, keepdims=True)


def hidden_back(weight, gzb, slope):
    length, units = slope.shape
    return call(
        hidden_back_kernel,
        "hidden_back",
        (struct((length, units), BF16), struct((1, units), F32)),
        [VMEM] * 3,
        (VMEM, VMEM),
        [],
        12,
        3,
        (weight, gzb, slope),
    )


def first_back_kernel(
    w_out, w_up, gh_ref, gz_ref, normed_ref, scale_ref, table_ref, first_ref, mixed0_ref, mixed1_ref,
    gz1_ref, gm_ref, sums_ref, pieces_own, pieces_sib, branch, d_out, d_up, *, orders,
):
    narrow = w_out.shape[1] // 2
    half = w_up.shape[1] // 2
    length = gh_ref.shape[0]
    first_t = first_ref[...].T
    spots = places(orders)

    @tiles(d_up.shape[1], 1024)
    def _(at):
        here = pl.ds(at, 1024)
        d_up[:, here] = jnp.dot(first_t, gh_ref[:, here], preferred_element_type=F32).astype(BF16)

    pack(spots, pieces_own, pieces_sib, d_up, narrow, half)
    gz1_ref[...] = lax.dot_general(gh_ref[...], w_up[...], NT, preferred_element_type=F32)
    sums_ref[...] = jnp.zeros_like(sums_ref)

    @tiles(length, 128)
    def _(at):
        here = pl.ds(at, 128)
        coming = gz_ref[here, :] + gz1_ref[here, :]
        unit = normed_ref[here, :]
        raised = coming * table_ref[GAIN1 : GAIN1 + 1, :]
        back = scale_ref[here, :] * (raised - row_mean(raised) - unit * row_mean(raised * unit))
        gz1_ref[here, :] = back
        branch[here, :] = back.astype(BF16)
        sums_ref[0:1, :] += jnp.sum(coming * unit, axis=0, keepdims=True)
        sums_ref[1:2, :] += jnp.sum(coming, axis=0, keepdims=True)
        sums_ref[2:3, :] += jnp.sum(back, axis=0, keepdims=True)

    branch_t = branch[...].T
    d_out[:, :narrow] = jnp.dot(branch_t, mixed0_ref[...], preferred_element_type=F32).astype(BF16)
    d_out[:, narrow:] = jnp.dot(branch_t, mixed1_ref[...], preferred_element_type=F32).astype(BF16)
    pack(spots, pieces_own, pieces_sib, d_out, 0, narrow)
    gm_ref[...] = jnp.dot(branch[...], w_out[...], preferred_element_type=F32).astype(BF16)


def first_back(orders, w_out, w_up, gh, gz, normed, scale, table, first_b, mixed0, mixed1):
    length, units = gh.shape
    width = gz.shape[1]
    piece = struct((width, (units + width) // 2), BF16)
    return call(
        lambda *refs: first_back_kernel(*refs, orders=orders),
        "first_back",
        (
            struct((length, width), F32),
            struct((length, width), BF16),
            struct((8, width), F32),
            piece,
            piece,
        ),
        [VMEM] * 10,
        (VMEM,) * 5,
        [
            pltpu.VMEM((length, width), BF16),
            pltpu.VMEM((width, width), BF16),
            pltpu.VMEM((width, units), BF16),
        ],
        20,
        12,
        (w_out, w_up, gh, gz, normed, scale, table, first_b, mixed0, mixed1),
    )


def attend_back_kernel(proj_ref, p_ref, gm_ref, dq_ref, dk_ref, dv_ref, dst, dqt, *, y):
    length = proj_ref.shape[0]
    pairs = dq_ref.shape[1] // 128
    lane = lax.broadcasted_iota(jnp.int32, (1, 128), 1)
    low = lane < 64

    def pair(g, carry):
        take = lambda which: proj_ref[:, pl.ds(pl.multiple_of(((y * 3 + which) * pairs + g) * 128, 128), 128)]
        query, keys, values = take(0), take(1), take(2)
        grad = gm_ref[:, pl.ds(pl.multiple_of((y * pairs + g) * 128, 128), 128)]
        keys_t = keys.T
        dks, dvs = [], []
        for head in range(2):
            here = low if head == 0 else jnp.logical_not(low)
            only = jnp.where(here, values, jnp.zeros_like(values))
            for at in range(0, length, 256):
                cols = slice(at, at + 256)
                gp = lax.dot_general(only, grad[cols], NT, preferred_element_type=F32)
                probs = p_ref[2 * g + head, :, cols].astype(F32)
                weighted = jnp.sum(probs * gp, axis=0, keepdims=True)
                dst[:, cols] = (probs * (gp - weighted)).astype(BF16)
            dqt[64 * head : 64 * head + 64, :] = (
                jnp.dot(keys_t[64 * head : 64 * head + 64], dst[...], preferred_element_type=F32) * 0.125
            ).astype(BF16)
            dks.append(jnp.dot(dst[...], query, preferred_element_type=F32))
            dvs.append(jnp.dot(p_ref[2 * g + head], grad, preferred_element_type=F32))
        cols = pl.ds(pl.multiple_of(g * 128, 128), 128)
        dq_ref[:, cols] = dqt[...].T
        dk_ref[:, cols] = (jnp.where(low, dks[0], dks[1]) * 0.125).astype(BF16)
        dv_ref[:, cols] = jnp.where(low, dvs[0], dvs[1]).astype(BF16)
        return carry

    lax.fori_loop(0, pairs, pair, 0)


def attend_back(proj, probs, grad_mixed, y):
    length, wide = proj.shape
    shape = struct((length, wide // 6), BF16)
    return call(
        lambda *refs: attend_back_kernel(*refs, y=y),
        "attend_back",
        (shape, shape, shape),
        [VMEM] * 3,
        (VMEM,) * 3,
        [pltpu.VMEM((length, length), BF16), pltpu.VMEM((128, length), BF16)],
        1,
        4,
        (proj, probs, grad_mixed),
    )


def last_kernel(x_ref, sums1_ref, sums2_ref, sum_up_ref, *refs, orders):
    parts, (pieces_own, pieces_sib, whole, vec) = refs[:6], refs[6:]
    half = parts[0].shape[1]
    rows = whole.shape[0]
    x_t = x_ref[...].T
    sums = [[], []]
    for y in range(2):
        for which in range(3):
            at = (y * 3 + which) * half
            value = parts[y * 3 + which][...]
            whole[:, at : at + half] = jnp.dot(x_t, value, preferred_element_type=F32).astype(BF16)
            if which != 1:
                sums[which // 2].append(jnp.sum(value.astype(F32), axis=0, keepdims=True))
    pack(places(orders), pieces_own, pieces_sib, whole, 0, 3 * half)
    vectors = sums[0] + sums[1] + [ref[i : i + 1, :] for ref in (sums1_ref, sums2_ref) for i in range(3)]
    at = 0
    across = vec.shape[1] // 128
    wide = []
    for vector in vectors + [sum_up_ref[...]]:
        for low in range(0, vector.shape[1], 128):
            wide.append(vector[:, low : low + 128])
    for row in range(8):
        vec[row : row + 1, :] = jnp.concatenate(wide[row * across : (row + 1) * across], axis=1)
    pieces_own[rows:, :] = vec[...].astype(BF16)
    pieces_sib[rows:, :] = vec[...].astype(BF16)


def last(orders, x, sums1, sums2, sum_up, parts):
    length, width = x.shape
    piece = struct((width + 8, 3 * width // 2), BF16)
    return call(
        lambda *refs: last_kernel(*refs, orders=orders),
        "last",
        (piece, piece),
        [VMEM] * 10,
        (VMEM, VMEM),
        [
            pltpu.VMEM((width, 3 * width), BF16),
            pltpu.VMEM((8, 3 * width // 2), F32),
        ],
        10,
        7,
        (x, sums1, sums2, sum_up) + tuple(parts),
    )


def vectors_kernel(one_ref, two_ref, qv_ref, up_ref, *refs):
    t = lax.axis_index("tp")
    rows, cols = one_ref.shape
    across = cols // 128
    value = one_ref[rows - 8 :, :].astype(F32)
    if two_ref is not None:
        value = value + two_ref[rows - 8 :, :].astype(F32)

    def block(at):
        row, low = at // across, at % across * 128
        return value[row : row + 1, low : low + 128]

    def take(out, row, first, other, count):
        for i in range(count):
            one = block(first + i)
            if other != first:
                one = jnp.where(t == 0, one, block(other + i))
            if row is None:
                out[i * 128 : (i + 1) * 128] = one[0]
            else:
                out[row : row + 1, i * 128 : (i + 1) * 128] = one

    narrow, wide = qv_ref.shape[1] // 128, up_ref.shape[0] // 128
    for which in range(2):
        take(qv_ref, which, 2 * which * narrow, (2 * which + 1) * narrow, narrow)
    for i, ref in enumerate(refs):
        take(ref, None, (4 + 2 * i) * narrow, (4 + 2 * i) * narrow, 2 * narrow)
    base = (4 + 2 * len(refs)) * narrow
    take(up_ref, None, base, base + wide, wide)


def vectors(one, two, local_width, local_units):
    shapes = [(2, local_width), (local_units,)] + [(2 * local_width,)] * 6
    given = (one,) if two is None else (one, two)

    def kernel(*refs):
        if two is None:
            refs = (refs[0], None) + refs[1:]
        vectors_kernel(*refs)

    return call(
        kernel,
        "vectors",
        tuple(struct(shape, F32) for shape in shapes),
        [VMEM] * len(given),
        (VMEM,) * 8,
        [],
        1,
        4,
        given,
    )


def add_kernel(*refs, low, high, vec, count):
    terms, out = refs[:-1], refs[-1]
    total = terms[0][low:high, :].astype(F32)
    for term in terms[1:count]:
        total = total + term[low:high, :].astype(F32)
    out[: high - low, :] = total.astype(BF16)
    if vec:
        total = 0.0
        for i in vec:
            total = total + terms[i][terms[i].shape[0] - 8 :, :].astype(F32)
        out[high - low :, :] = total.astype(BF16)


def add_up(terms, low, high, vec=(), lone=(), time=1):
    count, terms = len(terms), list(terms) + list(lone)
    cols = terms[0].shape[1]
    return call(
        lambda *refs: add_kernel(*refs, low=low, high=high, vec=vec, count=count),
        "add",
        struct((high - low + (8 if vec else 0), cols), BF16),
        [VMEM] * len(terms),
        VMEM,
        [],
        time,
        4,
        tuple(terms),
    )


def deliver_kernel(own_ref, core_ref, x_ref, y_ref, out_ref):
    c, t = lax.axis_index("ctx"), lax.axis_index("tp")
    sources = [(own_ref, 0), (core_ref, 0), (x_ref, 0), (x_ref, 1)] + [(y_ref, i) for i in range(4)]
    for i, (ref, at) in enumerate(sources):
        ctx = c ^ ((i & 1) + (i & 2))
        out_ref[ctx * 2 + (t ^ (i >> 2))] = ref[at]


def deliver(own, core, x, y):
    return call(
        deliver_kernel,
        "deliver",
        struct((2 * own.shape[0],) + own.shape[1:], BF16),
        [VMEM] * 4,
        VMEM,
        [],
        3,
        7,
        (own, core, x, y),
    )


def input_back_kernel(weight_ref, gz1_ref, *refs, fast):
    parts, chunks_ref = refs[:6], refs[6]
    half = parts[0].shape[1]
    total = gz1_ref[...]
    for i, part in enumerate(parts):
        total = total + lax.dot_general(
            part[...], weight_ref[:, i * half : (i + 1) * half], NT, preferred_element_type=F32
        )
    total = total.astype(BF16)
    count, block = chunks_ref.shape[:2]
    for i in range(count):
        spot = i
        if fast:
            c = lax.axis_index("ctx") ^ i
            spot = (c & 1) * 2 + (c >> 1)
        chunks_ref[spot] = total[i * block : (i + 1) * block]


def input_back(weight, gz1, parts, chunk, fast):
    length, width = gz1.shape
    return call(
        lambda *refs: input_back_kernel(*refs, fast=fast),
        "input_back",
        struct((length // chunk, chunk, width), BF16),
        [VMEM] * 8,
        VMEM,
        [],
        2,
        3,
        (weight, gz1) + tuple(parts),
    )


def settle_kernel(*refs, cuts, count):
    given, outs, four = refs[:count], refs[count:-1], refs[-1]
    rows = four.shape[0] // 4
    for i in range(4):
        ref = given[i * count // 4]
        owner = lax.axis_index("ctx") ^ ((i & 1) * 2 + (i >> 1))
        low = i % (4 // count) * rows
        four[pl.ds(pl.multiple_of(owner * rows, 16), rows), :] = ref[low : low + rows, :].astype(F32)
    for out, (low, high, form) in zip(outs, cuts):
        if form == "plain":
            out[...] = four[:, low:high]
        else:
            step = (high - low) // 3
            for j in range(3):
                out[j] = four[:, low + j * step : low + (j + 1) * step]


def settle(given, cuts):
    rows, cols = given[0].shape[0] * len(given) // 4, given[0].shape[1]
    shapes = {"plain": lambda n: (4 * rows, n), "three": lambda n: (3, 4 * rows, n // 3)}
    return call(
        lambda *refs: settle_kernel(*refs, cuts=cuts, count=len(given)),
        "settle",
        tuple(struct(shapes[form](high - low), F32) for low, high, form in cuts),
        [VMEM] * len(given),
        (VMEM,) * len(cuts),
        [pltpu.VMEM((4 * rows, cols), F32)],
        3,
        7,
        tuple(given),
    )


def cut(full):
    rows, cols = full.shape
    return full[:, : cols // 2], full[:, cols // 2 :]


def gather_plain(shard):
    rows = lax.all_gather(shard, "fsdp", axis=0, tiled=True)
    return lax.all_gather(rows, "tp", axis=1, tiled=True)


def reduce_plain(own, sib):
    full = jnp.concatenate([own, sib], axis=1)
    part = lax.psum_scatter(full, "tp", scatter_dimension=1, tiled=True)
    part = lax.psum_scatter(part, "fsdp", scatter_dimension=0, tiled=True)
    return lax.psum(part, "ctx").astype(F32)


def body(
    layer_input,
    doc_ids,
    w_qkv,
    b_qv,
    w_out,
    b_out,
    ln1_gain,
    ln1_bias,
    w_up,
    b_up,
    w_down,
    b_down,
    ln2_gain,
    ln2_bias,
    out_grad,
):
    sizes = (lax.axis_size("fsdp"), lax.axis_size("ctx"), lax.axis_size("tp"))
    micro, seqs, local_len, width = layer_input.shape
    length = local_len * sizes[1]
    shard_rows, local_width = w_qkv.shape[1:]
    local_units = w_up.shape[1]
    heads = width // HEAD_DIM
    fast = sizes == (4, 4, 2)
    t = lax.axis_index("tp")
    c = lax.axis_index("ctx")

    def mine(value):
        return lax.dynamic_index_in_dim(value, t, 1, keepdims=False)

    def to_owners(chunks):
        return lax.all_to_all(chunks, "ctx", 0, 0, tiled=True)

    def spread(chunks):
        out = lax.all_to_all(chunks, ("ctx", "tp"), 0, 0, tiled=True)
        return out.reshape(micro, seqs, local_len, width)

    shards = (
        jnp.swapaxes(w_qkv, 0, 1).reshape(shard_rows, 3 * local_width),
        jnp.concatenate([w_out.T, w_up], axis=1),
        w_down.T,
    )
    ids = mine(doc_ids).astype(BF16)[:, None, :]
    ids = jnp.pad(ids, ((0, 0), (0, 7), (0, width - local_len)))
    rows_in = jnp.concatenate([mine(layer_input), ids], axis=1)
    cot_in = mine(out_grad)
    gathers = GATHER if fast else (None,) * 3
    packs = tuple(packing(order) for order in SCATTER) if fast else (None,) * 3

    def swap(value, group, step):
        order = tuple(zip(*GATHER[group])) + (CORE,)
        return exchange(value, order[step], sizes)

    def shed(value, group, step):
        order = (CORE,) + tuple(zip(*SCATTER[group]))
        return exchange(value, order[step], sizes)

    def joined(*parts):
        return jnp.concatenate(parts, axis=0)

    if fast:
        def seen(value):
            return [lax.dynamic_index_in_dim(value, c ^ i, 0, keepdims=True) for i in range(4)]

        part = shard_rows // 4
        h1 = lax.dynamic_slice_in_dim(w_qkv, c * part, part, 1)
        h1 = jnp.swapaxes(h1, 0, 1).reshape(part, 3 * local_width)
        h2, h3 = [lax.dynamic_slice_in_dim(s, c * part, part, 0) for s in shards[1:]]
        g1 = swap(h1, 0, 0)
        h3 = after(h3, h1)
        x0, x1, x2, x3 = seen(after(rows_in, h1))
        g1, g3, x1, x2, x3, h2, cot_in, b_up = phase(g1, swap(h3, 2, 0), x1, x2, x3, h2, cot_in, b_up)
        h1, h3 = joined(h1, g1), joined(h3, g3)
        g1, g3, xk, xx, xd = phase(
            swap(h1, 0, 1), swap(h3, 2, 1), exchange(x1, CORE, sizes), exchange(x2, X, sizes), exchange(x3, FAR, sizes)
        )
        given = (x0, xk, joined(xx, xd))
        h1, h2, h3, cot_in, b_up = phase(joined(h1, g1), h2, joined(h3, g3), cot_in, b_up)
        g1, g2 = swap(h1, 0, 2), swap(h2, 1, 0)
        c0, c1, c2, c3 = seen(cot_in)
        c_send = joined(c1, c3)
        table, small = tables(b_qv, b_up, (b_out, ln1_gain, ln1_bias, b_down, ln2_gain, ln2_bias))
        g1, g2, c_send, small = phase(g1, g2, c_send, small)
        h1, h2, h3 = phase(joined(h1, g1), joined(h2, g2), h3)
        g1, g2, ck, got, f1 = phase(
            swap(h1, 0, 3),
            swap(h2, 1, 1),
            exchange(c_send, CORE, sizes),
            exchange(small, Y, sizes),
            exchange(h1, CORE, sizes),
        )
        small = joined(small, got)
        g1, h2, h3 = phase(g1, joined(h2, g2), h3)
        k1, g2, g3 = exchange(g1, CORE, sizes), swap(h2, 1, 2), swap(h3, 2, 2)
        (wq,) = unpack(gathers[0], (h1, g1), (f1, k1), (3 * width,))
        proj, rows_b, mask = project(wq, given, small, fast)
        proj, g2, c2, ck = phase(proj, g2, c2, ck)
        h2 = joined(h2, g2)
        g2 = swap(h2, 1, 3)
        mixed0, probs0 = attend(after(proj, h2), mask, 0)
        mixed0, g3, h2 = phase(mixed0, g3, h2)
        h3 = joined(h3, g3)
        f2, g3, f3 = exchange(h2, CORE, sizes), swap(h3, 2, 3), exchange(h3, CORE, sizes)
        mixed1, probs1 = attend(after(proj, h3, mixed0), mask, 1)
        mixed1, g2, f2 = phase(mixed1, g2, f2)
        g2, c_send = phase(g2, joined(c2, ck[1:]))
        k2, cx = exchange(g2, CORE, sizes), exchange(c_send, X, sizes)
        wo, wu = unpack(gathers[1], (h2, g2), (f2, k2), (width, 2 * local_units))
    else:
        parts = (shards[0], w_out.T, w_up, w_down.T)
        pieces = [cut(gather_plain(s)) for s in parts]
        split = lambda pair: ((pair[0],), (pair[1],))
        (wq,) = unpack(None, *split(pieces[0]), (3 * width,))
        (wo,) = unpack(None, *split(pieces[1]), (width,))
        (wu,) = unpack(None, *split(pieces[2]), (2 * local_units,))
        (wd,) = unpack(None, *split(pieces[3]), (2 * local_units,))
        order = lambda value: (value[:1], value[1:3], value[2:])
        given, cot = order(to_owners(rows_in)), order(to_owners(cot_in))
        table, small = tables(b_qv, b_up, (b_out, ln1_gain, ln1_bias, b_down, ln2_gain, ln2_bias))
        small = joined(small, exchange(small, Y, sizes))
        proj, rows_b, mask = project(wq, given, small, fast)
        mixed0, probs0 = attend(proj, mask, 0)
        mixed1, probs1 = attend(proj, mask, 1)

    normed1, scale1, first_b, act, slope = middle(wo, wu, mixed0, mixed1, rows_b, table, small)
    if fast:
        act, g3, f3, cx = phase(act, g3, f3, cx)
        cot = (c0, ck, cx)
        (wd,) = unpack(gathers[2], (h3, g3), (f3, exchange(g3, CORE, sizes)), (2 * local_units,))
    chunks, gz, gzb, sums2, down_own, down_sib = turn(packs[2], wd, act, normed1, cot, table, local_len)

    rows = shard_rows // 4
    if fast:
        down_sib, chunks, gzb = phase(down_sib, chunks, gzb)
        got, core_out = shed(down_sib, 2, 0), exchange(chunks[2:], CORE, sizes)
    gh, sum_up = hidden_back(wd, gzb, slope)
    if fast:
        gh, got, core_out = phase(gh, got, core_out)
        down = [down_own, got]
        send, x_send, gh = phase(
            add_up(down, 8 * rows, 16 * rows), joined(chunks[1:2], core_out[1:2]), gh
        )
        got, x_out = shed(send, 2, 1), exchange(x_send, X, sizes)
    gz1, grad_mixed, sums1, up_own, up_sib = first_back(
        packs[1], wo, wu, gh, gz, normed1, scale1, table, first_b, mixed0, mixed1
    )
    if fast:
        grad_mixed, up_sib, got, x_out = phase(grad_mixed, up_sib, got, x_out)
        down = down + [got]
        send, y_send, grad_mixed = phase(
            add_up(down, 4 * rows, 8 * rows), joined(chunks[:1], core_out[:1], x_out), grad_mixed
        )
        got, got2, y_out = shed(send, 2, 2), shed(up_sib, 1, 0), exchange(y_send, Y, sizes)
    parts0 = attend_back(proj, probs0, grad_mixed, 0)
    if fast:
        head, got2, grad_mixed = phase(parts0[0], got2, grad_mixed)
        parts0 = (head,) + tuple(parts0[1:])
        up = [up_own, got2]
        send2, grad_mixed = phase(add_up(up, 8 * rows, 16 * rows), grad_mixed)
        got2 = shed(send2, 1, 1)
    parts1 = attend_back(proj, probs1, grad_mixed, 1)
    parts = list(parts0) + list(parts1)
    if fast:
        parts[3], got = phase(parts[3], got)
        down = down + [got]
        send = add_up(down, 2 * rows, 4 * rows)
        got = shed(send, 2, 3)
        parts[3], send = phase(parts[3], send)
    chunks2 = input_back(wq, gz1, parts, local_len, fast)
    if fast:
        chunks2, y_out = phase(chunks2, y_out)
    parts[0] = after(parts[0], chunks2)
    qkv_own, qkv_sib = last(packs[0], rows_b, sums1, sums2, sum_up, parts)
    if fast:
        got3, core_x = shed(qkv_sib, 0, 0), exchange(chunks2[2:], CORE, sizes)
        chunks2, qkv_own, got2 = phase(chunks2, qkv_own, got2)
        up = up + [got2]
        send2 = add_up(up, 4 * rows, 8 * rows, time=30)
        send2, got3 = phase(send2, got3)
        got2 = shed(send2, 1, 2)
        got3, core_x = phase(got3, core_x)
        qkv = [qkv_own, got3]
        sent3 = add_up(qkv, 8 * rows, 16 * rows, (0, 1))
        x_send = joined(chunks2[1:2], core_x[1:2])
        got3 = shed(sent3, 0, 1)
        got3, x_send = phase(got3, x_send)
        qkv = qkv + [got3]
        send3 = add_up(qkv, 4 * rows, 8 * rows, (3, 2), [sent3])
        got3 = shed(send3, 0, 2)
        send3, got, x_send = phase(send3, got, x_send)
        down = down + [got]
        send = add_up(down, rows, 2 * rows)
        got, x_x = shed(send, 2, 4), exchange(x_send, X, sizes)
        send, got2 = phase(send, got2)
        up = up + [got2]
        send2 = add_up(up, 2 * rows, 4 * rows)
        got2 = shed(send2, 1, 3)
        got3, send2 = phase(got3, send2)
        qkv = qkv + [got3]
        sent3 = add_up(qkv, 2 * rows, 4 * rows, (4, 3), [send3])
        got3 = shed(sent3, 0, 3)
        sent3, got, x_x = phase(sent3, got, x_x)
        pair1 = add_up(down + [got], 0, rows)
        y_send = joined(chunks2[:1], core_x[:1], x_x)
        got, y_x = exchange(pair1, X, sizes), exchange(y_send, Y, sizes)
        pair1, got2 = phase(pair1, got2)
        up = up + [got2]
        send2 = add_up(up, rows, 2 * rows)
        got2 = shed(send2, 1, 4)
        layer_output = deliver(chunks, core_out, x_out, after(y_out, send2))
        got3, layer_output = phase(got3, layer_output)
        qkv = qkv + [got3]
        send3 = add_up(qkv, rows, 2 * rows, (5, 4), [sent3])
        got3 = shed(send3, 0, 4)
        send3, got, got2 = phase(send3, got, got2)
        pair1 = joined(pair1, got)
        up = up + [got2]
        pair2 = add_up(up, 0, rows)
        got1, got2 = exchange(pair1, CORE, sizes), exchange(pair2, X, sizes)
        got3, pair1, pair2 = phase(got3, pair1, pair2)
        qkv = qkv + [got3]
        sent_last = got3
        piece = add_up(qkv, 0, rows)
        got3 = [exchange(piece, dims, sizes) for dims in (X, CORE, FAR)]
        vec = vectors(after(send3, piece), sent_last, local_width, local_units)
        piece, got1, bup = phase(piece, got1, vec[1])
        vec = (vec[0], bup) + tuple(vec[2:])
        (grad_down,) = settle((pair1, got1), ((0, local_units, "plain"),))
        grad_down, got2 = phase(grad_down, got2)
        pair2 = joined(pair2, got2)
        got2 = exchange(pair2, CORE, sizes)
        pair2, y_x = phase(pair2, y_x)
        grad_x = deliver(chunks2, core_x, x_x, y_x)
        grad_x, *got3 = phase(grad_x, *got3)
        (grad_qkv,) = settle([piece] + got3, ((0, 3 * local_width, "three"),))
        grad_wout, grad_up = settle(
            (pair2, after(got2, grad_qkv)),
            ((0, local_width, "plain"), (local_width, local_width + local_units, "plain")),
        )
        layer_output = layer_output.reshape(micro, seqs, local_len, width)
        grad_x = grad_x.reshape(micro, seqs, local_len, width)
    else:
        layer_output = spread(jnp.repeat(chunks, 2, axis=0))
        grad_x = spread(jnp.repeat(chunks2, 2, axis=0))
        vec = lax.psum(qkv_own[width:].astype(F32), AXES)
        vec = vectors(vec, None, local_width, local_units)
        grad_down = reduce_plain(down_own, down_sib)
        both = reduce_plain(up_own, up_sib)
        grad_wout, grad_up = both[:, :local_width], both[:, local_width:]
        grad_qkv = reduce_plain(qkv_own[:width], qkv_sib[:width])
        grad_qkv = jnp.swapaxes(grad_qkv.reshape(shard_rows, 3, local_width), 0, 1)

    out_bqv, out_bup, g1, s1, bout, g2, s2, bdown = vec
    return (
        layer_output,
        grad_x,
        grad_qkv,
        out_bqv,
        grad_wout.T,
        bout,
        g1,
        s1,
        grad_up,
        out_bup,
        grad_down.T,
        bdown,
        g2,
        s2,
    )


def solution(mesh):
    return jax.shard_map(
        body,
        mesh=mesh,
        in_specs=(
            P(None, "fsdp", "ctx", None),
            P(None, "fsdp", "ctx"),
            P(None, "fsdp", "tp"),
            P(None, "tp"),
            P("tp", "fsdp"),
            P(),
            P(),
            P(),
            P("fsdp", "tp"),
            P("tp"),
            P("tp", "fsdp"),
            P(),
            P(),
            P(),
            P(None, "fsdp", "ctx", None),
        ),
        out_specs=(
            P(None, "fsdp", "ctx", None),
            P(None, "fsdp", "ctx", None),
            P(None, "fsdp", "tp"),
            P(None, "tp"),
            P("tp", "fsdp"),
            P(),
            P(),
            P(),
            P("fsdp", "tp"),
            P("tp"),
            P("tp", "fsdp"),
            P(),
            P(),
            P(),
        ),
        check_vma=False,
    )
```

```python
import jax
import jax.numpy as jnp
from jax import lax
from jax.experimental import pallas as pl
from jax.experimental.pallas import tpu as pltpu
from jax.sharding import PartitionSpec as P

HEAD_DIM = 64
AXES = ("fsdp", "ctx", "tp")
F32 = jnp.float32
BF16 = jnp.bfloat16
NEG = -1e30
NT = (((1,), (1,)), ((), ()))
VMEM = pl.BlockSpec(memory_space=pltpu.VMEM)
SMEM = pl.BlockSpec(memory_space=pltpu.SMEM)
ANY = pl.BlockSpec(memory_space=pl.ANY)


def partner(dim, z, c, t):
    if dim == "core":
        return z, c ^ 1, t
    if dim == "x":
        return z, c ^ 2, t
    if dim == "x+core":
        return z, c ^ 3, t
    if dim == "y":
        return z, c, t ^ 1
    return z ^ int(dim[1:]), c, t


def exchange(value, dims, sizes):
    nz, nc, nt = sizes
    pairs = []
    for z in range(nz):
        for c in range(nc):
            for t in range(nt):
                tz, tc, tt = partner(dims[c & 1], z, c, t)
                pairs.append(((z * nc + c) * nt + t, (tz * nc + tc) * nt + tt))
    return lax.ppermute(value, AXES, pairs)


GATHER = (
    (("z2", "z1", "y", "x"), ("z1", "z2", "x", "y")),
    (("z2", "z1", "y", "x"), ("z1", "z2", "x", "y")),
    (("x", "z2", "z1", "y"), ("y", "x", "z2", "z1")),
)
SCATTER = (
    (("x", "y", "z1", "z2"), ("y", "x", "z2", "z1")),
    (("x", "y", "z1", "z2"), ("z1", "z2", "y", "x")),
    (("y", "x", "z1", "z2"), ("z1", "z2", "x", "y")),
)
CORE = ("core", "core")
X = ("x", "x")
FAR = ("x+core", "x+core")
Y = ("y", "y")


def piece_place(order, core, here, index):
    z, x, t = here
    for bit, dim in enumerate(order):
        flip = (index >> bit) & 1
        if dim == "x":
            x = x ^ flip
        elif dim == "y":
            t = t ^ flip
        else:
            z = z ^ (flip * int(dim[1:]))
    return z * 4 + x * 2 + core, t


def places(orders):
    if orders is None:
        return [(i, half) for half in range(2) for i in range(16)]
    c = lax.axis_index("ctx")
    here = (lax.axis_index("fsdp"), c >> 1, lax.axis_index("tp"))
    spots = []
    for core in (c & 1, 1 - (c & 1)):
        for i in range(16):
            r0, t0 = piece_place(orders[0], core, here, i)
            r1, t1 = piece_place(orders[1], core, here, i)
            spots.append((jnp.where(core == 0, r0, r1), jnp.where(core == 0, t0, t1)))
    return spots


def packing(orders):
    return tuple(order[::-1] for order in orders)


def after(value, *first):
    return lax.optimization_barrier((value, first))[0]


def phase(*values):
    return lax.optimization_barrier(values)


def at_rows(place, count, unit=0):
    start = place * count
    return pl.ds(start if isinstance(start, int) else pl.multiple_of(start, unit or count), count)


def piece_copies(spots, near, far, sem, whole, low, cols, base=0):
    rows = whole.shape[0] // 16
    copies = []
    each = 16 // len(near)
    for half, refs in ((0, near), (1, far)):
        for i in range(16):
            row, col = spots[half * 16 + i]
            copy = pltpu.make_async_copy(
                refs[i // each].at[pl.ds(i % each * rows, rows), pl.ds(low, cols)],
                whole.at[at_rows(row, rows), at_rows(col, cols, 128)],
                sem.at[base + half * 16 + i],
            )
            copy.start()
            copies.append(copy)
    return copies


def pack(spots, own_ref, sib_ref, whole, low, cols):
    rows = whole.shape[0] // 16
    for half, ref in ((0, own_ref), (1, sib_ref)):
        for i in range(16):
            row, col = spots[half * 16 + i]
            ref[i * rows : (i + 1) * rows, low : low + cols] = whole[at_rows(row, rows), at_rows(col, cols, 128)]


def finish(copies):
    for copy in copies:
        copy.wait()


def tiles(count, step):
    def run(one):
        lax.fori_loop(0, count // step, lambda i, carry: (one(pl.multiple_of(i * step, step)), carry)[1], 0)

    return run


def row_mean(value):
    return jnp.mean(value, axis=-1, keepdims=True)


def struct(shape, dtype):
    return jax.ShapeDtypeStruct(shape, dtype)


def call(kernel, name, outs, specs, out_specs, scratch, time, room, args):
    return pl.pallas_call(
        kernel,
        name=name,
        out_shape=outs,
        in_specs=specs,
        out_specs=out_specs,
        scratch_shapes=scratch,
        compiler_params=pltpu.CompilerParams(vmem_limit_bytes=room << 20),
        cost_estimate=pl.CostEstimate(flops=time * 10**9, transcendentals=0, bytes_accessed=10**6),
    )(*args)


B_OUT, GAIN1, SHIFT1, B_DOWN, GAIN2, SHIFT2 = range(6)


def unpack_kernel(*refs, orders, count):
    near, far, outs, sem = refs[:count], refs[count : 2 * count], refs[2 * count : -1], refs[-1]
    copies = []
    spots = places(orders)
    low = 0
    for i, out in enumerate(outs):
        cols = out.shape[1] // 2
        copies += piece_copies(spots, near, far, sem, out, low, cols, 32 * i)
        low += cols
    finish(copies)


def unpack(orders, near, far, widths):
    count = len(near)
    rows = near[0].shape[0] * count
    return call(
        lambda *refs: unpack_kernel(*refs, orders=orders, count=count),
        "unpack",
        tuple(struct((rows, width), BF16) for width in widths),
        [ANY] * (2 * count),
        (VMEM,) * len(widths),
        [pltpu.SemaphoreType.DMA((32 * len(widths),))],
        5,
        2,
        tuple(near) + tuple(far),
    )


def sources(refs, fast):
    c = lax.axis_index("ctx") if fast else 0
    own, core, x = refs
    return [(c ^ 0, own, 0), (c ^ 1, core, 0), (c ^ 2, x, 0), (c ^ 3, x, 1)]


def tables_kernel(qv_ref, up_ref, *refs):
    rows, (table_ref, small_ref) = refs[:-2], refs[-2:]
    table_ref[...] = jnp.zeros_like(table_ref)
    for i, ref in enumerate(rows):
        table_ref[i : i + 1, :] = ref[...][None]
    width = qv_ref.shape[1]
    small_ref[:, :width] = qv_ref[0:1, :]
    small_ref[:, width : 2 * width] = qv_ref[1:2, :]
    small_ref[:, 2 * width :] = up_ref[...][None]


def tables(b_qv, b_up, rows):
    return call(
        tables_kernel,
        "tables",
        (struct((8, rows[0].shape[0]), F32), struct((1, b_qv.size + b_up.size), F32)),
        [VMEM] * (2 + len(rows)),
        (VMEM, VMEM),
        [],
        1,
        3,
        (b_qv, b_up) + tuple(rows),
    )


def project_kernel(weight_ref, own_ref, core_ref, far_ref, small_ref, proj_ref, x_ref, mask_ref, ids, *, fast):
    block = own_ref.shape[1] - 8
    count = 4
    for spot, ref, i in sources((own_ref, core_ref, far_ref), fast):
        x_ref[pl.ds(pl.multiple_of(spot * block, block), block), :] = ref[i, 0:block, :]
        ids[pl.ds(spot, 1), :] = ref[i, block:, 0:block].astype(F32)[0:1]
    for kb in range(count):
        column = jnp.broadcast_to(ids[kb : kb + 1], (block, block)).T
        for qb in range(count):
            mask_ref[kb * block : (kb + 1) * block, qb * block : (qb + 1) * block] = jnp.where(
                column == jnp.broadcast_to(ids[qb : qb + 1], (block, block)), 0.0, NEG
            )
    width = proj_ref.shape[1] // 6
    for y in range(2):
        row = pl.ds(lax.axis_index("tp") ^ y, 1)
        for which in range(3):
            at = (y * 3 + which) * width
            value = jnp.dot(x_ref[...], weight_ref[:, at : at + width], preferred_element_type=F32)
            if which != 1:
                low = 0 if which == 0 else width
                value = value + small_ref[row, low : low + width]
            proj_ref[:, at : at + width] = value.astype(BF16)


def project(weight, given, small, fast):
    width, wide = weight.shape
    block = given[0].shape[1] - 8
    length = 4 * block
    return call(
        lambda *refs: project_kernel(*refs, fast=fast),
        "project",
        (
            struct((length, wide), BF16),
            struct((length, width), BF16),
            struct((length, length), F32),
        ),
        [VMEM] * 5,
        (VMEM,) * 3,
        [pltpu.VMEM((8, block), F32)],
        5,
        3,
        (weight,) + tuple(given) + (small,),
    )


def attend_kernel(proj_ref, mask_ref, o_ref, p_ref, *, y):
    length = proj_ref.shape[0]
    pairs = o_ref.shape[1] // 128
    lane = lax.broadcasted_iota(jnp.int32, (1, 128), 1)

    def pair(g, carry):
        take = lambda which: proj_ref[:, pl.ds(pl.multiple_of(((y * 3 + which) * pairs + g) * 128, 128), 128)]
        query = take(0) * jnp.asarray(0.125, BF16)
        keys = take(1)
        values_t = take(2).T
        outs = []
        for head in range(2):
            here = (lane >= 64 * head) & (lane < 64 * head + 64)
            only = jnp.where(here, keys, jnp.zeros_like(keys))
            row = []
            for at in range(0, length, 256):
                scores = lax.dot_general(only, query[at : at + 256], NT, preferred_element_type=F32)
                scores = scores + mask_ref[:, at : at + 256]
                top = jnp.max(scores, axis=0, keepdims=True)
                raised = jnp.exp(scores - top)
                total = jnp.sum(raised, axis=0, keepdims=True)
                probs = (raised * (1.0 / total)).astype(BF16)
                p_ref[2 * g + head, :, at : at + 256] = probs
                row.append(
                    jnp.dot(values_t[64 * head : 64 * head + 64], probs, preferred_element_type=F32)
                )
            outs.append(jnp.concatenate(row, axis=1))
        both = jnp.concatenate(outs, axis=0).astype(BF16)
        o_ref[:, pl.ds(pl.multiple_of(g * 128, 128), 128)] = both.T
        return carry

    lax.fori_loop(0, pairs, pair, 0)


def attend(proj, mask, y):
    length, wide = proj.shape
    half = wide // 6
    return call(
        lambda *refs: attend_kernel(*refs, y=y),
        "attend",
        (struct((length, half), BF16), struct((half // HEAD_DIM, length, length), BF16)),
        [VMEM, VMEM],
        (VMEM, VMEM),
        [],
        12,
        3,
        (proj, mask),
    )


def middle_kernel(
    w_out, w_up, mixed0_ref, mixed1_ref, x_ref, table_ref, small_ref,
    normed_ref, scale_ref, first_ref, act_ref, slope_ref,
):
    length, units = act_ref.shape
    narrow, half = w_out.shape[1] // 2, units // 2
    normed_ref[...] = lax.dot_general(
        mixed0_ref[...], w_out[:, :narrow], NT, preferred_element_type=F32
    ) + lax.dot_general(mixed1_ref[...], w_out[:, narrow:], NT, preferred_element_type=F32)

    @tiles(length, 128)
    def _(at):
        here = pl.ds(at, 128)
        value = x_ref[here, :].astype(F32) + normed_ref[here, :] + table_ref[B_OUT : B_OUT + 1, :]
        centred = value - row_mean(value)
        scale = lax.rsqrt(row_mean(centred * centred) + 1e-12)
        unit = centred * scale
        normed_ref[here, :] = unit
        scale_ref[here, :] = scale
        first_ref[here, :] = (
            unit * table_ref[GAIN1 : GAIN1 + 1, :] + table_ref[SHIFT1 : SHIFT1 + 1, :]
        ).astype(BF16)

    for y in range(2):
        row = pl.ds(lax.axis_index("tp") ^ y, 1)

        @tiles(half, 512)
        def _(at):
            here = pl.ds(pl.multiple_of(y * half + at, 512), 512)
            bias = small_ref[row, pl.ds(pl.multiple_of(2 * narrow + at, 512), 512)]
            hidden = jnp.dot(first_ref[...], w_up[:, here], preferred_element_type=F32) + bias
            phi = 0.5 + 0.5 * lax.erf(hidden * 0.7071067811865476)
            act_ref[:, here] = (hidden * phi).astype(BF16)
            bell = jnp.exp(-0.5 * hidden * hidden) * 0.3989422804014327
            slope_ref[:, here] = (phi + hidden * bell).astype(BF16)


def middle(w_out, w_up, mixed0, mixed1, x, table, small):
    length, width = x.shape
    units = w_up.shape[1]
    return call(
        middle_kernel,
        "middle",
        (
            struct((length, width), F32),
            struct((length, 1), F32),
            struct((length, width), BF16),
            struct((length, units), BF16),
            struct((length, units), BF16),
        ),
        [VMEM] * 7,
        (VMEM,) * 5,
        [],
        12,
        6,
        (w_out, w_up, mixed0, mixed1, x, table, small),
    )


def turn_kernel(
    weight_ref, act_ref, normed_ref, own_ref, core_ref, far_ref, table_ref,
    chunks_ref, gz_ref, gzb_ref, sums_ref, down_own, down_sib, full, cot_ref, *, orders,
):
    length = act_ref.shape[0]
    block = chunks_ref.shape[1]
    for spot, ref, i in sources((own_ref, core_ref, far_ref), orders is not None):
        cot_ref[pl.ds(pl.multiple_of(spot * block, block), block), :] = ref[i]
    gz_ref[...] = lax.dot_general(act_ref[...], weight_ref[...], NT, preferred_element_type=F32)
    sums_ref[...] = jnp.zeros_like(sums_ref)
    row = lambda which: table_ref[which : which + 1, :]

    @tiles(length, 128)
    def _(at):
        here = pl.ds(at, 128)
        value = normed_ref[here, :] * row(GAIN1) + row(SHIFT1) + gz_ref[here, :] + row(B_DOWN)
        centred = value - row_mean(value)
        scale = lax.rsqrt(row_mean(centred * centred) + 1e-12)
        unit = centred * scale
        result = (unit * row(GAIN2) + row(SHIFT2)).astype(BF16)
        chunk = lax.div(at, block)
        if orders is not None:
            c = lax.axis_index("ctx") ^ chunk
            chunk = (c & 1) * 2 + (c >> 1)
        chunks_ref[chunk, pl.ds(pl.multiple_of(lax.rem(at, block), 128), 128), :] = result
        coming = cot_ref[here, :].astype(F32)
        raised = coming * row(GAIN2)
        back = scale * (raised - row_mean(raised) - unit * row_mean(raised * unit))
        gz_ref[here, :] = back
        gzb_ref[here, :] = back.astype(BF16)
        sums_ref[0:1, :] += jnp.sum(coming * unit, axis=0, keepdims=True)
        sums_ref[1:2, :] += jnp.sum(coming, axis=0, keepdims=True)
        sums_ref[2:3, :] += jnp.sum(back, axis=0, keepdims=True)

    back_t = gzb_ref[...].T

    @tiles(full.shape[1], 1024)
    def _(at):
        here = pl.ds(at, 1024)
        full[:, here] = jnp.dot(back_t, act_ref[:, here], preferred_element_type=F32).astype(BF16)

    pack(places(orders), down_own, down_sib, full, 0, down_own.shape[1])


def turn(orders, weight, act, normed, cot, table, chunk):
    length, units = act.shape
    width = normed.shape[1]
    piece = struct((width, units // 2), BF16)
    return call(
        lambda *refs: turn_kernel(*refs, orders=orders),
        "turn",
        (
            struct((length // chunk, chunk, width), BF16),
            struct((length, width), F32),
            struct((length, width), BF16),
            struct((8, width), F32),
            piece,
            piece,
        ),
        [VMEM] * 7,
        (VMEM,) * 6,
        [pltpu.VMEM((width, units), BF16), pltpu.VMEM((length, width), BF16)],
        14,
        10,
        (weight, act, normed) + tuple(cot) + (table,),
    )


def hidden_back_kernel(weight_ref, gzb_ref, slope_ref, gh_ref, sum_ref):
    @tiles(gh_ref.shape[1], 512)
    def _(at):
        here = pl.ds(at, 512)
        back = jnp.dot(gzb_ref[...], weight_ref[:, here], preferred_element_type=F32)
        back = (back * slope_ref[:, here].astype(F32)).astype(BF16)
        gh_ref[:, here] = back
        sum_ref[:, here] = jnp.sum(back.astype(F32), axis=0, keepdims=True)


def hidden_back(weight, gzb, slope):
    length, units = slope.shape
    return call(
        hidden_back_kernel,
        "hidden_back",
        (struct((length, units), BF16), struct((1, units), F32)),
        [VMEM] * 3,
        (VMEM, VMEM),
        [],
        12,
        3,
        (weight, gzb, slope),
    )


def first_back_kernel(
    w_out, w_up, gh_ref, gz_ref, normed_ref, scale_ref, table_ref, first_ref, mixed0_ref, mixed1_ref,
    gz1_ref, gm_ref, sums_ref, pieces_own, pieces_sib, branch, d_out, d_up, *, orders,
):
    narrow = w_out.shape[1] // 2
    half = w_up.shape[1] // 2
    length = gh_ref.shape[0]
    first_t = first_ref[...].T
    spots = places(orders)

    @tiles(d_up.shape[1], 1024)
    def _(at):
        here = pl.ds(at, 1024)
        d_up[:, here] = jnp.dot(first_t, gh_ref[:, here], preferred_element_type=F32).astype(BF16)

    pack(spots, pieces_own, pieces_sib, d_up, narrow, half)
    gz1_ref[...] = lax.dot_general(gh_ref[...], w_up[...], NT, preferred_element_type=F32)
    sums_ref[...] = jnp.zeros_like(sums_ref)

    @tiles(length, 128)
    def _(at):
        here = pl.ds(at, 128)
        coming = gz_ref[here, :] + gz1_ref[here, :]
        unit = normed_ref[here, :]
        raised = coming * table_ref[GAIN1 : GAIN1 + 1, :]
        back = scale_ref[here, :] * (raised - row_mean(raised) - unit * row_mean(raised * unit))
        gz1_ref[here, :] = back
        branch[here, :] = back.astype(BF16)
        sums_ref[0:1, :] += jnp.sum(coming * unit, axis=0, keepdims=True)
        sums_ref[1:2, :] += jnp.sum(coming, axis=0, keepdims=True)
        sums_ref[2:3, :] += jnp.sum(back, axis=0, keepdims=True)

    branch_t = branch[...].T
    d_out[:, :narrow] = jnp.dot(branch_t, mixed0_ref[...], preferred_element_type=F32).astype(BF16)
    d_out[:, narrow:] = jnp.dot(branch_t, mixed1_ref[...], preferred_element_type=F32).astype(BF16)
    pack(spots, pieces_own, pieces_sib, d_out, 0, narrow)
    gm_ref[...] = jnp.dot(branch[...], w_out[...], preferred_element_type=F32).astype(BF16)


def first_back(orders, w_out, w_up, gh, gz, normed, scale, table, first_b, mixed0, mixed1):
    length, units = gh.shape
    width = gz.shape[1]
    piece = struct((width, (units + width) // 2), BF16)
    return call(
        lambda *refs: first_back_kernel(*refs, orders=orders),
        "first_back",
        (
            struct((length, width), F32),
            struct((length, width), BF16),
            struct((8, width), F32),
            piece,
            piece,
        ),
        [VMEM] * 10,
        (VMEM,) * 5,
        [
            pltpu.VMEM((length, width), BF16),
            pltpu.VMEM((width, width), BF16),
            pltpu.VMEM((width, units), BF16),
        ],
        20,
        12,
        (w_out, w_up, gh, gz, normed, scale, table, first_b, mixed0, mixed1),
    )


def attend_back_kernel(proj_ref, p_ref, gm_ref, dq_ref, dk_ref, dv_ref, dst, dqt, *, y):
    length = proj_ref.shape[0]
    pairs = dq_ref.shape[1] // 128
    lane = lax.broadcasted_iota(jnp.int32, (1, 128), 1)
    low = lane < 64

    def pair(g, carry):
        take = lambda which: proj_ref[:, pl.ds(pl.multiple_of(((y * 3 + which) * pairs + g) * 128, 128), 128)]
        query, keys, values = take(0), take(1), take(2)
        grad = gm_ref[:, pl.ds(pl.multiple_of((y * pairs + g) * 128, 128), 128)]
        keys_t = keys.T
        dks, dvs = [], []
        for head in range(2):
            here = low if head == 0 else jnp.logical_not(low)
            only = jnp.where(here, values, jnp.zeros_like(values))
            for at in range(0, length, 256):
                cols = slice(at, at + 256)
                gp = lax.dot_general(only, grad[cols], NT, preferred_element_type=F32)
                probs = p_ref[2 * g + head, :, cols].astype(F32)
                weighted = jnp.sum(probs * gp, axis=0, keepdims=True)
                dst[:, cols] = (probs * (gp - weighted)).astype(BF16)
            dqt[64 * head : 64 * head + 64, :] = (
                jnp.dot(keys_t[64 * head : 64 * head + 64], dst[...], preferred_element_type=F32) * 0.125
            ).astype(BF16)
            dks.append(jnp.dot(dst[...], query, preferred_element_type=F32))
            dvs.append(jnp.dot(p_ref[2 * g + head], grad, preferred_element_type=F32))
        cols = pl.ds(pl.multiple_of(g * 128, 128), 128)
        dq_ref[:, cols] = dqt[...].T
        dk_ref[:, cols] = (jnp.where(low, dks[0], dks[1]) * 0.125).astype(BF16)
        dv_ref[:, cols] = jnp.where(low, dvs[0], dvs[1]).astype(BF16)
        return carry

    lax.fori_loop(0, pairs, pair, 0)


def attend_back(proj, probs, grad_mixed, y):
    length, wide = proj.shape
    shape = struct((length, wide // 6), BF16)
    return call(
        lambda *refs: attend_back_kernel(*refs, y=y),
        "attend_back",
        (shape, shape, shape),
        [VMEM] * 3,
        (VMEM,) * 3,
        [pltpu.VMEM((length, length), BF16), pltpu.VMEM((128, length), BF16)],
        1,
        4,
        (proj, probs, grad_mixed),
    )


def last_kernel(x_ref, sums1_ref, sums2_ref, sum_up_ref, *refs, orders):
    parts, (pieces_own, pieces_sib, whole, vec) = refs[:6], refs[6:]
    half = parts[0].shape[1]
    rows = whole.shape[0]
    x_t = x_ref[...].T
    sums = [[], []]
    for y in range(2):
        for which in range(3):
            at = (y * 3 + which) * half
            value = parts[y * 3 + which][...]
            whole[:, at : at + half] = jnp.dot(x_t, value, preferred_element_type=F32).astype(BF16)
            if which != 1:
                sums[which // 2].append(jnp.sum(value.astype(F32), axis=0, keepdims=True))
    pack(places(orders), pieces_own, pieces_sib, whole, 0, 3 * half)
    vectors = sums[0] + sums[1] + [ref[i : i + 1, :] for ref in (sums1_ref, sums2_ref) for i in range(3)]
    at = 0
    across = vec.shape[1] // 128
    wide = []
    for vector in vectors + [sum_up_ref[...]]:
        for low in range(0, vector.shape[1], 128):
            wide.append(vector[:, low : low + 128])
    for row in range(8):
        vec[row : row + 1, :] = jnp.concatenate(wide[row * across : (row + 1) * across], axis=1)
    pieces_own[rows:, :] = vec[...].astype(BF16)
    pieces_sib[rows:, :] = vec[...].astype(BF16)


def last(orders, x, sums1, sums2, sum_up, parts):
    length, width = x.shape
    piece = struct((width + 8, 3 * width // 2), BF16)
    return call(
        lambda *refs: last_kernel(*refs, orders=orders),
        "last",
        (piece, piece),
        [VMEM] * 10,
        (VMEM, VMEM),
        [
            pltpu.VMEM((width, 3 * width), BF16),
            pltpu.VMEM((8, 3 * width // 2), F32),
        ],
        10,
        7,
        (x, sums1, sums2, sum_up) + tuple(parts),
    )


def vectors_kernel(one_ref, two_ref, qv_ref, up_ref, *refs):
    t = lax.axis_index("tp")
    rows, cols = one_ref.shape
    across = cols // 128
    value = one_ref[rows - 8 :, :].astype(F32)
    if two_ref is not None:
        value = value + two_ref[rows - 8 :, :].astype(F32)

    def block(at):
        row, low = at // across, at % across * 128
        return value[row : row + 1, low : low + 128]

    def take(out, row, first, other, count):
        for i in range(count):
            one = block(first + i)
            if other != first:
                one = jnp.where(t == 0, one, block(other + i))
            if row is None:
                out[i * 128 : (i + 1) * 128] = one[0]
            else:
                out[row : row + 1, i * 128 : (i + 1) * 128] = one

    narrow, wide = qv_ref.shape[1] // 128, up_ref.shape[0] // 128
    for which in range(2):
        take(qv_ref, which, 2 * which * narrow, (2 * which + 1) * narrow, narrow)
    for i, ref in enumerate(refs):
        take(ref, None, (4 + 2 * i) * narrow, (4 + 2 * i) * narrow, 2 * narrow)
    base = (4 + 2 * len(refs)) * narrow
    take(up_ref, None, base, base + wide, wide)


def vectors(one, two, local_width, local_units):
    shapes = [(2, local_width), (local_units,)] + [(2 * local_width,)] * 6
    given = (one,) if two is None else (one, two)

    def kernel(*refs):
        if two is None:
            refs = (refs[0], None) + refs[1:]
        vectors_kernel(*refs)

    return call(
        kernel,
        "vectors",
        tuple(struct(shape, F32) for shape in shapes),
        [VMEM] * len(given),
        (VMEM,) * 8,
        [],
        1,
        4,
        given,
    )


def add_kernel(*refs, low, high, vec, count):
    terms, out = refs[:-1], refs[-1]
    total = terms[0][low:high, :].astype(F32)
    for term in terms[1:count]:
        total = total + term[low:high, :].astype(F32)
    out[: high - low, :] = total.astype(BF16)
    if vec:
        total = 0.0
        for i in vec:
            total = total + terms[i][terms[i].shape[0] - 8 :, :].astype(F32)
        out[high - low :, :] = total.astype(BF16)


def add_up(terms, low, high, vec=(), lone=(), time=1):
    count, terms = len(terms), list(terms) + list(lone)
    cols = terms[0].shape[1]
    return call(
        lambda *refs: add_kernel(*refs, low=low, high=high, vec=vec, count=count),
        "add",
        struct((high - low + (8 if vec else 0), cols), BF16),
        [VMEM] * len(terms),
        VMEM,
        [],
        time,
        4,
        tuple(terms),
    )


def deliver_kernel(own_ref, core_ref, x_ref, y_ref, out_ref):
    c, t = lax.axis_index("ctx"), lax.axis_index("tp")
    sources = [(own_ref, 0), (core_ref, 0), (x_ref, 0), (x_ref, 1)] + [(y_ref, i) for i in range(4)]
    for i, (ref, at) in enumerate(sources):
        ctx = c ^ ((i & 1) + (i & 2))
        out_ref[ctx * 2 + (t ^ (i >> 2))] = ref[at]


def deliver(own, core, x, y):
    return call(
        deliver_kernel,
        "deliver",
        struct((2 * own.shape[0],) + own.shape[1:], BF16),
        [VMEM] * 4,
        VMEM,
        [],
        3,
        7,
        (own, core, x, y),
    )


def input_back_kernel(weight_ref, gz1_ref, *refs, fast):
    parts, chunks_ref = refs[:6], refs[6]
    half = parts[0].shape[1]
    total = gz1_ref[...]
    for i, part in enumerate(parts):
        total = total + lax.dot_general(
            part[...], weight_ref[:, i * half : (i + 1) * half], NT, preferred_element_type=F32
        )
    total = total.astype(BF16)
    count, block = chunks_ref.shape[:2]
    for i in range(count):
        spot = i
        if fast:
            c = lax.axis_index("ctx") ^ i
            spot = (c & 1) * 2 + (c >> 1)
        chunks_ref[spot] = total[i * block : (i + 1) * block]


def input_back(weight, gz1, parts, chunk, fast):
    length, width = gz1.shape
    return call(
        lambda *refs: input_back_kernel(*refs, fast=fast),
        "input_back",
        struct((length // chunk, chunk, width), BF16),
        [VMEM] * 8,
        VMEM,
        [],
        2,
        3,
        (weight, gz1) + tuple(parts),
    )


def settle_kernel(*refs, cuts, count):
    given, outs, four = refs[:count], refs[count:-1], refs[-1]
    rows = four.shape[0] // 4
    for i in range(4):
        ref = given[i * count // 4]
        owner = lax.axis_index("ctx") ^ ((i & 1) * 2 + (i >> 1))
        low = i % (4 // count) * rows
        four[pl.ds(pl.multiple_of(owner * rows, 16), rows), :] = ref[low : low + rows, :].astype(F32)
    for out, (low, high, form) in zip(outs, cuts):
        if form == "plain":
            out[...] = four[:, low:high]
        else:
            step = (high - low) // 3
            for j in range(3):
                out[j] = four[:, low + j * step : low + (j + 1) * step]


def settle(given, cuts):
    rows, cols = given[0].shape[0] * len(given) // 4, given[0].shape[1]
    shapes = {"plain": lambda n: (4 * rows, n), "three": lambda n: (3, 4 * rows, n // 3)}
    return call(
        lambda *refs: settle_kernel(*refs, cuts=cuts, count=len(given)),
        "settle",
        tuple(struct(shapes[form](high - low), F32) for low, high, form in cuts),
        [VMEM] * len(given),
        (VMEM,) * len(cuts),
        [pltpu.VMEM((4 * rows, cols), F32)],
        3,
        7,
        tuple(given),
    )


def cut(full):
    rows, cols = full.shape
    return full[:, : cols // 2], full[:, cols // 2 :]


def gather_plain(shard):
    rows = lax.all_gather(shard, "fsdp", axis=0, tiled=True)
    return lax.all_gather(rows, "tp", axis=1, tiled=True)


def reduce_plain(own, sib):
    full = jnp.concatenate([own, sib], axis=1)
    part = lax.psum_scatter(full, "tp", scatter_dimension=1, tiled=True)
    part = lax.psum_scatter(part, "fsdp", scatter_dimension=0, tiled=True)
    return lax.psum(part, "ctx").astype(F32)


def body(
    layer_input,
    doc_ids,
    w_qkv,
    b_qv,
    w_out,
    b_out,
    ln1_gain,
    ln1_bias,
    w_up,
    b_up,
    w_down,
    b_down,
    ln2_gain,
    ln2_bias,
    out_grad,
):
    sizes = (lax.axis_size("fsdp"), lax.axis_size("ctx"), lax.axis_size("tp"))
    micro, seqs, local_len, width = layer_input.shape
    length = local_len * sizes[1]
    shard_rows, local_width = w_qkv.shape[1:]
    local_units = w_up.shape[1]
    heads = width // HEAD_DIM
    fast = sizes == (4, 4, 2)
    t = lax.axis_index("tp")
    c = lax.axis_index("ctx")

    def mine(value):
        return lax.dynamic_index_in_dim(value, t, 1, keepdims=False)

    def to_owners(chunks):
        return lax.all_to_all(chunks, "ctx", 0, 0, tiled=True)

    def spread(chunks):
        out = lax.all_to_all(chunks, ("ctx", "tp"), 0, 0, tiled=True)
        return out.reshape(micro, seqs, local_len, width)

    shards = (
        jnp.swapaxes(w_qkv, 0, 1).reshape(shard_rows, 3 * local_width),
        jnp.concatenate([w_out.T, w_up], axis=1),
        w_down.T,
    )
    ids = mine(doc_ids).astype(BF16)[:, None, :]
    ids = jnp.pad(ids, ((0, 0), (0, 7), (0, width - local_len)))
    rows_in = jnp.concatenate([mine(layer_input), ids], axis=1)
    cot_in = mine(out_grad)
    gathers = GATHER if fast else (None,) * 3
    packs = tuple(packing(order) for order in SCATTER) if fast else (None,) * 3

    def swap(value, group, step):
        order = tuple(zip(*GATHER[group])) + (CORE,)
        return exchange(value, order[step], sizes)

    def shed(value, group, step):
        order = (CORE,) + tuple(zip(*SCATTER[group]))
        return exchange(value, order[step], sizes)

    def joined(*parts):
        return jnp.concatenate(parts, axis=0)

    if fast:
        def seen(value):
            return [lax.dynamic_index_in_dim(value, c ^ i, 0, keepdims=True) for i in range(4)]

        part = shard_rows // 4
        h1 = lax.dynamic_slice_in_dim(w_qkv, c * part, part, 1)
        h1 = jnp.swapaxes(h1, 0, 1).reshape(part, 3 * local_width)
        h2, h3 = [lax.dynamic_slice_in_dim(s, c * part, part, 0) for s in shards[1:]]
        g1 = swap(h1, 0, 0)
        h3 = after(h3, h1)
        x0, x1, x2, x3 = seen(after(rows_in, h1))
        g1, g3, x1, x2, x3, h2, cot_in, b_up = phase(g1, swap(h3, 2, 0), x1, x2, x3, h2, cot_in, b_up)
        h1, h3 = joined(h1, g1), joined(h3, g3)
        g1, g3, xk, xx, xd = phase(
            swap(h1, 0, 1), swap(h3, 2, 1), exchange(x1, CORE, sizes), exchange(x2, X, sizes), exchange(x3, FAR, sizes)
        )
        given = (x0, xk, joined(xx, xd))
        h1, h2, h3, cot_in, b_up = phase(joined(h1, g1), h2, joined(h3, g3), cot_in, b_up)
        g1, g2 = swap(h1, 0, 2), swap(h2, 1, 0)
        c0, c1, c2, c3 = seen(cot_in)
        c_send = joined(c1, c3)
        table, small = tables(b_qv, b_up, (b_out, ln1_gain, ln1_bias, b_down, ln2_gain, ln2_bias))
        g1, g2, c_send, small = phase(g1, g2, c_send, small)
        h1, h2, h3 = phase(joined(h1, g1), joined(h2, g2), h3)
        g1, g2, ck, got, f1 = phase(
            swap(h1, 0, 3),
            swap(h2, 1, 1),
            exchange(c_send, CORE, sizes),
            exchange(small, Y, sizes),
            exchange(h1, CORE, sizes),
        )
        small = joined(small, got)
        g1, h2, h3 = phase(g1, joined(h2, g2), h3)
        k1, g2, g3 = exchange(g1, CORE, sizes), swap(h2, 1, 2), swap(h3, 2, 2)
        (wq,) = unpack(gathers[0], (h1, g1), (f1, k1), (3 * width,))
        proj, rows_b, mask = project(wq, given, small, fast)
        proj, g2, c2, ck = phase(proj, g2, c2, ck)
        h2 = joined(h2, g2)
        g2 = swap(h2, 1, 3)
        mixed0, probs0 = attend(after(proj, h2), mask, 0)
        mixed0, g3, h2 = phase(mixed0, g3, h2)
        h3 = joined(h3, g3)
        f2, g3, f3 = exchange(h2, CORE, sizes), swap(h3, 2, 3), exchange(h3, CORE, sizes)
        mixed1, probs1 = attend(after(proj, h3, mixed0), mask, 1)
        mixed1, g2, f2 = phase(mixed1, g2, f2)
        g2, c_send = phase(g2, joined(c2, ck[1:]))
        k2, cx = exchange(g2, CORE, sizes), exchange(c_send, X, sizes)
        wo, wu = unpack(gathers[1], (h2, g2), (f2, k2), (width, 2 * local_units))
    else:
        parts = (shards[0], w_out.T, w_up, w_down.T)
        pieces = [cut(gather_plain(s)) for s in parts]
        split = lambda pair: ((pair[0],), (pair[1],))
        (wq,) = unpack(None, *split(pieces[0]), (3 * width,))
        (wo,) = unpack(None, *split(pieces[1]), (width,))
        (wu,) = unpack(None, *split(pieces[2]), (2 * local_units,))
        (wd,) = unpack(None, *split(pieces[3]), (2 * local_units,))
        order = lambda value: (value[:1], value[1:3], value[2:])
        given, cot = order(to_owners(rows_in)), order(to_owners(cot_in))
        table, small = tables(b_qv, b_up, (b_out, ln1_gain, ln1_bias, b_down, ln2_gain, ln2_bias))
        small = joined(small, exchange(small, Y, sizes))
        proj, rows_b, mask = project(wq, given, small, fast)
        mixed0, probs0 = attend(proj, mask, 0)
        mixed1, probs1 = attend(proj, mask, 1)

    normed1, scale1, first_b, act, slope = middle(wo, wu, mixed0, mixed1, rows_b, table, small)
    if fast:
        act, g3, f3, cx = phase(act, g3, f3, cx)
        cot = (c0, ck, cx)
        (wd,) = unpack(gathers[2], (h3, g3), (f3, exchange(g3, CORE, sizes)), (2 * local_units,))
    chunks, gz, gzb, sums2, down_own, down_sib = turn(packs[2], wd, act, normed1, cot, table, local_len)

    rows = shard_rows // 4
    if fast:
        down_sib, chunks, gzb = phase(down_sib, chunks, gzb)
        got, core_out = shed(down_sib, 2, 0), exchange(chunks[2:], CORE, sizes)
    gh, sum_up = hidden_back(wd, gzb, slope)
    if fast:
        gh, got, core_out = phase(gh, got, core_out)
        down = [down_own, got]
        send, x_send, gh = phase(
            add_up(down, 8 * rows, 16 * rows), joined(chunks[1:2], core_out[1:2]), gh
        )
        got, x_out = shed(send, 2, 1), exchange(x_send, X, sizes)
    gz1, grad_mixed, sums1, up_own, up_sib = first_back(
        packs[1], wo, wu, gh, gz, normed1, scale1, table, first_b, mixed0, mixed1
    )
    if fast:
        grad_mixed, up_sib, got, x_out = phase(grad_mixed, up_sib, got, x_out)
        down = down + [got]
        send, y_send, grad_mixed = phase(
            add_up(down, 4 * rows, 8 * rows), joined(chunks[:1], core_out[:1], x_out), grad_mixed
        )
        got, got2, y_out = shed(send, 2, 2), shed(up_sib, 1, 0), exchange(y_send, Y, sizes)
    parts0 = attend_back(proj, probs0, grad_mixed, 0)
    if fast:
        head, got2, grad_mixed = phase(parts0[0], got2, grad_mixed)
        parts0 = (head,) + tuple(parts0[1:])
        up = [up_own, got2]
        send2, grad_mixed = phase(add_up(up, 8 * rows, 16 * rows), grad_mixed)
        got2 = shed(send2, 1, 1)
    parts1 = attend_back(proj, probs1, grad_mixed, 1)
    parts = list(parts0) + list(parts1)
    if fast:
        parts[3], got = phase(parts[3], got)
        down = down + [got]
        send = add_up(down, 2 * rows, 4 * rows)
        got = shed(send, 2, 3)
        parts[3], send = phase(parts[3], send)
    chunks2 = input_back(wq, gz1, parts, local_len, fast)
    if fast:
        chunks2, y_out = phase(chunks2, y_out)
    parts[0] = after(parts[0], chunks2)
    qkv_own, qkv_sib = last(packs[0], rows_b, sums1, sums2, sum_up, parts)
    if fast:
        got3, core_x = shed(qkv_sib, 0, 0), exchange(chunks2[2:], CORE, sizes)
        chunks2, qkv_own, got2 = phase(chunks2, qkv_own, got2)
        up = up + [got2]
        send2 = add_up(up, 4 * rows, 8 * rows, time=30)
        send2, got3 = phase(send2, got3)
        got2 = shed(send2, 1, 2)
        got3, core_x = phase(got3, core_x)
        qkv = [qkv_own, got3]
        sent3 = add_up(qkv, 8 * rows, 16 * rows, (0, 1))
        x_send = joined(chunks2[1:2], core_x[1:2])
        got3 = shed(sent3, 0, 1)
        got3, x_send = phase(got3, x_send)
        qkv = qkv + [got3]
        send3 = add_up(qkv, 4 * rows, 8 * rows, (3, 2), [sent3])
        got3 = shed(send3, 0, 2)
        send3, got, x_send = phase(send3, got, x_send)
        down = down + [got]
        send = add_up(down, rows, 2 * rows)
        got, x_x = shed(send, 2, 4), exchange(x_send, X, sizes)
        send, got2 = phase(send, got2)
        up = up + [got2]
        send2 = add_up(up, 2 * rows, 4 * rows)
        got2 = shed(send2, 1, 3)
        got3, send2 = phase(got3, send2)
        qkv = qkv + [got3]
        sent3 = add_up(qkv, 2 * rows, 4 * rows, (4, 3), [send3])
        got3 = shed(sent3, 0, 3)
        sent3, got, x_x = phase(sent3, got, x_x)
        pair1 = add_up(down + [got], 0, rows)
        y_send = joined(chunks2[:1], core_x[:1], x_x)
        got, y_x = exchange(pair1, X, sizes), exchange(y_send, Y, sizes)
        pair1, got2 = phase(pair1, got2)
        up = up + [got2]
        send2 = add_up(up, rows, 2 * rows)
        got2 = shed(send2, 1, 4)
        layer_output = deliver(chunks, core_out, x_out, after(y_out, send2))
        got3, layer_output = phase(got3, layer_output)
        qkv = qkv + [got3]
        send3 = add_up(qkv, rows, 2 * rows, (5, 4), [sent3])
        got3 = shed(send3, 0, 4)
        send3, got, got2 = phase(send3, got, got2)
        pair1 = joined(pair1, got)
        up = up + [got2]
        pair2 = add_up(up, 0, rows)
        got1, got2 = exchange(pair1, CORE, sizes), exchange(pair2, X, sizes)
        got3, pair1, pair2 = phase(got3, pair1, pair2)
        qkv = qkv + [got3]
        sent_last = got3
        piece = add_up(qkv, 0, rows)
        got3 = [exchange(piece, dims, sizes) for dims in (X, CORE, FAR)]
        vec = vectors(after(send3, piece), sent_last, local_width, local_units)
        piece, got1, bup = phase(piece, got1, vec[1])
        vec = (vec[0], bup) + tuple(vec[2:])
        (grad_down,) = settle((pair1, got1), ((0, local_units, "plain"),))
        grad_down, got2 = phase(grad_down, got2)
        pair2 = joined(pair2, got2)
        got2 = exchange(pair2, CORE, sizes)
        pair2, y_x = phase(pair2, y_x)
        grad_x = deliver(chunks2, core_x, x_x, y_x)
        grad_x, *got3 = phase(grad_x, *got3)
        (grad_qkv,) = settle([piece] + got3, ((0, 3 * local_width, "three"),))
        grad_wout, grad_up = settle(
            (pair2, after(got2, grad_qkv)),
            ((0, local_width, "plain"), (local_width, local_width + local_units, "plain")),
        )
        layer_output = layer_output.reshape(micro, seqs, local_len, width)
        grad_x = grad_x.reshape(micro, seqs, local_len, width)
    else:
        layer_output = spread(jnp.repeat(chunks, 2, axis=0))
        grad_x = spread(jnp.repeat(chunks2, 2, axis=0))
        vec = lax.psum(qkv_own[width:].astype(F32), AXES)
        vec = vectors(vec, None, local_width, local_units)
        grad_down = reduce_plain(down_own, down_sib)
        both = reduce_plain(up_own, up_sib)
        grad_wout, grad_up = both[:, :local_width], both[:, local_width:]
        grad_qkv = reduce_plain(qkv_own[:width], qkv_sib[:width])
        grad_qkv = jnp.swapaxes(grad_qkv.reshape(shard_rows, 3, local_width), 0, 1)

    out_bqv, out_bup, g1, s1, bout, g2, s2, bdown = vec
    return (
        layer_output,
        grad_x,
        grad_qkv,
        out_bqv,
        grad_wout.T,
        bout,
        g1,
        s1,
        grad_up,
        out_bup,
        grad_down.T,
        bdown,
        g2,
        s2,
    )


def solution(mesh):
    return jax.shard_map(
        body,
        mesh=mesh,
        in_specs=(
            P(None, "fsdp", "ctx", None),
            P(None, "fsdp", "ctx"),
            P(None, "fsdp", "tp"),
            P(None, "tp"),
            P("tp", "fsdp"),
            P(),
            P(),
            P(),
            P("fsdp", "tp"),
            P("tp"),
            P("tp", "fsdp"),
            P(),
            P(),
            P(),
            P(None, "fsdp", "ctx", None),
        ),
        out_specs=(
            P(None, "fsdp", "ctx", None),
            P(None, "fsdp", "ctx", None),
            P(None, "fsdp", "tp"),
            P(None, "tp"),
            P("tp", "fsdp"),
            P(),
            P(),
            P(),
            P("fsdp", "tp"),
            P("tp"),
            P("tp", "fsdp"),
            P(),
            P(),
            P(),
        ),
        check_vma=False,
    )
```

```python
import jax
import jax.numpy as jnp
from jax import lax
from jax.experimental import pallas as pl
from jax.experimental.pallas import tpu as pltpu
from jax.sharding import PartitionSpec as P

HEAD_DIM = 64
AXES = ("fsdp", "ctx", "tp")
F32 = jnp.float32
BF16 = jnp.bfloat16
NEG = -1e30
NT = (((1,), (1,)), ((), ()))
VMEM = pl.BlockSpec(memory_space=pltpu.VMEM)
SMEM = pl.BlockSpec(memory_space=pltpu.SMEM)
ANY = pl.BlockSpec(memory_space=pl.ANY)


def partner(dim, z, c, t):
    if dim == "core":
        return z, c ^ 1, t
    if dim == "x":
        return z, c ^ 2, t
    if dim == "x+core":
        return z, c ^ 3, t
    if dim == "y":
        return z, c, t ^ 1
    return z ^ int(dim[1:]), c, t


def exchange(value, dims, sizes):
    nz, nc, nt = sizes
    pairs = []
    for z in range(nz):
        for c in range(nc):
            for t in range(nt):
                tz, tc, tt = partner(dims[c & 1], z, c, t)
                pairs.append(((z * nc + c) * nt + t, (tz * nc + tc) * nt + tt))
    return lax.ppermute(value, AXES, pairs)


GATHER = (
    (("z2", "z1", "y", "x"), ("z1", "z2", "x", "y")),
    (("z2", "z1", "y", "x"), ("z1", "z2", "x", "y")),
    (("x", "z2", "z1", "y"), ("y", "x", "z2", "z1")),
)
SCATTER = (
    (("x", "y", "z1", "z2"), ("y", "x", "z2", "z1")),
    (("x", "y", "z1", "z2"), ("z1", "z2", "y", "x")),
    (("y", "x", "z1", "z2"), ("z1", "z2", "x", "y")),
)
CORE = ("core", "core")
X = ("x", "x")
FAR = ("x+core", "x+core")
Y = ("y", "y")


def piece_place(order, core, here, index):
    z, x, t = here
    for bit, dim in enumerate(order):
        flip = (index >> bit) & 1
        if dim == "x":
            x = x ^ flip
        elif dim == "y":
            t = t ^ flip
        else:
            z = z ^ (flip * int(dim[1:]))
    return z * 4 + x * 2 + core, t


def places(orders):
    if orders is None:
        return [(i, half) for half in range(2) for i in range(16)]
    c = lax.axis_index("ctx")
    here = (lax.axis_index("fsdp"), c >> 1, lax.axis_index("tp"))
    spots = []
    for core in (c & 1, 1 - (c & 1)):
        for i in range(16):
            r0, t0 = piece_place(orders[0], core, here, i)
            r1, t1 = piece_place(orders[1], core, here, i)
            spots.append((jnp.where(core == 0, r0, r1), jnp.where(core == 0, t0, t1)))
    return spots


def packing(orders):
    return tuple(order[::-1] for order in orders)


def after(value, *first):
    return lax.optimization_barrier((value, first))[0]


def phase(*values):
    return lax.optimization_barrier(values)


def at_rows(place, count, unit=0):
    start = place * count
    return pl.ds(start if isinstance(start, int) else pl.multiple_of(start, unit or count), count)


def piece_copies(spots, near, far, sem, whole, low, cols, base=0):
    rows = whole.shape[0] // 16
    copies = []
    each = 16 // len(near)
    for half, refs in ((0, near), (1, far)):
        for i in range(16):
            row, col = spots[half * 16 + i]
            copy = pltpu.make_async_copy(
                refs[i // each].at[pl.ds(i % each * rows, rows), pl.ds(low, cols)],
                whole.at[at_rows(row, rows), at_rows(col, cols, 128)],
                sem.at[base + half * 16 + i],
            )
            copy.start()
            copies.append(copy)
    return copies


def pack(spots, own_ref, sib_ref, whole, low, cols):
    rows = whole.shape[0] // 16
    for half, ref in ((0, own_ref), (1, sib_ref)):
        for i in range(16):
            row, col = spots[half * 16 + i]
            ref[i * rows : (i + 1) * rows, low : low + cols] = whole[at_rows(row, rows), at_rows(col, cols, 128)]


def finish(copies):
    for copy in copies:
        copy.wait()


def tiles(count, step):
    def run(one):
        lax.fori_loop(0, count // step, lambda i, carry: (one(pl.multiple_of(i * step, step)), carry)[1], 0)

    return run


def row_mean(value):
    return jnp.mean(value, axis=-1, keepdims=True)


def struct(shape, dtype):
    return jax.ShapeDtypeStruct(shape, dtype)


def call(kernel, name, outs, specs, out_specs, scratch, time, room, args):
    return pl.pallas_call(
        kernel,
        name=name,
        out_shape=outs,
        in_specs=specs,
        out_specs=out_specs,
        scratch_shapes=scratch,
        compiler_params=pltpu.CompilerParams(vmem_limit_bytes=room << 20),
        cost_estimate=pl.CostEstimate(flops=time * 10**9, transcendentals=0, bytes_accessed=10**6),
    )(*args)


B_OUT, GAIN1, SHIFT1, B_DOWN, GAIN2, SHIFT2 = range(6)


def unpack_kernel(*refs, orders, count):
    near, far, outs, sem = refs[:count], refs[count : 2 * count], refs[2 * count : -1], refs[-1]
    copies = []
    spots = places(orders)
    low = 0
    for i, out in enumerate(outs):
        cols = out.shape[1] // 2
        copies += piece_copies(spots, near, far, sem, out, low, cols, 32 * i)
        low += cols
    finish(copies)


def unpack(orders, near, far, widths):
    count = len(near)
    rows = near[0].shape[0] * count
    return call(
        lambda *refs: unpack_kernel(*refs, orders=orders, count=count),
        "unpack",
        tuple(struct((rows, width), BF16) for width in widths),
        [ANY] * (2 * count),
        (VMEM,) * len(widths),
        [pltpu.SemaphoreType.DMA((32 * len(widths),))],
        5,
        2,
        tuple(near) + tuple(far),
    )


def sources(refs, fast):
    c = lax.axis_index("ctx") if fast else 0
    own, core, x = refs
    return [(c ^ 0, own, 0), (c ^ 1, core, 0), (c ^ 2, x, 0), (c ^ 3, x, 1)]


def tables_kernel(qv_ref, up_ref, *refs):
    rows, (table_ref, small_ref) = refs[:-2], refs[-2:]
    table_ref[...] = jnp.zeros_like(table_ref)
    for i, ref in enumerate(rows):
        table_ref[i : i + 1, :] = ref[...][None]
    width = qv_ref.shape[1]
    small_ref[:, :width] = qv_ref[0:1, :]
    small_ref[:, width : 2 * width] = qv_ref[1:2, :]
    small_ref[:, 2 * width :] = up_ref[...][None]


def tables(b_qv, b_up, rows):
    return call(
        tables_kernel,
        "tables",
        (struct((8, rows[0].shape[0]), F32), struct((1, b_qv.size + b_up.size), F32)),
        [VMEM] * (2 + len(rows)),
        (VMEM, VMEM),
        [],
        1,
        3,
        (b_qv, b_up) + tuple(rows),
    )


def project_kernel(weight_ref, own_ref, core_ref, far_ref, small_ref, proj_ref, x_ref, mask_ref, ids, *, fast):
    block = own_ref.shape[1] - 8
    count = 4
    for spot, ref, i in sources((own_ref, core_ref, far_ref), fast):
        x_ref[pl.ds(pl.multiple_of(spot * block, block), block), :] = ref[i, 0:block, :]
        ids[pl.ds(spot, 1), :] = ref[i, block:, 0:block].astype(F32)[0:1]
    for kb in range(count):
        column = jnp.broadcast_to(ids[kb : kb + 1], (block, block)).T
        for qb in range(count):
            mask_ref[kb * block : (kb + 1) * block, qb * block : (qb + 1) * block] = jnp.where(
                column == jnp.broadcast_to(ids[qb : qb + 1], (block, block)), 0.0, NEG
            )
    width = proj_ref.shape[1] // 6
    for y in range(2):
        row = pl.ds(lax.axis_index("tp") ^ y, 1)
        for which in range(3):
            at = (y * 3 + which) * width
            value = jnp.dot(x_ref[...], weight_ref[:, at : at + width], preferred_element_type=F32)
            if which != 1:
                low = 0 if which == 0 else width
                value = value + small_ref[row, low : low + width]
            proj_ref[:, at : at + width] = value.astype(BF16)


def project(weight, given, small, fast):
    width, wide = weight.shape
    block = given[0].shape[1] - 8
    length = 4 * block
    return call(
        lambda *refs: project_kernel(*refs, fast=fast),
        "project",
        (
            struct((length, wide), BF16),
            struct((length, width), BF16),
            struct((length, length), F32),
        ),
        [VMEM] * 5,
        (VMEM,) * 3,
        [pltpu.VMEM((8, block), F32)],
        5,
        3,
        (weight,) + tuple(given) + (small,),
    )


def attend_kernel(proj_ref, mask_ref, o_ref, p_ref, *, y):
    length = proj_ref.shape[0]
    pairs = o_ref.shape[1] // 128
    lane = lax.broadcasted_iota(jnp.int32, (1, 128), 1)

    def pair(g, carry):
        take = lambda which: proj_ref[:, pl.ds(pl.multiple_of(((y * 3 + which) * pairs + g) * 128, 128), 128)]
        query = take(0) * jnp.asarray(0.125, BF16)
        keys = take(1)
        values_t = take(2).T
        outs = []
        for head in range(2):
            here = (lane >= 64 * head) & (lane < 64 * head + 64)
            only = jnp.where(here, keys, jnp.zeros_like(keys))
            row = []
            for at in range(0, length, 256):
                scores = lax.dot_general(only, query[at : at + 256], NT, preferred_element_type=F32)
                scores = scores + mask_ref[:, at : at + 256]
                top = jnp.max(scores, axis=0, keepdims=True)
                raised = jnp.exp(scores - top)
                total = jnp.sum(raised, axis=0, keepdims=True)
                probs = (raised * (1.0 / total)).astype(BF16)
                p_ref[2 * g + head, :, at : at + 256] = probs
                row.append(
                    jnp.dot(values_t[64 * head : 64 * head + 64], probs, preferred_element_type=F32)
                )
            outs.append(jnp.concatenate(row, axis=1))
        both = jnp.concatenate(outs, axis=0).astype(BF16)
        o_ref[:, pl.ds(pl.multiple_of(g * 128, 128), 128)] = both.T
        return carry

    lax.fori_loop(0, pairs, pair, 0)


def attend(proj, mask, y):
    length, wide = proj.shape
    half = wide // 6
    return call(
        lambda *refs: attend_kernel(*refs, y=y),
        "attend",
        (struct((length, half), BF16), struct((half // HEAD_DIM, length, length), BF16)),
        [VMEM, VMEM],
        (VMEM, VMEM),
        [],
        12,
        3,
        (proj, mask),
    )


def middle_kernel(
    w_out, w_up, mixed0_ref, mixed1_ref, x_ref, table_ref, small_ref,
    normed_ref, scale_ref, first_ref, act_ref, slope_ref,
):
    length, units = act_ref.shape
    narrow, half = w_out.shape[1] // 2, units // 2
    normed_ref[...] = lax.dot_general(
        mixed0_ref[...], w_out[:, :narrow], NT, preferred_element_type=F32
    ) + lax.dot_general(mixed1_ref[...], w_out[:, narrow:], NT, preferred_element_type=F32)

    @tiles(length, 128)
    def _(at):
        here = pl.ds(at, 128)
        value = x_ref[here, :].astype(F32) + normed_ref[here, :] + table_ref[B_OUT : B_OUT + 1, :]
        centred = value - row_mean(value)
        scale = lax.rsqrt(row_mean(centred * centred) + 1e-12)
        unit = centred * scale
        normed_ref[here, :] = unit
        scale_ref[here, :] = scale
        first_ref[here, :] = (
            unit * table_ref[GAIN1 : GAIN1 + 1, :] + table_ref[SHIFT1 : SHIFT1 + 1, :]
        ).astype(BF16)

    for y in range(2):
        row = pl.ds(lax.axis_index("tp") ^ y, 1)

        @tiles(half, 512)
        def _(at):
            here = pl.ds(pl.multiple_of(y * half + at, 512), 512)
            bias = small_ref[row, pl.ds(pl.multiple_of(2 * narrow + at, 512), 512)]
            hidden = jnp.dot(first_ref[...], w_up[:, here], preferred_element_type=F32) + bias
            phi = 0.5 + 0.5 * lax.erf(hidden * 0.7071067811865476)
            act_ref[:, here] = (hidden * phi).astype(BF16)
            bell = jnp.exp(-0.5 * hidden * hidden) * 0.3989422804014327
            slope_ref[:, here] = (phi + hidden * bell).astype(BF16)


def middle(w_out, w_up, mixed0, mixed1, x, table, small):
    length, width = x.shape
    units = w_up.shape[1]
    return call(
        middle_kernel,
        "middle",
        (
            struct((length, width), F32),
            struct((length, 1), F32),
            struct((length, width), BF16),
            struct((length, units), BF16),
            struct((length, units), BF16),
        ),
        [VMEM] * 7,
        (VMEM,) * 5,
        [],
        12,
        6,
        (w_out, w_up, mixed0, mixed1, x, table, small),
    )


def turn_kernel(
    weight_ref, act_ref, normed_ref, own_ref, core_ref, far_ref, table_ref,
    chunks_ref, gz_ref, gzb_ref, sums_ref, down_own, down_sib, full, cot_ref, *, orders,
):
    length = act_ref.shape[0]
    block = chunks_ref.shape[1]
    for spot, ref, i in sources((own_ref, core_ref, far_ref), orders is not None):
        cot_ref[pl.ds(pl.multiple_of(spot * block, block), block), :] = ref[i]
    gz_ref[...] = lax.dot_general(act_ref[...], weight_ref[...], NT, preferred_element_type=F32)
    sums_ref[...] = jnp.zeros_like(sums_ref)
    row = lambda which: table_ref[which : which + 1, :]

    @tiles(length, 128)
    def _(at):
        here = pl.ds(at, 128)
        value = normed_ref[here, :] * row(GAIN1) + row(SHIFT1) + gz_ref[here, :] + row(B_DOWN)
        centred = value - row_mean(value)
        scale = lax.rsqrt(row_mean(centred * centred) + 1e-12)
        unit = centred * scale
        result = (unit * row(GAIN2) + row(SHIFT2)).astype(BF16)
        chunk = lax.div(at, block)
        if orders is not None:
            c = lax.axis_index("ctx") ^ chunk
            chunk = (c & 1) * 2 + (c >> 1)
        chunks_ref[chunk, pl.ds(pl.multiple_of(lax.rem(at, block), 128), 128), :] = result
        coming = cot_ref[here, :].astype(F32)
        raised = coming * row(GAIN2)
        back = scale * (raised - row_mean(raised) - unit * row_mean(raised * unit))
        gz_ref[here, :] = back
        gzb_ref[here, :] = back.astype(BF16)
        sums_ref[0:1, :] += jnp.sum(coming * unit, axis=0, keepdims=True)
        sums_ref[1:2, :] += jnp.sum(coming, axis=0, keepdims=True)
        sums_ref[2:3, :] += jnp.sum(back, axis=0, keepdims=True)

    back_t = gzb_ref[...].T

    @tiles(full.shape[1], 1024)
    def _(at):
        here = pl.ds(at, 1024)
        full[:, here] = jnp.dot(back_t, act_ref[:, here], preferred_element_type=F32).astype(BF16)

    pack(places(orders), down_own, down_sib, full, 0, down_own.shape[1])


def turn(orders, weight, act, normed, cot, table, chunk):
    length, units = act.shape
    width = normed.shape[1]
    piece = struct((width, units // 2), BF16)
    return call(
        lambda *refs: turn_kernel(*refs, orders=orders),
        "turn",
        (
            struct((length // chunk, chunk, width), BF16),
            struct((length, width), F32),
            struct((length, width), BF16),
            struct((8, width), F32),
            piece,
            piece,
        ),
        [VMEM] * 7,
        (VMEM,) * 6,
        [pltpu.VMEM((width, units), BF16), pltpu.VMEM((length, width), BF16)],
        14,
        10,
        (weight, act, normed) + tuple(cot) + (table,),
    )


def hidden_back_kernel(weight_ref, gzb_ref, slope_ref, gh_ref, sum_ref):
    @tiles(gh_ref.shape[1], 512)
    def _(at):
        here = pl.ds(at, 512)
        back = jnp.dot(gzb_ref[...], weight_ref[:, here], preferred_element_type=F32)
        back = (back * slope_ref[:, here].astype(F32)).astype(BF16)
        gh_ref[:, here] = back
        sum_ref[:, here] = jnp.sum(back.astype(F32), axis=0, keepdims=True)


def hidden_back(weight, gzb, slope):
    length, units = slope.shape
    return call(
        hidden_back_kernel,
        "hidden_back",
        (struct((length, units), BF16), struct((1, units), F32)),
        [VMEM] * 3,
        (VMEM, VMEM),
        [],
        12,
        3,
        (weight, gzb, slope),
    )


def first_back_kernel(
    w_out, w_up, gh_ref, gz_ref, normed_ref, scale_ref, table_ref, first_ref, mixed0_ref, mixed1_ref,
    gz1_ref, gm_ref, sums_ref, pieces_own, pieces_sib, branch, d_out, d_up, *, orders,
):
    narrow = w_out.shape[1] // 2
    half = w_up.shape[1] // 2
    length = gh_ref.shape[0]
    first_t = first_ref[...].T
    spots = places(orders)

    @tiles(d_up.shape[1], 1024)
    def _(at):
        here = pl.ds(at, 1024)
        d_up[:, here] = jnp.dot(first_t, gh_ref[:, here], preferred_element_type=F32).astype(BF16)

    pack(spots, pieces_own, pieces_sib, d_up, narrow, half)
    gz1_ref[...] = lax.dot_general(gh_ref[...], w_up[...], NT, preferred_element_type=F32)
    sums_ref[...] = jnp.zeros_like(sums_ref)

    @tiles(length, 128)
    def _(at):
        here = pl.ds(at, 128)
        coming = gz_ref[here, :] + gz1_ref[here, :]
        unit = normed_ref[here, :]
        raised = coming * table_ref[GAIN1 : GAIN1 + 1, :]
        back = scale_ref[here, :] * (raised - row_mean(raised) - unit * row_mean(raised * unit))
        gz1_ref[here, :] = back
        branch[here, :] = back.astype(BF16)
        sums_ref[0:1, :] += jnp.sum(coming * unit, axis=0, keepdims=True)
        sums_ref[1:2, :] += jnp.sum(coming, axis=0, keepdims=True)
        sums_ref[2:3, :] += jnp.sum(back, axis=0, keepdims=True)

    branch_t = branch[...].T
    d_out[:, :narrow] = jnp.dot(branch_t, mixed0_ref[...], preferred_element_type=F32).astype(BF16)
    d_out[:, narrow:] = jnp.dot(branch_t, mixed1_ref[...], preferred_element_type=F32).astype(BF16)
    pack(spots, pieces_own, pieces_sib, d_out, 0, narrow)
    gm_ref[...] = jnp.dot(branch[...], w_out[...], preferred_element_type=F32).astype(BF16)


def first_back(orders, w_out, w_up, gh, gz, normed, scale, table, first_b, mixed0, mixed1):
    length, units = gh.shape
    width = gz.shape[1]
    piece = struct((width, (units + width) // 2), BF16)
    return call(
        lambda *refs: first_back_kernel(*refs, orders=orders),
        "first_back",
        (
            struct((length, width), F32),
            struct((length, width), BF16),
            struct((8, width), F32),
            piece,
            piece,
        ),
        [VMEM] * 10,
        (VMEM,) * 5,
        [
            pltpu.VMEM((length, width), BF16),
            pltpu.VMEM((width, width), BF16),
            pltpu.VMEM((width, units), BF16),
        ],
        20,
        12,
        (w_out, w_up, gh, gz, normed, scale, table, first_b, mixed0, mixed1),
    )


def attend_back_kernel(proj_ref, p_ref, gm_ref, dq_ref, dk_ref, dv_ref, dst, dqt, *, y):
    length = proj_ref.shape[0]
    pairs = dq_ref.shape[1] // 128
    lane = lax.broadcasted_iota(jnp.int32, (1, 128), 1)
    low = lane < 64

    def pair(g, carry):
        take = lambda which: proj_ref[:, pl.ds(pl.multiple_of(((y * 3 + which) * pairs + g) * 128, 128), 128)]
        query, keys, values = take(0), take(1), take(2)
        grad = gm_ref[:, pl.ds(pl.multiple_of((y * pairs + g) * 128, 128), 128)]
        keys_t = keys.T
        dks, dvs = [], []
        for head in range(2):
            here = low if head == 0 else jnp.logical_not(low)
            only = jnp.where(here, values, jnp.zeros_like(values))
            for at in range(0, length, 256):
                cols = slice(at, at + 256)
                gp = lax.dot_general(only, grad[cols], NT, preferred_element_type=F32)
                probs = p_ref[2 * g + head, :, cols].astype(F32)
                weighted = jnp.sum(probs * gp, axis=0, keepdims=True)
                dst[:, cols] = (probs * (gp - weighted)).astype(BF16)
            dqt[64 * head : 64 * head + 64, :] = (
                jnp.dot(keys_t[64 * head : 64 * head + 64], dst[...], preferred_element_type=F32) * 0.125
            ).astype(BF16)
            dks.append(jnp.dot(dst[...], query, preferred_element_type=F32))
            dvs.append(jnp.dot(p_ref[2 * g + head], grad, preferred_element_type=F32))
        cols = pl.ds(pl.multiple_of(g * 128, 128), 128)
        dq_ref[:, cols] = dqt[...].T
        dk_ref[:, cols] = (jnp.where(low, dks[0], dks[1]) * 0.125).astype(BF16)
        dv_ref[:, cols] = jnp.where(low, dvs[0], dvs[1]).astype(BF16)
        return carry

    lax.fori_loop(0, pairs, pair, 0)


def attend_back(proj, probs, grad_mixed, y):
    length, wide = proj.shape
    shape = struct((length, wide // 6), BF16)
    return call(
        lambda *refs: attend_back_kernel(*refs, y=y),
        "attend_back",
        (shape, shape, shape),
        [VMEM] * 3,
        (VMEM,) * 3,
        [pltpu.VMEM((length, length), BF16), pltpu.VMEM((128, length), BF16)],
        1,
        4,
        (proj, probs, grad_mixed),
    )


def last_kernel(x_ref, sums1_ref, sums2_ref, sum_up_ref, *refs, orders):
    parts, (pieces_own, pieces_sib, whole, vec) = refs[:6], refs[6:]
    half = parts[0].shape[1]
    rows = whole.shape[0]
    x_t = x_ref[...].T
    sums = [[], []]
    for y in range(2):
        for which in range(3):
            at = (y * 3 + which) * half
            value = parts[y * 3 + which][...]
            whole[:, at : at + half] = jnp.dot(x_t, value, preferred_element_type=F32).astype(BF16)
            if which != 1:
                sums[which // 2].append(jnp.sum(value.astype(F32), axis=0, keepdims=True))
    pack(places(orders), pieces_own, pieces_sib, whole, 0, 3 * half)
    vectors = sums[0] + sums[1] + [ref[i : i + 1, :] for ref in (sums1_ref, sums2_ref) for i in range(3)]
    at = 0
    across = vec.shape[1] // 128
    wide = []
    for vector in vectors + [sum_up_ref[...]]:
        for low in range(0, vector.shape[1], 128):
            wide.append(vector[:, low : low + 128])
    for row in range(8):
        vec[row : row + 1, :] = jnp.concatenate(wide[row * across : (row + 1) * across], axis=1)
    pieces_own[rows:, :] = vec[...].astype(BF16)
    pieces_sib[rows:, :] = vec[...].astype(BF16)


def last(orders, x, sums1, sums2, sum_up, parts):
    length, width = x.shape
    piece = struct((width + 8, 3 * width // 2), BF16)
    return call(
        lambda *refs: last_kernel(*refs, orders=orders),
        "last",
        (piece, piece),
        [VMEM] * 10,
        (VMEM, VMEM),
        [
            pltpu.VMEM((width, 3 * width), BF16),
            pltpu.VMEM((8, 3 * width // 2), F32),
        ],
        10,
        7,
        (x, sums1, sums2, sum_up) + tuple(parts),
    )


def vectors_kernel(one_ref, two_ref, qv_ref, up_ref, *refs):
    t = lax.axis_index("tp")
    rows, cols = one_ref.shape
    across = cols // 128
    value = one_ref[rows - 8 :, :].astype(F32)
    if two_ref is not None:
        value = value + two_ref[rows - 8 :, :].astype(F32)

    def block(at):
        row, low = at // across, at % across * 128
        return value[row : row + 1, low : low + 128]

    def take(out, row, first, other, count):
        for i in range(count):
            one = block(first + i)
            if other != first:
                one = jnp.where(t == 0, one, block(other + i))
            if row is None:
                out[i * 128 : (i + 1) * 128] = one[0]
            else:
                out[row : row + 1, i * 128 : (i + 1) * 128] = one

    narrow, wide = qv_ref.shape[1] // 128, up_ref.shape[0] // 128
    for which in range(2):
        take(qv_ref, which, 2 * which * narrow, (2 * which + 1) * narrow, narrow)
    for i, ref in enumerate(refs):
        take(ref, None, (4 + 2 * i) * narrow, (4 + 2 * i) * narrow, 2 * narrow)
    base = (4 + 2 * len(refs)) * narrow
    take(up_ref, None, base, base + wide, wide)


def vectors(one, two, local_width, local_units):
    shapes = [(2, local_width), (local_units,)] + [(2 * local_width,)] * 6
    given = (one,) if two is None else (one, two)

    def kernel(*refs):
        if two is None:
            refs = (refs[0], None) + refs[1:]
        vectors_kernel(*refs)

    return call(
        kernel,
        "vectors",
        tuple(struct(shape, F32) for shape in shapes),
        [VMEM] * len(given),
        (VMEM,) * 8,
        [],
        1,
        4,
        given,
    )


def add_kernel(*refs, low, high, vec, count):
    terms, out = refs[:-1], refs[-1]
    total = terms[0][low:high, :].astype(F32)
    for term in terms[1:count]:
        total = total + term[low:high, :].astype(F32)
    out[: high - low, :] = total.astype(BF16)
    if vec:
        total = 0.0
        for i in vec:
            total = total + terms[i][terms[i].shape[0] - 8 :, :].astype(F32)
        out[high - low :, :] = total.astype(BF16)


def add_up(terms, low, high, vec=(), lone=(), time=1):
    count, terms = len(terms), list(terms) + list(lone)
    cols = terms[0].shape[1]
    return call(
        lambda *refs: add_kernel(*refs, low=low, high=high, vec=vec, count=count),
        "add",
        struct((high - low + (8 if vec else 0), cols), BF16),
        [VMEM] * len(terms),
        VMEM,
        [],
        time,
        4,
        tuple(terms),
    )


def deliver_kernel(own_ref, core_ref, x_ref, y_ref, out_ref):
    c, t = lax.axis_index("ctx"), lax.axis_index("tp")
    sources = [(own_ref, 0), (core_ref, 0), (x_ref, 0), (x_ref, 1)] + [(y_ref, i) for i in range(4)]
    for i, (ref, at) in enumerate(sources):
        ctx = c ^ ((i & 1) + (i & 2))
        out_ref[ctx * 2 + (t ^ (i >> 2))] = ref[at]


def deliver(own, core, x, y):
    return call(
        deliver_kernel,
        "deliver",
        struct((2 * own.shape[0],) + own.shape[1:], BF16),
        [VMEM] * 4,
        VMEM,
        [],
        3,
        7,
        (own, core, x, y),
    )


def input_back_kernel(weight_ref, gz1_ref, *refs, fast):
    parts, chunks_ref = refs[:6], refs[6]
    half = parts[0].shape[1]
    total = gz1_ref[...]
    for i, part in enumerate(parts):
        total = total + lax.dot_general(
            part[...], weight_ref[:, i * half : (i + 1) * half], NT, preferred_element_type=F32
        )
    total = total.astype(BF16)
    count, block = chunks_ref.shape[:2]
    for i in range(count):
        spot = i
        if fast:
            c = lax.axis_index("ctx") ^ i
            spot = (c & 1) * 2 + (c >> 1)
        chunks_ref[spot] = total[i * block : (i + 1) * block]


def input_back(weight, gz1, parts, chunk, fast):
    length, width = gz1.shape
    return call(
        lambda *refs: input_back_kernel(*refs, fast=fast),
        "input_back",
        struct((length // chunk, chunk, width), BF16),
        [VMEM] * 8,
        VMEM,
        [],
        2,
        3,
        (weight, gz1) + tuple(parts),
    )


def settle_kernel(*refs, cuts, count):
    given, outs, four = refs[:count], refs[count:-1], refs[-1]
    rows = four.shape[0] // 4
    for i in range(4):
        ref = given[i * count // 4]
        owner = lax.axis_index("ctx") ^ ((i & 1) * 2 + (i >> 1))
        low = i % (4 // count) * rows
        four[pl.ds(pl.multiple_of(owner * rows, 16), rows), :] = ref[low : low + rows, :].astype(F32)
    for out, (low, high, form) in zip(outs, cuts):
        if form == "plain":
            out[...] = four[:, low:high]
        else:
            step = (high - low) // 3
            for j in range(3):
                out[j] = four[:, low + j * step : low + (j + 1) * step]


def settle(given, cuts):
    rows, cols = given[0].shape[0] * len(given) // 4, given[0].shape[1]
    shapes = {"plain": lambda n: (4 * rows, n), "three": lambda n: (3, 4 * rows, n // 3)}
    return call(
        lambda *refs: settle_kernel(*refs, cuts=cuts, count=len(given)),
        "settle",
        tuple(struct(shapes[form](high - low), F32) for low, high, form in cuts),
        [VMEM] * len(given),
        (VMEM,) * len(cuts),
        [pltpu.VMEM((4 * rows, cols), F32)],
        3,
        7,
        tuple(given),
    )


def cut(full):
    rows, cols = full.shape
    return full[:, : cols // 2], full[:, cols // 2 :]


def gather_plain(shard):
    rows = lax.all_gather(shard, "fsdp", axis=0, tiled=True)
    return lax.all_gather(rows, "tp", axis=1, tiled=True)


def reduce_plain(own, sib):
    full = jnp.concatenate([own, sib], axis=1)
    part = lax.psum_scatter(full, "tp", scatter_dimension=1, tiled=True)
    part = lax.psum_scatter(part, "fsdp", scatter_dimension=0, tiled=True)
    return lax.psum(part, "ctx").astype(F32)


def body(
    layer_input,
    doc_ids,
    w_qkv,
    b_qv,
    w_out,
    b_out,
    ln1_gain,
    ln1_bias,
    w_up,
    b_up,
    w_down,
    b_down,
    ln2_gain,
    ln2_bias,
    out_grad,
):
    sizes = (lax.axis_size("fsdp"), lax.axis_size("ctx"), lax.axis_size("tp"))
    micro, seqs, local_len, width = layer_input.shape
    length = local_len * sizes[1]
    shard_rows, local_width = w_qkv.shape[1:]
    local_units = w_up.shape[1]
    heads = width // HEAD_DIM
    fast = sizes == (4, 4, 2)
    t = lax.axis_index("tp")
    c = lax.axis_index("ctx")

    def mine(value):
        return lax.dynamic_index_in_dim(value, t, 1, keepdims=False)

    def to_owners(chunks):
        return lax.all_to_all(chunks, "ctx", 0, 0, tiled=True)

    def spread(chunks):
        out = lax.all_to_all(chunks, ("ctx", "tp"), 0, 0, tiled=True)
        return out.reshape(micro, seqs, local_len, width)

    shards = (
        jnp.swapaxes(w_qkv, 0, 1).reshape(shard_rows, 3 * local_width),
        jnp.concatenate([w_out.T, w_up], axis=1),
        w_down.T,
    )
    ids = mine(doc_ids).astype(BF16)[:, None, :]
    ids = jnp.pad(ids, ((0, 0), (0, 7), (0, width - local_len)))
    rows_in = jnp.concatenate([mine(layer_input), ids], axis=1)
    cot_in = mine(out_grad)
    gathers = GATHER if fast else (None,) * 3
    packs = tuple(packing(order) for order in SCATTER) if fast else (None,) * 3

    def swap(value, group, step):
        order = tuple(zip(*GATHER[group])) + (CORE,)
        return exchange(value, order[step], sizes)

    def shed(value, group, step):
        order = (CORE,) + tuple(zip(*SCATTER[group]))
        return exchange(value, order[step], sizes)

    def joined(*parts):
        return jnp.concatenate(parts, axis=0)

    if fast:
        def seen(value):
            return [lax.dynamic_index_in_dim(value, c ^ i, 0, keepdims=True) for i in range(4)]

        part = shard_rows // 4
        h1 = lax.dynamic_slice_in_dim(w_qkv, c * part, part, 1)
        h1 = jnp.swapaxes(h1, 0, 1).reshape(part, 3 * local_width)
        h2, h3 = [lax.dynamic_slice_in_dim(s, c * part, part, 0) for s in shards[1:]]
        g1 = swap(h1, 0, 0)
        h3 = after(h3, h1)
        x0, x1, x2, x3 = seen(after(rows_in, h1))
        g1, g3, x1, x2, x3, h2, cot_in, b_up = phase(g1, swap(h3, 2, 0), x1, x2, x3, h2, cot_in, b_up)
        h1, h3 = joined(h1, g1), joined(h3, g3)
        g1, g3, xk, xx, xd = phase(
            swap(h1, 0, 1), swap(h3, 2, 1), exchange(x1, CORE, sizes), exchange(x2, X, sizes), exchange(x3, FAR, sizes)
        )
        given = (x0, xk, joined(xx, xd))
        h1, h2, h3, cot_in, b_up = phase(joined(h1, g1), h2, joined(h3, g3), cot_in, b_up)
        g1, g2 = swap(h1, 0, 2), swap(h2, 1, 0)
        c0, c1, c2, c3 = seen(cot_in)
        c_send = joined(c1, c3)
        table, small = tables(b_qv, b_up, (b_out, ln1_gain, ln1_bias, b_down, ln2_gain, ln2_bias))
        g1, g2, c_send, small = phase(g1, g2, c_send, small)
        h1, h2, h3 = phase(joined(h1, g1), joined(h2, g2), h3)
        g1, g2, ck, got, f1 = phase(
            swap(h1, 0, 3),
            swap(h2, 1, 1),
            exchange(c_send, CORE, sizes),
            exchange(small, Y, sizes),
            exchange(h1, CORE, sizes),
        )
        small = joined(small, got)
        g1, h2, h3 = phase(g1, joined(h2, g2), h3)
        k1, g2, g3 = exchange(g1, CORE, sizes), swap(h2, 1, 2), swap(h3, 2, 2)
        (wq,) = unpack(gathers[0], (h1, g1), (f1, k1), (3 * width,))
        proj, rows_b, mask = project(wq, given, small, fast)
        proj, g2, c2, ck = phase(proj, g2, c2, ck)
        h2 = joined(h2, g2)
        g2 = swap(h2, 1, 3)
        mixed0, probs0 = attend(after(proj, h2), mask, 0)
        mixed0, g3, h2 = phase(mixed0, g3, h2)
        h3 = joined(h3, g3)
        f2, g3, f3 = exchange(h2, CORE, sizes), swap(h3, 2, 3), exchange(h3, CORE, sizes)
        mixed1, probs1 = attend(after(proj, h3, mixed0), mask, 1)
        mixed1, g2, f2 = phase(mixed1, g2, f2)
        g2, c_send = phase(g2, joined(c2, ck[1:]))
        k2, cx = exchange(g2, CORE, sizes), exchange(c_send, X, sizes)
        wo, wu = unpack(gathers[1], (h2, g2), (f2, k2), (width, 2 * local_units))
    else:
        parts = (shards[0], w_out.T, w_up, w_down.T)
        pieces = [cut(gather_plain(s)) for s in parts]
        split = lambda pair: ((pair[0],), (pair[1],))
        (wq,) = unpack(None, *split(pieces[0]), (3 * width,))
        (wo,) = unpack(None, *split(pieces[1]), (width,))
        (wu,) = unpack(None, *split(pieces[2]), (2 * local_units,))
        (wd,) = unpack(None, *split(pieces[3]), (2 * local_units,))
        order = lambda value: (value[:1], value[1:3], value[2:])
        given, cot = order(to_owners(rows_in)), order(to_owners(cot_in))
        table, small = tables(b_qv, b_up, (b_out, ln1_gain, ln1_bias, b_down, ln2_gain, ln2_bias))
        small = joined(small, exchange(small, Y, sizes))
        proj, rows_b, mask = project(wq, given, small, fast)
        mixed0, probs0 = attend(proj, mask, 0)
        mixed1, probs1 = attend(proj, mask, 1)

    normed1, scale1, first_b, act, slope = middle(wo, wu, mixed0, mixed1, rows_b, table, small)
    if fast:
        act, g3, f3, cx = phase(act, g3, f3, cx)
        cot = (c0, ck, cx)
        (wd,) = unpack(gathers[2], (h3, g3), (f3, exchange(g3, CORE, sizes)), (2 * local_units,))
    chunks, gz, gzb, sums2, down_own, down_sib = turn(packs[2], wd, act, normed1, cot, table, local_len)

    rows = shard_rows // 4
    if fast:
        down_sib, chunks, gzb = phase(down_sib, chunks, gzb)
        got, core_out = shed(down_sib, 2, 0), exchange(chunks[2:], CORE, sizes)
    gh, sum_up = hidden_back(wd, gzb, slope)
    if fast:
        gh, got, core_out = phase(gh, got, core_out)
        down = [down_own, got]
        send, x_send, gh = phase(
            add_up(down, 8 * rows, 16 * rows), joined(chunks[1:2], core_out[1:2]), gh
        )
        got, x_out = shed(send, 2, 1), exchange(x_send, X, sizes)
    gz1, grad_mixed, sums1, up_own, up_sib = first_back(
        packs[1], wo, wu, gh, gz, normed1, scale1, table, first_b, mixed0, mixed1
    )
    if fast:
        grad_mixed, up_sib, got, x_out = phase(grad_mixed, up_sib, got, x_out)
        down = down + [got]
        send, y_send, grad_mixed = phase(
            add_up(down, 4 * rows, 8 * rows), joined(chunks[:1], core_out[:1], x_out), grad_mixed
        )
        got, got2, y_out = shed(send, 2, 2), shed(up_sib, 1, 0), exchange(y_send, Y, sizes)
    parts0 = attend_back(proj, probs0, grad_mixed, 0)
    if fast:
        head, got2, grad_mixed = phase(parts0[0], got2, grad_mixed)
        parts0 = (head,) + tuple(parts0[1:])
        up = [up_own, got2]
        send2, grad_mixed = phase(add_up(up, 8 * rows, 16 * rows), grad_mixed)
        got2 = shed(send2, 1, 1)
    parts1 = attend_back(proj, probs1, grad_mixed, 1)
    parts = list(parts0) + list(parts1)
    if fast:
        parts[3], got = phase(parts[3], got)
        down = down + [got]
        send = add_up(down, 2 * rows, 4 * rows)
        got = shed(send, 2, 3)
        parts[3], send = phase(parts[3], send)
    chunks2 = input_back(wq, gz1, parts, local_len, fast)
    if fast:
        chunks2, y_out = phase(chunks2, y_out)
    parts[0] = after(parts[0], chunks2)
    qkv_own, qkv_sib = last(packs[0], rows_b, sums1, sums2, sum_up, parts)
    if fast:
        got3, core_x = shed(qkv_sib, 0, 0), exchange(chunks2[2:], CORE, sizes)
        chunks2, qkv_own, got2 = phase(chunks2, qkv_own, got2)
        up = up + [got2]
        send2 = add_up(up, 4 * rows, 8 * rows, time=30)
        send2, got3 = phase(send2, got3)
        got2 = shed(send2, 1, 2)
        got3, core_x = phase(got3, core_x)
        qkv = [qkv_own, got3]
        sent3 = add_up(qkv, 8 * rows, 16 * rows, (0, 1))
        x_send = joined(chunks2[1:2], core_x[1:2])
        got3 = shed(sent3, 0, 1)
        got3, x_send = phase(got3, x_send)
        qkv = qkv + [got3]
        send3 = add_up(qkv, 4 * rows, 8 * rows, (3, 2), [sent3])
        got3 = shed(send3, 0, 2)
        send3, got, x_send = phase(send3, got, x_send)
        down = down + [got]
        send = add_up(down, rows, 2 * rows)
        got, x_x = shed(send, 2, 4), exchange(x_send, X, sizes)
        send, got2 = phase(send, got2)
        up = up + [got2]
        send2 = add_up(up, 2 * rows, 4 * rows)
        got2 = shed(send2, 1, 3)
        got3, send2 = phase(got3, send2)
        qkv = qkv + [got3]
        sent3 = add_up(qkv, 2 * rows, 4 * rows, (4, 3), [send3])
        got3 = shed(sent3, 0, 3)
        sent3, got, x_x = phase(sent3, got, x_x)
        pair1 = add_up(down + [got], 0, rows)
        y_send = joined(chunks2[:1], core_x[:1], x_x)
        got, y_x = exchange(pair1, X, sizes), exchange(y_send, Y, sizes)
        pair1, got2 = phase(pair1, got2)
        up = up + [got2]
        send2 = add_up(up, rows, 2 * rows)
        got2 = shed(send2, 1, 4)
        layer_output = deliver(chunks, core_out, x_out, after(y_out, send2))
        got3, layer_output = phase(got3, layer_output)
        qkv = qkv + [got3]
        send3 = add_up(qkv, rows, 2 * rows, (5, 4), [sent3])
        got3 = shed(send3, 0, 4)
        send3, got, got2 = phase(send3, got, got2)
        pair1 = joined(pair1, got)
        up = up + [got2]
        pair2 = add_up(up, 0, rows)
        got2 = exchange(pair2, X, sizes)
        got3, pair1, pair2 = phase(got3, pair1, pair2)
        qkv = qkv + [got3]
        sent_last = got3
        piece = add_up(qkv, 0, rows)
        got3 = [exchange(piece, dims, sizes) for dims in (X, CORE, FAR)]
        got1 = exchange(after(pair1, piece), CORE, sizes)
        vec = vectors(after(send3, piece), sent_last, local_width, local_units)
        piece, got1, bup = phase(piece, got1, vec[1])
        vec = (vec[0], bup) + tuple(vec[2:])
        (grad_down,) = settle((pair1, got1), ((0, local_units, "plain"),))
        grad_down, got2 = phase(grad_down, got2)
        pair2 = joined(pair2, got2)
        got2 = exchange(pair2, CORE, sizes)
        pair2, y_x = phase(pair2, y_x)
        grad_x = deliver(chunks2, core_x, x_x, y_x)
        grad_x, *got3 = phase(grad_x, *got3)
        (grad_qkv,) = settle([piece] + got3, ((0, 3 * local_width, "three"),))
        grad_wout, grad_up = settle(
            (pair2, after(got2, grad_qkv)),
            ((0, local_width, "plain"), (local_width, local_width + local_units, "plain")),
        )
        layer_output = layer_output.reshape(micro, seqs, local_len, width)
        grad_x = grad_x.reshape(micro, seqs, local_len, width)
    else:
        layer_output = spread(jnp.repeat(chunks, 2, axis=0))
        grad_x = spread(jnp.repeat(chunks2, 2, axis=0))
        vec = lax.psum(qkv_own[width:].astype(F32), AXES)
        vec = vectors(vec, None, local_width, local_units)
        grad_down = reduce_plain(down_own, down_sib)
        both = reduce_plain(up_own, up_sib)
        grad_wout, grad_up = both[:, :local_width], both[:, local_width:]
        grad_qkv = reduce_plain(qkv_own[:width], qkv_sib[:width])
        grad_qkv = jnp.swapaxes(grad_qkv.reshape(shard_rows, 3, local_width), 0, 1)

    out_bqv, out_bup, g1, s1, bout, g2, s2, bdown = vec
    return (
        layer_output,
        grad_x,
        grad_qkv,
        out_bqv,
        grad_wout.T,
        bout,
        g1,
        s1,
        grad_up,
        out_bup,
        grad_down.T,
        bdown,
        g2,
        s2,
    )


def solution(mesh):
    return jax.shard_map(
        body,
        mesh=mesh,
        in_specs=(
            P(None, "fsdp", "ctx", None),
            P(None, "fsdp", "ctx"),
            P(None, "fsdp", "tp"),
            P(None, "tp"),
            P("tp", "fsdp"),
            P(),
            P(),
            P(),
            P("fsdp", "tp"),
            P("tp"),
            P("tp", "fsdp"),
            P(),
            P(),
            P(),
            P(None, "fsdp", "ctx", None),
        ),
        out_specs=(
            P(None, "fsdp", "ctx", None),
            P(None, "fsdp", "ctx", None),
            P(None, "fsdp", "tp"),
            P(None, "tp"),
            P("tp", "fsdp"),
            P(),
            P(),
            P(),
            P("fsdp", "tp"),
            P("tp"),
            P("tp", "fsdp"),
            P(),
            P(),
            P(),
        ),
        check_vma=False,
    )
```
